32 devices in a mesh: dp: 4 (over y, x), fsdp: 8 (over z, core).
Axes of the slice: x: 2, y: 2, z: 4, core: 2. Of those that a mesh axis runs over, the one named last changes fastest.
Arguments:
- tokens: bfloat16 [8, 2048, 1792], P('dp', 'fsdp'), may hold values from -6 to 6
- cotangent: bfloat16 [8, 2048, 1792], P('dp', 'fsdp'), may hold values from -6 to 6
- lengths: int32 [8], P('dp'), may hold values from 1024 to 2048, as said below
- w_qk: float32 [1792, 512], P(('dp', 'fsdp')), may hold values from -0.125 to 0.125
- w_value: float32 [1792, 1792], P(('dp', 'fsdp')), may hold values from -0.125 to 0.125
- w_out: float32 [1792, 1792], P(('dp', 'fsdp')), may hold values from -1.5 to 1.5
- w_gu: float32 [1792, 9728], P(('dp', 'fsdp')), may hold values from -0.125 to 0.125
- w_down: float32 [1792, 4864], P(('dp', 'fsdp')), may hold values from -0.21875 to 0.21875
- small_params: float32 [1792, 5], P(('dp', 'fsdp')), may hold values from 0.5 to 1.5
- m_qk: float32 [1792, 512], P(('dp', 'fsdp')), may hold values from -28672 to 28672
- m_value: float32 [1792, 1792], P(('dp', 'fsdp')), may hold values from -14336 to 14336
- m_out: float32 [1792, 1792], P(('dp', 'fsdp')), may hold values from -1280 to 1280
- m_gu: float32 [1792, 9728], P(('dp', 'fsdp')), may hold values from -5120 to 5120
- m_down: float32 [1792, 4864], P(('dp', 'fsdp')), may hold values from -3584 to 3584
- m_small: float32 [1792, 5], P(('dp', 'fsdp')), may hold values from -19941.367 to 19941.367
- v_qk: float32 [1792, 512], P(('dp', 'fsdp')), may hold values from 12939.913 to 51759.652
- v_value: float32 [1792, 1792], P(('dp', 'fsdp')), may hold values from 3533.0715 to 14129.249
- v_out: float32 [1792, 1792], P(('dp', 'fsdp')), may hold values from 26.888407 to 107.54147
- v_gu: float32 [1792, 9728], P(('dp', 'fsdp')), may hold values from 448.69705 to 1795.236
- v_down: float32 [1792, 4864], P(('dp', 'fsdp')), may hold values from 233.0624 to 932.2496
- v_small: float32 [1792, 5], P(('dp', 'fsdp')), may hold values from 1163.5137 to 28711.144
Outputs:
- layer_out: bfloat16 [8, 2048, 1792], P('dp', 'fsdp')
- input_grad: float32 [8, 2048, 1792], P('dp', 'fsdp')
- grad_qk: float32 [1792, 512], P(('dp', 'fsdp'))
- grad_value: float32 [1792, 1792], P(('dp', 'fsdp'))
- grad_out: float32 [1792, 1792], P(('dp', 'fsdp'))
- grad_gu: float32 [1792, 9728], P(('dp', 'fsdp'))
- grad_down: float32 [1792, 4864], P(('dp', 'fsdp'))
- grad_small: float32 [1792, 5], P(('dp', 'fsdp'))
- new_qk: float32 [1792, 512], P(('dp', 'fsdp'))
- new_value: float32 [1792, 1792], P(('dp', 'fsdp'))
- new_out: float32 [1792, 1792], P(('dp', 'fsdp'))
- new_gu: float32 [1792, 9728], P(('dp', 'fsdp'))
- new_down: float32 [1792, 4864], P(('dp', 'fsdp'))
- new_small: float32 [1792, 5], P(('dp', 'fsdp'))
- moment_qk: float32 [1792, 512], P(('dp', 'fsdp'))
- moment_value: float32 [1792, 1792], P(('dp', 'fsdp'))
- moment_out: float32 [1792, 1792], P(('dp', 'fsdp'))
- moment_gu: float32 [1792, 9728], P(('dp', 'fsdp'))
- moment_down: float32 [1792, 4864], P(('dp', 'fsdp'))
- moment_small: float32 [1792, 5], P(('dp', 'fsdp'))
The draws below stay inside these ranges and needn't reach their ends.
Inputs may be any that keep to these rules, and one draw needn't show every extreme that they name: `lengths`: each slot holds one sequence from its first position; positions at or past its length are padding. Some slot has length 2048 and some 2048 // 2.
All inputs are finite; a program needn't handle non-finite values.
Results may differ from the reference program's by a relative error of at most 0.015.
The reference program's roundings to bfloat16 on the way count: a program that leaves them out, or rounds other values in their place, can miss the bound.
Values may be sent and summed in bfloat16 or wider, within the bound.
A program may use at most 576 MiB of HBM per device.

```python
import math
import jax
import jax.numpy as jnp
from jax import lax

D = 1792
H = 16
F = 16
FF = 4864
KS = 3
SLOT = 2048
STEP = 10
SLOTS = 8
TOKENS = 16384


def draw_lengths(key, part):
    first_key, second_key = jax.random.split(jax.random.fold_in(key, 17))
    drawn = jax.random.randint(first_key, (SLOTS,), SLOT // 2, SLOT + 1, dtype=jnp.int32)
    order = jax.random.permutation(second_key, SLOTS)
    drawn = drawn.at[order[0]].set(SLOT).at[order[1]].set(SLOT // 2)
    return drawn.astype(jnp.int32)


def column_scales():
    factors = jnp.array([27.0] * KS + [67.0, 39.0], jnp.float32)
    return factors * SLOT ** (-0.4125) * TOKENS ** 0.5


def draw_m_small(key, part):
    noise = jax.random.normal(jax.random.fold_in(key, 29), (D, KS + 2), jnp.float32)
    noise = jnp.clip(noise, -6.0, 6.0)
    return (9.0 * column_scales()[None, :] * noise).astype(jnp.float32)


def draw_v_small(key, part):
    spread = jax.random.uniform(jax.random.fold_in(key, 31), (D, KS + 2), jnp.float32, 0.0, 1.3862944)
    scales = column_scales()
    return ((scales * scales)[None, :] / 19.0 * jnp.exp(spread)).astype(jnp.float32)


def with_spikes(values, rng, source, target, parts, factor):
    def block_of(dim):
        return (jnp.arange(values.shape[dim]) // (values.shape[dim] // parts)).reshape((-1,) + (1,) * (values.ndim - 1 - dim))

    first = jax.random.permutation(rng, parts)[block_of(target)]
    other_side = (block_of(target) + parts // 2) % parts
    return jnp.where((block_of(source) == first) | (block_of(source) == other_side), factor * values, values)


def level_of(rng, extent, pieces, least, largest):
    loudness, own = 1.0, jax.random.fold_in(rng, 6)
    for axis_at, shards_of in pieces:
        draws = jnp.exp(jax.random.uniform(jax.random.fold_in(own, axis_at), (shards_of,), jnp.float32, least / len(pieces), largest / len(pieces)))
        loudness = loudness * jnp.repeat(draws, extent[axis_at] // shards_of).reshape([-1 if axis == axis_at else 1 for axis in range(len(extent))])
    return loudness


def gaussian(rng, shape, scale, reach, shards=(), held_as=jnp.bfloat16):
    factor_of = level_of(rng, shape, shards, -0.22, 0.18) if shards else 1.0
    values = jax.random.normal(rng, shape, jnp.float32) * scale * factor_of
    return jnp.minimum(jnp.maximum(values, -reach), reach).astype(held_as)


def noise_with(stream_key, extent, scale, reach, pieces, heavy, held_as=jnp.bfloat16):
    values = scale * jax.random.normal(stream_key, extent, jnp.float32)
    if pieces:
        values = values * level_of(stream_key, extent, pieces, -0.22, 0.18)
    return jnp.clip(with_spikes(values, jax.random.fold_in(stream_key, 3), *heavy), -reach, reach).astype(held_as)


def setup_inputs(seed: int = 0) -> dict:
    streams_of = jax.random.split(jax.random.key(seed), 22)
    return {
        "tokens": gaussian(streams_of[0], (SLOTS, SLOT, D), 1.0, 6.0, ((0, 4), (1, 8))),
        "cotangent": noise_with(streams_of[1], (SLOTS, SLOT, D), 1.0, 6.0, ((0, 4), (1, 8)), (0, 2, 4, 2.0)),
        "lengths": draw_lengths(jax.random.fold_in(streams_of[21], 71), 0),
        "w_qk": gaussian(streams_of[3], (D, 2 * H * F), D ** -0.5, 0.125, ((0, 32),), jnp.float32),
        "w_value": gaussian(streams_of[4], (D, D), D ** -0.5, 0.125, ((0, 32),), jnp.float32),
        "w_out": gaussian(streams_of[5], (D, D), (max(D // 128, 1)) ** -0.5, 1.5, ((0, 32),), jnp.float32),
        "w_gu": gaussian(streams_of[6], (D, 2 * FF), D ** -0.5, 0.125, ((0, 32),), jnp.float32),
        "w_down": gaussian(streams_of[7], (D, FF), (FF * SLOT ** 0.825 * 0.0003) ** -0.5, 0.21875, ((0, 32),), jnp.float32),
        "small_params": jnp.clip(1.0 + 0.1 * jax.random.normal(streams_of[8], (D, KS + 2), jnp.float32), 0.5, 1.5),
        "m_qk": gaussian(streams_of[9], (D, 2 * H * F), (306 * SLOT ** -0.4125 * (D * H ** -1 * F ** -1) ** 0.5 * TOKENS ** 0.5), 28672.0, ((0, 32),), jnp.float32),
        "m_value": gaussian(streams_of[10], (D, D), (423 * SLOT ** -0.4125 * TOKENS ** 0.5), 14336.0, ((0, 32),), jnp.float32),
        "m_out": gaussian(streams_of[11], (D, D), (37 * SLOT ** -0.4125 * TOKENS ** 0.5), 1280.0, ((0, 32),), jnp.float32),
        "m_gu": gaussian(streams_of[12], (D, 2 * FF), (248 * SLOT ** -0.4125 * (D * FF ** -1) ** 0.5 * TOKENS ** 0.5), 5120.0, ((0, 32),), jnp.float32),
        "m_down": gaussian(streams_of[13], (D, FF), (4.7 * TOKENS ** 0.5), 3584.0, ((0, 32),), jnp.float32),
        "m_small": draw_m_small(jax.random.fold_in(streams_of[21], 71), 0),
        "v_qk": jnp.clip(jnp.exp(math.log(51759.652) - 1.3862944 * jax.random.uniform(streams_of[15], (D, 2 * H * F), jnp.float32) ** level_of(streams_of[15], (D, 2 * H * F), ((0, 32),), -0.2, 0.2)), 12939.913, 51759.652),
        "v_value": jnp.clip(jnp.exp(math.log(14129.249) - 1.3860794 * jax.random.uniform(streams_of[16], (D, D), jnp.float32) ** level_of(streams_of[16], (D, D), ((0, 32),), -0.2, 0.2)), 3533.0715, 14129.249),
        "v_out": jnp.clip(jnp.exp(math.log(107.54147) - 1.3861814 * jax.random.uniform(streams_of[17], (D, D), jnp.float32) ** level_of(streams_of[17], (D, D), ((0, 32),), -0.2, 0.2)), 26.888407, 107.54147),
        "v_gu": jnp.clip(jnp.exp(math.log(1795.236) - 1.3865438 * jax.random.uniform(streams_of[18], (D, 2 * FF), jnp.float32) ** level_of(streams_of[18], (D, 2 * FF), ((0, 32),), -0.2, 0.2)), 448.69705, 1795.236),
        "v_down": jnp.clip(jnp.exp(math.log(932.2496) - 1.3862944 * jax.random.uniform(streams_of[19], (D, FF), jnp.float32) ** level_of(streams_of[19], (D, FF), ((0, 32),), -0.2, 0.2)), 233.0624, 932.2496),
        "v_small": draw_v_small(jax.random.fold_in(streams_of[21], 71), 0),
    }


norm_epsilon = 1e-06
beta_first = 0.9
beta_second = 0.95
adam_epsilon = 1e-08
weight_decay = 3e-05
highest_precision = lax.Precision.HIGHEST

@jax.custom_vjp
def low(v):
    return lax.optimization_barrier(v.astype(jnp.bfloat16)).astype(jnp.float32)

@jax.custom_vjp
def low_back(v):
    return v

def low_keep(v):
    return (low(v), None)

def low_pass(kept, grad):
    return (grad,)

def back_keep(v):
    return (v, None)

def back_low(kept, grad):
    return (low(grad),)
low.defvjp(low_keep, low_pass)
low_back.defvjp(back_keep, back_low)

def matmul(left_side, right_side):
    return jnp.dot(left_side, right_side, precision=highest_precision)

def rms_norm(values, gain_row):
    inverse = lax.rsqrt(lax.optimization_barrier(jnp.mean(values * values, axis=-1, keepdims=True)) + norm_epsilon)
    return values * inverse * gain_row

def slot_attention(queries, key_heads, values):
    length = queries.shape[0]
    block_rows = min(512, length)
    scale_factor = 1.0 / math.sqrt(F)
    columns = jnp.arange(length, dtype=jnp.int32)

    def one_block(block_index):
        row_start = block_index * block_rows
        rows_query = lax.dynamic_slice_in_dim(queries, row_start, block_rows, 0)
        scores = jnp.einsum('thf,uhf->htu', rows_query, key_heads, precision=highest_precision) * scale_factor
        positions = row_start + jnp.arange(block_rows, dtype=jnp.int32)
        allowed = columns[None, None, :] <= positions[None, :, None]
        kernel = jnp.where(allowed, 1.0 + scores + 0.5 * scores * scores, 0.0)
        numerator = jnp.einsum('htu,uhe->the', kernel, values, precision=highest_precision)
        denominator = lax.optimization_barrier(jnp.sum(kernel, axis=-1))
        return numerator / jnp.transpose(denominator)[:, :, None]
    blocks = lax.map(jax.checkpoint(one_block), jnp.arange(length // block_rows, dtype=jnp.int32))
    return blocks.reshape(length, H, D // H)

def slot_forward(weights, inputs, valid_row):
    w_qk, w_value, w_out, w_gu, w_down, small_set = weights
    length = inputs.shape[0]
    normed_first = low(rms_norm(inputs, small_set[:, KS]))
    query_key = low(low_back(matmul(normed_first, w_qk)))
    queries = query_key[:, :H * F].reshape(length, H, F)
    key_heads = query_key[:, H * F:].reshape(length, H, F)
    value_pre = low(low_back(matmul(normed_first, w_value)))
    padded = jnp.concatenate([jnp.zeros((KS - 1, D), jnp.float32), value_pre], axis=0)
    convolved = small_set[:, 0] * padded[KS - 1:KS - 1 + length]
    for tap_index in range(1, KS):
        convolved = convolved + small_set[:, tap_index] * padded[KS - 1 - tap_index:KS - 1 - tap_index + length]
    values = low(low_back(convolved)).reshape(length, H, D // H)
    mixer_out = low(low_back(slot_attention(queries, key_heads, values).reshape(length, D)))
    after_mixer = inputs + low_back(matmul(mixer_out, w_out))
    normed_second = low(rms_norm(after_mixer, small_set[:, KS + 1]))
    gate_up = low_back(matmul(normed_second, w_gu))
    hidden = low(jax.nn.silu(gate_up[:, :FF]) * gate_up[:, FF:])
    result = after_mixer + low_back(matmul(hidden, jnp.transpose(w_down)))
    return valid_row[:, None] * result

def adam_update(weight, gradient, first_moment, second_moment, learn_rate, decay_rate):
    first_new = beta_first * first_moment + (1.0 - beta_first) * gradient
    second_new = beta_second * second_moment + (1.0 - beta_second) * gradient * gradient
    first_hat = first_new / (1.0 - beta_first ** STEP)
    second_hat = second_new / (1.0 - beta_second ** STEP)
    new_weight = weight - learn_rate * first_hat / (jnp.sqrt(second_hat) + adam_epsilon) - decay_rate * weight
    return (new_weight, second_new)

def reference(tokens, cotangent, lengths, w_qk, w_value, w_out, w_gu, w_down, small_params, m_qk, m_value, m_out, m_gu, m_down, m_small, v_qk, v_value, v_out, v_gu, v_down, v_small):
    valid_mask = (jnp.arange(SLOT, dtype=jnp.int32)[None, :] < lengths[:, None]).astype(jnp.float32)
    masters = (w_qk, w_value, w_out, w_gu, w_down, small_params)

    def forward(inputs, params):
        rounded = tuple((low(matrix) for matrix in params))

        def per_slot(slot_pair):
            return slot_forward(rounded, slot_pair[0], slot_pair[1])
        return lax.map(per_slot, (inputs, valid_mask))
    output, pullback = jax.vjp(forward, tokens.astype(jnp.float32), masters)
    input_grad, weight_grads = pullback(cotangent.astype(jnp.float32))
    firsts = (m_qk, m_value, m_out, m_gu, m_down, m_small)
    seconds = (v_qk, v_value, v_out, v_gu, v_down, v_small)
    learn_rates = (0.05 / math.sqrt(D), 0.05 / math.sqrt(D), 0.05 / math.sqrt(max(D // 128, 1)), 0.05 / math.sqrt(D), 0.05 / math.sqrt(0.0003 * FF * SLOT ** 0.825), 0.014)
    decays = (weight_decay, weight_decay, weight_decay, weight_decay, weight_decay, 0.0)
    new_weights = []
    new_seconds = []
    for position in range(6):
        updated, moment = adam_update(masters[position], weight_grads[position], firsts[position], seconds[position], learn_rates[position], decays[position])
        new_weights.append(updated)
        new_seconds.append(moment)
    return (output.astype(jnp.bfloat16), input_grad, weight_grads[0], weight_grads[1], weight_grads[2], weight_grads[3], weight_grads[4], weight_grads[5], new_weights[0], new_weights[1], new_weights[2], new_weights[3], new_weights[4], new_weights[5], new_seconds[0], new_seconds[1], new_seconds[2], new_seconds[3], new_seconds[4], new_seconds[5])
```

```python
import functools
import math

import jax
import jax.numpy as jnp
import numpy as np
from jax import lax
from jax.experimental import pallas as pl
from jax.experimental.pallas import tpu as pltpu
from jax.sharding import Mesh
from jax.sharding import PartitionSpec as P

D = 1792
H = 16
F = 16
FF = 4864
KS = 3
SLOT = 2048
STEP = 10

CORES = 2
HC = H // CORES
HW = D // H
VC = HC * HW
QC = HC * F
FC = FF // CORES
LANES = 128
FEATS = 256
FROWS = 160
SCALE = 1.0 / math.sqrt(F)

norm_epsilon = 1e-06
beta_first = 0.9
beta_second = 0.95
adam_epsilon = 1e-08
weight_decay = 3e-05

bf16 = jnp.bfloat16
f32 = jnp.float32


def feature_tables():
    index = np.full((8, FEATS), -4096, np.int32)
    scale = np.zeros((8, FEATS), np.float32)
    scale[0, 0] = scale[1, 0] = scale[2, 0] = 1.0
    at = 1
    for i in range(F):
        index[0, at] = i
        scale[1, at] = 1.0
        scale[2, at] = SCALE
        at += 1
    for i in range(F):
        for j in range(i, F):
            index[0, at] = i
            index[1, at] = j
            scale[2, at] = (1.0 if i == j else 2.0) * 0.5 * SCALE * SCALE
            at += 1
    return index, scale


def dot(a, b):
    return lax.dot_general(a, b, (((1,), (0,)), ((), ())), preferred_element_type=f32)


def dot_nt(a, b):
    return lax.dot_general(a, b, (((1,), (1,)), ((), ())), preferred_element_type=f32)


def dot_tn(a, b):
    return lax.dot_general(a, b, (((0,), (0,)), ((), ())), preferred_element_type=f32)


def selectors(index_ref, head):
    lane = lax.broadcasted_iota(jnp.int32, (LANES, FEATS), 0) - head * F
    first = jnp.where(lane == index_ref[0:1, :], 1.0, 0.0).astype(bf16)
    second = jnp.where(lane == index_ref[1:2, :], 1.0, 0.0).astype(bf16)
    return first, second


def factors(rows, first, second, scale_ref):
    return (dot(rows, first) + scale_ref[0:1, :], dot(rows, second) + scale_ref[1:2, :])


def window(head):
    start = head * HW
    base = min(start // LANES * LANES, VC - 2 * LANES)
    return base, start - base


def head_columns(ref, head):
    base, offset = window(head)
    wide = ref[:, base : base + 2 * LANES].astype(f32)
    if offset:
        wide = pltpu.roll(wide, 2 * LANES - offset, 1)
    return wide[:, :LANES]


def add_head_columns(ref, head, block):
    base, offset = window(head)
    wide = jnp.concatenate([block, jnp.zeros_like(block)], axis=1)
    if offset:
        wide = pltpu.roll(wide, offset, 1)
    ref[:, base : base + 2 * LANES] += wide


def with_one(block):
    lane = lax.broadcasted_iota(jnp.int32, block.shape, 1)
    return jnp.where(lane < HW, block, jnp.where(lane == HW, 1.0, 0.0))


def only_head(rows, head):
    lane = lax.broadcasted_iota(jnp.int32, rows.shape, 1)
    inside = (lane >= head * F) & (lane < head * F + F)
    return jnp.where(inside, rows.astype(f32), 0.0).astype(bf16)


def state_kernel(index_ref, scale_ref, k_ref, v_ref, state_ref):
    keys = k_ref[...]
    for head in range(HC):
        first, second = selectors(index_ref, head)
        one, two = factors(keys, first, second, scale_ref)
        phi = (one * two * scale_ref[2:3, :]).astype(bf16)
        values = with_one(head_columns(v_ref, head)).astype(bf16)
        state_ref[0, head] = dot_tn(phi, values)[:FROWS]


def scores_of(q_head, keys):
    scores = dot_nt(q_head, keys) * SCALE
    row = lax.broadcasted_iota(jnp.int32, scores.shape, 0)
    column = lax.broadcasted_iota(jnp.int32, scores.shape, 1)
    return scores, column <= row


def forward_kernel(index_ref, scale_ref, q_ref, k_ref, v_ref, before_ref, mixer_ref, den_ref, wide):
    queries = q_ref[...]
    keys = k_ref[...]
    wide[...] = jnp.zeros_like(wide)
    lane = lax.broadcasted_iota(jnp.int32, (queries.shape[0], LANES), 1)
    dens = jnp.zeros((queries.shape[0], LANES), f32)
    for head in range(HC):
        first, second = selectors(index_ref, head)
        one, two = factors(queries, first, second, scale_ref)
        phi = (one * two).astype(bf16)
        values = with_one(head_columns(v_ref, head)).astype(bf16)
        scores, allowed = scores_of(only_head(queries, head), keys)
        kernel = jnp.where(allowed, 1.0 + scores + 0.5 * scores * scores, 0.0).astype(bf16)
        total = dot(kernel, values) + dot(phi[:, :FROWS], before_ref[0, head])
        den = total[:, HW : HW + 1]
        add_head_columns(wide, head, jnp.where(lane < HW, total / den, 0.0))
        dens = jnp.where(lane == head, den, dens)
    mixer_ref[...] = wide[...].astype(bf16)
    den_ref[...] = dens


def pull_kernel(index_ref, scale_ref, q_ref, gm_ref, mixer_ref, den_ref, state_ref, gnum_ref):
    queries = q_ref[...]
    lane = lax.broadcasted_iota(jnp.int32, (queries.shape[0], LANES), 1)
    for head in range(HC):
        first, second = selectors(index_ref, head)
        one, two = factors(queries, first, second, scale_ref)
        phi = (one * two).astype(bf16)
        den = den_ref[:, head : head + 1]
        grad = jnp.where(lane < HW, head_columns(gm_ref, head), 0.0)
        mixer = head_columns(mixer_ref, head)
        pulled = -jnp.sum(grad * mixer, axis=1, keepdims=True)
        grad = (jnp.where(lane == HW, pulled, grad) / den).astype(bf16)
        gnum_ref[:, head * LANES : (head + 1) * LANES] = grad
        state_ref[0, head] = dot_tn(phi, grad)[:FROWS]


def backward_kernel(
    index_ref, scale_ref, q_ref, k_ref, v_ref, gnum_ref, before_ref, after_ref, gqk_ref, gv_ref, wide
):
    queries = q_ref[...]
    keys = k_ref[...]
    wide[...] = jnp.zeros_like(wide)
    lane = lax.broadcasted_iota(jnp.int32, (queries.shape[0], LANES), 1)
    grad_q = jnp.zeros((queries.shape[0], LANES), f32)
    grad_k = jnp.zeros((queries.shape[0], LANES), f32)
    for head in range(HC):
        first, second = selectors(index_ref, head)
        coef = scale_ref[2:3, :]
        q_one, q_two = factors(queries, first, second, scale_ref)
        k_one, k_two = factors(keys, first, second, scale_ref)
        values = with_one(head_columns(v_ref, head)).astype(bf16)
        gnum = gnum_ref[:, head * LANES : (head + 1) * LANES]
        q_head = only_head(queries, head)
        k_head = only_head(keys, head)
        scores, allowed = scores_of(q_head, keys)
        kernel = jnp.where(allowed, 1.0 + scores + 0.5 * scores * scores, 0.0).astype(bf16)
        grad_kernel = dot_nt(gnum, values)
        grad_scores = (jnp.where(allowed, grad_kernel * (1.0 + scores), 0.0) * SCALE).astype(bf16)
        phi_k = (k_one * k_two * coef).astype(bf16)
        after = after_ref[0, head]
        before = before_ref[0, head]
        grad_v = dot_tn(kernel, gnum) + dot(phi_k[:, :FROWS], after)
        add_head_columns(wide, head, jnp.where(lane < HW, grad_v, 0.0))
        empty = jnp.zeros((FEATS - FROWS, LANES), bf16)
        grad_phi_q = dot_nt(gnum, jnp.concatenate([before, empty], axis=0))
        grad_phi_k = dot_nt(values, jnp.concatenate([after, empty], axis=0)) * coef
        grad_q += dot(grad_scores, k_head)
        grad_q += dot_nt((grad_phi_q * q_two).astype(bf16), first)
        grad_q += dot_nt((grad_phi_q * q_one).astype(bf16), second)
        grad_k += dot_tn(grad_scores, q_head)
        grad_k += dot_nt((grad_phi_k * k_two).astype(bf16), first)
        grad_k += dot_nt((grad_phi_k * k_one).astype(bf16), second)
    gqk_ref[:, :LANES] = grad_q.astype(bf16)
    gqk_ref[:, LANES:] = grad_k.astype(bf16)
    gv_ref[...] = wide[...].astype(bf16)


def per_slot(kernel, slots, rows, ins, outs, scratch, flops):
    def table():
        return pl.BlockSpec((8, FEATS), lambda s: (0, 0))

    def row_spec(width, column=0):
        return pl.BlockSpec((rows, width), lambda s: (s, column))

    def state_spec():
        return pl.BlockSpec((1, HC, FROWS, LANES), lambda s: (s, 0, 0, 0))

    def spec(kind):
        return state_spec() if kind == "state" else row_spec(*kind)

    def shape(kind, dtype):
        if kind == "state":
            return jax.ShapeDtypeStruct((slots, HC, FROWS, LANES), dtype)
        return jax.ShapeDtypeStruct((slots * rows, kind[0]), dtype)

    return pl.pallas_call(
        kernel,
        grid=(slots,),
        in_specs=[table(), table()] + [spec(kind) for kind in ins],
        out_specs=[spec(kind) for kind, _ in outs],
        out_shape=[shape(kind, dtype) for kind, dtype in outs],
        scratch_shapes=scratch,
        compiler_params=pltpu.CompilerParams(vmem_limit_bytes=56 << 20),
        cost_estimate=pl.CostEstimate(flops=flops, bytes_accessed=8 << 20, transcendentals=0),
    )


def shifted(array, axis, by):
    count = lax.axis_size(axis)
    return lax.ppermute(array, axis, [(i, (i + by) % count) for i in range(count)])


def passed_along(array, axis, by):
    count = lax.axis_size(axis)
    pairs = [(i, i + by) for i in range(count) if 0 <= i + by < count]
    return lax.ppermute(array, axis, pairs)


def both_cores(mine, theirs, axis):
    first = lax.axis_index("core") == 0
    return jnp.concatenate(
        [jnp.where(first, mine, theirs), jnp.where(first, theirs, mine)], axis=axis
    )


def swapped(array):
    return lax.ppermute(array, "core", [(0, 1), (1, 0)])


def part_of(array, axis, index):
    return lax.dynamic_index_in_dim(array, index, axis, keepdims=False)


def gather_stage(piece, axis, dim):
    count, mine = lax.axis_size(axis), lax.axis_index(axis)
    arrived = [(mine, piece)]
    for by in range(1, count):
        arrived.append(((mine - by) % count, shifted(piece, axis, by)))
    whole = jnp.zeros(piece.shape[:dim] + (count,) + piece.shape[dim:], piece.dtype)
    for source, block in arrived:
        whole = lax.dynamic_update_index_in_dim(whole, block, source, dim)
    return whole


def gather_rows(piece, x_first):
    block = gather_stage(piece, "z", 0)
    if x_first:
        block = gather_stage(block, "x", 0)
        block = gather_stage(block, "y", 0)
    else:
        block = gather_stage(block, "y", 0)
        block = gather_stage(block, "x", 1)
    return block.reshape(D, piece.shape[1])


def scatter_stage(blocks, axis, out_dtype):
    count, mine = lax.axis_size(axis), lax.axis_index(axis)
    arrived = []
    for by in range(1, count):
        arrived.append(shifted(blocks((mine + by) % count), axis, by))
    total = lax.optimization_barrier(blocks(mine)).astype(f32)
    for block in arrived:
        total = total + block.astype(f32)
    return total.astype(out_dtype)


def scatter_rows(left_t, right, x_first):
    y_size, x_size, z_size = lax.axis_size("y"), lax.axis_size("x"), lax.axis_size("z")
    chip_rows = D // (y_size * x_size * z_size)
    columns = right.shape[1]
    view = left_t.reshape(y_size, x_size, z_size * chip_rows, left_t.shape[1])
    first_axis, first_dim = ("x", 1) if x_first else ("y", 0)
    second_axis = "y" if x_first else "x"

    def product(target):
        rows = part_of(view, first_dim, target).reshape(-1, left_t.shape[1])
        return dot(rows, right).astype(bf16)

    return scatter_tail(scatter_stage(product, first_axis, bf16), second_axis, z_size, chip_rows, columns)


def scatter_tail(total, second_axis, z_size, chip_rows, columns):
    second = total.reshape(lax.axis_size(second_axis), z_size * chip_rows, columns)
    total = scatter_stage(lambda target: part_of(second, 0, target), second_axis, bf16)
    third = total.reshape(z_size, chip_rows, columns)
    return scatter_stage(lambda target: part_of(third, 0, target), "z", f32)


def scatter_array(array, x_first):
    y_size, x_size, z_size = lax.axis_size("y"), lax.axis_size("x"), lax.axis_size("z")
    chip_rows = D // (y_size * x_size * z_size)
    columns = array.shape[1]
    view = array.reshape(y_size, x_size, z_size * chip_rows, columns)
    first_axis, first_dim = ("x", 1) if x_first else ("y", 0)
    second_axis = "y" if x_first else "x"
    total = scatter_stage(
        lambda target: part_of(view, first_dim, target).reshape(-1, columns), first_axis, bf16
    )
    return scatter_tail(total, second_axis, z_size, chip_rows, columns)


def chain(local, up):
    count = lax.axis_size("z")
    total = jnp.zeros_like(local)
    for hop in range(1, count):
        pair = (hop - 1, hop) if up else (count - hop, count - hop - 1)
        message = (total + local).astype(bf16)
        total = total + lax.ppermute(message, "z", [pair]).astype(f32)
    return total.astype(bf16)


def norm_scale(values):
    inverse = lax.rsqrt(jnp.mean(values * values, axis=-1, keepdims=True) + norm_epsilon)
    return (values * inverse, inverse)


def norm_backward(grad_normed, scaled, inverse, gain_row):
    grad_scaled = grad_normed * gain_row[None, :]
    grad_input = inverse * (
        grad_scaled - scaled * jnp.mean(grad_scaled * scaled, axis=-1, keepdims=True)
    )
    return (grad_input, jnp.sum(grad_normed * scaled, axis=0))


def adam_update(weight, gradient, first_moment, second_moment, learn_rate, decay_rate):
    first_new = beta_first * first_moment + (1.0 - beta_first) * gradient
    second_new = beta_second * second_moment + (1.0 - beta_second) * gradient * gradient
    first_hat = first_new / (1.0 - beta_first**STEP)
    second_hat = second_new / (1.0 - beta_second**STEP)
    new_weight = (
        weight
        - learn_rate * first_hat / (jnp.sqrt(second_hat) + adam_epsilon)
        - decay_rate * weight
    )
    return (new_weight, second_new)


def local(
    tokens,
    cotangent,
    lengths,
    w_qk,
    w_value,
    w_out,
    w_gu,
    w_down,
    small_params,
    m_qk,
    m_value,
    m_out,
    m_gu,
    m_down,
    m_small,
    v_qk,
    v_value,
    v_out,
    v_gu,
    v_down,
    v_small,
):
    slots, slot_rows, _ = tokens.shape
    owned = w_qk.shape[0]
    rows = slots * slot_rows
    chip_slot = CORES * slot_rows
    chip_rows = slots * chip_slot
    core, z_at = lax.axis_index("core"), lax.axis_index("z")
    other = 1 - core

    def own_rows(array):
        return part_of(array.reshape(slots, CORES, slot_rows, -1), 1, core).reshape(rows, -1)

    def other_rows(array):
        return part_of(array.reshape(slots, CORES, slot_rows, -1), 1, other).reshape(rows, -1)

    def chip_order(mine, theirs):
        width = mine.shape[-1]
        shape = (slots, 1, slot_rows, width)
        return both_cores(mine.reshape(shape), theirs.reshape(shape), 1).reshape(chip_rows, width)

    def on_chip(array):
        return chip_order(array, swapped(array))

    columns_of = [
        w_qk.astype(bf16).reshape(owned, 2, CORES, QC),
        w_value.astype(bf16).reshape(owned, 1, CORES, VC),
        w_out.astype(bf16).reshape(owned, 1, CORES, VC),
        w_gu.astype(bf16).reshape(owned, 2, CORES, FC),
        w_down.astype(bf16).reshape(owned, 1, CORES, FC),
    ]
    small_low = jnp.pad(small_params.astype(bf16), ((0, 0), (0, LANES - (KS + 2))))

    def shard(which, index):
        parts = [part_of(columns_of[i], 2, index).reshape(owned, -1) for i in which]
        return jnp.concatenate(parts, axis=1) if len(parts) > 1 else parts[0]

    def chip_shard(which, extra=None):
        mine, theirs = shard(which, core), shard(which, other)
        arrived = swapped(theirs if extra is None else jnp.concatenate([theirs, extra], axis=1))
        mine = mine if extra is None else jnp.concatenate([mine, extra], axis=1)
        return both_cores(mine, arrived, 0)

    attention_shard = chip_shard((0, 1), small_low)
    rest_shard = chip_shard((2, 3, 4))
    half = (2 * QC + VC + LANES) // 2
    early = jnp.concatenate(
        [
            gather_rows(attention_shard[:, :half], True),
            gather_rows(attention_shard[:, half:], False),
        ],
        axis=1,
    )
    qk_full = early[:, : 2 * QC]
    value_full = early[:, 2 * QC : 2 * QC + VC]
    small_float = early[:, 2 * QC + VC :][:, : KS + 2].astype(f32)
    out_half = gather_rows(rest_shard[:, :VC], True)
    out_full = both_cores(out_half, swapped(out_half), 1)
    gate_full = gather_rows(rest_shard[:, VC : VC + FC], False)
    up_full = gather_rows(rest_shard[:, VC + FC : VC + 2 * FC], True)
    cut = FC // 2 // LANES * LANES
    down_shard = rest_shard[:, VC + 2 * FC :]
    down_pieces = (gather_rows(down_shard[:, :cut], False), gather_rows(down_shard[:, cut:], True))
    down_full = jnp.concatenate(down_pieces, axis=1)

    gain_first, gain_second = small_float[:, KS], small_float[:, KS + 1]
    taps = [part_of(small_float[:, j].reshape(CORES, VC), 0, core) for j in range(KS)]

    tokens_chip = on_chip(tokens.reshape(rows, D))
    scaled_chip, _ = norm_scale(tokens_chip.astype(f32))
    normed_chip = (scaled_chip * gain_first[None, :]).astype(bf16)
    inputs = tokens.reshape(rows, D).astype(f32)
    scaled_first, inverse_first = norm_scale(inputs)
    query_key = dot(normed_chip, qk_full).astype(bf16)
    value_pre = dot(normed_chip, value_full).astype(bf16).reshape(slots, chip_slot, VC)
    earlier = passed_along(value_pre[:, chip_slot - (KS - 1) :, :], "z", 1)
    extended = jnp.concatenate([earlier, value_pre], axis=1).astype(f32)

    def tap_rows(j):
        return extended[:, KS - 1 - j : KS - 1 - j + chip_slot, :]

    convolved = taps[0] * tap_rows(0)
    for j in range(1, KS):
        convolved = convolved + taps[j] * tap_rows(j)
    values = convolved.astype(bf16).reshape(chip_rows, VC)

    index_np, scale_np = feature_tables()
    tables = (jnp.asarray(index_np), jnp.asarray(scale_np))
    q_spec, k_spec, v_spec = (LANES, 0), (LANES, 1), (VC,)
    call = functools.partial(per_slot, slots=slots, rows=chip_slot)
    unit = 2 * chip_rows * HC * LANES * FEATS
    wide = [pltpu.VMEM((chip_slot, VC), f32)]
    (state_own,) = call(
        state_kernel, ins=[k_spec, v_spec], outs=[("state", f32)], scratch=[], flops=4 * unit
    )(*tables, query_key, values)
    before = chain(state_own, True)
    mixer, dens = call(
        forward_kernel,
        ins=[q_spec, k_spec, v_spec, "state"],
        outs=[(v_spec, bf16), ((LANES,), f32)],
        scratch=wide,
        flops=8 * unit,
    )(*tables, query_key, query_key, values, before)

    mixer_full = both_cores(mixer, swapped(mixer), 1)
    after_mixer = inputs + dot(own_rows(mixer_full), out_full)
    scaled_second, inverse_second = norm_scale(after_mixer)
    second_low = (scaled_second * gain_second[None, :]).astype(bf16)
    second_chip = on_chip(second_low)

    gate = dot(second_chip, gate_full)
    upward = dot(second_chip, up_full)
    sigmoid_gate = jax.nn.sigmoid(gate)
    silu_gate = gate * sigmoid_gate
    hidden = (silu_gate * upward).astype(bf16)

    positions = z_at * chip_slot + jnp.arange(chip_slot, dtype=jnp.int32)
    valid_chip = (positions[None, :] < lengths[:, None]).astype(f32).reshape(chip_rows, 1)
    valid = own_rows(valid_chip)
    cotangent_chip = on_chip(cotangent.reshape(rows, D))
    grad_result_chip = (valid_chip * cotangent_chip.astype(f32)).astype(bf16)
    grad_result = valid * cotangent.reshape(rows, D).astype(f32)

    scattered_down = (
        scatter_rows(jnp.transpose(grad_result_chip), hidden[:, :cut], True),
        scatter_rows(jnp.transpose(grad_result_chip), hidden[:, cut:], False),
    )
    down_other = swapped(dot_nt(other_rows(hidden), down_full))
    down_result = dot_nt(own_rows(hidden), down_full) + down_other
    layer_out = (valid * (after_mixer + down_result)).astype(bf16).reshape(tokens.shape)

    grad_hidden = dot(grad_result_chip, down_full)
    grad_upward = (grad_hidden * silu_gate).astype(bf16)
    grad_gate = (
        grad_hidden * upward * sigmoid_gate * (1.0 + gate * (1.0 - sigmoid_gate))
    ).astype(bf16)
    second_other = dot_nt(other_rows(grad_gate), gate_full) + dot_nt(
        other_rows(grad_upward), up_full
    )
    second_own = dot_nt(own_rows(grad_gate), gate_full) + dot_nt(own_rows(grad_upward), up_full)
    grad_second = second_own + swapped(second_other)
    second_t = jnp.transpose(second_chip)
    scattered_gate = scatter_rows(second_t, grad_gate, False)
    scattered_up = scatter_rows(second_t, grad_upward, True)

    grad_after_norm, grad_gain_second = norm_backward(
        grad_second, scaled_second, inverse_second, gain_second
    )
    grad_after = grad_result + grad_after_norm
    grad_after_low = grad_after.astype(bf16)
    grad_mixer = dot_nt(grad_after_low, out_full).astype(bf16).reshape(rows, CORES, VC)
    grad_mixer_chip = chip_order(
        part_of(grad_mixer, 1, core), swapped(part_of(grad_mixer, 1, other))
    )
    after_columns = grad_after_low.reshape(rows, CORES, VC)
    grad_after_chip = chip_order(
        part_of(after_columns, 1, core), swapped(part_of(after_columns, 1, other))
    )
    scattered_out = scatter_rows(jnp.transpose(mixer_full), grad_after_chip, False)

    wide_spec = (HC * LANES,)
    pulled, grad_num = call(
        pull_kernel,
        ins=[q_spec, v_spec, v_spec, (LANES,)],
        outs=[("state", f32), (wide_spec, bf16)],
        scratch=[],
        flops=4 * unit,
    )(*tables, query_key, grad_mixer_chip, mixer, dens)
    after = chain(pulled, False)
    grad_query_key, grad_values = call(
        backward_kernel,
        ins=[q_spec, k_spec, v_spec, wide_spec, "state", "state"],
        outs=[((2 * LANES,), bf16), (v_spec, bf16)],
        scratch=wide,
        flops=24 * unit,
    )(*tables, query_key, query_key, values, grad_num, before, after)

    grad_values = grad_values.reshape(slots, chip_slot, VC)
    later = passed_along(grad_values[:, : KS - 1, :], "z", -1)
    grad_extended = jnp.concatenate([grad_values, later], axis=1).astype(f32)
    grad_pre = taps[0] * grad_extended[:, :chip_slot, :]
    for j in range(1, KS):
        grad_pre = grad_pre + taps[j] * grad_extended[:, j : j + chip_slot, :]
    grad_pre = grad_pre.reshape(chip_rows, VC).astype(bf16)
    grad_values_float = grad_values.astype(f32)
    tap_grads = [jnp.sum(grad_values_float * tap_rows(j), axis=(0, 1)) for j in range(KS)]

    first_other = dot_nt(other_rows(grad_query_key), qk_full) + dot_nt(
        other_rows(grad_pre), value_full
    )
    first_own = dot_nt(own_rows(grad_query_key), qk_full) + dot_nt(own_rows(grad_pre), value_full)
    grad_first = first_own + swapped(first_other)
    normed_t = jnp.transpose(normed_chip)
    scattered_value = scatter_rows(normed_t, grad_pre, True)
    scattered_qk = scatter_rows(normed_t, grad_query_key, False)
    grad_input_norm, grad_gain_first = norm_backward(
        grad_first, scaled_first, inverse_first, gain_first
    )
    input_grad = (grad_after + grad_input_norm).reshape(tokens.shape)

    def whole_feature(part):
        return lax.dynamic_update_slice(jnp.zeros((D,), f32), part, (core * VC,))

    small_terms = jnp.stack(
        [whole_feature(part) for part in tap_grads] + [grad_gain_first, grad_gain_second], axis=1
    )
    small_terms = jnp.pad(small_terms, ((0, 0), (0, LANES - (KS + 2)))).astype(bf16)
    scattered_small = scatter_array(small_terms, True)

    def rows_of(array, index):
        return part_of(array.reshape(CORES, owned, -1), 0, index)

    def finish(*parts):
        merged = jnp.concatenate(parts, axis=1) if len(parts) > 1 else parts[0]
        return rows_of(merged, core), swapped(rows_of(merged, other))

    def columns(*parts):
        mine, theirs = finish(*parts)
        return both_cores(mine, theirs, 1)

    def two_columns(mine, theirs, width):
        shape = (owned, 2, 1, width)
        return both_cores(mine.reshape(shape), theirs.reshape(shape), 2).reshape(owned, -1)

    grad_down_own = columns(*scattered_down)
    grad_gu_own = two_columns(*finish(scattered_gate, scattered_up), FC)
    grad_out_own = columns(scattered_out)
    grad_value_own = columns(scattered_value)
    grad_qk_own = two_columns(*finish(scattered_qk), QC)
    small_mine, small_theirs = finish(scattered_small)
    grad_small_own = (small_mine + small_theirs)[:, : KS + 2]

    grads_all = (
        grad_qk_own,
        grad_value_own,
        grad_out_own,
        grad_gu_own,
        grad_down_own,
        grad_small_own,
    )
    masters = (w_qk, w_value, w_out, w_gu, w_down, small_params)
    firsts = (m_qk, m_value, m_out, m_gu, m_down, m_small)
    seconds = (v_qk, v_value, v_out, v_gu, v_down, v_small)
    learn_rates = (
        0.05 / math.sqrt(D),
        0.05 / math.sqrt(D),
        0.05 / math.sqrt(max(D // 128, 1)),
        0.05 / math.sqrt(D),
        0.05 / math.sqrt(0.0003 * FF * SLOT**0.825),
        0.014,
    )
    decays = (weight_decay, weight_decay, weight_decay, weight_decay, weight_decay, 0.0)
    new_weights = []
    new_seconds = []
    for position in range(6):
        updated, moment = adam_update(
            masters[position],
            grads_all[position],
            firsts[position],
            seconds[position],
            learn_rates[position],
            decays[position],
        )
        new_weights.append(updated)
        new_seconds.append(moment)
    return (layer_out, input_grad) + grads_all + tuple(new_weights) + tuple(new_seconds)


def solution(mesh):
    dp, fsdp = mesh.shape["dp"], mesh.shape["fsdp"]
    y_size = 2 if dp % 2 == 0 else 1
    split = Mesh(
        mesh.devices.reshape(y_size, dp // y_size, fsdp // CORES, CORES), ("y", "x", "z", "core")
    )
    slot_axes, row_axes = ("y", "x"), ("z", "core")
    activation = P(slot_axes, row_axes, None)
    weight = P(slot_axes + row_axes, None)
    return jax.shard_map(
        local,
        mesh=split,
        in_specs=(activation, activation, P(slot_axes)) + (weight,) * 18,
        out_specs=(activation, activation) + (weight,) * 18,
        check_vma=False,
    )
```

```python
import functools
import math

import jax
import jax.numpy as jnp
import numpy as np
from jax import lax
from jax.experimental import pallas as pl
from jax.experimental.pallas import tpu as pltpu
from jax.sharding import Mesh
from jax.sharding import PartitionSpec as P

D = 1792
H = 16
F = 16
FF = 4864
KS = 3
SLOT = 2048
STEP = 10

CORES = 2
HC = H // CORES
HW = D // H
VC = HC * HW
QC = HC * F
FC = FF // CORES
LANES = 128
FEATS = 256
FROWS = 160
SCALE = 1.0 / math.sqrt(F)

norm_epsilon = 1e-06
beta_first = 0.9
beta_second = 0.95
adam_epsilon = 1e-08
weight_decay = 3e-05

bf16 = jnp.bfloat16
f32 = jnp.float32


def feature_tables():
    index = np.full((8, FEATS), -4096, np.int32)
    scale = np.zeros((8, FEATS), np.float32)
    scale[0, 0] = scale[1, 0] = scale[2, 0] = 1.0
    at = 1
    for i in range(F):
        index[0, at] = i
        scale[1, at] = 1.0
        scale[2, at] = SCALE
        at += 1
    for i in range(F):
        for j in range(i, F):
            index[0, at] = i
            index[1, at] = j
            scale[2, at] = (1.0 if i == j else 2.0) * 0.5 * SCALE * SCALE
            at += 1
    return index, scale


def dot(a, b):
    return lax.dot_general(a, b, (((1,), (0,)), ((), ())), preferred_element_type=f32)


def dot_nt(a, b):
    return lax.dot_general(a, b, (((1,), (1,)), ((), ())), preferred_element_type=f32)


def dot_tn(a, b):
    return lax.dot_general(a, b, (((0,), (0,)), ((), ())), preferred_element_type=f32)


def selectors(index_ref, head):
    lane = lax.broadcasted_iota(jnp.int32, (LANES, FEATS), 0) - head * F
    first = jnp.where(lane == index_ref[0:1, :], 1.0, 0.0).astype(bf16)
    second = jnp.where(lane == index_ref[1:2, :], 1.0, 0.0).astype(bf16)
    return first, second


def factors(rows, first, second, scale_ref):
    return (dot(rows, first) + scale_ref[0:1, :], dot(rows, second) + scale_ref[1:2, :])


def window(head):
    start = head * HW
    base = min(start // LANES * LANES, VC - 2 * LANES)
    return base, start - base


def both_halves(core_ref, ref, columns):
    core = core_ref[0]
    return jnp.concatenate([ref[core, :, columns], ref[1 - core, :, columns]], axis=0)


def store_halves(core_ref, ref, rows, columns):
    core, half = core_ref[0], rows.shape[0] // CORES
    ref[core, :, columns] = rows[:half]
    ref[1 - core, :, columns] = rows[half:]


def head_columns(core_ref, ref, head):
    base, offset = window(head)
    wide = both_halves(core_ref, ref, slice(base, base + 2 * LANES)).astype(f32)
    if offset:
        wide = pltpu.roll(wide, 2 * LANES - offset, 1)
    return wide[:, :LANES]


def add_head_columns(ref, head, block):
    base, offset = window(head)
    wide = jnp.concatenate([block, jnp.zeros_like(block)], axis=1)
    if offset:
        wide = pltpu.roll(wide, offset, 1)
    ref[:, base : base + 2 * LANES] += wide


def with_one(block):
    lane = lax.broadcasted_iota(jnp.int32, block.shape, 1)
    return jnp.where(lane < HW, block, jnp.where(lane == HW, 1.0, 0.0))


def only_head(rows, head):
    lane = lax.broadcasted_iota(jnp.int32, rows.shape, 1)
    inside = (lane >= head * F) & (lane < head * F + F)
    return jnp.where(inside, rows.astype(f32), 0.0).astype(bf16)


def state_kernel(core_ref, index_ref, scale_ref, k_ref, v_ref, state_ref):
    keys = both_halves(core_ref, k_ref, slice(None))
    for head in range(HC):
        first, second = selectors(index_ref, head)
        one, two = factors(keys, first, second, scale_ref)
        phi = (one * two * scale_ref[2:3, :]).astype(bf16)
        values = with_one(head_columns(core_ref, v_ref, head)).astype(bf16)
        state_ref[0, head] = dot_tn(phi, values)[:FROWS]


def scores_of(q_head, keys):
    scores = dot_nt(q_head, keys) * SCALE
    row = lax.broadcasted_iota(jnp.int32, scores.shape, 0)
    column = lax.broadcasted_iota(jnp.int32, scores.shape, 1)
    return scores, column <= row


def forward_kernel(core_ref, index_ref, scale_ref, q_ref, k_ref, v_ref, before_ref, mixer_ref, den_ref, wide):
    queries = both_halves(core_ref, q_ref, slice(None))
    keys = both_halves(core_ref, k_ref, slice(None))
    wide[...] = jnp.zeros_like(wide)
    lane = lax.broadcasted_iota(jnp.int32, (queries.shape[0], LANES), 1)
    dens = jnp.zeros((queries.shape[0], LANES), f32)
    for head in range(HC):
        first, second = selectors(index_ref, head)
        one, two = factors(queries, first, second, scale_ref)
        phi = (one * two).astype(bf16)
        values = with_one(head_columns(core_ref, v_ref, head)).astype(bf16)
        scores, allowed = scores_of(only_head(queries, head), keys)
        kernel = jnp.where(allowed, 1.0 + scores + 0.5 * scores * scores, 0.0).astype(bf16)
        total = dot(kernel, values) + dot(phi[:, :FROWS], before_ref[0, head])
        den = total[:, HW : HW + 1]
        add_head_columns(wide, head, jnp.where(lane < HW, total / den, 0.0))
        dens = jnp.where(lane == head, den, dens)
    store_halves(core_ref, mixer_ref, wide[...].astype(bf16), slice(None))
    store_halves(core_ref, den_ref, dens, slice(None))


def pull_kernel(core_ref, index_ref, scale_ref, q_ref, gm_ref, mixer_ref, den_ref, state_ref, gnum_ref):
    queries = both_halves(core_ref, q_ref, slice(None))
    lane = lax.broadcasted_iota(jnp.int32, (queries.shape[0], LANES), 1)
    dens = both_halves(core_ref, den_ref, slice(None))
    for head in range(HC):
        first, second = selectors(index_ref, head)
        one, two = factors(queries, first, second, scale_ref)
        phi = (one * two).astype(bf16)
        den = dens[:, head : head + 1]
        grad = jnp.where(lane < HW, head_columns(core_ref, gm_ref, head), 0.0)
        mixer = head_columns(core_ref, mixer_ref, head)
        pulled = -jnp.sum(grad * mixer, axis=1, keepdims=True)
        grad = (jnp.where(lane == HW, pulled, grad) / den).astype(bf16)
        store_halves(core_ref, gnum_ref, grad, slice(head * LANES, (head + 1) * LANES))
        state_ref[0, head] = dot_tn(phi, grad)[:FROWS]


def backward_kernel(
    core_ref, index_ref, scale_ref, q_ref, k_ref, v_ref, gnum_ref, before_ref, after_ref, gqk_ref, gv_ref, wide
):
    queries = both_halves(core_ref, q_ref, slice(None))
    keys = both_halves(core_ref, k_ref, slice(None))
    wide[...] = jnp.zeros_like(wide)
    lane = lax.broadcasted_iota(jnp.int32, (queries.shape[0], LANES), 1)
    grad_q = jnp.zeros((queries.shape[0], LANES), f32)
    grad_k = jnp.zeros((queries.shape[0], LANES), f32)
    for head in range(HC):
        first, second = selectors(index_ref, head)
        coef = scale_ref[2:3, :]
        q_one, q_two = factors(queries, first, second, scale_ref)
        k_one, k_two = factors(keys, first, second, scale_ref)
        values = with_one(head_columns(core_ref, v_ref, head)).astype(bf16)
        gnum = both_halves(core_ref, gnum_ref, slice(head * LANES, (head + 1) * LANES))
        q_head = only_head(queries, head)
        k_head = only_head(keys, head)
        scores, allowed = scores_of(q_head, keys)
        kernel = jnp.where(allowed, 1.0 + scores + 0.5 * scores * scores, 0.0).astype(bf16)
        grad_kernel = dot_nt(gnum, values)
        grad_scores = (jnp.where(allowed, grad_kernel * (1.0 + scores), 0.0) * SCALE).astype(bf16)
        phi_k = (k_one * k_two * coef).astype(bf16)
        after = after_ref[0, head]
        before = before_ref[0, head]
        grad_v = dot_tn(kernel, gnum) + dot(phi_k[:, :FROWS], after)
        add_head_columns(wide, head, jnp.where(lane < HW, grad_v, 0.0))
        empty = jnp.zeros((FEATS - FROWS, LANES), bf16)
        grad_phi_q = dot_nt(gnum, jnp.concatenate([before, empty], axis=0))
        grad_phi_k = dot_nt(values, jnp.concatenate([after, empty], axis=0)) * coef
        grad_q += dot(grad_scores, k_head)
        grad_q += dot_nt((grad_phi_q * q_two).astype(bf16), first)
        grad_q += dot_nt((grad_phi_q * q_one).astype(bf16), second)
        grad_k += dot_tn(grad_scores, q_head)
        grad_k += dot_nt((grad_phi_k * k_two).astype(bf16), first)
        grad_k += dot_nt((grad_phi_k * k_one).astype(bf16), second)
    store_halves(core_ref, gqk_ref, grad_q.astype(bf16), slice(0, LANES))
    store_halves(core_ref, gqk_ref, grad_k.astype(bf16), slice(LANES, 2 * LANES))
    store_halves(core_ref, gv_ref, wide[...].astype(bf16), slice(None))


def per_slot(kernel, slots, rows, ins, outs, scratch, flops):
    def table():
        return pl.BlockSpec((8, FEATS), lambda s, core: (0, 0))

    def row_spec(width, column=0):
        return pl.BlockSpec((CORES, None, rows, width), lambda s, core: (0, s, 0, column))

    def state_spec():
        return pl.BlockSpec((1, HC, FROWS, LANES), lambda s, core: (s, 0, 0, 0))

    def spec(kind):
        return state_spec() if kind == "state" else row_spec(*kind)

    def shape(kind, dtype):
        if kind == "state":
            return jax.ShapeDtypeStruct((slots, HC, FROWS, LANES), dtype)
        return jax.ShapeDtypeStruct((CORES, slots, rows, kind[0]), dtype)

    return pl.pallas_call(
        kernel,
        grid_spec=pltpu.PrefetchScalarGridSpec(
            num_scalar_prefetch=1,
            grid=(slots,),
            in_specs=[table(), table()] + [spec(kind) for kind in ins],
            out_specs=[spec(kind) for kind, _ in outs],
            scratch_shapes=scratch,
        ),
        out_shape=[shape(kind, dtype) for kind, dtype in outs],
        compiler_params=pltpu.CompilerParams(vmem_limit_bytes=56 << 20),
        cost_estimate=pl.CostEstimate(flops=flops, bytes_accessed=8 << 20, transcendentals=0),
    )


def passed_along(array, axis, by):
    count = lax.axis_size(axis)
    pairs = [(i, i + by) for i in range(count) if 0 <= i + by < count]
    return lax.ppermute(array, axis, pairs)


def both_cores(mine, theirs, axis):
    first = lax.axis_index("core") == 0
    return jnp.concatenate(
        [jnp.where(first, mine, theirs), jnp.where(first, theirs, mine)], axis=axis
    )


def swapped(array):
    return lax.ppermute(array, "core", [(0, 1), (1, 0)])


def part_of(array, axis, index):
    return lax.dynamic_index_in_dim(array, index, axis, keepdims=False)


def bits_of(axis):
    return [(axis, bit) for bit in reversed(range(lax.axis_size(axis).bit_length() - 1))]


def bit_at(axis, bit):
    return (lax.axis_index(axis) >> bit) & 1


def exchanged(array, axis, bit):
    count = lax.axis_size(axis)
    return lax.ppermute(array, axis, [(i, i ^ (1 << bit)) for i in range(count)])


def tied(*arrays):
    return lax.optimization_barrier(arrays)


class Gather:
    def __init__(self, piece, x_first):
        self.columns = piece.shape[1]
        self.block = piece
        low_first = lambda axis: bits_of(axis)[::-1]
        self.plan = [(step, at) for at, step in enumerate(bits_of("z"))]
        if x_first:
            self.plan += [(step, 0) for step in low_first("x") + low_first("y")]
        else:
            self.plan += [(step, 0) for step in low_first("y")]
            self.plan += [(step, len(bits_of("y"))) for step in low_first("x")]

    def stage(self):
        (axis, bit), dim = self.plan.pop(0)
        mine = bit_at(axis, bit)
        arrived = exchanged(self.block, axis, bit)
        shape = self.block.shape[:dim] + (2,) + self.block.shape[dim:]
        whole = jnp.zeros(shape, self.block.dtype)
        whole = lax.dynamic_update_index_in_dim(whole, self.block, mine, dim)
        self.block = lax.dynamic_update_index_in_dim(whole, arrived, 1 - mine, dim)
        return self

    def along_z(self):
        while self.plan[0][0][0] == "z":
            self.stage()
        return self

    def rest(self):
        while self.plan:
            self.stage()
        return self.block.reshape(D, self.columns)


class Scatter:
    def __init__(self, terms, x_first):
        self.dims = bits_of("y") + bits_of("x") + bits_of("z")
        order = ("x", "y") if x_first else ("y", "x")
        self.plan = bits_of(order[0]) + bits_of(order[1]) + bits_of("z")[::-1]
        rows = D >> len(self.dims)
        self.terms = [terms.reshape((2,) * len(self.dims) + (rows, terms.shape[1]))]

    def total(self, terms):
        total = terms[0].astype(f32)
        for term in terms[1:]:
            total = total + term.astype(f32)
        return total

    def stage(self):
        step = self.plan.pop(0)
        dim, mine = self.dims.index(step), bit_at(*step)
        self.dims.remove(step)
        sent = self.total([part_of(term, dim, 1 - mine) for term in self.terms]).astype(bf16)
        self.terms = [part_of(term, dim, mine) for term in self.terms]
        self.terms.append(exchanged(sent, *step))
        return self

    def rest(self):
        while self.plan:
            self.stage()
        return self.total(self.terms)


def chain(local, up):
    count = lax.axis_size("z")
    total = jnp.zeros_like(local)
    for hop in range(1, count):
        pair = (hop - 1, hop) if up else (count - hop, count - hop - 1)
        message = (total + local).astype(bf16)
        total = total + lax.ppermute(message, "z", [pair]).astype(f32)
    return total.astype(bf16)


def mesh_exchange(y, x, z, core, axis):
    if axis == "y":
        return (1 - y, x, z, core)
    if axis == "x":
        return (y, 1 - x, z, core)
    if axis == "z0":
        return (y, x, z + 1 - 2 * (z % 2), core)
    return (y, x, (z + 2) % 4, core)


ORDERS = (("y", "x", "z0", "z1"), ("x", "y", "z0", "z1"))


def reduce_kernel(
    tiles,
    second_ref,
    normed_ref,
    mixer_ref,
    gate_ref,
    up_ref,
    value_ref,
    after_ref,
    qk_ref,
    small_ref,
    out_ref,
    terms,
    sums,
    halves,
    quarters,
    got_terms,
    got_sums,
    got_halves,
    got_quarters,
    send_sem,
    recv_sem,
):
    y, x, z, core = (lax.axis_index(axis) for axis in ("y", "x", "z", "core"))
    ffn, mid, total = tiles
    places = {"y": y, "x": x, "z0": z % 2, "z1": z // 2}
    block = terms.shape[4]

    barrier = pltpu.get_barrier_semaphore()
    for axis in ORDERS[0]:
        pl.semaphore_signal(
            barrier,
            inc=1,
            device_id=mesh_exchange(y, x, z, core, axis),
            device_id_type=pl.DeviceIdType.MESH,
        )
    pl.semaphore_wait(barrier, len(ORDERS[0]))

    def transfer(stream, stage, chunk):
        axis = ORDERS[stream][stage]
        there = 1 - places[axis]
        slot, landing = chunk % 2, chunk % 4
        if stage == 0 and stream == 0:
            source = terms.at[stream, slot, there]
        elif stage == 0:
            source = terms.at[stream, slot, :, there]
        elif stage == 1:
            source = sums.at[stream, slot, there]
        elif stage == 2:
            source = halves.at[stream, slot, :, there]
        else:
            source = quarters.at[stream, slot, there]
        target = (got_terms, got_sums, got_halves, got_quarters)[stage].at[stream, landing]
        return pltpu.make_async_remote_copy(
            src_ref=source,
            dst_ref=target,
            send_sem=send_sem.at[stream, stage, slot],
            recv_sem=recv_sem.at[stream, stage, landing],
            device_id=mesh_exchange(y, x, z, core, axis),
            device_id_type=pl.DeviceIdType.MESH,
        )

    def add(a, b):
        return a.astype(f32) + b.astype(f32)

    def product(stream, chunk, left_ref, right_ref, tile):
        columns = right_ref[:, pl.ds(pl.multiple_of(tile * LANES, LANES), LANES)]

        @pl.loop(0, 4)
        def _(part):
            rows = left_ref[pl.ds(pl.multiple_of(part * block, block), block), :]
            terms[stream, chunk % 2, part // 2, part % 2] = dot(rows, columns).astype(bf16)

    def begin(chunk):
        @pl.when(chunk < ffn)
        def _():
            product(0, chunk, second_ref, gate_ref, chunk)
            product(1, chunk, second_ref, up_ref, chunk)

        @pl.when((chunk >= ffn) & (chunk < ffn + mid))
        def _():
            product(0, chunk, normed_ref, value_ref, chunk - ffn)
            product(1, chunk, mixer_ref, after_ref, chunk - ffn)

        @pl.when(chunk == ffn + mid)
        def _():
            product(0, chunk, normed_ref, qk_ref, 0)
            product(1, chunk, normed_ref, qk_ref, 1)

        @pl.when(chunk == ffn + mid + 1)
        def _():
            for part in range(4):
                rows = small_ref[part * block : (part + 1) * block, :]
                terms[0, chunk % 2, part // 2, part % 2] = rows
                terms[1, chunk % 2, part // 2, part % 2] = rows

        for stream in range(2):
            transfer(stream, 0, chunk).start()

    def advance(stage, chunk):
        for stream in range(2):
            axis = ORDERS[stream][stage]
            here = places[axis]
            slot, landing = chunk % 2, chunk % 4
            transfer(stream, stage, chunk).wait()
            if stage == 0:
                own = terms[stream, slot, here] if stream == 0 else terms[stream, slot, :, here]
                sums[stream, slot] = add(own, got_terms[stream, landing]).astype(bf16)
            elif stage == 1:
                total = add(sums[stream, slot, here], got_sums[stream, landing]).astype(bf16)
                halves[stream, slot] = total.reshape(halves.shape[2:])
            elif stage == 2:
                own = halves[stream, slot, :, here]
                quarters[stream, slot] = add(own, got_halves[stream, landing]).astype(bf16)
            else:
                total = add(quarters[stream, slot, here], got_quarters[stream, landing])
                out_ref[stream, :, pl.ds(pl.multiple_of(chunk * LANES, LANES), LANES)] = total
            if stage < 3:
                transfer(stream, stage + 1, chunk).start()

    @pl.loop(0, total + 4)
    def _(step):
        @pl.when(step < total)
        def _():
            begin(step)

        for stage in range(4):

            @pl.when((step >= stage + 1) & (step < total + stage + 1))
            def _(stage=stage):
                advance(stage, step - stage - 1)


def reduced(second_t, normed_t, mixer_t, grad_gate, grad_up, grad_pre, grad_after, grad_qk, small):
    ffn, mid = grad_gate.shape[1] // LANES, grad_pre.shape[1] // LANES
    total = ffn + mid + 2
    block, rows = D // 4, D // 16
    dma = pltpu.SemaphoreType.DMA
    tokens = second_t.shape[1]
    return pl.pallas_call(
        functools.partial(reduce_kernel, (ffn, mid, total)),
        out_shape=jax.ShapeDtypeStruct((2, rows, total * LANES), f32),
        in_specs=[pl.BlockSpec(memory_space=pltpu.VMEM)] * 9,
        out_specs=pl.BlockSpec(memory_space=pltpu.VMEM),
        scratch_shapes=[
            pltpu.VMEM((2, 2, 2, 2, block, LANES), bf16),
            pltpu.VMEM((2, 2, 2, block, LANES), bf16),
            pltpu.VMEM((2, 2, 2, 2, rows, LANES), bf16),
            pltpu.VMEM((2, 2, 2, rows, LANES), bf16),
            pltpu.VMEM((2, 4, 2, block, LANES), bf16),
            pltpu.VMEM((2, 4, block, LANES), bf16),
            pltpu.VMEM((2, 4, 2, rows, LANES), bf16),
            pltpu.VMEM((2, 4, rows, LANES), bf16),
            dma((2, 4, 2)),
            dma((2, 4, 4)),
        ],
        compiler_params=pltpu.CompilerParams(
            collective_id=0, has_side_effects=True, vmem_limit_bytes=58 << 20
        ),
        cost_estimate=pl.CostEstimate(
            flops=4 * D * tokens * total * LANES, bytes_accessed=400 << 20, transcendentals=0
        ),
    )(second_t, normed_t, mixer_t, grad_gate, grad_up, grad_pre, grad_after, grad_qk, small)


def norm_scale(values):
    inverse = lax.rsqrt(jnp.mean(values * values, axis=-1, keepdims=True) + norm_epsilon)
    return (values * inverse, inverse)


def norm_backward(grad_normed, scaled, inverse, gain_row):
    grad_scaled = grad_normed * gain_row[None, :]
    grad_input = inverse * (
        grad_scaled - scaled * jnp.mean(grad_scaled * scaled, axis=-1, keepdims=True)
    )
    return (grad_input, jnp.sum(grad_normed * scaled, axis=0))


def adam_update(weight, gradient, first_moment, second_moment, learn_rate, decay_rate):
    first_new = beta_first * first_moment + (1.0 - beta_first) * gradient
    second_new = beta_second * second_moment + (1.0 - beta_second) * gradient * gradient
    first_hat = first_new / (1.0 - beta_first**STEP)
    second_hat = second_new / (1.0 - beta_second**STEP)
    new_weight = (
        weight
        - learn_rate * first_hat / (jnp.sqrt(second_hat) + adam_epsilon)
        - decay_rate * weight
    )
    return (new_weight, second_new)


def local(
    tokens,
    cotangent,
    lengths,
    w_qk,
    w_value,
    w_out,
    w_gu,
    w_down,
    small_params,
    m_qk,
    m_value,
    m_out,
    m_gu,
    m_down,
    m_small,
    v_qk,
    v_value,
    v_out,
    v_gu,
    v_down,
    v_small,
):
    slots, slot_rows, _ = tokens.shape
    owned = w_qk.shape[0]
    rows = slots * slot_rows
    core, z_at = lax.axis_index("core"), lax.axis_index("z")
    other = 1 - core
    first_core = core == 0

    def on_chip(array):
        return jnp.concatenate([array, swapped(array)], axis=0)

    def halves(array):
        return array.reshape(CORES, slots, slot_rows, -1)

    columns_of = [
        w_qk.astype(bf16).reshape(owned, 2, CORES, QC),
        w_value.astype(bf16).reshape(owned, 1, CORES, VC),
        w_out.astype(bf16).reshape(owned, 1, CORES, VC),
        w_gu.astype(bf16).reshape(owned, 2, CORES, FC),
        w_down.astype(bf16).reshape(owned, 1, CORES, FC),
    ]
    small_low = jnp.pad(small_params.astype(bf16), ((0, 0), (0, LANES - (KS + 2))))

    def shard(which, index):
        parts = [part_of(columns_of[i], 2, index).reshape(owned, -1) for i in which]
        return jnp.concatenate(parts, axis=1) if len(parts) > 1 else parts[0]

    def chip_shard(which, extra=None):
        mine, theirs = shard(which, core), shard(which, other)
        arrived = swapped(theirs if extra is None else jnp.concatenate([theirs, extra], axis=1))
        mine = mine if extra is None else jnp.concatenate([mine, extra], axis=1)
        return both_cores(mine, arrived, 0)

    attention_shard = chip_shard((0, 1), small_low)
    rest_shard = chip_shard((2, 3, 4))
    half = (2 * QC + VC + LANES) // 2
    cut = FC // 2 // LANES * LANES
    down_at = VC + 2 * FC
    own_tokens = tokens.reshape(rows, D)
    other_tokens = swapped(own_tokens)
    wide_part = 4 * LANES
    early_a = Gather(attention_shard[:, :half], True)
    early_b = Gather(attention_shard[:, half:], False)
    early_a.along_z(), early_b.along_z()
    early_a.block, other_tokens = tied(early_a.block, other_tokens)
    early = jnp.concatenate([early_a.rest(), early_b.rest()], axis=1)

    def gathered(start, width):
        return lax.all_gather(rest_shard[:, start : start + width], ("y", "x", "z"), axis=0, tiled=True)

    out_half = gathered(0, VC)
    gate_full = gathered(VC, FC)
    up_full = gathered(VC + FC, FC)
    last_shard, early = tied(rest_shard[:, down_at:], early)
    down_a = Gather(last_shard[:, :cut], True)
    down_b = Gather(last_shard[:, cut:], False)
    down_full = jnp.concatenate([down_a.rest(), down_b.rest()], axis=1)

    qk_full = early[:, : 2 * QC]
    value_full = early[:, 2 * QC : 2 * QC + VC]
    small_float = early[:, 2 * QC + VC :][:, : KS + 2].astype(f32)
    out_full = both_cores(out_half, swapped(out_half), 1)
    gain_first, gain_second = small_float[:, KS], small_float[:, KS + 1]
    taps = [part_of(small_float[:, j].reshape(CORES, VC), 0, core) for j in range(KS)]

    inputs = tokens.reshape(rows, D).astype(f32)
    scaled_first, inverse_first = norm_scale(inputs)
    scaled_chip, _ = norm_scale(
        jnp.concatenate([own_tokens, other_tokens], axis=0).astype(f32)
    )
    normed_chip = (scaled_chip * gain_first[None, :]).astype(bf16)
    query_key = halves(dot(normed_chip, qk_full).astype(bf16))
    value_pre = halves(dot(normed_chip, value_full).astype(bf16))
    tail = value_pre[:, :, slot_rows - (KS - 1) :, :]
    from_chip = passed_along(part_of(tail, 0, other), "z", 1)
    from_core = part_of(tail, 0, core)
    earlier = jnp.stack(
        [jnp.where(first_core, from_chip, from_core), jnp.where(first_core, from_core, from_chip)]
    )
    extended = jnp.concatenate([earlier, value_pre], axis=2).astype(f32)

    def tap_rows(j):
        return extended[:, :, KS - 1 - j : KS - 1 - j + slot_rows, :]

    convolved = taps[0] * tap_rows(0)
    for j in range(1, KS):
        convolved = convolved + taps[j] * tap_rows(j)
    values = convolved.astype(bf16)

    index_np, scale_np = feature_tables()
    tables = (core.astype(jnp.int32).reshape(1), jnp.asarray(index_np), jnp.asarray(scale_np))
    q_spec, k_spec, v_spec = (LANES, 0), (LANES, 1), (VC,)
    call = functools.partial(per_slot, slots=slots, rows=slot_rows)
    unit = 2 * CORES * rows * HC * LANES * FEATS
    wide = [pltpu.VMEM((CORES * slot_rows, VC), f32)]
    (state_own,) = call(
        state_kernel, ins=[k_spec, v_spec], outs=[("state", f32)], scratch=[], flops=4 * unit
    )(*tables, query_key, values)
    before = chain(state_own, True)
    mixer, dens = call(
        forward_kernel,
        ins=[q_spec, k_spec, v_spec, "state"],
        outs=[(v_spec, bf16), ((LANES,), f32)],
        scratch=wide,
        flops=8 * unit,
    )(*tables, query_key, query_key, values, before)

    mixer_flat = mixer.reshape(CORES * rows, VC)
    mixer_theirs = swapped(mixer_flat)
    mixer_own = both_cores(mixer_flat[:rows], mixer_theirs[rows:], 1)
    mixer_other = both_cores(mixer_flat[rows:], mixer_theirs[:rows], 1)
    after_mixer = inputs + dot(mixer_own, out_full)
    scaled_second, inverse_second = norm_scale(after_mixer)
    second_low = (scaled_second * gain_second[None, :]).astype(bf16)
    second_chip = on_chip(second_low)

    gate = dot(second_chip, gate_full)
    upward = dot(second_chip, up_full)
    sigmoid_gate = jax.nn.sigmoid(gate)
    silu_gate = gate * sigmoid_gate
    hidden = (silu_gate * upward).astype(bf16)

    half_at = jnp.where(first_core, jnp.arange(CORES), 1 - jnp.arange(CORES))
    positions = (z_at * CORES + half_at)[:, None] * slot_rows + jnp.arange(slot_rows)[None, :]
    valid_chip = positions[:, None, :] < lengths[None, :, None]
    valid_chip = valid_chip.astype(f32).reshape(CORES * rows, 1)
    valid = valid_chip[:rows]
    query_key, cotangent_late = lax.optimization_barrier((query_key, cotangent))
    cotangent_chip = on_chip(cotangent_late.reshape(rows, D))
    mixer, cotangent_chip = tied(mixer, cotangent_chip)
    grad_result_chip = (valid_chip * cotangent_chip.astype(f32)).astype(bf16)
    grad_result = valid * cotangent.reshape(rows, D).astype(f32)

    def scattered(terms):
        return lax.psum_scatter(terms, ("y", "x", "z"), scatter_dimension=0, tiled=True)

    down_terms, grad_result_chip = tied(
        dot_tn(grad_result_chip, hidden).astype(bf16), grad_result_chip
    )
    scatter_down = scattered(down_terms)
    down_other = swapped(dot_nt(hidden[rows:], down_full))
    grad_hidden = dot(grad_result_chip, down_full)
    grad_upward = (grad_hidden * silu_gate).astype(bf16)
    grad_gate = (
        grad_hidden * upward * sigmoid_gate * (1.0 + gate * (1.0 - sigmoid_gate))
    ).astype(bf16)
    second_other = dot_nt(grad_gate[rows:], gate_full) + dot_nt(grad_upward[rows:], up_full)
    second_own = dot_nt(grad_gate[:rows], gate_full) + dot_nt(grad_upward[:rows], up_full)
    second_own, down_other = tied(second_own, down_other)
    grad_second = second_own + swapped(second_other)
    down_result = dot_nt(hidden[:rows], down_full) + down_other
    layer_out = (valid * (after_mixer + down_result)).astype(bf16).reshape(tokens.shape)

    grad_after_norm, grad_gain_second = norm_backward(
        grad_second, scaled_second, inverse_second, gain_second
    )
    grad_after = grad_result + grad_after_norm
    grad_after_low = grad_after.astype(bf16)
    grad_mixer = dot_nt(grad_after_low, out_full).astype(bf16).reshape(rows, CORES, VC)
    grad_mixer_chip = jnp.concatenate(
        [part_of(grad_mixer, 1, core), swapped(part_of(grad_mixer, 1, other))], axis=0
    )
    after_columns = grad_after_low.reshape(rows, CORES, VC)
    grad_after_chip = jnp.concatenate(
        [part_of(after_columns, 1, core), swapped(part_of(after_columns, 1, other))], axis=0
    )
    mixer_chip = jnp.concatenate([mixer_own, mixer_other], axis=0)

    wide_spec = (HC * LANES,)
    pulled, grad_num = call(
        pull_kernel,
        ins=[q_spec, v_spec, v_spec, (LANES,)],
        outs=[("state", f32), (wide_spec, bf16)],
        scratch=[],
        flops=4 * unit,
    )(*tables, query_key, halves(grad_mixer_chip), mixer, dens)
    from_later = chain(pulled, False)
    grad_query_key, grad_values = call(
        backward_kernel,
        ins=[q_spec, k_spec, v_spec, wide_spec, "state", "state"],
        outs=[((2 * LANES,), bf16), (v_spec, bf16)],
        scratch=wide,
        flops=24 * unit,
    )(*tables, query_key, query_key, values, grad_num, before, from_later)

    head = grad_values[:, :, : KS - 1, :]
    from_chip = passed_along(part_of(head, 0, core), "z", -1)
    from_core = part_of(head, 0, other)
    later = jnp.stack(
        [jnp.where(first_core, from_core, from_chip), jnp.where(first_core, from_chip, from_core)]
    )
    grad_extended = jnp.concatenate([grad_values, later], axis=2).astype(f32)
    grad_pre = taps[0] * grad_extended[:, :, :slot_rows, :]
    for j in range(1, KS):
        grad_pre = grad_pre + taps[j] * grad_extended[:, :, j : j + slot_rows, :]
    grad_pre = grad_pre.reshape(CORES * rows, VC).astype(bf16)
    grad_query_key = grad_query_key.reshape(CORES * rows, 2 * QC)
    grad_values_float = grad_values.astype(f32)
    tap_grads = [jnp.sum(grad_values_float * tap_rows(j), axis=(0, 1, 2)) for j in range(KS)]

    first_other = dot_nt(grad_query_key[rows:], qk_full) + dot_nt(grad_pre[rows:], value_full)
    first_own = dot_nt(grad_query_key[:rows], qk_full) + dot_nt(grad_pre[:rows], value_full)
    grad_first = first_own + swapped(first_other)
    grad_gain_first = jnp.sum(first_own * scaled_chip[:rows], axis=0) + jnp.sum(
        first_other * scaled_chip[rows:], axis=0
    )

    def whole_feature(part):
        return lax.dynamic_update_slice(jnp.zeros((D,), f32), part, (core * VC,))

    small_terms = jnp.stack(
        [whole_feature(part) for part in tap_grads] + [grad_gain_first, grad_gain_second], axis=1
    )
    small_terms = jnp.pad(small_terms, ((0, 0), (0, LANES - (KS + 2)))).astype(bf16)
    operands = (
        grad_gate,
        grad_upward,
        grad_pre,
        grad_after_chip,
        grad_query_key,
        small_terms,
    )
    in_kernel = tuple(lax.axis_size(axis) for axis in ("y", "x", "z")) == (2, 2, 4)
    if in_kernel:
        lefts = [jnp.transpose(left) for left in (second_chip, normed_chip, mixer_chip)]
        sums = reduced(*lefts, *operands)
        gate_to, mid_to = FC, FC + VC
        sum_gate, sum_up = sums[0, :, :gate_to], sums[1, :, :gate_to]
        sum_value, sum_out = sums[0, :, gate_to:mid_to], sums[1, :, gate_to:mid_to]
        sum_last = jnp.concatenate(
            [sums[0, :, mid_to : mid_to + QC], sums[1, :, mid_to : mid_to + QC], sums[0, :, mid_to + QC :]],
            axis=1,
        )
    else:
        sum_gate = Scatter(dot_tn(second_chip, grad_gate).astype(bf16), False).rest()
        sum_up = Scatter(dot_tn(second_chip, grad_upward).astype(bf16), True).rest()
        sum_value = Scatter(dot_tn(normed_chip, grad_pre).astype(bf16), False).rest()
        sum_out = Scatter(dot_tn(mixer_chip, grad_after_chip).astype(bf16), True).rest()
        qk_terms = dot_tn(normed_chip, grad_query_key).astype(bf16)
        sum_last = Scatter(jnp.concatenate([qk_terms, small_terms], axis=1), True).rest()
    grad_input_norm, _ = norm_backward(grad_first, scaled_first, inverse_first, gain_first)
    input_grad = (grad_after + grad_input_norm).reshape(tokens.shape)

    def rows_of(array, index):
        return part_of(array.reshape(CORES, owned, -1), 0, index)

    def finish(*parts):
        merged = jnp.concatenate(parts, axis=1) if len(parts) > 1 else parts[0]
        mine, theirs = rows_of(merged, core), swapped(rows_of(merged, other))
        return mine.astype(f32), theirs.astype(f32)

    def columns(*parts):
        mine, theirs = finish(*parts)
        return both_cores(mine, theirs, 1)

    def two_columns(mine, theirs, width):
        shape = (owned, 2, 1, width)
        return both_cores(mine.reshape(shape), theirs.reshape(shape), 2).reshape(owned, -1)

    grad_down_own = columns(scatter_down)
    grad_gu_own = two_columns(*finish(sum_gate, sum_up), FC)
    grad_out_own = columns(sum_out)
    grad_value_own = columns(sum_value)
    last_mine, last_theirs = finish(sum_last)
    grad_qk_own = two_columns(last_mine[:, : 2 * QC], last_theirs[:, : 2 * QC], QC)
    grad_small_own = (last_mine + last_theirs)[:, 2 * QC : 2 * QC + KS + 2]

    grads_all = (
        grad_qk_own,
        grad_value_own,
        grad_out_own,
        grad_gu_own,
        grad_down_own,
        grad_small_own,
    )
    masters = (w_qk, w_value, w_out, w_gu, w_down, small_params)
    firsts = (m_qk, m_value, m_out, m_gu, m_down, m_small)
    seconds = (v_qk, v_value, v_out, v_gu, v_down, v_small)
    learn_rates = (
        0.05 / math.sqrt(D),
        0.05 / math.sqrt(D),
        0.05 / math.sqrt(max(D // 128, 1)),
        0.05 / math.sqrt(D),
        0.05 / math.sqrt(0.0003 * FF * SLOT**0.825),
        0.014,
    )
    decays = (weight_decay, weight_decay, weight_decay, weight_decay, weight_decay, 0.0)
    new_weights = []
    new_seconds = []
    for position in range(6):
        updated, moment = adam_update(
            masters[position],
            grads_all[position],
            firsts[position],
            seconds[position],
            learn_rates[position],
            decays[position],
        )
        new_weights.append(updated)
        new_seconds.append(moment)
    return (layer_out, input_grad) + grads_all + tuple(new_weights) + tuple(new_seconds)


def solution(mesh):
    dp, fsdp = mesh.shape["dp"], mesh.shape["fsdp"]
    y_size = 2 if dp % 2 == 0 else 1
    split = Mesh(
        mesh.devices.reshape(y_size, dp // y_size, fsdp // CORES, CORES), ("y", "x", "z", "core")
    )
    slot_axes, row_axes = ("y", "x"), ("z", "core")
    activation = P(slot_axes, row_axes, None)
    weight = P(slot_axes + row_axes, None)
    return jax.shard_map(
        local,
        mesh=split,
        in_specs=(activation, activation, P(slot_axes)) + (weight,) * 18,
        out_specs=(activation, activation) + (weight,) * 18,
        check_vma=False,
    )
```

```python
import functools
import math

import jax
import jax.numpy as jnp
import numpy as np
from jax import lax
from jax.experimental import pallas as pl
from jax.experimental.pallas import tpu as pltpu
from jax.sharding import Mesh
from jax.sharding import PartitionSpec as P

D = 1792
H = 16
F = 16
FF = 4864
KS = 3
SLOT = 2048
STEP = 10

CORES = 2
HC = H // CORES
HW = D // H
VC = HC * HW
QC = HC * F
FC = FF // CORES
LANES = 128
FEATS = 256
FROWS = 160
SCALE = 1.0 / math.sqrt(F)

norm_epsilon = 1e-06
beta_first = 0.9
beta_second = 0.95
adam_epsilon = 1e-08
weight_decay = 3e-05

bf16 = jnp.bfloat16
f32 = jnp.float32


def feature_tables():
    index = np.full((8, FEATS), -4096, np.int32)
    scale = np.zeros((8, FEATS), np.float32)
    scale[0, 0] = scale[1, 0] = scale[2, 0] = 1.0
    at = 1
    for i in range(F):
        index[0, at] = i
        scale[1, at] = 1.0
        scale[2, at] = SCALE
        at += 1
    for i in range(F):
        for j in range(i, F):
            index[0, at] = i
            index[1, at] = j
            scale[2, at] = (1.0 if i == j else 2.0) * 0.5 * SCALE * SCALE
            at += 1
    return index, scale


def dot(a, b):
    return lax.dot_general(a, b, (((1,), (0,)), ((), ())), preferred_element_type=f32)


def dot_nt(a, b):
    return lax.dot_general(a, b, (((1,), (1,)), ((), ())), preferred_element_type=f32)


def dot_tn(a, b):
    return lax.dot_general(a, b, (((0,), (0,)), ((), ())), preferred_element_type=f32)


def selectors(index_ref, head):
    lane = lax.broadcasted_iota(jnp.int32, (LANES, FEATS), 0) - head * F
    first = jnp.where(lane == index_ref[0:1, :], 1.0, 0.0).astype(bf16)
    second = jnp.where(lane == index_ref[1:2, :], 1.0, 0.0).astype(bf16)
    return first, second


def factors(rows, first, second, scale_ref):
    return (dot(rows, first) + scale_ref[0:1, :], dot(rows, second) + scale_ref[1:2, :])


def window(head):
    start = head * HW
    base = min(start // LANES * LANES, VC - 2 * LANES)
    return base, start - base


def both_halves(core_ref, ref, columns):
    core = core_ref[0]
    return jnp.concatenate([ref[core, :, columns], ref[1 - core, :, columns]], axis=0)


def store_halves(core_ref, ref, rows, columns):
    core, half = core_ref[0], rows.shape[0] // CORES
    ref[core, :, columns] = rows[:half]
    ref[1 - core, :, columns] = rows[half:]


def head_columns(core_ref, ref, head):
    base, offset = window(head)
    wide = both_halves(core_ref, ref, slice(base, base + 2 * LANES)).astype(f32)
    if offset:
        wide = pltpu.roll(wide, 2 * LANES - offset, 1)
    return wide[:, :LANES]


def add_head_columns(ref, head, block):
    base, offset = window(head)
    wide = jnp.concatenate([block, jnp.zeros_like(block)], axis=1)
    if offset:
        wide = pltpu.roll(wide, offset, 1)
    ref[:, base : base + 2 * LANES] += wide


def with_one(block):
    lane = lax.broadcasted_iota(jnp.int32, block.shape, 1)
    return jnp.where(lane < HW, block, jnp.where(lane == HW, 1.0, 0.0))


def only_head(rows, head):
    lane = lax.broadcasted_iota(jnp.int32, rows.shape, 1)
    inside = (lane >= head * F) & (lane < head * F + F)
    return jnp.where(inside, rows.astype(f32), 0.0).astype(bf16)


def state_kernel(core_ref, index_ref, scale_ref, k_ref, v_ref, state_ref):
    keys = both_halves(core_ref, k_ref, slice(None))
    for head in range(HC):
        first, second = selectors(index_ref, head)
        one, two = factors(keys, first, second, scale_ref)
        phi = (one * two * scale_ref[2:3, :]).astype(bf16)
        values = with_one(head_columns(core_ref, v_ref, head)).astype(bf16)
        state_ref[0, head] = dot_tn(phi, values)[:FROWS]


def scores_of(q_head, keys):
    scores = dot_nt(q_head, keys) * SCALE
    row = lax.broadcasted_iota(jnp.int32, scores.shape, 0)
    column = lax.broadcasted_iota(jnp.int32, scores.shape, 1)
    return scores, column <= row


def forward_kernel(core_ref, index_ref, scale_ref, q_ref, k_ref, v_ref, before_ref, mixer_ref, den_ref, wide):
    queries = both_halves(core_ref, q_ref, slice(None))
    keys = both_halves(core_ref, k_ref, slice(None))
    wide[...] = jnp.zeros_like(wide)
    lane = lax.broadcasted_iota(jnp.int32, (queries.shape[0], LANES), 1)
    dens = jnp.zeros((queries.shape[0], LANES), f32)
    for head in range(HC):
        first, second = selectors(index_ref, head)
        one, two = factors(queries, first, second, scale_ref)
        phi = (one * two).astype(bf16)
        values = with_one(head_columns(core_ref, v_ref, head)).astype(bf16)
        scores, allowed = scores_of(only_head(queries, head), keys)
        kernel = jnp.where(allowed, 1.0 + scores + 0.5 * scores * scores, 0.0).astype(bf16)
        total = dot(kernel, values) + dot(phi[:, :FROWS], before_ref[0, head])
        den = total[:, HW : HW + 1]
        add_head_columns(wide, head, jnp.where(lane < HW, total / den, 0.0))
        dens = jnp.where(lane == head, den, dens)
    store_halves(core_ref, mixer_ref, wide[...].astype(bf16), slice(None))
    store_halves(core_ref, den_ref, dens, slice(None))


def pull_kernel(core_ref, index_ref, scale_ref, q_ref, gm_ref, mixer_ref, den_ref, state_ref, gnum_ref):
    queries = both_halves(core_ref, q_ref, slice(None))
    lane = lax.broadcasted_iota(jnp.int32, (queries.shape[0], LANES), 1)
    dens = both_halves(core_ref, den_ref, slice(None))
    for head in range(HC):
        first, second = selectors(index_ref, head)
        one, two = factors(queries, first, second, scale_ref)
        phi = (one * two).astype(bf16)
        den = dens[:, head : head + 1]
        grad = jnp.where(lane < HW, head_columns(core_ref, gm_ref, head), 0.0)
        mixer = head_columns(core_ref, mixer_ref, head)
        pulled = -jnp.sum(grad * mixer, axis=1, keepdims=True)
        grad = (jnp.where(lane == HW, pulled, grad) / den).astype(bf16)
        store_halves(core_ref, gnum_ref, grad, slice(head * LANES, (head + 1) * LANES))
        state_ref[0, head] = dot_tn(phi, grad)[:FROWS]


def backward_kernel(
    core_ref, index_ref, scale_ref, q_ref, k_ref, v_ref, gnum_ref, before_ref, after_ref, gqk_ref, gv_ref, wide
):
    queries = both_halves(core_ref, q_ref, slice(None))
    keys = both_halves(core_ref, k_ref, slice(None))
    wide[...] = jnp.zeros_like(wide)
    lane = lax.broadcasted_iota(jnp.int32, (queries.shape[0], LANES), 1)
    grad_q = jnp.zeros((queries.shape[0], LANES), f32)
    grad_k = jnp.zeros((queries.shape[0], LANES), f32)
    for head in range(HC):
        first, second = selectors(index_ref, head)
        coef = scale_ref[2:3, :]
        q_one, q_two = factors(queries, first, second, scale_ref)
        k_one, k_two = factors(keys, first, second, scale_ref)
        values = with_one(head_columns(core_ref, v_ref, head)).astype(bf16)
        gnum = both_halves(core_ref, gnum_ref, slice(head * LANES, (head + 1) * LANES))
        q_head = only_head(queries, head)
        k_head = only_head(keys, head)
        scores, allowed = scores_of(q_head, keys)
        kernel = jnp.where(allowed, 1.0 + scores + 0.5 * scores * scores, 0.0).astype(bf16)
        grad_kernel = dot_nt(gnum, values)
        grad_scores = (jnp.where(allowed, grad_kernel * (1.0 + scores), 0.0) * SCALE).astype(bf16)
        phi_k = (k_one * k_two * coef).astype(bf16)
        after = after_ref[0, head]
        before = before_ref[0, head]
        grad_v = dot_tn(kernel, gnum) + dot(phi_k[:, :FROWS], after)
        add_head_columns(wide, head, jnp.where(lane < HW, grad_v, 0.0))
        empty = jnp.zeros((FEATS - FROWS, LANES), bf16)
        grad_phi_q = dot_nt(gnum, jnp.concatenate([before, empty], axis=0))
        grad_phi_k = dot_nt(values, jnp.concatenate([after, empty], axis=0)) * coef
        grad_q += dot(grad_scores, k_head)
        grad_q += dot_nt((grad_phi_q * q_two).astype(bf16), first)
        grad_q += dot_nt((grad_phi_q * q_one).astype(bf16), second)
        grad_k += dot_tn(grad_scores, q_head)
        grad_k += dot_nt((grad_phi_k * k_two).astype(bf16), first)
        grad_k += dot_nt((grad_phi_k * k_one).astype(bf16), second)
    store_halves(core_ref, gqk_ref, grad_q.astype(bf16), slice(0, LANES))
    store_halves(core_ref, gqk_ref, grad_k.astype(bf16), slice(LANES, 2 * LANES))
    store_halves(core_ref, gv_ref, wide[...].astype(bf16), slice(None))


def per_slot(kernel, slots, rows, ins, outs, scratch, flops):
    def table():
        return pl.BlockSpec((8, FEATS), lambda s, core: (0, 0))

    def row_spec(width, column=0):
        return pl.BlockSpec((CORES, None, rows, width), lambda s, core: (0, s, 0, column))

    def state_spec():
        return pl.BlockSpec((1, HC, FROWS, LANES), lambda s, core: (s, 0, 0, 0))

    def spec(kind):
        return state_spec() if kind == "state" else row_spec(*kind)

    def shape(kind, dtype):
        if kind == "state":
            return jax.ShapeDtypeStruct((slots, HC, FROWS, LANES), dtype)
        return jax.ShapeDtypeStruct((CORES, slots, rows, kind[0]), dtype)

    return pl.pallas_call(
        kernel,
        grid_spec=pltpu.PrefetchScalarGridSpec(
            num_scalar_prefetch=1,
            grid=(slots,),
            in_specs=[table(), table()] + [spec(kind) for kind in ins],
            out_specs=[spec(kind) for kind, _ in outs],
            scratch_shapes=scratch,
        ),
        out_shape=[shape(kind, dtype) for kind, dtype in outs],
        compiler_params=pltpu.CompilerParams(vmem_limit_bytes=56 << 20),
        cost_estimate=pl.CostEstimate(flops=flops, bytes_accessed=8 << 20, transcendentals=0),
    )


def passed_along(array, axis, by):
    count = lax.axis_size(axis)
    pairs = [(i, i + by) for i in range(count) if 0 <= i + by < count]
    return lax.ppermute(array, axis, pairs)


def both_cores(mine, theirs, axis):
    first = lax.axis_index("core") == 0
    return jnp.concatenate(
        [jnp.where(first, mine, theirs), jnp.where(first, theirs, mine)], axis=axis
    )


def swapped(array):
    return lax.ppermute(array, "core", [(0, 1), (1, 0)])


def part_of(array, axis, index):
    return lax.dynamic_index_in_dim(array, index, axis, keepdims=False)


def bits_of(axis):
    return [(axis, bit) for bit in reversed(range(lax.axis_size(axis).bit_length() - 1))]


def bit_at(axis, bit):
    return (lax.axis_index(axis) >> bit) & 1


def exchanged(array, axis, bit):
    count = lax.axis_size(axis)
    return lax.ppermute(array, axis, [(i, i ^ (1 << bit)) for i in range(count)])


def tied(*arrays):
    return lax.optimization_barrier(arrays)


class Gather:
    def __init__(self, piece, x_first):
        self.columns = piece.shape[1]
        self.block = piece
        low_first = lambda axis: bits_of(axis)[::-1]
        self.plan = [(step, at) for at, step in enumerate(bits_of("z"))]
        if x_first:
            self.plan += [(step, 0) for step in low_first("x") + low_first("y")]
        else:
            self.plan += [(step, 0) for step in low_first("y")]
            self.plan += [(step, len(bits_of("y"))) for step in low_first("x")]

    def stage(self):
        (axis, bit), dim = self.plan.pop(0)
        mine = bit_at(axis, bit)
        arrived = exchanged(self.block, axis, bit)
        shape = self.block.shape[:dim] + (2,) + self.block.shape[dim:]
        whole = jnp.zeros(shape, self.block.dtype)
        whole = lax.dynamic_update_index_in_dim(whole, self.block, mine, dim)
        self.block = lax.dynamic_update_index_in_dim(whole, arrived, 1 - mine, dim)
        return self

    def along_z(self):
        while self.plan[0][0][0] == "z":
            self.stage()
        return self

    def rest(self):
        while self.plan:
            self.stage()
        return self.block.reshape(D, self.columns)


class Scatter:
    def __init__(self, terms, x_first):
        self.dims = bits_of("y") + bits_of("x") + bits_of("z")
        order = ("x", "y") if x_first else ("y", "x")
        self.plan = bits_of(order[0]) + bits_of(order[1]) + bits_of("z")[::-1]
        rows = D >> len(self.dims)
        self.terms = [terms.reshape((2,) * len(self.dims) + (rows, terms.shape[1]))]

    def total(self, terms):
        total = terms[0].astype(f32)
        for term in terms[1:]:
            total = total + term.astype(f32)
        return total

    def stage(self):
        step = self.plan.pop(0)
        dim, mine = self.dims.index(step), bit_at(*step)
        self.dims.remove(step)
        sent = self.total([part_of(term, dim, 1 - mine) for term in self.terms]).astype(bf16)
        self.terms = [part_of(term, dim, mine) for term in self.terms]
        self.terms.append(exchanged(sent, *step))
        return self

    def rest(self):
        while self.plan:
            self.stage()
        return self.total(self.terms)


def chain(local, up):
    count = lax.axis_size("z")
    total = jnp.zeros_like(local)
    for hop in range(1, count):
        pair = (hop - 1, hop) if up else (count - hop, count - hop - 1)
        message = (total + local).astype(bf16)
        total = total + lax.ppermute(message, "z", [pair]).astype(f32)
    return total.astype(bf16)


def mesh_exchange(y, x, z, core, axis):
    if axis == "core":
        return (y, x, z, 1 - core)
    if axis == "y":
        return (1 - y, x, z, core)
    if axis == "x":
        return (y, 1 - x, z, core)
    if axis == "z0":
        return (y, x, z + 1 - 2 * (z % 2), core)
    return (y, x, (z + 2) % 4, core)


ORDERS = (("y", "x", "z0", "z1"), ("x", "y", "z0", "z1"))


def reduce_kernel(
    down_a_ref,
    gate_ref,
    down_b_ref,
    up_ref,
    last_a_ref,
    last_b_ref,
    qk_ref,
    value_ref,
    out_ref,
    gu_ref,
    down_ref,
    small_ref,
    sums,
    halves,
    quarters,
    finals,
    got_terms,
    got_sums,
    got_halves,
    got_quarters,
    send_sem,
    recv_sem,
):
    y, x, z, core = places_of()
    places = {"y": y, "x": x, "z0": z % 2, "z1": z // 2}

    def tiles(ref):
        return ref.shape[-1] // LANES

    parts, count = ([], []), 0
    for stream, refs in enumerate(((down_a_ref, gate_ref, last_a_ref), (down_b_ref, up_ref, last_b_ref))):
        at = 0
        for ref in refs:
            parts[stream].append((ref, len(ref.shape) == 3, at, at + tiles(ref)))
            at += tiles(ref)
        count = max(count, at)
    own_down = core * tiles_of(FC)
    own_value = core * tiles_of(VC)
    small_at = parts[1][2][2] + tiles_of(VC) + 1
    places_out = (
        (
            (down_ref, own_down, 0, parts[0][0][3]),
            (gu_ref, own_down, parts[0][1][2], parts[0][1][3]),
            (value_ref, own_value, parts[0][2][2], parts[0][2][2] + tiles_of(VC)),
            (qk_ref, core, parts[0][2][3] - 1, parts[0][2][3]),
        ),
        (
            (down_ref, own_down + parts[0][0][3], 0, parts[1][0][3]),
            (gu_ref, CORES * tiles_of(FC) + own_down, parts[1][1][2], parts[1][1][3]),
            (out_ref, own_value, parts[1][2][2], parts[1][2][2] + tiles_of(VC)),
            (qk_ref, CORES + core, small_at - 1, small_at),
            (small_ref, core, small_at, small_at + 1),
        ),
    )
    greet(y, x, z, core, True)

    def columns(tile):
        return pl.ds(pl.multiple_of(tile * LANES, LANES), LANES)

    def transfer(stream, stage, chunk, source, target=None):
        landing = chunk % 4
        if target is None:
            target = (got_terms, got_sums, got_halves, got_quarters)[stage].at[stream, landing]
        axis = (ORDERS[stream] + ("core",))[stage]
        return pltpu.make_async_remote_copy(
            src_ref=source,
            dst_ref=target,
            send_sem=send_sem.at[stream, stage, landing],
            recv_sem=recv_sem.at[stream, stage, landing],
            device_id=mesh_exchange(y, x, z, core, axis),
            device_id_type=pl.DeviceIdType.MESH,
        )

    def first_view(stream, ref, tile, place):
        ref = ref.at[:, :, :, columns(tile)]
        return ref.at[place] if stream == 0 else ref.at[:, place]

    def source_of(stream, stage, chunk):
        there = 1 - places[ORDERS[stream][stage]]
        if stage == 1:
            return sums.at[stream, chunk % 2, there]
        if stage == 2:
            return halves.at[stream, chunk % 2, :, there]
        return quarters.at[stream, chunk % 2, there]

    def add(a, b):
        return a.astype(f32) + b.astype(f32)

    def begin(stream, chunk):
        ref, _, start, stop = parts[stream][2]

        @pl.when((chunk >= start) & (chunk < stop))
        def _():
            there = 1 - places[ORDERS[stream][0]]
            transfer(stream, 0, chunk, first_view(stream, ref, chunk - start, there)).start()

    def second(stream, chunk):
        for ref, summed, start, stop in parts[stream]:

            @pl.when((chunk >= start) & (chunk < stop))
            def _(ref=ref, summed=summed, start=start):
                tile = chunk - start
                if summed:
                    sums[stream, chunk % 2] = ref[:, :, columns(tile)]
                else:
                    there = 1 - places[ORDERS[stream][0]]
                    transfer(stream, 0, chunk, first_view(stream, ref, tile, there)).wait()
                    own = first_view(stream, ref, tile, places[ORDERS[stream][0]])[...]
                    sums[stream, chunk % 2] = add(own, got_terms[stream, chunk % 4]).astype(bf16)

        transfer(stream, 1, chunk, source_of(stream, 1, chunk)).start()

    def advance(stream, stage, chunk):
        here = places[ORDERS[stream][stage]]
        slot, landing = chunk % 2, chunk % 4
        transfer(stream, stage, chunk, source_of(stream, stage, chunk)).wait()
        if stage == 1:
            total = add(sums[stream, slot, here], got_sums[stream, landing]).astype(bf16)
            halves[stream, slot] = total.reshape(halves.shape[2:])
        elif stage == 2:
            own = halves[stream, slot, :, here]
            quarters[stream, slot] = add(own, got_halves[stream, landing]).astype(bf16)
        else:
            total = add(quarters[stream, slot, here], got_quarters[stream, landing])
            finals[stream, slot] = total.reshape(finals.shape[2:])
        if stage < 3:
            transfer(stream, stage + 1, chunk, source_of(stream, stage + 1, chunk)).start()

    def hand_over(stream, chunk, waiting):
        for ref, first, start, stop in places_out[stream]:

            @pl.when((chunk >= start) & (chunk < stop))
            def _(ref=ref, first=first, start=start):
                target = ref.at[:, columns(first + chunk - start)]
                copy = transfer(stream, 4, chunk, finals.at[stream, chunk % 2, 1 - core], target)
                if waiting:
                    copy.wait()
                else:
                    target[...] = finals[stream, chunk % 2, core]
                    copy.start()

    @pl.loop(0, count + 5)
    def _(step):
        for stream in range(2):
            total = parts[stream][2][3]

            @pl.when(step < total)
            def _(stream=stream):
                begin(stream, step)

        for stage in range(5):
            for stream in range(2):
                total = parts[stream][2][3]

                @pl.when((step >= stage + 1) & (step < total + stage + 1))
                def _(stage=stage, stream=stream):
                    chunk = step - stage - 1
                    if stage == 0:
                        second(stream, chunk)
                    elif stage < 4:
                        advance(stream, stage, chunk)
                    else:
                        hand_over(stream, chunk, True)
                    if stage == 3:
                        hand_over(stream, chunk, False)


def tiles_of(width):
    return width // LANES


def first_exchange(terms, axis):
    view = terms.reshape(2, 2, D // 4, terms.shape[1])
    dim = 0 if axis == "y" else 1
    mine = bit_at(axis, 0)
    arrived = exchanged(part_of(view, dim, 1 - mine), axis, 0)
    return (part_of(view, dim, mine).astype(f32) + arrived.astype(f32)).astype(bf16)


def reduced(down_a, gate, down_b, up, last_a, last_b, owned):
    block, rows = D // 4, D // 16
    dma = pltpu.SemaphoreType.DMA
    last_a, last_b = (last.reshape(2, 2, block, last.shape[1]) for last in (last_a, last_b))
    widths = (2 * CORES * QC, CORES * VC, CORES * VC, 2 * CORES * FC, CORES * FC, CORES * LANES)
    return pl.pallas_call(
        reduce_kernel,
        out_shape=[jax.ShapeDtypeStruct((owned, width), f32) for width in widths],
        in_specs=[pl.BlockSpec(memory_space=pltpu.VMEM)] * 6,
        out_specs=[pl.BlockSpec(memory_space=pltpu.VMEM)] * 6,
        scratch_shapes=[
            pltpu.VMEM((2, 2, 2, block, LANES), bf16),
            pltpu.VMEM((2, 2, 2, 2, rows, LANES), bf16),
            pltpu.VMEM((2, 2, 2, rows, LANES), bf16),
            pltpu.VMEM((2, 2, CORES, owned, LANES), f32),
            pltpu.VMEM((2, 4, 2, block, LANES), bf16),
            pltpu.VMEM((2, 4, block, LANES), bf16),
            pltpu.VMEM((2, 4, 2, rows, LANES), bf16),
            pltpu.VMEM((2, 4, rows, LANES), bf16),
            dma((2, 5, 4)),
            dma((2, 5, 4)),
        ],
        compiler_params=pltpu.CompilerParams(
            collective_id=0, has_side_effects=True, vmem_limit_bytes=56 << 20
        ),
        cost_estimate=pl.CostEstimate(flops=0, bytes_accessed=1024, transcendentals=0),
    )(down_a, gate, down_b, up, last_a, last_b)


def places_of():
    y, x, z, core = (lax.axis_index(axis) for axis in ("y", "x", "z", "core"))
    return y, x, z, core


def greet(y, x, z, core, both_cores=False):
    barrier = pltpu.get_barrier_semaphore()
    partners = ORDERS[0] + (("core",) if both_cores else ())
    for axis in partners:
        pl.semaphore_signal(
            barrier,
            inc=1,
            device_id=mesh_exchange(y, x, z, core, axis),
            device_id_type=pl.DeviceIdType.MESH,
        )
    pl.semaphore_wait(barrier, len(partners))


GATHER_ORDERS = (("z1", "z0", "x", "y"), ("z1", "z0", "y", "x"))


def gather_view(ref, order, stage, y, x, z):
    if stage == 0:
        return ref.at[y, x, z // 2, z % 2]
    if stage == 1:
        return ref.at[y, x, :, z % 2]
    if stage == 2:
        return ref.at[y, x]
    return ref.at[y] if order == 0 else ref.at[:, x]


def gather_kernel(tiles, shard_ref, full_ref, send_sem, recv_sem):
    y, x, z, core = places_of()
    full_ref[y, x, z // 2, z % 2] = shard_ref[...]
    greet(y, x, z, core)

    def transfer(stage, tile, order):
        columns = pl.ds(pl.multiple_of(tile * LANES, LANES), LANES)
        view = gather_view(full_ref.at[:, :, :, :, :, columns], order, stage, y, x, z)
        return pltpu.make_async_remote_copy(
            src_ref=view,
            dst_ref=view,
            send_sem=send_sem.at[stage, tile],
            recv_sem=recv_sem.at[stage, tile],
            device_id=mesh_exchange(y, x, z, core, GATHER_ORDERS[order][stage]),
            device_id_type=pl.DeviceIdType.MESH,
        )

    pairs = (tiles + 1) // 2

    def each(step, behind, act):
        for order in range(2):
            tile = 2 * (step - behind) + order

            @pl.when((tile >= 0) & (tile < tiles))
            def _(tile=tile, order=order):
                act(tile, order)

    @pl.loop(0, pairs + 4)
    def _(step):
        each(step, 0, lambda tile, order: transfer(0, tile, order).start())
        for stage in range(4):

            def act(tile, order, stage=stage):
                transfer(stage, tile, order).wait()
                if stage < 3:
                    transfer(stage + 1, tile, order).start()

            each(step, stage + 1, act)


def gathered_rows(shard):
    rows, width = shard.shape
    tiles = width // LANES
    full = pl.pallas_call(
        functools.partial(gather_kernel, tiles),
        out_shape=jax.ShapeDtypeStruct((2, 2, 2, 2, rows, width), bf16),
        in_specs=[pl.BlockSpec(memory_space=pltpu.VMEM)],
        out_specs=pl.BlockSpec(memory_space=pltpu.VMEM),
        scratch_shapes=[
            pltpu.SemaphoreType.DMA((4, tiles)),
            pltpu.SemaphoreType.DMA((4, tiles)),
        ],
        compiler_params=pltpu.CompilerParams(
            collective_id=1, has_side_effects=True, vmem_limit_bytes=40 << 20
        ),
        cost_estimate=pl.CostEstimate(flops=0, bytes_accessed=1024, transcendentals=0),
    )(shard)
    return full.reshape(D, width)


SLOTS = 10


def feed_forward_kernel(
    tiles,
    second_ref,
    grad_ref,
    shard_ref,
    hidden_ref,
    grad_gate_ref,
    grad_up_ref,
    down_own_ref,
    down_other_ref,
    second_own_ref,
    second_other_ref,
    held,
    down_ref,
    grad_second_ref,
    send_sem,
    recv_sem,
    out_sem,
):
    y, x, z, core = places_of()
    down_ref[...] = jnp.zeros_like(down_ref)
    grad_second_ref[...] = jnp.zeros_like(grad_second_ref)
    greet(y, x, z, core)
    tokens = second_ref.shape[0]
    block = 256 if tokens % 256 == 0 else tokens

    def transfer(stage, tile, order):
        slot = tile % SLOTS
        view = gather_view(held.at[slot], order, stage, y, x, z)
        return pltpu.make_async_remote_copy(
            src_ref=view,
            dst_ref=view,
            send_sem=send_sem.at[stage, slot],
            recv_sem=recv_sem.at[stage, slot],
            device_id=mesh_exchange(y, x, z, core, GATHER_ORDERS[order][stage]),
            device_id_type=pl.DeviceIdType.MESH,
        )

    def compute(tile):
        weights = held.at[tile % SLOTS]
        columns = pl.ds(pl.multiple_of(tile * LANES, LANES), LANES)

        @pl.loop(0, tokens // block)
        def _(part):
            rows = pl.ds(pl.multiple_of(part * block, block), block)
            both = weights[:, :, :, :, :, : 2 * LANES].reshape(D, 2 * LANES)
            down = weights[:, :, :, :, :, 2 * LANES :].reshape(D, LANES)
            gate_up = dot(second_ref[rows, :], both)
            gate, upward = gate_up[:, :LANES], gate_up[:, LANES:]
            grad_hidden = dot(grad_ref[rows, :], down)
            sigmoid_gate = 1.0 / (1.0 + jnp.exp(-gate))
            silu_gate = gate * sigmoid_gate
            hidden = (silu_gate * upward).astype(bf16)
            grad_upward = (grad_hidden * silu_gate).astype(bf16)
            grad_gate = (
                grad_hidden * upward * sigmoid_gate * (1.0 + gate * (1.0 - sigmoid_gate))
            ).astype(bf16)
            hidden_ref[rows, columns] = hidden
            grad_up_ref[rows, columns] = grad_upward
            grad_gate_ref[rows, columns] = grad_gate
            down_ref[rows, :] += dot_nt(hidden, down)
            grad_second_ref[rows, :] += dot_nt(
                jnp.concatenate([grad_gate, grad_upward], axis=1), both
            )

    pairs = (tiles + 1) // 2

    def each(step, behind, act):
        for order in range(2):
            tile = 2 * (step - behind) + order

            @pl.when((tile >= 0) & (tile < tiles))
            def _(tile=tile, order=order):
                act(tile, order)

    def send_on(stage):
        def act(tile, order):
            transfer(stage, tile, order).wait()
            transfer(stage + 1, tile, order).start()

        return act

    def finish(tile, order):
        transfer(3, tile, order).wait()
        compute(tile)

    def begin(tile, order):
        held[tile % SLOTS, y, x, z // 2, z % 2] = shard_ref[tile]
        transfer(0, tile, order).start()

    @pl.loop(0, pairs + 4)
    def _(step):
        each(step, 2, send_on(1))
        each(step, 3, send_on(2))
        each(step, 4, finish)
        each(step, 1, send_on(0))
        each(step, 0, begin)

    half = tokens // 2
    copies = [
        pltpu.make_async_copy(source, target, out_sem.at[at])
        for at, (source, target) in enumerate(
            (
                (grad_second_ref.at[half:], second_other_ref),
                (grad_second_ref.at[:half], second_own_ref),
                (down_ref.at[half:], down_other_ref),
                (down_ref.at[:half], down_own_ref),
            )
        )
    ]
    for copy in copies:
        copy.start()
    for copy in copies:
        copy.wait()


def feed_forward(second, grad_result, gate_shard, up_shard, down_shard):
    tokens = second.shape[0]
    rows, width = gate_shard.shape
    tiles = width // LANES
    parts = [shard.reshape(rows, tiles, LANES) for shard in (gate_shard, up_shard, down_shard)]
    shard = jnp.transpose(jnp.stack(parts, axis=2), (1, 0, 2, 3)).reshape(tiles, rows, 3 * LANES)
    narrow = jax.ShapeDtypeStruct((tokens, width), bf16)
    part = jax.ShapeDtypeStruct((tokens // 2, D), f32)
    return pl.pallas_call(
        functools.partial(feed_forward_kernel, tiles),
        out_shape=(narrow,) * 3 + (part,) * 4,
        in_specs=[pl.BlockSpec(memory_space=pltpu.VMEM)] * 3,
        out_specs=[pl.BlockSpec(memory_space=pltpu.VMEM)] * 3 + [pl.BlockSpec(memory_space=pl.ANY)] * 4,
        scratch_shapes=[
            pltpu.VMEM((SLOTS, 2, 2, 2, 2, rows, 3 * LANES), bf16),
            pltpu.VMEM((tokens, D), f32),
            pltpu.VMEM((tokens, D), f32),
            pltpu.SemaphoreType.DMA((4, SLOTS)),
            pltpu.SemaphoreType.DMA((4, SLOTS)),
            pltpu.SemaphoreType.DMA((4,)),
        ],
        compiler_params=pltpu.CompilerParams(
            collective_id=2, has_side_effects=True, vmem_limit_bytes=60 << 20
        ),
        cost_estimate=pl.CostEstimate(flops=0, bytes_accessed=1024, transcendentals=0),
    )(second, grad_result, shard)


def norm_scale(values):
    inverse = lax.rsqrt(jnp.mean(values * values, axis=-1, keepdims=True) + norm_epsilon)
    return (values * inverse, inverse)


def norm_backward(grad_normed, scaled, inverse, gain_row):
    grad_scaled = grad_normed * gain_row[None, :]
    grad_input = inverse * (
        grad_scaled - scaled * jnp.mean(grad_scaled * scaled, axis=-1, keepdims=True)
    )
    return (grad_input, jnp.sum(grad_normed * scaled, axis=0))


def adam_update(weight, gradient, first_moment, second_moment, learn_rate, decay_rate):
    first_new = beta_first * first_moment + (1.0 - beta_first) * gradient
    second_new = beta_second * second_moment + (1.0 - beta_second) * gradient * gradient
    first_hat = first_new / (1.0 - beta_first**STEP)
    second_hat = second_new / (1.0 - beta_second**STEP)
    new_weight = (
        weight
        - learn_rate * first_hat / (jnp.sqrt(second_hat) + adam_epsilon)
        - decay_rate * weight
    )
    return (new_weight, second_new)


def local(
    tokens,
    cotangent,
    lengths,
    w_qk,
    w_value,
    w_out,
    w_gu,
    w_down,
    small_params,
    m_qk,
    m_value,
    m_out,
    m_gu,
    m_down,
    m_small,
    v_qk,
    v_value,
    v_out,
    v_gu,
    v_down,
    v_small,
):
    slots, slot_rows, _ = tokens.shape
    owned = w_qk.shape[0]
    rows = slots * slot_rows
    core, z_at = lax.axis_index("core"), lax.axis_index("z")
    other = 1 - core
    first_core = core == 0

    def on_chip(array):
        return jnp.concatenate([array, swapped(array)], axis=0)

    def halves(array):
        return array.reshape(CORES, slots, slot_rows, -1)

    columns_of = [
        w_qk.astype(bf16).reshape(owned, 2, CORES, QC),
        w_value.astype(bf16).reshape(owned, 1, CORES, VC),
        w_out.astype(bf16).reshape(owned, 1, CORES, VC),
        w_gu.astype(bf16).reshape(owned, 2, CORES, FC),
        w_down.astype(bf16).reshape(owned, 1, CORES, FC),
    ]
    small_low = jnp.pad(small_params.astype(bf16), ((0, 0), (0, LANES - (KS + 2))))

    def shard(which, index):
        parts = [part_of(columns_of[i], 2, index).reshape(owned, -1) for i in which]
        return jnp.concatenate(parts, axis=1) if len(parts) > 1 else parts[0]

    def chip_shard(which, extra=None):
        mine, theirs = shard(which, core), shard(which, other)
        arrived = swapped(theirs if extra is None else jnp.concatenate([theirs, extra], axis=1))
        mine = mine if extra is None else jnp.concatenate([mine, extra], axis=1)
        return both_cores(mine, arrived, 0)

    attention_shard = chip_shard((0, 1), small_low)
    rest_shard = chip_shard((2, 3, 4))
    in_kernel = tuple(lax.axis_size(axis) for axis in ("y", "x", "z")) == (2, 2, 4)
    early_width = 2 * QC + VC + LANES
    half = early_width // 2
    cut = FC // 2 // LANES * LANES
    down_at = VC + 2 * FC
    own_tokens = tokens.reshape(rows, D)
    other_tokens = swapped(own_tokens)
    wide_part = 4 * LANES
    if in_kernel:
        full = gathered_rows(jnp.concatenate([attention_shard, rest_shard[:, :VC]], axis=1))
        early, out_half = full[:, :early_width], full[:, early_width:]
    else:
        early_a = Gather(attention_shard[:, :half], True)
        early_b = Gather(attention_shard[:, half:], False)
        early = jnp.concatenate([early_a.rest(), early_b.rest()], axis=1)

        def gathered(start, width):
            return lax.all_gather(rest_shard[:, start : start + width], ("y", "x", "z"), axis=0, tiled=True)

        out_half = gathered(0, VC)
        gate_full = gathered(VC, FC)
        up_full = gathered(VC + FC, FC)
        last_shard, early = tied(rest_shard[:, down_at:], early)
        down_a = Gather(last_shard[:, :cut], True)
        down_b = Gather(last_shard[:, cut:], False)
        down_full = jnp.concatenate([down_a.rest(), down_b.rest()], axis=1)

    qk_full = early[:, : 2 * QC]
    value_full = early[:, 2 * QC : 2 * QC + VC]
    small_float = early[:, 2 * QC + VC :][:, : KS + 2].astype(f32)
    out_full = both_cores(out_half, swapped(out_half), 1)
    gain_first, gain_second = small_float[:, KS], small_float[:, KS + 1]
    taps = [part_of(small_float[:, j].reshape(CORES, VC), 0, core) for j in range(KS)]

    inputs = tokens.reshape(rows, D).astype(f32)
    scaled_first, inverse_first = norm_scale(inputs)
    scaled_chip, _ = norm_scale(
        jnp.concatenate([own_tokens, other_tokens], axis=0).astype(f32)
    )
    normed_chip = (scaled_chip * gain_first[None, :]).astype(bf16)
    query_key = halves(dot(normed_chip, qk_full).astype(bf16))
    value_pre = halves(dot(normed_chip, value_full).astype(bf16))
    tail = value_pre[:, :, slot_rows - (KS - 1) :, :]
    from_chip = passed_along(part_of(tail, 0, other), "z", 1)
    from_core = part_of(tail, 0, core)
    earlier = jnp.stack(
        [jnp.where(first_core, from_chip, from_core), jnp.where(first_core, from_core, from_chip)]
    )
    extended = jnp.concatenate([earlier, value_pre], axis=2).astype(f32)

    def tap_rows(j):
        return extended[:, :, KS - 1 - j : KS - 1 - j + slot_rows, :]

    convolved = taps[0] * tap_rows(0)
    for j in range(1, KS):
        convolved = convolved + taps[j] * tap_rows(j)
    values = convolved.astype(bf16)

    index_np, scale_np = feature_tables()
    tables = (core.astype(jnp.int32).reshape(1), jnp.asarray(index_np), jnp.asarray(scale_np))
    q_spec, k_spec, v_spec = (LANES, 0), (LANES, 1), (VC,)
    call = functools.partial(per_slot, slots=slots, rows=slot_rows)
    unit = 2 * CORES * rows * HC * LANES * FEATS
    wide = [pltpu.VMEM((CORES * slot_rows, VC), f32)]
    (state_own,) = call(
        state_kernel, ins=[k_spec, v_spec], outs=[("state", f32)], scratch=[], flops=4 * unit
    )(*tables, query_key, values)
    before = chain(state_own, True)
    mixer, dens = call(
        forward_kernel,
        ins=[q_spec, k_spec, v_spec, "state"],
        outs=[(v_spec, bf16), ((LANES,), f32)],
        scratch=wide,
        flops=8 * unit,
    )(*tables, query_key, query_key, values, before)

    mixer_flat = mixer.reshape(CORES * rows, VC)
    mixer_theirs = swapped(mixer_flat)
    mixer_own = both_cores(mixer_flat[:rows], mixer_theirs[rows:], 1)
    mixer_other = both_cores(mixer_flat[rows:], mixer_theirs[:rows], 1)
    after_mixer = inputs + dot(mixer_own, out_full)
    scaled_second, inverse_second = norm_scale(after_mixer)
    second_low = (scaled_second * gain_second[None, :]).astype(bf16)
    second_chip = on_chip(second_low)

    half_at = jnp.where(first_core, jnp.arange(CORES), 1 - jnp.arange(CORES))
    positions = (z_at * CORES + half_at)[:, None] * slot_rows + jnp.arange(slot_rows)[None, :]
    valid_chip = positions[:, None, :] < lengths[None, :, None]
    valid_chip = valid_chip.astype(f32).reshape(CORES * rows, 1)
    valid = valid_chip[:rows]
    query_key, cotangent_late = lax.optimization_barrier((query_key, cotangent))
    cotangent_chip = on_chip(cotangent_late.reshape(rows, D))
    mixer, cotangent_chip = tied(mixer, cotangent_chip)
    grad_result_chip = (valid_chip * cotangent_chip.astype(f32)).astype(bf16)
    grad_result = valid * cotangent.reshape(rows, D).astype(f32)

    if in_kernel:
        hidden, grad_gate, grad_upward, *ffn_parts = feed_forward(
            second_chip,
            grad_result_chip,
            rest_shard[:, VC : VC + FC],
            rest_shard[:, VC + FC : down_at],
            rest_shard[:, down_at:],
        )
        down_own, down_other, second_own, second_other = ffn_parts
        grad_second = second_own + swapped(second_other)
        down_result = down_own + swapped(down_other)
        down_terms = dot_tn(grad_result_chip, hidden).astype(bf16)
        gate_terms = dot_tn(second_chip, grad_gate).astype(bf16)
        up_terms = dot_tn(second_chip, grad_upward).astype(bf16)
        grad_second, gate_terms, up_terms, down_terms = tied(
            grad_second, gate_terms, up_terms, down_terms
        )
        sum_gate, sum_up = first_exchange(gate_terms, "y"), first_exchange(up_terms, "x")
        at = 10 * LANES
        sum_down = (
            first_exchange(down_terms[:, :at], "y"),
            first_exchange(down_terms[:, at:], "x"),
        )
    else:
        gate = dot(second_chip, gate_full)
        upward = dot(second_chip, up_full)
        sigmoid_gate = jax.nn.sigmoid(gate)
        silu_gate = gate * sigmoid_gate
        hidden = (silu_gate * upward).astype(bf16)
        grad_hidden = dot(grad_result_chip, down_full)
        grad_upward = (grad_hidden * silu_gate).astype(bf16)
        grad_gate = (
            grad_hidden * upward * sigmoid_gate * (1.0 + gate * (1.0 - sigmoid_gate))
        ).astype(bf16)
        second_part = dot_nt(grad_gate, gate_full) + dot_nt(grad_upward, up_full)
        grad_second = second_part[:rows] + swapped(second_part[rows:])
        down_part = dot_nt(hidden, down_full)
        down_result = down_part[:rows] + swapped(down_part[rows:])
    layer_out = (valid * (after_mixer + down_result)).astype(bf16).reshape(tokens.shape)

    grad_after_norm, grad_gain_second = norm_backward(
        grad_second, scaled_second, inverse_second, gain_second
    )
    grad_after = grad_result + grad_after_norm
    grad_after_low = grad_after.astype(bf16)
    grad_mixer = dot_nt(grad_after_low, out_full).astype(bf16).reshape(rows, CORES, VC)
    grad_mixer_chip = jnp.concatenate(
        [part_of(grad_mixer, 1, core), swapped(part_of(grad_mixer, 1, other))], axis=0
    )
    after_columns = grad_after_low.reshape(rows, CORES, VC)
    grad_after_chip = jnp.concatenate(
        [part_of(after_columns, 1, core), swapped(part_of(after_columns, 1, other))], axis=0
    )
    mixer_chip = jnp.concatenate([mixer_own, mixer_other], axis=0)

    wide_spec = (HC * LANES,)
    pulled, grad_num = call(
        pull_kernel,
        ins=[q_spec, v_spec, v_spec, (LANES,)],
        outs=[("state", f32), (wide_spec, bf16)],
        scratch=[],
        flops=4 * unit,
    )(*tables, query_key, halves(grad_mixer_chip), mixer, dens)
    from_later = chain(pulled, False)
    grad_query_key, grad_values = call(
        backward_kernel,
        ins=[q_spec, k_spec, v_spec, wide_spec, "state", "state"],
        outs=[((2 * LANES,), bf16), (v_spec, bf16)],
        scratch=wide,
        flops=24 * unit,
    )(*tables, query_key, query_key, values, grad_num, before, from_later)

    head = grad_values[:, :, : KS - 1, :]
    from_chip = passed_along(part_of(head, 0, core), "z", -1)
    from_core = part_of(head, 0, other)
    later = jnp.stack(
        [jnp.where(first_core, from_core, from_chip), jnp.where(first_core, from_chip, from_core)]
    )
    grad_extended = jnp.concatenate([grad_values, later], axis=2).astype(f32)
    grad_pre = taps[0] * grad_extended[:, :, :slot_rows, :]
    for j in range(1, KS):
        grad_pre = grad_pre + taps[j] * grad_extended[:, :, j : j + slot_rows, :]
    grad_pre = grad_pre.reshape(CORES * rows, VC).astype(bf16)
    grad_query_key = grad_query_key.reshape(CORES * rows, 2 * QC)
    grad_values_float = grad_values.astype(f32)
    tap_grads = [jnp.sum(grad_values_float * tap_rows(j), axis=(0, 1, 2)) for j in range(KS)]

    first_other = dot_nt(grad_query_key[rows:], qk_full) + dot_nt(grad_pre[rows:], value_full)
    first_own = dot_nt(grad_query_key[:rows], qk_full) + dot_nt(grad_pre[:rows], value_full)
    grad_first = first_own + swapped(first_other)
    grad_gain_first = jnp.sum(first_own * scaled_chip[:rows], axis=0) + jnp.sum(
        first_other * scaled_chip[rows:], axis=0
    )

    def whole_feature(part):
        return lax.dynamic_update_slice(jnp.zeros((D,), f32), part, (core * VC,))

    small_terms = jnp.stack(
        [whole_feature(part) for part in tap_grads] + [grad_gain_first, grad_gain_second], axis=1
    )
    small_terms = jnp.pad(small_terms, ((0, 0), (0, LANES - (KS + 2)))).astype(bf16)
    if in_kernel:
        value_terms = dot_tn(normed_chip, grad_pre).astype(bf16)
        out_terms = dot_tn(mixer_chip, grad_after_chip).astype(bf16)
        qk_terms = dot_tn(normed_chip, grad_query_key).astype(bf16)
        grad_qk_own, grad_value_own, grad_out_own, grad_gu_own, grad_down_own, small_both = reduced(
            sum_down[0],
            sum_gate,
            sum_down[1],
            sum_up,
            jnp.concatenate([value_terms, qk_terms[:, :QC]], axis=1),
            jnp.concatenate([out_terms, qk_terms[:, QC:], small_terms], axis=1),
            owned,
        )
        grad_small_own = (small_both[:, :LANES] + small_both[:, LANES:])[:, : KS + 2]
    else:
        sum_down = Scatter(dot_tn(grad_result_chip, hidden).astype(bf16), True).rest()
        sum_gate = Scatter(dot_tn(second_chip, grad_gate).astype(bf16), False).rest()
        sum_up = Scatter(dot_tn(second_chip, grad_upward).astype(bf16), True).rest()
        sum_value = Scatter(dot_tn(normed_chip, grad_pre).astype(bf16), False).rest()
        sum_out = Scatter(dot_tn(mixer_chip, grad_after_chip).astype(bf16), True).rest()
        qk_terms = dot_tn(normed_chip, grad_query_key).astype(bf16)
        sum_last = Scatter(jnp.concatenate([qk_terms, small_terms], axis=1), True).rest()
    grad_input_norm, _ = norm_backward(grad_first, scaled_first, inverse_first, gain_first)
    input_grad = (grad_after + grad_input_norm).reshape(tokens.shape)

    def rows_of(array, index):
        return part_of(array.reshape(CORES, owned, -1), 0, index)

    def finish(*parts):
        merged = jnp.concatenate(parts, axis=1) if len(parts) > 1 else parts[0]
        mine, theirs = rows_of(merged, core), swapped(rows_of(merged, other))
        return mine.astype(f32), theirs.astype(f32)

    def columns(*parts):
        mine, theirs = finish(*parts)
        return both_cores(mine, theirs, 1)

    def two_columns(mine, theirs, width):
        shape = (owned, 2, 1, width)
        return both_cores(mine.reshape(shape), theirs.reshape(shape), 2).reshape(owned, -1)

    if not in_kernel:
        grad_down_own = columns(sum_down)
        grad_gu_own = two_columns(*finish(sum_gate, sum_up), FC)
        grad_out_own = columns(sum_out)
        grad_value_own = columns(sum_value)
        last_mine, last_theirs = finish(sum_last)
        grad_qk_own = two_columns(last_mine[:, : 2 * QC], last_theirs[:, : 2 * QC], QC)
        grad_small_own = (last_mine + last_theirs)[:, 2 * QC : 2 * QC + KS + 2]

    grads_all = (
        grad_qk_own,
        grad_value_own,
        grad_out_own,
        grad_gu_own,
        grad_down_own,
        grad_small_own,
    )
    masters = (w_qk, w_value, w_out, w_gu, w_down, small_params)
    firsts = (m_qk, m_value, m_out, m_gu, m_down, m_small)
    seconds = (v_qk, v_value, v_out, v_gu, v_down, v_small)
    learn_rates = (
        0.05 / math.sqrt(D),
        0.05 / math.sqrt(D),
        0.05 / math.sqrt(max(D // 128, 1)),
        0.05 / math.sqrt(D),
        0.05 / math.sqrt(0.0003 * FF * SLOT**0.825),
        0.014,
    )
    decays = (weight_decay, weight_decay, weight_decay, weight_decay, weight_decay, 0.0)
    new_weights = []
    new_seconds = []
    for position in range(6):
        updated, moment = adam_update(
            masters[position],
            grads_all[position],
            firsts[position],
            seconds[position],
            learn_rates[position],
            decays[position],
        )
        new_weights.append(updated)
        new_seconds.append(moment)
    return (layer_out, input_grad) + grads_all + tuple(new_weights) + tuple(new_seconds)


def solution(mesh):
    dp, fsdp = mesh.shape["dp"], mesh.shape["fsdp"]
    y_size = 2 if dp % 2 == 0 else 1
    split = Mesh(
        mesh.devices.reshape(y_size, dp // y_size, fsdp // CORES, CORES), ("y", "x", "z", "core")
    )
    slot_axes, row_axes = ("y", "x"), ("z", "core")
    activation = P(slot_axes, row_axes, None)
    weight = P(slot_axes + row_axes, None)
    return jax.shard_map(
        local,
        mesh=split,
        in_specs=(activation, activation, P(slot_axes)) + (weight,) * 18,
        out_specs=(activation, activation) + (weight,) * 18,
        check_vma=False,
    )
```

```python
import functools
import math

import jax
import jax.numpy as jnp
import numpy as np
from jax import lax
from jax.experimental import pallas as pl
from jax.experimental.pallas import tpu as pltpu
from jax.sharding import Mesh
from jax.sharding import PartitionSpec as P

D = 1792
H = 16
F = 16
FF = 4864
KS = 3
SLOT = 2048
STEP = 10

CORES = 2
HC = H // CORES
HW = D // H
VC = HC * HW
QC = HC * F
FC = FF // CORES
LANES = 128
FEATS = 256
FROWS = 160
SCALE = 1.0 / math.sqrt(F)

norm_epsilon = 1e-06
beta_first = 0.9
beta_second = 0.95
adam_epsilon = 1e-08
weight_decay = 3e-05

bf16 = jnp.bfloat16
f32 = jnp.float32


def feature_tables():
    index = np.full((8, FEATS), -4096, np.int32)
    scale = np.zeros((8, FEATS), np.float32)
    scale[0, 0] = scale[1, 0] = scale[2, 0] = 1.0
    at = 1
    for i in range(F):
        index[0, at] = i
        scale[1, at] = 1.0
        scale[2, at] = SCALE
        at += 1
    for i in range(F):
        for j in range(i, F):
            index[0, at] = i
            index[1, at] = j
            scale[2, at] = (1.0 if i == j else 2.0) * 0.5 * SCALE * SCALE
            at += 1
    return index, scale


def dot(a, b):
    return lax.dot_general(a, b, (((1,), (0,)), ((), ())), preferred_element_type=f32)


def dot_nt(a, b):
    return lax.dot_general(a, b, (((1,), (1,)), ((), ())), preferred_element_type=f32)


def dot_tn(a, b):
    return lax.dot_general(a, b, (((0,), (0,)), ((), ())), preferred_element_type=f32)


def selectors(index_ref, head):
    lane = lax.broadcasted_iota(jnp.int32, (LANES, FEATS), 0) - head * F
    first = jnp.where(lane == index_ref[0:1, :], 1.0, 0.0).astype(bf16)
    second = jnp.where(lane == index_ref[1:2, :], 1.0, 0.0).astype(bf16)
    return first, second


def factors(rows, first, second, scale_ref):
    return (dot(rows, first) + scale_ref[0:1, :], dot(rows, second) + scale_ref[1:2, :])


def window(head):
    start = head * HW
    base = min(start // LANES * LANES, VC - 2 * LANES)
    return base, start - base


def both_halves(core_ref, ref, columns):
    core = core_ref[0]
    return jnp.concatenate([ref[core, :, columns], ref[1 - core, :, columns]], axis=0)


def store_halves(core_ref, ref, rows, columns):
    core, half = core_ref[0], rows.shape[0] // CORES
    ref[core, :, columns] = rows[:half]
    ref[1 - core, :, columns] = rows[half:]


def head_columns(core_ref, ref, head):
    base, offset = window(head)
    wide = both_halves(core_ref, ref, slice(base, base + 2 * LANES)).astype(f32)
    if offset:
        wide = pltpu.roll(wide, 2 * LANES - offset, 1)
    return wide[:, :LANES]


def add_head_columns(ref, head, block):
    base, offset = window(head)
    wide = jnp.concatenate([block, jnp.zeros_like(block)], axis=1)
    if offset:
        wide = pltpu.roll(wide, offset, 1)
    ref[:, base : base + 2 * LANES] += wide


def with_one(block):
    lane = lax.broadcasted_iota(jnp.int32, block.shape, 1)
    return jnp.where(lane < HW, block, jnp.where(lane == HW, 1.0, 0.0))


def only_head(rows, head):
    lane = lax.broadcasted_iota(jnp.int32, rows.shape, 1)
    inside = (lane >= head * F) & (lane < head * F + F)
    return jnp.where(inside, rows.astype(f32), 0.0).astype(bf16)


def state_kernel(core_ref, index_ref, scale_ref, k_ref, v_ref, state_ref):
    keys = both_halves(core_ref, k_ref, slice(None))
    for head in range(HC):
        first, second = selectors(index_ref, head)
        one, two = factors(keys, first, second, scale_ref)
        phi = (one * two * scale_ref[2:3, :]).astype(bf16)
        values = with_one(head_columns(core_ref, v_ref, head)).astype(bf16)
        state_ref[0, head] = dot_tn(phi, values)[:FROWS]


def scores_of(q_head, keys):
    scores = dot_nt(q_head, keys) * SCALE
    row = lax.broadcasted_iota(jnp.int32, scores.shape, 0)
    column = lax.broadcasted_iota(jnp.int32, scores.shape, 1)
    return scores, column <= row


def forward_kernel(core_ref, index_ref, scale_ref, q_ref, k_ref, v_ref, before_ref, mixer_ref, den_ref, wide):
    queries = both_halves(core_ref, q_ref, slice(None))
    keys = both_halves(core_ref, k_ref, slice(None))
    wide[...] = jnp.zeros_like(wide)
    lane = lax.broadcasted_iota(jnp.int32, (queries.shape[0], LANES), 1)
    dens = jnp.zeros((queries.shape[0], LANES), f32)
    for head in range(HC):
        first, second = selectors(index_ref, head)
        one, two = factors(queries, first, second, scale_ref)
        phi = (one * two).astype(bf16)
        values = with_one(head_columns(core_ref, v_ref, head)).astype(bf16)
        scores, allowed = scores_of(only_head(queries, head), keys)
        kernel = jnp.where(allowed, 1.0 + scores + 0.5 * scores * scores, 0.0).astype(bf16)
        total = dot(kernel, values) + dot(phi[:, :FROWS], before_ref[0, head])
        den = total[:, HW : HW + 1]
        add_head_columns(wide, head, jnp.where(lane < HW, total / den, 0.0))
        dens = jnp.where(lane == head, den, dens)
    store_halves(core_ref, mixer_ref, wide[...].astype(bf16), slice(None))
    store_halves(core_ref, den_ref, dens, slice(None))


def pull_kernel(core_ref, index_ref, scale_ref, q_ref, gm_ref, mixer_ref, den_ref, state_ref, gnum_ref):
    queries = both_halves(core_ref, q_ref, slice(None))
    lane = lax.broadcasted_iota(jnp.int32, (queries.shape[0], LANES), 1)
    dens = both_halves(core_ref, den_ref, slice(None))
    for head in range(HC):
        first, second = selectors(index_ref, head)
        one, two = factors(queries, first, second, scale_ref)
        phi = (one * two).astype(bf16)
        den = dens[:, head : head + 1]
        grad = jnp.where(lane < HW, head_columns(core_ref, gm_ref, head), 0.0)
        mixer = head_columns(core_ref, mixer_ref, head)
        pulled = -jnp.sum(grad * mixer, axis=1, keepdims=True)
        grad = (jnp.where(lane == HW, pulled, grad) / den).astype(bf16)
        store_halves(core_ref, gnum_ref, grad, slice(head * LANES, (head + 1) * LANES))
        state_ref[0, head] = dot_tn(phi, grad)[:FROWS]


def backward_kernel(
    core_ref, index_ref, scale_ref, q_ref, k_ref, v_ref, gnum_ref, before_ref, after_ref, gqk_ref, gv_ref, wide
):
    queries = both_halves(core_ref, q_ref, slice(None))
    keys = both_halves(core_ref, k_ref, slice(None))
    wide[...] = jnp.zeros_like(wide)
    lane = lax.broadcasted_iota(jnp.int32, (queries.shape[0], LANES), 1)
    grad_q = jnp.zeros((queries.shape[0], LANES), f32)
    grad_k = jnp.zeros((queries.shape[0], LANES), f32)
    for head in range(HC):
        first, second = selectors(index_ref, head)
        coef = scale_ref[2:3, :]
        q_one, q_two = factors(queries, first, second, scale_ref)
        k_one, k_two = factors(keys, first, second, scale_ref)
        values = with_one(head_columns(core_ref, v_ref, head)).astype(bf16)
        gnum = both_halves(core_ref, gnum_ref, slice(head * LANES, (head + 1) * LANES))
        q_head = only_head(queries, head)
        k_head = only_head(keys, head)
        scores, allowed = scores_of(q_head, keys)
        kernel = jnp.where(allowed, 1.0 + scores + 0.5 * scores * scores, 0.0).astype(bf16)
        grad_kernel = dot_nt(gnum, values)
        grad_scores = (jnp.where(allowed, grad_kernel * (1.0 + scores), 0.0) * SCALE).astype(bf16)
        phi_k = (k_one * k_two * coef).astype(bf16)
        after = after_ref[0, head]
        before = before_ref[0, head]
        grad_v = dot_tn(kernel, gnum) + dot(phi_k[:, :FROWS], after)
        add_head_columns(wide, head, jnp.where(lane < HW, grad_v, 0.0))
        empty = jnp.zeros((FEATS - FROWS, LANES), bf16)
        grad_phi_q = dot_nt(gnum, jnp.concatenate([before, empty], axis=0))
        grad_phi_k = dot_nt(values, jnp.concatenate([after, empty], axis=0)) * coef
        grad_q += dot(grad_scores, k_head)
        grad_q += dot_nt((grad_phi_q * q_two).astype(bf16), first)
        grad_q += dot_nt((grad_phi_q * q_one).astype(bf16), second)
        grad_k += dot_tn(grad_scores, q_head)
        grad_k += dot_nt((grad_phi_k * k_two).astype(bf16), first)
        grad_k += dot_nt((grad_phi_k * k_one).astype(bf16), second)
    store_halves(core_ref, gqk_ref, grad_q.astype(bf16), slice(0, LANES))
    store_halves(core_ref, gqk_ref, grad_k.astype(bf16), slice(LANES, 2 * LANES))
    store_halves(core_ref, gv_ref, wide[...].astype(bf16), slice(None))


def per_slot(kernel, slots, rows, ins, outs, scratch, flops):
    def table():
        return pl.BlockSpec((8, FEATS), lambda s, core: (0, 0))

    def row_spec(width, column=0):
        return pl.BlockSpec((CORES, None, rows, width), lambda s, core: (0, s, 0, column))

    def state_spec():
        return pl.BlockSpec((1, HC, FROWS, LANES), lambda s, core: (s, 0, 0, 0))

    def spec(kind):
        return state_spec() if kind == "state" else row_spec(*kind)

    def shape(kind, dtype):
        if kind == "state":
            return jax.ShapeDtypeStruct((slots, HC, FROWS, LANES), dtype)
        return jax.ShapeDtypeStruct((CORES, slots, rows, kind[0]), dtype)

    return pl.pallas_call(
        kernel,
        grid_spec=pltpu.PrefetchScalarGridSpec(
            num_scalar_prefetch=1,
            grid=(slots,),
            in_specs=[table(), table()] + [spec(kind) for kind in ins],
            out_specs=[spec(kind) for kind, _ in outs],
            scratch_shapes=scratch,
        ),
        out_shape=[shape(kind, dtype) for kind, dtype in outs],
        compiler_params=pltpu.CompilerParams(vmem_limit_bytes=56 << 20),
        cost_estimate=pl.CostEstimate(flops=flops, bytes_accessed=8 << 20, transcendentals=0),
    )


def linked(kernel, up, ids):
    def run(*refs):
        y, x, z, core = places_of()
        last = lax.axis_size("z") - 1
        *refs, sent, send_sem, recv_sem = refs
        total_ref = refs[-1]
        by = 1 if up else last
        receives, sends = (z > 0, z < last) if up else (z < last, z > 0)

        barrier = pltpu.get_barrier_semaphore()
        for step in (1, last):
            pl.semaphore_signal(
                barrier,
                inc=1,
                device_id=(y, x, lax.rem(z + step, last + 1), core),
                device_id_type=pl.DeviceIdType.MESH,
            )
        pl.semaphore_wait(barrier, 2)

        def transfer(slot, head):
            return pltpu.make_async_remote_copy(
                src_ref=sent.at[slot, head],
                dst_ref=total_ref.at[slot, head],
                send_sem=send_sem.at[slot, head],
                recv_sem=recv_sem.at[slot, head],
                device_id=(y, x, lax.rem(z + by, last + 1), core),
                device_id_type=pl.DeviceIdType.MESH,
            )

        @pl.when(jnp.logical_not(receives))
        def _():
            total_ref[...] = jnp.zeros_like(total_ref)

        @pl.loop(0, sent.shape[0])
        def _(slot):
            for head in range(HC):
                term = kernel([core], slot, head, *refs[:-1])

                @pl.when(receives)
                def _(head=head):
                    transfer(slot, head).wait_recv()

                @pl.when(sends)
                def _(head=head, term=term):
                    sent[slot, head] = (total_ref[slot, head].astype(f32) + term).astype(bf16)
                    transfer(slot, head).start()

        @pl.when(sends)
        def _():
            @pl.loop(0, sent.shape[0])
            def _(slot):
                for head in range(HC):
                    transfer(slot, head).wait_send()

    def call(*operands, slots, extra=()):
        state = jax.ShapeDtypeStruct((slots, HC, FROWS, LANES), bf16)
        vmem = pl.BlockSpec(memory_space=pltpu.VMEM)
        return pl.pallas_call(
            run,
            out_shape=list(extra) + [state],
            in_specs=[vmem] * len(operands),
            out_specs=[vmem] * (len(extra) + 1),
            scratch_shapes=[
                pltpu.VMEM((slots, HC, FROWS, LANES), bf16),
                pltpu.SemaphoreType.DMA((slots, HC)),
                pltpu.SemaphoreType.DMA((slots, HC)),
            ],
            compiler_params=pltpu.CompilerParams(
                collective_id=ids, has_side_effects=True, vmem_limit_bytes=40 << 20
            ),
            cost_estimate=pl.CostEstimate(flops=0, bytes_accessed=1024, transcendentals=0),
        )(*operands)

    return call


def key_term(core_ref, slot, head, index_ref, scale_ref, qk_ref, v_ref):
    keys = both_halves(core_ref, qk_ref.at[:, slot], slice(LANES, 2 * LANES))
    first, second = selectors(index_ref, head)
    one, two = factors(keys, first, second, scale_ref)
    phi = (one * two * scale_ref[2:3, :]).astype(bf16)
    values = with_one(head_columns(core_ref, v_ref.at[:, slot], head)).astype(bf16)
    return dot_tn(phi, values)[:FROWS]


def query_term(core_ref, slot, head, index_ref, scale_ref, qk_ref, gm_ref, mixer_ref, den_ref, gnum_ref):
    queries = both_halves(core_ref, qk_ref.at[:, slot], slice(0, LANES))
    first, second = selectors(index_ref, head)
    one, two = factors(queries, first, second, scale_ref)
    phi = (one * two).astype(bf16)
    den = both_halves(core_ref, den_ref.at[:, slot], slice(None))[:, head : head + 1]
    lane = lax.broadcasted_iota(jnp.int32, (queries.shape[0], LANES), 1)
    grad = jnp.where(lane < HW, head_columns(core_ref, gm_ref.at[:, slot], head), 0.0)
    mixer = head_columns(core_ref, mixer_ref.at[:, slot], head)
    pulled = -jnp.sum(grad * mixer, axis=1, keepdims=True)
    grad = (jnp.where(lane == HW, pulled, grad) / den).astype(bf16)
    store_halves(core_ref, gnum_ref.at[:, slot], grad, slice(head * LANES, (head + 1) * LANES))
    return dot_tn(phi, grad)[:FROWS]


def passed_along(array, axis, by):
    count = lax.axis_size(axis)
    pairs = [(i, i + by) for i in range(count) if 0 <= i + by < count]
    return lax.ppermute(array, axis, pairs)


def both_cores(mine, theirs, axis):
    first = lax.axis_index("core") == 0
    return jnp.concatenate(
        [jnp.where(first, mine, theirs), jnp.where(first, theirs, mine)], axis=axis
    )


def swapped(array):
    return lax.ppermute(array, "core", [(0, 1), (1, 0)])


def part_of(array, axis, index):
    return lax.dynamic_index_in_dim(array, index, axis, keepdims=False)


def bits_of(axis):
    return [(axis, bit) for bit in reversed(range(lax.axis_size(axis).bit_length() - 1))]


def bit_at(axis, bit):
    return (lax.axis_index(axis) >> bit) & 1


def exchanged(array, axis, bit):
    count = lax.axis_size(axis)
    return lax.ppermute(array, axis, [(i, i ^ (1 << bit)) for i in range(count)])


def tied(*arrays):
    return lax.optimization_barrier(arrays)


class Gather:
    def __init__(self, piece, x_first):
        self.columns = piece.shape[1]
        self.block = piece
        low_first = lambda axis: bits_of(axis)[::-1]
        self.plan = [(step, at) for at, step in enumerate(bits_of("z"))]
        if x_first:
            self.plan += [(step, 0) for step in low_first("x") + low_first("y")]
        else:
            self.plan += [(step, 0) for step in low_first("y")]
            self.plan += [(step, len(bits_of("y"))) for step in low_first("x")]

    def stage(self):
        (axis, bit), dim = self.plan.pop(0)
        mine = bit_at(axis, bit)
        arrived = exchanged(self.block, axis, bit)
        shape = self.block.shape[:dim] + (2,) + self.block.shape[dim:]
        whole = jnp.zeros(shape, self.block.dtype)
        whole = lax.dynamic_update_index_in_dim(whole, self.block, mine, dim)
        self.block = lax.dynamic_update_index_in_dim(whole, arrived, 1 - mine, dim)
        return self

    def along_z(self):
        while self.plan[0][0][0] == "z":
            self.stage()
        return self

    def rest(self):
        while self.plan:
            self.stage()
        return self.block.reshape(D, self.columns)


class Scatter:
    def __init__(self, terms, x_first):
        self.dims = bits_of("y") + bits_of("x") + bits_of("z")
        order = ("x", "y") if x_first else ("y", "x")
        self.plan = bits_of(order[0]) + bits_of(order[1]) + bits_of("z")[::-1]
        rows = D >> len(self.dims)
        self.terms = [terms.reshape((2,) * len(self.dims) + (rows, terms.shape[1]))]

    def total(self, terms):
        total = terms[0].astype(f32)
        for term in terms[1:]:
            total = total + term.astype(f32)
        return total

    def stage(self):
        step = self.plan.pop(0)
        dim, mine = self.dims.index(step), bit_at(*step)
        self.dims.remove(step)
        sent = self.total([part_of(term, dim, 1 - mine) for term in self.terms]).astype(bf16)
        self.terms = [part_of(term, dim, mine) for term in self.terms]
        self.terms.append(exchanged(sent, *step))
        return self

    def rest(self):
        while self.plan:
            self.stage()
        return self.total(self.terms)


def chain(local, up):
    count = lax.axis_size("z")
    total = jnp.zeros_like(local)
    for hop in range(1, count):
        pair = (hop - 1, hop) if up else (count - hop, count - hop - 1)
        message = (total + local).astype(bf16)
        total = total + lax.ppermute(message, "z", [pair]).astype(f32)
    return total.astype(bf16)


def mesh_exchange(y, x, z, core, axis):
    if axis == "core":
        return (y, x, z, 1 - core)
    if axis == "y":
        return (1 - y, x, z, core)
    if axis == "x":
        return (y, 1 - x, z, core)
    if axis == "z0":
        return (y, x, z + 1 - 2 * (z % 2), core)
    return (y, x, (z + 2) % 4, core)


ORDERS = (("y", "x", "z0", "z1"), ("x", "y", "z0", "z1"))


WIDE = 2 * LANES


def reduce_kernel(
    down_a_ref,
    gate_ref,
    down_b_ref,
    up_ref,
    last_a_ref,
    last_b_ref,
    small_terms_ref,
    qk_ref,
    value_ref,
    out_ref,
    gu_ref,
    down_ref,
    small_ref,
    sums,
    halves,
    quarters,
    finals,
    got_terms,
    got_sums,
    got_halves,
    got_quarters,
    send_sem,
    recv_sem,
):
    y, x, z, core = places_of()
    places = {"y": y, "x": x, "z0": z % 2, "z1": z // 2}

    parts, count = ([], []), 0
    all_refs = (
        (down_a_ref, gate_ref, last_a_ref),
        (down_b_ref, up_ref, last_b_ref, small_terms_ref),
    )
    for stream, refs in enumerate(all_refs):
        at = 0
        for ref in refs:
            chunks = ref.shape[-1] // WIDE
            parts[stream].append((ref, len(ref.shape) == 3, at, at + chunks))
            at += chunks
        count = max(count, at)
    hidden, width = FC // LANES, VC // LANES
    down_a = (hidden + 1) // 2
    down_b = hidden - down_a
    gate_at, last_a = 2 * parts[0][1][2], 2 * parts[0][2][2]
    up_at, last_b, small_at = (2 * parts[1][at][2] for at in (1, 2, 3))
    places_out = (
        (
            (down_ref, core * hidden, 0, down_a),
            (gu_ref, core * hidden, gate_at, gate_at + hidden),
            (value_ref, core * width, last_a, last_a + width),
            (qk_ref, core, last_a + width, last_a + width + 1),
            (qk_ref, CORES + core, last_a + width + 1, last_a + width + 2),
        ),
        (
            (down_ref, core * hidden + down_a, 0, down_b),
            (gu_ref, (CORES + core) * hidden, up_at, up_at + hidden),
            (out_ref, core * width, last_b, last_b + width),
            (small_ref, core, small_at, small_at + 1),
        ),
    )
    greet(y, x, z, core, True)

    def columns(tile):
        return pl.ds(pl.multiple_of(tile * LANES, LANES), LANES)

    def wide_columns(chunk):
        return pl.ds(pl.multiple_of(chunk * WIDE, WIDE), WIDE)

    def transfer(stream, stage, chunk, source, target=None):
        landing = chunk % 4
        if target is None:
            target = (got_terms, got_sums, got_halves, got_quarters)[stage].at[stream, landing]
        axis = (ORDERS[stream] + ("core", "core"))[stage]
        return pltpu.make_async_remote_copy(
            src_ref=source,
            dst_ref=target,
            send_sem=send_sem.at[stream, stage, landing],
            recv_sem=recv_sem.at[stream, stage, landing],
            device_id=mesh_exchange(y, x, z, core, axis),
            device_id_type=pl.DeviceIdType.MESH,
        )

    def first_view(stream, ref, tile, place):
        ref = ref.at[:, :, :, wide_columns(tile)]
        return ref.at[place] if stream == 0 else ref.at[:, place]

    def source_of(stream, stage, chunk):
        there = 1 - places[ORDERS[stream][stage]]
        if stage == 1:
            return sums.at[stream, chunk % 2, there]
        if stage == 2:
            return halves.at[stream, chunk % 2, :, there]
        return quarters.at[stream, chunk % 2, there]

    def add(a, b):
        return a.astype(f32) + b.astype(f32)

    def begin(stream, chunk):
        for ref, _, start, stop in parts[stream][2:]:

            @pl.when((chunk >= start) & (chunk < stop))
            def _(ref=ref, start=start):
                there = 1 - places[ORDERS[stream][0]]
                transfer(stream, 0, chunk, first_view(stream, ref, chunk - start, there)).start()

    def second(stream, chunk):
        for ref, summed, start, stop in parts[stream]:

            @pl.when((chunk >= start) & (chunk < stop))
            def _(ref=ref, summed=summed, start=start):
                tile = chunk - start
                if summed:
                    sums[stream, chunk % 2] = ref[:, :, wide_columns(tile)]
                else:
                    there = 1 - places[ORDERS[stream][0]]
                    transfer(stream, 0, chunk, first_view(stream, ref, tile, there)).wait()
                    own = first_view(stream, ref, tile, places[ORDERS[stream][0]])[...]
                    sums[stream, chunk % 2] = add(own, got_terms[stream, chunk % 4]).astype(bf16)

        transfer(stream, 1, chunk, source_of(stream, 1, chunk)).start()

    def advance(stream, stage, chunk):
        here = places[ORDERS[stream][stage]]
        slot, landing = chunk % 2, chunk % 4
        transfer(stream, stage, chunk, source_of(stream, stage, chunk)).wait()
        if stage == 1:
            total = add(sums[stream, slot, here], got_sums[stream, landing]).astype(bf16)
            halves[stream, slot] = total.reshape(halves.shape[2:])
        elif stage == 2:
            own = halves[stream, slot, :, here]
            quarters[stream, slot] = add(own, got_halves[stream, landing]).astype(bf16)
        else:
            total = add(quarters[stream, slot, here], got_quarters[stream, landing])
            finals[stream, slot] = total.reshape(finals.shape[2:])
        if stage < 3:
            transfer(stream, stage + 1, chunk, source_of(stream, stage + 1, chunk)).start()

    def hand_over(stream, chunk, waiting):
        for at in range(2):
            tile = 2 * chunk + at
            lanes = slice(at * LANES, (at + 1) * LANES)
            for ref, first, start, stop in places_out[stream]:

                @pl.when((tile >= start) & (tile < stop))
                def _(at=at, tile=tile, lanes=lanes, ref=ref, first=first, start=start):
                    target = ref.at[:, columns(first + tile - start)]
                    source = finals.at[stream, chunk % 2, 1 - core, :, lanes]
                    copy = transfer(stream, 4 + at, chunk, source, target)
                    if waiting:
                        copy.wait()
                    else:
                        target[...] = finals[stream, chunk % 2, core, :, lanes]
                        copy.start()

    @pl.loop(0, count + 5)
    def _(step):
        for stream in range(2):
            total = parts[stream][-1][3]

            @pl.when(step < total)
            def _(stream=stream):
                begin(stream, step)

        for stage in range(5):
            for stream in range(2):
                total = parts[stream][-1][3]

                @pl.when((step >= stage + 1) & (step < total + stage + 1))
                def _(stage=stage, stream=stream):
                    chunk = step - stage - 1
                    if stage == 0:
                        second(stream, chunk)
                    elif stage < 4:
                        advance(stream, stage, chunk)
                    else:
                        hand_over(stream, chunk, True)
                    if stage == 3:
                        hand_over(stream, chunk, False)


def reduced(down_a, gate, down_b, up, last_a, last_b, small, owned):
    block, rows = D // 4, D // 16
    dma = pltpu.SemaphoreType.DMA
    last_a, last_b, small = (last.reshape(2, 2, block, -1) for last in (last_a, last_b, small))
    widths = (2 * CORES * QC, CORES * VC, CORES * VC, 2 * CORES * FC, CORES * FC, CORES * LANES)
    return pl.pallas_call(
        reduce_kernel,
        out_shape=[jax.ShapeDtypeStruct((owned, width), f32) for width in widths],
        in_specs=[pl.BlockSpec(memory_space=pltpu.VMEM)] * 7,
        out_specs=[pl.BlockSpec(memory_space=pltpu.VMEM)] * 6,
        scratch_shapes=[
            pltpu.VMEM((2, 2, 2, block, WIDE), bf16),
            pltpu.VMEM((2, 2, 2, 2, rows, WIDE), bf16),
            pltpu.VMEM((2, 2, 2, rows, WIDE), bf16),
            pltpu.VMEM((2, 2, CORES, owned, WIDE), f32),
            pltpu.VMEM((2, 4, 2, block, WIDE), bf16),
            pltpu.VMEM((2, 4, block, WIDE), bf16),
            pltpu.VMEM((2, 4, 2, rows, WIDE), bf16),
            pltpu.VMEM((2, 4, rows, WIDE), bf16),
            dma((2, 6, 4)),
            dma((2, 6, 4)),
        ],
        compiler_params=pltpu.CompilerParams(
            collective_id=0, has_side_effects=True, vmem_limit_bytes=56 << 20
        ),
        cost_estimate=pl.CostEstimate(flops=0, bytes_accessed=1024, transcendentals=0),
    )(down_a, gate, down_b, up, last_a, last_b, small)


def places_of():
    y, x, z, core = (lax.axis_index(axis) for axis in ("y", "x", "z", "core"))
    return y, x, z, core


def greet(y, x, z, core, both_cores=False):
    barrier = pltpu.get_barrier_semaphore()
    partners = ORDERS[0] + (("core",) if both_cores else ())
    for axis in partners:
        pl.semaphore_signal(
            barrier,
            inc=1,
            device_id=mesh_exchange(y, x, z, core, axis),
            device_id_type=pl.DeviceIdType.MESH,
        )
    pl.semaphore_wait(barrier, len(partners))


GATHER_ORDERS = (("z1", "z0", "x", "y"), ("z1", "z0", "y", "x"))


def gather_view(ref, order, stage, y, x, z):
    if stage == 0:
        return ref.at[y, x, z // 2, z % 2]
    if stage == 1:
        return ref.at[y, x, :, z % 2]
    if stage == 2:
        return ref.at[y, x]
    return ref.at[y] if order == 0 else ref.at[:, x]


def gather_kernel(tiles, shard_ref, full_ref, send_sem, recv_sem):
    y, x, z, core = places_of()
    full_ref[y, x, z // 2, z % 2] = shard_ref[...]
    greet(y, x, z, core)

    def transfer(stage, tile, order):
        columns = pl.ds(pl.multiple_of(tile * LANES, LANES), LANES)
        view = gather_view(full_ref.at[:, :, :, :, :, columns], order, stage, y, x, z)
        return pltpu.make_async_remote_copy(
            src_ref=view,
            dst_ref=view,
            send_sem=send_sem.at[stage, tile],
            recv_sem=recv_sem.at[stage, tile],
            device_id=mesh_exchange(y, x, z, core, GATHER_ORDERS[order][stage]),
            device_id_type=pl.DeviceIdType.MESH,
        )

    pairs = (tiles + 1) // 2

    def each(step, behind, act):
        for order in range(2):
            tile = 2 * (step - behind) + order

            @pl.when((tile >= 0) & (tile < tiles))
            def _(tile=tile, order=order):
                act(tile, order)

    @pl.loop(0, pairs + 4)
    def _(step):
        each(step, 0, lambda tile, order: transfer(0, tile, order).start())
        for stage in range(4):

            def act(tile, order, stage=stage):
                transfer(stage, tile, order).wait()
                if stage < 3:
                    transfer(stage + 1, tile, order).start()

            each(step, stage + 1, act)


def gathered_rows(shard):
    rows, width = shard.shape
    tiles = width // LANES
    full = pl.pallas_call(
        functools.partial(gather_kernel, tiles),
        out_shape=jax.ShapeDtypeStruct((2, 2, 2, 2, rows, width), bf16),
        in_specs=[pl.BlockSpec(memory_space=pltpu.VMEM)],
        out_specs=pl.BlockSpec(memory_space=pltpu.VMEM),
        scratch_shapes=[
            pltpu.SemaphoreType.DMA((4, tiles)),
            pltpu.SemaphoreType.DMA((4, tiles)),
        ],
        compiler_params=pltpu.CompilerParams(
            collective_id=1, has_side_effects=True, vmem_limit_bytes=40 << 20
        ),
        cost_estimate=pl.CostEstimate(flops=0, bytes_accessed=1024, transcendentals=0),
    )(shard)
    return full.reshape(D, width)


SLOTS = 10


def feed_forward_kernel(
    tiles,
    second_ref,
    grad_ref,
    shard_ref,
    gate_send_ref,
    gate_keep_ref,
    up_send_ref,
    up_keep_ref,
    down_a_send_ref,
    down_a_keep_ref,
    down_b_send_ref,
    down_b_keep_ref,
    down_own_ref,
    down_other_ref,
    second_own_ref,
    second_other_ref,
    held,
    down_ref,
    grad_second_ref,
    second_t_ref,
    grad_t_ref,
    narrow,
    terms,
    send_sem,
    recv_sem,
    out_sem,
    terms_sem,
):
    y, x, z, core = places_of()
    down_ref[...] = jnp.zeros_like(down_ref)
    grad_second_ref[...] = jnp.zeros_like(grad_second_ref)
    greet(y, x, z, core)
    tokens = second_ref.shape[0]
    block = 256 if tokens % 256 == 0 else tokens

    def transfer(stage, tile, order):
        slot = tile % SLOTS
        view = gather_view(held.at[slot], order, stage, y, x, z)
        return pltpu.make_async_remote_copy(
            src_ref=view,
            dst_ref=view,
            send_sem=send_sem.at[stage, slot],
            recv_sem=recv_sem.at[stage, slot],
            device_id=mesh_exchange(y, x, z, core, GATHER_ORDERS[order][stage]),
            device_id_type=pl.DeviceIdType.MESH,
        )

    down_a = (tiles + 1) // 2
    down_b = tiles - down_a

    def compute(tile):
        weights = held.at[tile % SLOTS]

        @pl.loop(0, tokens // block)
        def _(part):
            rows = pl.ds(pl.multiple_of(part * block, block), block)
            both = weights[:, :, :, :, :, : 2 * LANES].reshape(D, 2 * LANES)
            down = weights[:, :, :, :, :, 2 * LANES :].reshape(D, LANES)
            gate_up = dot(second_ref[rows, :], both)
            gate, upward = gate_up[:, :LANES], gate_up[:, LANES:]
            grad_hidden = dot(grad_ref[rows, :], down)
            sigmoid_gate = 1.0 / (1.0 + jnp.exp(-gate))
            silu_gate = gate * sigmoid_gate
            hidden = (silu_gate * upward).astype(bf16)
            grad_upward = (grad_hidden * silu_gate).astype(bf16)
            grad_gate = (
                grad_hidden * upward * sigmoid_gate * (1.0 + gate * (1.0 - sigmoid_gate))
            ).astype(bf16)
            grads = jnp.concatenate([grad_gate, grad_upward], axis=1)
            narrow[rows, : 2 * LANES] = grads
            narrow[rows, 2 * LANES :] = hidden
            down_ref[rows, :] += dot_nt(hidden, down)
            grad_second_ref[rows, :] += dot_nt(grads, both)

    def weight_terms(tile):
        slot = tile % 2

        @pl.loop(0, 4)
        def _(part):
            rows = pl.ds(pl.multiple_of(part * quarter, quarter), quarter)
            grads = dot(second_t_ref[rows, :], narrow[:, : 2 * LANES])
            terms[slot, part // 2, part % 2, :, : 2 * LANES] = grads.astype(bf16)
            down = dot(grad_t_ref[rows, :], narrow[:, 2 * LANES :])
            terms[slot, part // 2, part % 2, :, 2 * LANES :] = down.astype(bf16)

    quarter = D // 4

    def terms_copies(tile):
        slot = tile % 2

        gate, up = (gate_send_ref, gate_keep_ref), (up_send_ref, up_keep_ref)
        first, second = (down_a_send_ref, down_a_keep_ref), (down_b_send_ref, down_b_keep_ref)

        def pair(index, stream, refs, at, sem):
            here = (y, x)[stream]
            columns = pl.ds(pl.multiple_of(at * LANES, LANES), LANES)
            copies = []
            for way, (place, ref) in enumerate(zip((1 - here, here), refs)):
                source = terms.at[slot, :, :, :, index * LANES : (index + 1) * LANES]
                source = source.at[place] if stream == 0 else source.at[:, place]
                copies.append(
                    pltpu.make_async_copy(source, ref.at[:, :, columns], terms_sem.at[slot, sem, way])
                )
            return copies

        early = tile < down_a
        return (
            (None, pair(0, 0, gate, tile, 0)),
            (None, pair(1, 1, up, tile, 1)),
            (early, pair(2, 0, first, jnp.where(early, tile, 0), 2)),
            (tile >= down_a, pair(2, 1, second, jnp.where(early, 0, tile - down_a), 2)),
            (tile == tiles - 1, pair(0, 0, gate, tiles, 3)),
            (tile == tiles - 1, pair(1, 1, up, tiles, 4)),
            (tile == tiles - 1, pair(2, 1, second, down_b, 5)),
        )

    def all_copies(tile, act):
        for condition, copies in terms_copies(tile):
            if condition is None:
                for copy in copies:
                    act(copy)
            else:

                @pl.when(condition)
                def _(copies=copies):
                    for copy in copies:
                        act(copy)

    pairs = (tiles + 1) // 2

    def each(step, behind, act):
        for order in range(2):
            tile = 2 * (step - behind) + order

            @pl.when((tile >= 0) & (tile < tiles))
            def _(tile=tile, order=order):
                act(tile, order)

    def send_on(stage):
        def act(tile, order):
            transfer(stage, tile, order).wait()
            transfer(stage + 1, tile, order).start()

        return act

    def finish(tile, order):
        transfer(3, tile, order).wait()
        compute(tile)

        @pl.when(tile >= 2)
        def _():
            all_copies(tile - 2, lambda copy: copy.wait())

        weight_terms(tile)
        all_copies(tile, lambda copy: copy.start())

    def begin(tile, order):
        held[tile % SLOTS, y, x, z // 2, z % 2] = shard_ref[tile]
        transfer(0, tile, order).start()

    @pl.loop(0, pairs + 4)
    def _(step):
        each(step, 2, send_on(1))
        each(step, 3, send_on(2))
        each(step, 4, finish)
        each(step, 1, send_on(0))
        each(step, 0, begin)

        @pl.when(step < tokens // block)
        def _():
            rows = pl.ds(pl.multiple_of(step * block, block), block)
            second_t_ref[:, rows] = second_ref[rows, :].T
            grad_t_ref[:, rows] = grad_ref[rows, :].T

    @pl.loop(tiles - 2, tiles)
    def _(tile):
        all_copies(tile, lambda copy: copy.wait())

    half = tokens // 2
    copies = [
        pltpu.make_async_copy(source, target, out_sem.at[at])
        for at, (source, target) in enumerate(
            (
                (grad_second_ref.at[half:], second_other_ref),
                (grad_second_ref.at[:half], second_own_ref),
                (down_ref.at[half:], down_other_ref),
                (down_ref.at[:half], down_own_ref),
            )
        )
    ]
    for copy in copies:
        copy.start()
    for copy in copies:
        copy.wait()


def feed_forward(second, grad_result, gate_shard, up_shard, down_shard):
    tokens = second.shape[0]
    rows, width = gate_shard.shape
    tiles = width // LANES
    parts = [shard.reshape(rows, tiles, LANES) for shard in (gate_shard, up_shard, down_shard)]
    shard = jnp.transpose(jnp.stack(parts, axis=2), (1, 0, 2, 3)).reshape(tiles, rows, 3 * LANES)
    down_a = (tiles + 1) // 2
    terms = [
        jax.ShapeDtypeStruct((2, D // 4, count * LANES), bf16)
        for count in (tiles + 1, tiles + 1, down_a, down_a)
        for _ in range(2)
    ]
    part = jax.ShapeDtypeStruct((tokens // 2, D), f32)
    dma = pltpu.SemaphoreType.DMA
    results = pl.pallas_call(
        functools.partial(feed_forward_kernel, tiles),
        out_shape=terms + [part] * 4,
        in_specs=[pl.BlockSpec(memory_space=pltpu.VMEM)] * 3,
        out_specs=[pl.BlockSpec(memory_space=pl.ANY)] * 12,
        scratch_shapes=[
            pltpu.VMEM((SLOTS, 2, 2, 2, 2, rows, 3 * LANES), bf16),
            pltpu.VMEM((tokens, D), f32),
            pltpu.VMEM((tokens, D), f32),
            pltpu.VMEM((D, tokens), bf16),
            pltpu.VMEM((D, tokens), bf16),
            pltpu.VMEM((tokens, 3 * LANES), bf16),
            pltpu.VMEM((2, 2, 2, D // 4, 3 * LANES), bf16),
            dma((4, SLOTS)),
            dma((4, SLOTS)),
            dma((4,)),
            dma((2, 6, 2)),
        ],
        compiler_params=pltpu.CompilerParams(
            collective_id=2, has_side_effects=True, vmem_limit_bytes=60 << 20
        ),
        cost_estimate=pl.CostEstimate(flops=0, bytes_accessed=1024, transcendentals=0),
    )(second, grad_result, shard)
    return list(zip(results[0:8:2], results[1:8:2])), results[8:]


def norm_scale(values):
    inverse = lax.rsqrt(jnp.mean(values * values, axis=-1, keepdims=True) + norm_epsilon)
    return (values * inverse, inverse)


def norm_backward(grad_normed, scaled, inverse, gain_row):
    grad_scaled = grad_normed * gain_row[None, :]
    grad_input = inverse * (
        grad_scaled - scaled * jnp.mean(grad_scaled * scaled, axis=-1, keepdims=True)
    )
    return (grad_input, jnp.sum(grad_normed * scaled, axis=0))


def adam_update(weight, gradient, first_moment, second_moment, learn_rate, decay_rate):
    first_new = beta_first * first_moment + (1.0 - beta_first) * gradient
    second_new = beta_second * second_moment + (1.0 - beta_second) * gradient * gradient
    first_hat = first_new / (1.0 - beta_first**STEP)
    second_hat = second_new / (1.0 - beta_second**STEP)
    new_weight = (
        weight
        - learn_rate * first_hat / (jnp.sqrt(second_hat) + adam_epsilon)
        - decay_rate * weight
    )
    return (new_weight, second_new)


def local(
    tokens,
    cotangent,
    lengths,
    w_qk,
    w_value,
    w_out,
    w_gu,
    w_down,
    small_params,
    m_qk,
    m_value,
    m_out,
    m_gu,
    m_down,
    m_small,
    v_qk,
    v_value,
    v_out,
    v_gu,
    v_down,
    v_small,
):
    slots, slot_rows, _ = tokens.shape
    owned = w_qk.shape[0]
    rows = slots * slot_rows
    core, z_at = lax.axis_index("core"), lax.axis_index("z")
    other = 1 - core
    first_core = core == 0

    def on_chip(array):
        return jnp.concatenate([array, swapped(array)], axis=0)

    def halves(array):
        return array.reshape(CORES, slots, slot_rows, -1)

    columns_of = [
        w_qk.astype(bf16).reshape(owned, 2, CORES, QC),
        w_value.astype(bf16).reshape(owned, 1, CORES, VC),
        w_out.astype(bf16).reshape(owned, 1, CORES, VC),
        w_gu.astype(bf16).reshape(owned, 2, CORES, FC),
        w_down.astype(bf16).reshape(owned, 1, CORES, FC),
    ]
    small_low = jnp.pad(small_params.astype(bf16), ((0, 0), (0, LANES - (KS + 2))))

    def shard(which, index):
        parts = [part_of(columns_of[i], 2, index).reshape(owned, -1) for i in which]
        return jnp.concatenate(parts, axis=1) if len(parts) > 1 else parts[0]

    def chip_shard(which, extra=None):
        mine, theirs = shard(which, core), shard(which, other)
        arrived = swapped(theirs if extra is None else jnp.concatenate([theirs, extra], axis=1))
        mine = mine if extra is None else jnp.concatenate([mine, extra], axis=1)
        return both_cores(mine, arrived, 0)

    attention_shard = chip_shard((0, 1), small_low)
    rest_shard = chip_shard((2, 3, 4))
    in_kernel = tuple(lax.axis_size(axis) for axis in ("y", "x", "z")) == (2, 2, 4)
    early_width = 2 * QC + VC + LANES
    half = early_width // 2
    cut = FC // 2 // LANES * LANES
    down_at = VC + 2 * FC
    own_tokens = tokens.reshape(rows, D)
    other_tokens = swapped(own_tokens)
    wide_part = 4 * LANES
    if in_kernel:
        full = gathered_rows(jnp.concatenate([attention_shard, rest_shard[:, :VC]], axis=1))
        early, out_half = full[:, :early_width], full[:, early_width:]
    else:
        early_a = Gather(attention_shard[:, :half], True)
        early_b = Gather(attention_shard[:, half:], False)
        early = jnp.concatenate([early_a.rest(), early_b.rest()], axis=1)

        def gathered(start, width):
            return lax.all_gather(rest_shard[:, start : start + width], ("y", "x", "z"), axis=0, tiled=True)

        out_half = gathered(0, VC)
        gate_full = gathered(VC, FC)
        up_full = gathered(VC + FC, FC)
        last_shard, early = tied(rest_shard[:, down_at:], early)
        down_a = Gather(last_shard[:, :cut], True)
        down_b = Gather(last_shard[:, cut:], False)
        down_full = jnp.concatenate([down_a.rest(), down_b.rest()], axis=1)

    qk_full = early[:, : 2 * QC]
    value_full = early[:, 2 * QC : 2 * QC + VC]
    small_float = early[:, 2 * QC + VC :][:, : KS + 2].astype(f32)
    out_full = both_cores(out_half, swapped(out_half), 1)
    gain_first, gain_second = small_float[:, KS], small_float[:, KS + 1]
    taps = [part_of(small_float[:, j].reshape(CORES, VC), 0, core) for j in range(KS)]

    inputs = tokens.reshape(rows, D).astype(f32)
    scaled_first, inverse_first = norm_scale(inputs)
    scaled_chip, _ = norm_scale(
        jnp.concatenate([own_tokens, other_tokens], axis=0).astype(f32)
    )
    normed_chip = (scaled_chip * gain_first[None, :]).astype(bf16)
    query_key = halves(dot(normed_chip, qk_full).astype(bf16))
    value_pre = halves(dot(normed_chip, value_full).astype(bf16))
    tail = value_pre[:, :, slot_rows - (KS - 1) :, :]
    from_chip = passed_along(part_of(tail, 0, other), "z", 1)
    from_core = part_of(tail, 0, core)
    earlier = jnp.stack(
        [jnp.where(first_core, from_chip, from_core), jnp.where(first_core, from_core, from_chip)]
    )
    extended = jnp.concatenate([earlier, value_pre], axis=2).astype(f32)

    def tap_rows(j):
        return extended[:, :, KS - 1 - j : KS - 1 - j + slot_rows, :]

    convolved = taps[0] * tap_rows(0)
    for j in range(1, KS):
        convolved = convolved + taps[j] * tap_rows(j)
    values = convolved.astype(bf16)

    index_np, scale_np = feature_tables()
    tables = (core.astype(jnp.int32).reshape(1), jnp.asarray(index_np), jnp.asarray(scale_np))
    q_spec, k_spec, v_spec = (LANES, 0), (LANES, 1), (VC,)
    call = functools.partial(per_slot, slots=slots, rows=slot_rows)
    unit = 2 * CORES * rows * HC * LANES * FEATS
    wide = [pltpu.VMEM((CORES * slot_rows, VC), f32)]
    if in_kernel:
        (before,) = linked(key_term, True, 3)(*tables[1:], query_key, values, slots=slots)
    else:
        (state_own,) = call(
            state_kernel, ins=[k_spec, v_spec], outs=[("state", f32)], scratch=[], flops=4 * unit
        )(*tables, query_key, values)
        before = chain(state_own, True)
    mixer, dens = call(
        forward_kernel,
        ins=[q_spec, k_spec, v_spec, "state"],
        outs=[(v_spec, bf16), ((LANES,), f32)],
        scratch=wide,
        flops=8 * unit,
    )(*tables, query_key, query_key, values, before)

    mixer_flat = mixer.reshape(CORES * rows, VC)
    mixer_theirs = swapped(mixer_flat)

    def beside(mine, theirs):
        whole = jnp.zeros((mine.shape[0], CORES * mine.shape[1]), mine.dtype)
        for index, part in ((core, mine), (other, theirs)):
            whole = lax.dynamic_update_slice_in_dim(whole, part, index * mine.shape[1], 1)
        return whole

    mixer_own = beside(mixer_flat[:rows], mixer_theirs[rows:])
    mixer_other = beside(mixer_flat[rows:], mixer_theirs[:rows])
    after_mixer = inputs + dot(mixer_own, out_full)
    scaled_second, inverse_second = norm_scale(after_mixer)
    second_low = (scaled_second * gain_second[None, :]).astype(bf16)
    second_chip = on_chip(second_low)

    half_at = jnp.where(first_core, jnp.arange(CORES), 1 - jnp.arange(CORES))
    positions = (z_at * CORES + half_at)[:, None] * slot_rows + jnp.arange(slot_rows)[None, :]
    valid_chip = positions[:, None, :] < lengths[None, :, None]
    valid_chip = valid_chip.astype(f32).reshape(CORES * rows, 1)
    valid = valid_chip[:rows]
    query_key, cotangent_late = lax.optimization_barrier((query_key, cotangent))
    cotangent_chip = on_chip(cotangent_late.reshape(rows, D))
    mixer, cotangent_chip = tied(mixer, cotangent_chip)
    grad_result_chip = (valid_chip * cotangent_chip.astype(f32)).astype(bf16)
    grad_result = valid * cotangent.reshape(rows, D).astype(f32)

    if in_kernel:
        ffn_terms, ffn_parts = feed_forward(
            second_chip,
            grad_result_chip,
            rest_shard[:, VC : VC + FC],
            rest_shard[:, VC + FC : down_at],
            rest_shard[:, down_at:],
        )
        down_own, down_other, second_own, second_other = ffn_parts
        grad_second = second_own + swapped(second_other)
        down_result = down_own + swapped(down_other)
        (send_gate, keep_gate), (send_up, keep_up), *down_pairs = ffn_terms
        (send_down_a, keep_down_a), (send_down_b, keep_down_b) = down_pairs
        got_gate, got_up = exchanged(send_gate, "y", 0), exchanged(send_up, "x", 0)
    else:
        gate = dot(second_chip, gate_full)
        upward = dot(second_chip, up_full)
        sigmoid_gate = jax.nn.sigmoid(gate)
        silu_gate = gate * sigmoid_gate
        hidden = (silu_gate * upward).astype(bf16)
        grad_hidden = dot(grad_result_chip, down_full)
        grad_upward = (grad_hidden * silu_gate).astype(bf16)
        grad_gate = (
            grad_hidden * upward * sigmoid_gate * (1.0 + gate * (1.0 - sigmoid_gate))
        ).astype(bf16)
        second_part = dot_nt(grad_gate, gate_full) + dot_nt(grad_upward, up_full)
        grad_second = second_part[:rows] + swapped(second_part[rows:])
        down_part = dot_nt(hidden, down_full)
        down_result = down_part[:rows] + swapped(down_part[rows:])
    layer_out = (valid * (after_mixer + down_result)).astype(bf16).reshape(tokens.shape)

    grad_after_norm, grad_gain_second = norm_backward(
        grad_second, scaled_second, inverse_second, gain_second
    )
    grad_after = grad_result + grad_after_norm
    grad_after_low = grad_after.astype(bf16)
    grad_mixer = dot_nt(grad_after_low, out_full).astype(bf16)

    def core_columns(array):
        mine, theirs = (
            lax.dynamic_slice_in_dim(array, index * VC, VC, axis=1) for index in (core, other)
        )
        return jnp.concatenate([mine, swapped(theirs)], axis=0)

    grad_mixer_chip = core_columns(grad_mixer)
    grad_after_chip = core_columns(grad_after_low)
    mixer_chip = lax.optimization_barrier(jnp.concatenate([mixer_own, mixer_other], axis=0))

    wide_spec = (HC * LANES,)
    if in_kernel:
        grad_num, from_later = linked(query_term, False, 4)(
            *tables[1:],
            query_key,
            halves(grad_mixer_chip),
            mixer,
            dens,
            slots=slots,
            extra=(jax.ShapeDtypeStruct((CORES, slots, slot_rows, HC * LANES), bf16),),
        )
    else:
        pulled, grad_num = call(
            pull_kernel,
            ins=[q_spec, v_spec, v_spec, (LANES,)],
            outs=[("state", f32), (wide_spec, bf16)],
            scratch=[],
            flops=4 * unit,
        )(*tables, query_key, halves(grad_mixer_chip), mixer, dens)
        from_later = chain(pulled, False)
    grad_query_key, grad_values = call(
        backward_kernel,
        ins=[q_spec, k_spec, v_spec, wide_spec, "state", "state"],
        outs=[((2 * LANES,), bf16), (v_spec, bf16)],
        scratch=wide,
        flops=24 * unit,
    )(*tables, query_key, query_key, values, grad_num, before, from_later)

    if in_kernel:
        got_gate, got_up, send_down_a, send_down_b, grad_values = tied(
            got_gate, got_up, send_down_a, send_down_b, grad_values
        )

        def summed(keep, got):
            return (keep.astype(f32) + got.astype(f32)).astype(bf16)

        sum_gate, sum_up = summed(keep_gate, got_gate), summed(keep_up, got_up)
        sum_down_a = summed(keep_down_a, exchanged(send_down_a, "y", 0))
        sum_down_b = summed(keep_down_b, exchanged(send_down_b, "x", 0))
    head = grad_values[:, :, : KS - 1, :]
    from_chip = passed_along(part_of(head, 0, core), "z", -1)
    from_core = part_of(head, 0, other)
    later = jnp.stack(
        [jnp.where(first_core, from_core, from_chip), jnp.where(first_core, from_chip, from_core)]
    )
    grad_extended = jnp.concatenate([grad_values, later], axis=2).astype(f32)
    grad_pre = taps[0] * grad_extended[:, :, :slot_rows, :]
    for j in range(1, KS):
        grad_pre = grad_pre + taps[j] * grad_extended[:, :, j : j + slot_rows, :]
    grad_pre = grad_pre.reshape(CORES * rows, VC).astype(bf16)
    grad_query_key = grad_query_key.reshape(CORES * rows, 2 * QC)
    grad_values_float = grad_values.astype(f32)
    tap_grads = [jnp.sum(grad_values_float * tap_rows(j), axis=(0, 1, 2)) for j in range(KS)]

    first_other = dot_nt(grad_query_key[rows:], qk_full) + dot_nt(grad_pre[rows:], value_full)
    first_own = dot_nt(grad_query_key[:rows], qk_full) + dot_nt(grad_pre[:rows], value_full)
    grad_first = first_own + swapped(first_other)
    grad_gain_first = jnp.sum(first_own * scaled_chip[:rows], axis=0) + jnp.sum(
        first_other * scaled_chip[rows:], axis=0
    )

    def whole_feature(part):
        return lax.dynamic_update_slice(jnp.zeros((D,), f32), part, (core * VC,))

    small_terms = jnp.stack(
        [whole_feature(part) for part in tap_grads] + [grad_gain_first, grad_gain_second], axis=1
    )
    small_terms = jnp.pad(small_terms, ((0, 0), (0, LANES - (KS + 2)))).astype(bf16)
    if in_kernel:
        empty = jnp.zeros((CORES * rows, LANES), bf16)
        last_a = jnp.concatenate([grad_pre, grad_query_key, empty], axis=1)
        last_b = jnp.concatenate([grad_after_chip, empty], axis=1)
        grad_qk_own, grad_value_own, grad_out_own, grad_gu_own, grad_down_own, small_both = reduced(
            sum_down_a,
            sum_gate,
            sum_down_b,
            sum_up,
            dot_tn(normed_chip, last_a).astype(bf16),
            dot_tn(mixer_chip, last_b).astype(bf16),
            jnp.pad(small_terms, ((0, 0), (0, LANES))),
            owned,
        )
        grad_small_own = (small_both[:, :LANES] + small_both[:, LANES:])[:, : KS + 2]
    else:
        sum_down = Scatter(dot_tn(grad_result_chip, hidden).astype(bf16), True).rest()
        sum_gate = Scatter(dot_tn(second_chip, grad_gate).astype(bf16), False).rest()
        sum_up = Scatter(dot_tn(second_chip, grad_upward).astype(bf16), True).rest()
        sum_value = Scatter(dot_tn(normed_chip, grad_pre).astype(bf16), False).rest()
        sum_out = Scatter(dot_tn(mixer_chip, grad_after_chip).astype(bf16), True).rest()
        qk_terms = dot_tn(normed_chip, grad_query_key).astype(bf16)
        sum_last = Scatter(jnp.concatenate([qk_terms, small_terms], axis=1), True).rest()
    grad_input_norm, _ = norm_backward(grad_first, scaled_first, inverse_first, gain_first)
    input_grad = (grad_after + grad_input_norm).reshape(tokens.shape)

    def rows_of(array, index):
        return part_of(array.reshape(CORES, owned, -1), 0, index)

    def finish(*parts):
        merged = jnp.concatenate(parts, axis=1) if len(parts) > 1 else parts[0]
        mine, theirs = rows_of(merged, core), swapped(rows_of(merged, other))
        return mine.astype(f32), theirs.astype(f32)

    def columns(*parts):
        mine, theirs = finish(*parts)
        return both_cores(mine, theirs, 1)

    def two_columns(mine, theirs, width):
        shape = (owned, 2, 1, width)
        return both_cores(mine.reshape(shape), theirs.reshape(shape), 2).reshape(owned, -1)

    if not in_kernel:
        grad_down_own = columns(sum_down)
        grad_gu_own = two_columns(*finish(sum_gate, sum_up), FC)
        grad_out_own = columns(sum_out)
        grad_value_own = columns(sum_value)
        last_mine, last_theirs = finish(sum_last)
        grad_qk_own = two_columns(last_mine[:, : 2 * QC], last_theirs[:, : 2 * QC], QC)
        grad_small_own = (last_mine + last_theirs)[:, 2 * QC : 2 * QC + KS + 2]

    grads_all = (
        grad_qk_own,
        grad_value_own,
        grad_out_own,
        grad_gu_own,
        grad_down_own,
        grad_small_own,
    )
    masters = (w_qk, w_value, w_out, w_gu, w_down, small_params)
    firsts = (m_qk, m_value, m_out, m_gu, m_down, m_small)
    seconds = (v_qk, v_value, v_out, v_gu, v_down, v_small)
    learn_rates = (
        0.05 / math.sqrt(D),
        0.05 / math.sqrt(D),
        0.05 / math.sqrt(max(D // 128, 1)),
        0.05 / math.sqrt(D),
        0.05 / math.sqrt(0.0003 * FF * SLOT**0.825),
        0.014,
    )
    decays = (weight_decay, weight_decay, weight_decay, weight_decay, weight_decay, 0.0)
    new_weights = []
    new_seconds = []
    for position in range(6):
        updated, moment = adam_update(
            masters[position],
            grads_all[position],
            firsts[position],
            seconds[position],
            learn_rates[position],
            decays[position],
        )
        new_weights.append(updated)
        new_seconds.append(moment)
    return (layer_out, input_grad) + grads_all + tuple(new_weights) + tuple(new_seconds)


def solution(mesh):
    dp, fsdp = mesh.shape["dp"], mesh.shape["fsdp"]
    y_size = 2 if dp % 2 == 0 else 1
    split = Mesh(
        mesh.devices.reshape(y_size, dp // y_size, fsdp // CORES, CORES), ("y", "x", "z", "core")
    )
    slot_axes, row_axes = ("y", "x"), ("z", "core")
    activation = P(slot_axes, row_axes, None)
    weight = P(slot_axes + row_axes, None)
    return jax.shard_map(
        local,
        mesh=split,
        in_specs=(activation, activation, P(slot_axes)) + (weight,) * 18,
        out_specs=(activation, activation) + (weight,) * 18,
        check_vma=False,
    )
```

```python
import functools
import math

import jax
import jax.numpy as jnp
import numpy as np
from jax import lax
from jax.experimental import pallas as pl
from jax.experimental.pallas import tpu as pltpu
from jax.sharding import Mesh
from jax.sharding import PartitionSpec as P

D = 1792
H = 16
F = 16
FF = 4864
KS = 3
SLOT = 2048
STEP = 10

CORES = 2
HC = H // CORES
HW = D // H
VC = HC * HW
QC = HC * F
FC = FF // CORES
LANES = 128
FEATS = 256
FROWS = 160
SCALE = 1.0 / math.sqrt(F)

norm_epsilon = 1e-06
beta_first = 0.9
beta_second = 0.95
adam_epsilon = 1e-08
weight_decay = 3e-05

bf16 = jnp.bfloat16
f32 = jnp.float32


def feature_tables():
    index = np.full((8, FEATS), -4096, np.int32)
    scale = np.zeros((8, FEATS), np.float32)
    scale[0, 0] = scale[1, 0] = scale[2, 0] = 1.0
    at = 1
    for i in range(F):
        index[0, at] = i
        scale[1, at] = 1.0
        scale[2, at] = SCALE
        at += 1
    for i in range(F):
        for j in range(i, F):
            index[0, at] = i
            index[1, at] = j
            scale[2, at] = (1.0 if i == j else 2.0) * 0.5 * SCALE * SCALE
            at += 1
    return index, scale


def dot(a, b):
    return lax.dot_general(a, b, (((1,), (0,)), ((), ())), preferred_element_type=f32)


def dot_nt(a, b):
    return lax.dot_general(a, b, (((1,), (1,)), ((), ())), preferred_element_type=f32)


def dot_tn(a, b):
    return lax.dot_general(a, b, (((0,), (0,)), ((), ())), preferred_element_type=f32)


def selectors(index_ref, head):
    lane = lax.broadcasted_iota(jnp.int32, (LANES, FEATS), 0) - head * F
    first = jnp.where(lane == index_ref[0:1, :], 1.0, 0.0).astype(bf16)
    second = jnp.where(lane == index_ref[1:2, :], 1.0, 0.0).astype(bf16)
    return first, second


def factors(rows, first, second, scale_ref):
    return (dot(rows, first) + scale_ref[0:1, :], dot(rows, second) + scale_ref[1:2, :])


def window(head):
    start = head * HW
    base = min(start // LANES * LANES, VC - 2 * LANES)
    return base, start - base


def both_halves(core_ref, ref, columns):
    core = core_ref[0]
    return jnp.concatenate([ref[core, :, columns], ref[1 - core, :, columns]], axis=0)


def store_halves(core_ref, ref, rows, columns):
    core, half = core_ref[0], rows.shape[0] // CORES
    ref[core, :, columns] = rows[:half]
    ref[1 - core, :, columns] = rows[half:]


def head_columns(core_ref, ref, head):
    base, offset = window(head)
    wide = both_halves(core_ref, ref, slice(base, base + 2 * LANES)).astype(f32)
    if offset:
        wide = pltpu.roll(wide, 2 * LANES - offset, 1)
    return wide[:, :LANES]


def add_head_columns(ref, head, block):
    base, offset = window(head)
    wide = jnp.concatenate([block, jnp.zeros_like(block)], axis=1)
    if offset:
        wide = pltpu.roll(wide, offset, 1)
    ref[:, base : base + 2 * LANES] += wide


def with_one(block):
    lane = lax.broadcasted_iota(jnp.int32, block.shape, 1)
    return jnp.where(lane < HW, block, jnp.where(lane == HW, 1.0, 0.0))


def only_head(rows, head):
    lane = lax.broadcasted_iota(jnp.int32, rows.shape, 1)
    inside = (lane >= head * F) & (lane < head * F + F)
    return jnp.where(inside, rows.astype(f32), 0.0).astype(bf16)


def state_kernel(core_ref, index_ref, scale_ref, k_ref, v_ref, state_ref):
    keys = both_halves(core_ref, k_ref, slice(None))
    for head in range(HC):
        first, second = selectors(index_ref, head)
        one, two = factors(keys, first, second, scale_ref)
        phi = (one * two * scale_ref[2:3, :]).astype(bf16)
        values = with_one(head_columns(core_ref, v_ref, head)).astype(bf16)
        state_ref[0, head] = dot_tn(phi, values)[:FROWS]


def scores_of(q_head, keys):
    scores = dot_nt(q_head, keys) * SCALE
    row = lax.broadcasted_iota(jnp.int32, scores.shape, 0)
    column = lax.broadcasted_iota(jnp.int32, scores.shape, 1)
    return scores, column <= row


def forward_kernel(core_ref, index_ref, scale_ref, q_ref, k_ref, v_ref, before_ref, mixer_ref, den_ref, wide):
    queries = both_halves(core_ref, q_ref, slice(None))
    keys = both_halves(core_ref, k_ref, slice(None))
    wide[...] = jnp.zeros_like(wide)
    lane = lax.broadcasted_iota(jnp.int32, (queries.shape[0], LANES), 1)
    dens = jnp.zeros((queries.shape[0], LANES), f32)
    for head in range(HC):
        first, second = selectors(index_ref, head)
        one, two = factors(queries, first, second, scale_ref)
        phi = (one * two).astype(bf16)
        values = with_one(head_columns(core_ref, v_ref, head)).astype(bf16)
        scores, allowed = scores_of(only_head(queries, head), keys)
        kernel = jnp.where(allowed, 1.0 + scores + 0.5 * scores * scores, 0.0).astype(bf16)
        total = dot(kernel, values) + dot(phi[:, :FROWS], before_ref[0, head])
        den = total[:, HW : HW + 1]
        add_head_columns(wide, head, jnp.where(lane < HW, total / den, 0.0))
        dens = jnp.where(lane == head, den, dens)
    store_halves(core_ref, mixer_ref, wide[...].astype(bf16), slice(None))
    store_halves(core_ref, den_ref, dens, slice(None))


def pull_kernel(core_ref, index_ref, scale_ref, q_ref, gm_ref, mixer_ref, den_ref, state_ref, gnum_ref):
    queries = both_halves(core_ref, q_ref, slice(None))
    lane = lax.broadcasted_iota(jnp.int32, (queries.shape[0], LANES), 1)
    dens = both_halves(core_ref, den_ref, slice(None))
    for head in range(HC):
        first, second = selectors(index_ref, head)
        one, two = factors(queries, first, second, scale_ref)
        phi = (one * two).astype(bf16)
        den = dens[:, head : head + 1]
        grad = jnp.where(lane < HW, head_columns(core_ref, gm_ref, head), 0.0)
        mixer = head_columns(core_ref, mixer_ref, head)
        pulled = -jnp.sum(grad * mixer, axis=1, keepdims=True)
        grad = (jnp.where(lane == HW, pulled, grad) / den).astype(bf16)
        store_halves(core_ref, gnum_ref, grad, slice(head * LANES, (head + 1) * LANES))
        state_ref[0, head] = dot_tn(phi, grad)[:FROWS]


def backward_kernel(
    core_ref, index_ref, scale_ref, q_ref, k_ref, v_ref, gnum_ref, before_ref, after_ref, gqk_ref, gv_ref, wide
):
    queries = both_halves(core_ref, q_ref, slice(None))
    keys = both_halves(core_ref, k_ref, slice(None))
    wide[...] = jnp.zeros_like(wide)
    lane = lax.broadcasted_iota(jnp.int32, (queries.shape[0], LANES), 1)
    grad_q = jnp.zeros((queries.shape[0], LANES), f32)
    grad_k = jnp.zeros((queries.shape[0], LANES), f32)
    for head in range(HC):
        first, second = selectors(index_ref, head)
        coef = scale_ref[2:3, :]
        q_one, q_two = factors(queries, first, second, scale_ref)
        k_one, k_two = factors(keys, first, second, scale_ref)
        values = with_one(head_columns(core_ref, v_ref, head)).astype(bf16)
        gnum = both_halves(core_ref, gnum_ref, slice(head * LANES, (head + 1) * LANES))
        q_head = only_head(queries, head)
        k_head = only_head(keys, head)
        scores, allowed = scores_of(q_head, keys)
        kernel = jnp.where(allowed, 1.0 + scores + 0.5 * scores * scores, 0.0).astype(bf16)
        grad_kernel = dot_nt(gnum, values)
        grad_scores = (jnp.where(allowed, grad_kernel * (1.0 + scores), 0.0) * SCALE).astype(bf16)
        phi_k = (k_one * k_two * coef).astype(bf16)
        after = after_ref[0, head]
        before = before_ref[0, head]
        grad_v = dot_tn(kernel, gnum) + dot(phi_k[:, :FROWS], after)
        add_head_columns(wide, head, jnp.where(lane < HW, grad_v, 0.0))
        empty = jnp.zeros((FEATS - FROWS, LANES), bf16)
        grad_phi_q = dot_nt(gnum, jnp.concatenate([before, empty], axis=0))
        grad_phi_k = dot_nt(values, jnp.concatenate([after, empty], axis=0)) * coef
        grad_q += dot(grad_scores, k_head)
        grad_q += dot_nt((grad_phi_q * q_two).astype(bf16), first)
        grad_q += dot_nt((grad_phi_q * q_one).astype(bf16), second)
        grad_k += dot_tn(grad_scores, q_head)
        grad_k += dot_nt((grad_phi_k * k_two).astype(bf16), first)
        grad_k += dot_nt((grad_phi_k * k_one).astype(bf16), second)
    store_halves(core_ref, gqk_ref, grad_q.astype(bf16), slice(0, LANES))
    store_halves(core_ref, gqk_ref, grad_k.astype(bf16), slice(LANES, 2 * LANES))
    store_halves(core_ref, gv_ref, wide[...].astype(bf16), slice(None))


def per_slot(kernel, slots, rows, ins, outs, scratch, flops):
    def table():
        return pl.BlockSpec((8, FEATS), lambda s, core: (0, 0))

    def row_spec(width, column=0):
        return pl.BlockSpec((CORES, None, rows, width), lambda s, core: (0, s, 0, column))

    def state_spec():
        return pl.BlockSpec((1, HC, FROWS, LANES), lambda s, core: (s, 0, 0, 0))

    def spec(kind):
        return state_spec() if kind == "state" else row_spec(*kind)

    def shape(kind, dtype):
        if kind == "state":
            return jax.ShapeDtypeStruct((slots, HC, FROWS, LANES), dtype)
        return jax.ShapeDtypeStruct((CORES, slots, rows, kind[0]), dtype)

    return pl.pallas_call(
        kernel,
        grid_spec=pltpu.PrefetchScalarGridSpec(
            num_scalar_prefetch=1,
            grid=(slots,),
            in_specs=[table(), table()] + [spec(kind) for kind in ins],
            out_specs=[spec(kind) for kind, _ in outs],
            scratch_shapes=scratch,
        ),
        out_shape=[shape(kind, dtype) for kind, dtype in outs],
        compiler_params=pltpu.CompilerParams(vmem_limit_bytes=56 << 20),
        cost_estimate=pl.CostEstimate(flops=flops, bytes_accessed=8 << 20, transcendentals=0),
    )


def linked(kernel, up, ids):
    def run(*refs):
        y, x, z, core = places_of()
        last = lax.axis_size("z") - 1
        *refs, sent, send_sem, recv_sem = refs
        total_ref = refs[-1]
        by = 1 if up else last
        receives, sends = (z > 0, z < last) if up else (z < last, z > 0)

        barrier = pltpu.get_barrier_semaphore()
        for step in (1, last):
            pl.semaphore_signal(
                barrier,
                inc=1,
                device_id=(y, x, lax.rem(z + step, last + 1), core),
                device_id_type=pl.DeviceIdType.MESH,
            )
        pl.semaphore_wait(barrier, 2)

        def transfer(slot, head):
            return pltpu.make_async_remote_copy(
                src_ref=sent.at[slot, head],
                dst_ref=total_ref.at[slot, head],
                send_sem=send_sem.at[slot, head],
                recv_sem=recv_sem.at[slot, head],
                device_id=(y, x, lax.rem(z + by, last + 1), core),
                device_id_type=pl.DeviceIdType.MESH,
            )

        @pl.when(jnp.logical_not(receives))
        def _():
            total_ref[...] = jnp.zeros_like(total_ref)

        @pl.loop(0, sent.shape[0])
        def _(slot):
            for head in range(HC):
                term = kernel([core], slot, head, *refs[:-1])

                @pl.when(receives)
                def _(head=head):
                    transfer(slot, head).wait_recv()

                @pl.when(sends)
                def _(head=head, term=term):
                    sent[slot, head] = (total_ref[slot, head].astype(f32) + term).astype(bf16)
                    transfer(slot, head).start()

        @pl.when(sends)
        def _():
            @pl.loop(0, sent.shape[0])
            def _(slot):
                for head in range(HC):
                    transfer(slot, head).wait_send()

    def call(*operands, slots, extra=()):
        state = jax.ShapeDtypeStruct((slots, HC, FROWS, LANES), bf16)
        vmem = pl.BlockSpec(memory_space=pltpu.VMEM)
        return pl.pallas_call(
            run,
            out_shape=list(extra) + [state],
            in_specs=[vmem] * len(operands),
            out_specs=[vmem] * (len(extra) + 1),
            scratch_shapes=[
                pltpu.VMEM((slots, HC, FROWS, LANES), bf16),
                pltpu.SemaphoreType.DMA((slots, HC)),
                pltpu.SemaphoreType.DMA((slots, HC)),
            ],
            compiler_params=pltpu.CompilerParams(
                collective_id=ids, has_side_effects=True, vmem_limit_bytes=40 << 20
            ),
            cost_estimate=pl.CostEstimate(flops=0, bytes_accessed=1024, transcendentals=0),
        )(*operands)

    return call


def key_term(core_ref, slot, head, index_ref, scale_ref, qk_ref, v_ref):
    keys = both_halves(core_ref, qk_ref.at[:, slot], slice(LANES, 2 * LANES))
    first, second = selectors(index_ref, head)
    one, two = factors(keys, first, second, scale_ref)
    phi = (one * two * scale_ref[2:3, :]).astype(bf16)
    values = with_one(head_columns(core_ref, v_ref.at[:, slot], head)).astype(bf16)
    return dot_tn(phi, values)[:FROWS]


def query_term(core_ref, slot, head, index_ref, scale_ref, qk_ref, gm_ref, mixer_ref, den_ref, gnum_ref):
    queries = both_halves(core_ref, qk_ref.at[:, slot], slice(0, LANES))
    first, second = selectors(index_ref, head)
    one, two = factors(queries, first, second, scale_ref)
    phi = (one * two).astype(bf16)
    den = both_halves(core_ref, den_ref.at[:, slot], slice(None))[:, head : head + 1]
    lane = lax.broadcasted_iota(jnp.int32, (queries.shape[0], LANES), 1)
    grad = jnp.where(lane < HW, head_columns(core_ref, gm_ref.at[:, slot], head), 0.0)
    mixer = head_columns(core_ref, mixer_ref.at[:, slot], head)
    pulled = -jnp.sum(grad * mixer, axis=1, keepdims=True)
    grad = (jnp.where(lane == HW, pulled, grad) / den).astype(bf16)
    store_halves(core_ref, gnum_ref.at[:, slot], grad, slice(head * LANES, (head + 1) * LANES))
    return dot_tn(phi, grad)[:FROWS]


def passed_along(array, axis, by):
    count = lax.axis_size(axis)
    pairs = [(i, i + by) for i in range(count) if 0 <= i + by < count]
    return lax.ppermute(array, axis, pairs)


def both_cores(mine, theirs, axis):
    first = lax.axis_index("core") == 0
    return jnp.concatenate(
        [jnp.where(first, mine, theirs), jnp.where(first, theirs, mine)], axis=axis
    )


def swapped(array):
    return lax.ppermute(array, "core", [(0, 1), (1, 0)])


def part_of(array, axis, index):
    return lax.dynamic_index_in_dim(array, index, axis, keepdims=False)


def bits_of(axis):
    return [(axis, bit) for bit in reversed(range(lax.axis_size(axis).bit_length() - 1))]


def bit_at(axis, bit):
    return (lax.axis_index(axis) >> bit) & 1


def exchanged(array, axis, bit):
    count = lax.axis_size(axis)
    return lax.ppermute(array, axis, [(i, i ^ (1 << bit)) for i in range(count)])


def tied(*arrays):
    return lax.optimization_barrier(arrays)


class Gather:
    def __init__(self, piece, x_first):
        self.columns = piece.shape[1]
        self.block = piece
        low_first = lambda axis: bits_of(axis)[::-1]
        self.plan = [(step, at) for at, step in enumerate(bits_of("z"))]
        if x_first:
            self.plan += [(step, 0) for step in low_first("x") + low_first("y")]
        else:
            self.plan += [(step, 0) for step in low_first("y")]
            self.plan += [(step, len(bits_of("y"))) for step in low_first("x")]

    def stage(self):
        (axis, bit), dim = self.plan.pop(0)
        mine = bit_at(axis, bit)
        arrived = exchanged(self.block, axis, bit)
        shape = self.block.shape[:dim] + (2,) + self.block.shape[dim:]
        whole = jnp.zeros(shape, self.block.dtype)
        whole = lax.dynamic_update_index_in_dim(whole, self.block, mine, dim)
        self.block = lax.dynamic_update_index_in_dim(whole, arrived, 1 - mine, dim)
        return self

    def along_z(self):
        while self.plan[0][0][0] == "z":
            self.stage()
        return self

    def rest(self):
        while self.plan:
            self.stage()
        return self.block.reshape(D, self.columns)


class Scatter:
    def __init__(self, terms, x_first):
        self.dims = bits_of("y") + bits_of("x") + bits_of("z")
        order = ("x", "y") if x_first else ("y", "x")
        self.plan = bits_of(order[0]) + bits_of(order[1]) + bits_of("z")[::-1]
        rows = D >> len(self.dims)
        self.terms = [terms.reshape((2,) * len(self.dims) + (rows, terms.shape[1]))]

    def total(self, terms):
        total = terms[0].astype(f32)
        for term in terms[1:]:
            total = total + term.astype(f32)
        return total

    def stage(self):
        step = self.plan.pop(0)
        dim, mine = self.dims.index(step), bit_at(*step)
        self.dims.remove(step)
        sent = self.total([part_of(term, dim, 1 - mine) for term in self.terms]).astype(bf16)
        self.terms = [part_of(term, dim, mine) for term in self.terms]
        self.terms.append(exchanged(sent, *step))
        return self

    def rest(self):
        while self.plan:
            self.stage()
        return self.total(self.terms)


def chain(local, up):
    count = lax.axis_size("z")
    total = jnp.zeros_like(local)
    for hop in range(1, count):
        pair = (hop - 1, hop) if up else (count - hop, count - hop - 1)
        message = (total + local).astype(bf16)
        total = total + lax.ppermute(message, "z", [pair]).astype(f32)
    return total.astype(bf16)


def mesh_exchange(y, x, z, core, axis):
    if axis == "core":
        return (y, x, z, 1 - core)
    if axis == "y":
        return (1 - y, x, z, core)
    if axis == "x":
        return (y, 1 - x, z, core)
    if axis == "z0":
        return (y, x, z + 1 - 2 * (z % 2), core)
    return (y, x, (z + 2) % 4, core)


ORDERS = (("y", "x", "z0", "z1"), ("x", "y", "z0", "z1"))


WIDE = 2 * LANES


def reduce_kernel(
    down_a_ref,
    gate_ref,
    down_b_ref,
    up_ref,
    last_a_ref,
    last_b_ref,
    small_terms_ref,
    qk_ref,
    value_ref,
    out_ref,
    gu_ref,
    down_ref,
    small_ref,
    sums,
    halves,
    quarters,
    finals,
    got_terms,
    got_sums,
    got_halves,
    got_quarters,
    send_sem,
    recv_sem,
):
    y, x, z, core = places_of()
    places = {"y": y, "x": x, "z0": z % 2, "z1": z // 2}

    parts, count = ([], []), 0
    all_refs = (
        (down_a_ref, gate_ref, last_a_ref),
        (down_b_ref, up_ref, last_b_ref, small_terms_ref),
    )
    for stream, refs in enumerate(all_refs):
        at = 0
        for ref in refs:
            chunks = ref.shape[-1] // WIDE
            parts[stream].append((ref, len(ref.shape) == 3, at, at + chunks))
            at += chunks
        count = max(count, at)
    hidden, width = FC // LANES, VC // LANES
    down_a = (hidden + 1) // 2
    down_b = hidden - down_a
    gate_at, last_a = 2 * parts[0][1][2], 2 * parts[0][2][2]
    up_at, last_b, small_at = (2 * parts[1][at][2] for at in (1, 2, 3))
    places_out = (
        (
            (down_ref, core * hidden, 0, down_a),
            (gu_ref, core * hidden, gate_at, gate_at + hidden),
            (value_ref, core * width, last_a, last_a + width),
            (qk_ref, core, last_a + width, last_a + width + 1),
            (qk_ref, CORES + core, last_a + width + 1, last_a + width + 2),
        ),
        (
            (down_ref, core * hidden + down_a, 0, down_b),
            (gu_ref, (CORES + core) * hidden, up_at, up_at + hidden),
            (out_ref, core * width, last_b, last_b + width),
            (small_ref, core, small_at, small_at + 1),
        ),
    )
    greet(y, x, z, core, True)

    def columns(tile):
        return pl.ds(pl.multiple_of(tile * LANES, LANES), LANES)

    def wide_columns(chunk):
        return pl.ds(pl.multiple_of(chunk * WIDE, WIDE), WIDE)

    def transfer(stream, stage, chunk, source, target=None):
        landing = chunk % 4
        if target is None:
            target = (got_terms, got_sums, got_halves, got_quarters)[stage].at[stream, landing]
        axis = (ORDERS[stream] + ("core", "core"))[stage]
        return pltpu.make_async_remote_copy(
            src_ref=source,
            dst_ref=target,
            send_sem=send_sem.at[stream, stage, landing],
            recv_sem=recv_sem.at[stream, stage, landing],
            device_id=mesh_exchange(y, x, z, core, axis),
            device_id_type=pl.DeviceIdType.MESH,
        )

    def first_view(stream, ref, tile, place):
        ref = ref.at[:, :, :, wide_columns(tile)]
        return ref.at[place] if stream == 0 else ref.at[:, place]

    def source_of(stream, stage, chunk):
        there = 1 - places[ORDERS[stream][stage]]
        if stage == 1:
            return sums.at[stream, chunk % 2, there]
        if stage == 2:
            return halves.at[stream, chunk % 2, :, there]
        return quarters.at[stream, chunk % 2, there]

    def add(a, b):
        return a.astype(f32) + b.astype(f32)

    def begin(stream, chunk):
        for ref, _, start, stop in parts[stream][2:]:

            @pl.when((chunk >= start) & (chunk < stop))
            def _(ref=ref, start=start):
                there = 1 - places[ORDERS[stream][0]]
                transfer(stream, 0, chunk, first_view(stream, ref, chunk - start, there)).start()

    def second(stream, chunk):
        for ref, summed, start, stop in parts[stream]:

            @pl.when((chunk >= start) & (chunk < stop))
            def _(ref=ref, summed=summed, start=start):
                tile = chunk - start
                if summed:
                    sums[stream, chunk % 2] = ref[:, :, wide_columns(tile)]
                else:
                    there = 1 - places[ORDERS[stream][0]]
                    transfer(stream, 0, chunk, first_view(stream, ref, tile, there)).wait()
                    own = first_view(stream, ref, tile, places[ORDERS[stream][0]])[...]
                    sums[stream, chunk % 2] = add(own, got_terms[stream, chunk % 4]).astype(bf16)

        transfer(stream, 1, chunk, source_of(stream, 1, chunk)).start()

    def advance(stream, stage, chunk):
        here = places[ORDERS[stream][stage]]
        slot, landing = chunk % 2, chunk % 4
        transfer(stream, stage, chunk, source_of(stream, stage, chunk)).wait()
        if stage == 1:
            total = add(sums[stream, slot, here], got_sums[stream, landing]).astype(bf16)
            halves[stream, slot] = total.reshape(halves.shape[2:])
        elif stage == 2:
            own = halves[stream, slot, :, here]
            quarters[stream, slot] = add(own, got_halves[stream, landing]).astype(bf16)
        else:
            total = add(quarters[stream, slot, here], got_quarters[stream, landing])
            finals[stream, slot] = total.reshape(finals.shape[2:])
        if stage < 3:
            transfer(stream, stage + 1, chunk, source_of(stream, stage + 1, chunk)).start()

    def hand_over(stream, chunk, waiting):
        for at in range(2):
            tile = 2 * chunk + at
            lanes = slice(at * LANES, (at + 1) * LANES)
            for ref, first, start, stop in places_out[stream]:

                @pl.when((tile >= start) & (tile < stop))
                def _(at=at, tile=tile, lanes=lanes, ref=ref, first=first, start=start):
                    target = ref.at[:, columns(first + tile - start)]
                    source = finals.at[stream, chunk % 2, 1 - core, :, lanes]
                    copy = transfer(stream, 4 + at, chunk, source, target)
                    if waiting:
                        copy.wait()
                    else:
                        target[...] = finals[stream, chunk % 2, core, :, lanes]
                        copy.start()

    @pl.loop(0, count + 5)
    def _(step):
        for stream in range(2):
            total = parts[stream][-1][3]

            @pl.when(step < total)
            def _(stream=stream):
                begin(stream, step)

        for stage in range(5):
            for stream in range(2):
                total = parts[stream][-1][3]

                @pl.when((step >= stage + 1) & (step < total + stage + 1))
                def _(stage=stage, stream=stream):
                    chunk = step - stage - 1
                    if stage == 0:
                        second(stream, chunk)
                    elif stage < 4:
                        advance(stream, stage, chunk)
                    else:
                        hand_over(stream, chunk, True)
                    if stage == 3:
                        hand_over(stream, chunk, False)


def reduced(down_a, gate, down_b, up, last_a, last_b, small, owned):
    block, rows = D // 4, D // 16
    dma = pltpu.SemaphoreType.DMA
    last_a, last_b, small = (last.reshape(2, 2, block, -1) for last in (last_a, last_b, small))
    widths = (2 * CORES * QC, CORES * VC, CORES * VC, 2 * CORES * FC, CORES * FC, CORES * LANES)
    return pl.pallas_call(
        reduce_kernel,
        out_shape=[jax.ShapeDtypeStruct((owned, width), f32) for width in widths],
        in_specs=[pl.BlockSpec(memory_space=pltpu.VMEM)] * 7,
        out_specs=[pl.BlockSpec(memory_space=pltpu.VMEM)] * 6,
        scratch_shapes=[
            pltpu.VMEM((2, 2, 2, block, WIDE), bf16),
            pltpu.VMEM((2, 2, 2, 2, rows, WIDE), bf16),
            pltpu.VMEM((2, 2, 2, rows, WIDE), bf16),
            pltpu.VMEM((2, 2, CORES, owned, WIDE), f32),
            pltpu.VMEM((2, 4, 2, block, WIDE), bf16),
            pltpu.VMEM((2, 4, block, WIDE), bf16),
            pltpu.VMEM((2, 4, 2, rows, WIDE), bf16),
            pltpu.VMEM((2, 4, rows, WIDE), bf16),
            dma((2, 6, 4)),
            dma((2, 6, 4)),
        ],
        compiler_params=pltpu.CompilerParams(
            collective_id=0, has_side_effects=True, vmem_limit_bytes=56 << 20
        ),
        cost_estimate=pl.CostEstimate(flops=0, bytes_accessed=1024, transcendentals=0),
    )(down_a, gate, down_b, up, last_a, last_b, small)


def places_of():
    y, x, z, core = (lax.axis_index(axis) for axis in ("y", "x", "z", "core"))
    return y, x, z, core


def greet(y, x, z, core, both_cores=False):
    barrier = pltpu.get_barrier_semaphore()
    partners = ORDERS[0] + (("core",) if both_cores else ())
    for axis in partners:
        pl.semaphore_signal(
            barrier,
            inc=1,
            device_id=mesh_exchange(y, x, z, core, axis),
            device_id_type=pl.DeviceIdType.MESH,
        )
    pl.semaphore_wait(barrier, len(partners))


GATHER_ORDERS = (("z1", "z0", "x", "y"), ("z1", "z0", "y", "x"), ("x", "y", "z1", "z0"))


def gather_view(ref, order, stage, y, x, z):
    if stage == 0:
        return ref.at[y, x, z // 2, z % 2]
    if order == 2:
        if stage == 1:
            return ref.at[y, :, z // 2, z % 2]
        return ref.at[:, :, z // 2, z % 2] if stage == 2 else ref.at[:, :, :, z % 2]
    if stage == 1:
        return ref.at[y, x, :, z % 2]
    if stage == 2:
        return ref.at[y, x]
    return ref.at[y] if order == 0 else ref.at[:, x]


def gather_kernel(tiles, shard_ref, full_ref, send_sem, recv_sem):
    y, x, z, core = places_of()
    full_ref[y, x, z // 2, z % 2] = shard_ref[...]
    greet(y, x, z, core)

    def transfer(stage, tile, order):
        columns = pl.ds(pl.multiple_of(tile * LANES, LANES), LANES)
        view = gather_view(full_ref.at[:, :, :, :, :, columns], order, stage, y, x, z)
        return pltpu.make_async_remote_copy(
            src_ref=view,
            dst_ref=view,
            send_sem=send_sem.at[stage, tile],
            recv_sem=recv_sem.at[stage, tile],
            device_id=mesh_exchange(y, x, z, core, GATHER_ORDERS[order][stage]),
            device_id_type=pl.DeviceIdType.MESH,
        )

    pairs = (tiles + 1) // 2

    def each(step, behind, act):
        for order in range(2):
            tile = 2 * (step - behind) + order

            @pl.when((tile >= 0) & (tile < tiles))
            def _(tile=tile, order=order):
                act(tile, order)

    @pl.loop(0, pairs + 4)
    def _(step):
        each(step, 0, lambda tile, order: transfer(0, tile, order).start())
        for stage in range(4):

            def act(tile, order, stage=stage):
                transfer(stage, tile, order).wait()
                if stage < 3:
                    transfer(stage + 1, tile, order).start()

            each(step, stage + 1, act)


def gathered_rows(shard):
    rows, width = shard.shape
    tiles = width // LANES
    full = pl.pallas_call(
        functools.partial(gather_kernel, tiles),
        out_shape=jax.ShapeDtypeStruct((2, 2, 2, 2, rows, width), bf16),
        in_specs=[pl.BlockSpec(memory_space=pltpu.VMEM)],
        out_specs=pl.BlockSpec(memory_space=pltpu.VMEM),
        scratch_shapes=[
            pltpu.SemaphoreType.DMA((4, tiles)),
            pltpu.SemaphoreType.DMA((4, tiles)),
        ],
        compiler_params=pltpu.CompilerParams(
            collective_id=1, has_side_effects=True, vmem_limit_bytes=40 << 20
        ),
        cost_estimate=pl.CostEstimate(flops=0, bytes_accessed=1024, transcendentals=0),
    )(shard)
    return full.reshape(D, width)


SLOTS = 10
ACROSS = 3


def feed_forward_kernel(
    tiles,
    second_ref,
    grad_ref,
    shard_ref,
    early_ref,
    gate_send_ref,
    gate_keep_ref,
    up_send_ref,
    up_keep_ref,
    down_a_send_ref,
    down_a_keep_ref,
    down_b_send_ref,
    down_b_keep_ref,
    down_own_ref,
    down_other_ref,
    second_own_ref,
    second_other_ref,
    held,
    down_ref,
    grad_second_ref,
    second_t_ref,
    grad_t_ref,
    narrow,
    terms,
    send_sem,
    recv_sem,
    out_sem,
    terms_sem,
    early_sem,
):
    y, x, z, core = places_of()
    streamed = shard_ref.shape[0]
    ready = tiles - streamed
    paired = streamed - ACROSS
    before_across = (ready + paired) // 2 - 2
    count = (tiles + 1) // 2

    def pair_of(turn):
        within = turn - before_across
        between = jnp.where(within % 2 == 0, count - 2 + within // 2, before_across + within // 2)
        return jnp.where(within < 0, turn, between)

    def early_copies(pair):
        copies = []
        for at in range(2):
            for part in range(3):
                start = (part * ready + 2 * pair + at) * LANES
                copies.append(
                    pltpu.make_async_copy(
                        early_ref.at[:, :, :, :, :, start : start + LANES],
                        held.at[SLOTS - 2 + at, :, :, :, :, :, part * LANES : (part + 1) * LANES],
                        early_sem.at[at, part],
                    )
                )
        return copies

    if ready:
        for copy in early_copies(0):
            copy.start()
    down_ref[...] = jnp.zeros_like(down_ref)
    grad_second_ref[...] = jnp.zeros_like(grad_second_ref)
    greet(y, x, z, core)
    tokens = second_ref.shape[0]
    block = 512 if tokens % 512 == 0 else tokens

    def transfer(stage, tile, order):
        slot = SLOTS + tile if order == 2 else tile % SLOTS
        view = gather_view(held.at[slot], order, stage, y, x, z)
        return pltpu.make_async_remote_copy(
            src_ref=view,
            dst_ref=view,
            send_sem=send_sem.at[stage, slot],
            recv_sem=recv_sem.at[stage, slot],
            device_id=mesh_exchange(y, x, z, core, GATHER_ORDERS[order][stage]),
            device_id_type=pl.DeviceIdType.MESH,
        )


    def compute(slots):
        def both(part):
            lanes = slice(part * LANES, (part + 1) * LANES)
            return jnp.concatenate(
                [held[slot, :, :, :, :, :, lanes].reshape(D, LANES) for slot in slots], axis=1
            )

        @pl.loop(0, tokens // block)
        def _(at):
            rows = pl.ds(pl.multiple_of(at * block, block), block)
            gate = dot(second_ref[rows, :], both(0))
            upward = dot(second_ref[rows, :], both(1))
            grad_hidden = dot(grad_ref[rows, :], both(2))
            sigmoid_gate = 1.0 / (1.0 + jnp.exp(-gate))
            silu_gate = gate * sigmoid_gate
            narrow[rows, 2 * WIDE :] = (silu_gate * upward).astype(bf16)
            narrow[rows, WIDE : 2 * WIDE] = (grad_hidden * silu_gate).astype(bf16)
            narrow[rows, :WIDE] = (
                grad_hidden * upward * sigmoid_gate * (1.0 + gate * (1.0 - sigmoid_gate))
            ).astype(bf16)
            down_ref[rows, :] += dot_nt(narrow[rows, 2 * WIDE :], both(2))
            grad_second_ref[rows, :] += dot_nt(narrow[rows, :WIDE], both(0)) + dot_nt(
                narrow[rows, WIDE : 2 * WIDE], both(1)
            )

    quarter = D // 4

    def weight_terms(turn):
        slot = turn % 2

        @pl.loop(0, 4)
        def _(part):
            rows = pl.ds(pl.multiple_of(part * quarter, quarter), quarter)
            grads = dot(second_t_ref[rows, :], narrow[:, : 2 * WIDE])
            terms[slot, part // 2, part % 2, :, : 2 * WIDE] = grads.astype(bf16)
            down = dot(grad_t_ref[rows, :], narrow[:, 2 * WIDE :])
            terms[slot, part // 2, part % 2, :, 2 * WIDE :] = down.astype(bf16)

    def terms_copies(turn):
        slot, pair = turn % 2, pair_of(turn)
        gate, up = (gate_send_ref, gate_keep_ref), (up_send_ref, up_keep_ref)
        first, second = (down_a_send_ref, down_a_keep_ref), (down_b_send_ref, down_b_keep_ref)

        def apart(index, stream, refs, at):
            here = (y, x)[stream]
            columns = pl.ds(pl.multiple_of(at * WIDE, WIDE), WIDE)
            copies = []
            for way, (place, ref) in enumerate(zip((1 - here, here), refs)):
                source = terms.at[slot, :, :, :, index * WIDE : (index + 1) * WIDE]
                source = source.at[place] if stream == 0 else source.at[:, place]
                copies.append(
                    pltpu.make_async_copy(source, ref.at[:, :, columns], terms_sem.at[slot, index, way])
                )
            return copies

        split = (tiles + 1) // 4
        early = pair < split
        return (
            (None, apart(0, 0, gate, pair)),
            (None, apart(1, 1, up, pair)),
            (early, apart(2, 0, first, jnp.where(early, pair, 0))),
            (pair >= split, apart(2, 1, second, jnp.where(early, 0, pair - split))),
        )

    def all_copies(turn, act):
        for condition, copies in terms_copies(turn):
            if condition is None:
                for copy in copies:
                    act(copy)
            else:

                @pl.when(condition)
                def _(copies=copies):
                    for copy in copies:
                        act(copy)

    pairs = paired // 2

    def each(step, behind, act):
        for order in range(2):
            tile = 2 * (step - behind) + order

            @pl.when((tile >= 0) & (tile < paired))
            def _(tile=tile, order=order):
                act(tile, order)

    def send_on(stage):
        def act(tile, order):
            transfer(stage, tile, order).wait()
            transfer(stage + 1, tile, order).start()

        return act

    def work(slots, turn):
        compute(slots)

        @pl.when(turn >= 2)
        def _():
            all_copies(turn - 2, lambda copy: copy.wait())

        weight_terms(turn)
        all_copies(turn, lambda copy: copy.start())

    def begin(tile, order):
        held[tile % SLOTS, y, x, z // 2, z % 2] = shard_ref[tile]
        transfer(0, tile, order).start()

    def finish(pair):
        for order in range(2):
            transfer(3, 2 * pair + order, order).wait()
        slots = tuple((2 * pair + order) % SLOTS for order in range(2))
        turn = ready // 2 + pair
        work(slots, jnp.where(turn >= before_across, 2 * turn - before_across + 1, turn))

    def begin_across(tile):
        held[SLOTS + tile, y, x, z // 2, z % 2] = shard_ref[paired + tile]
        transfer(0, tile, 2).start()

    def advance_across(step):
        for tile in range(ACROSS):

            @pl.when(step == 2 * tile)
            def _(tile=tile):
                begin_across(tile)

            for stage in range(4):

                @pl.when(step == 2 * tile + stage + 1)
                def _(tile=tile, stage=stage):
                    transfer(stage, tile, 2).wait()
                    if stage < 3:
                        transfer(stage + 1, tile, 2).start()

    def on_early(pair):
        for copy in early_copies(pair):
            copy.wait()
        work((SLOTS - 2, SLOTS - 1), jnp.int32(pair))
        if 2 * pair + 2 < ready:
            for copy in early_copies(pair + 1):
                copy.start()

    @pl.loop(0, pairs + 4)
    def _(step):
        each(step, 2, send_on(1))
        each(step, 3, send_on(2))
        advance_across(step)
        for pair in range(ready // 2):

            @pl.when(step == 2 + pair)
            def _(pair=pair):
                on_early(pair)


        @pl.when(step >= 4)
        def _():
            finish(step - 4)

        @pl.when(step == pairs + 1)
        def _():
            work((SLOTS, SLOTS + 1), jnp.int32(before_across))

        @pl.when(step == pairs + 2)
        def _():
            held[2] = jnp.zeros(held.shape[1:], bf16)
            work((SLOTS + 2, 2), jnp.int32(before_across + 2))

        each(step, 1, send_on(0))
        each(step, 0, begin)

        @pl.when(step < 2)
        def _():
            rows = pl.ds(pl.multiple_of(step * (tokens // 2), tokens // 2), tokens // 2)
            second_t_ref[:, rows] = second_ref[rows, :].T
            grad_t_ref[:, rows] = grad_ref[rows, :].T

    @pl.loop(count - 2, count)
    def _(turn):
        all_copies(turn, lambda copy: copy.wait())

    half = tokens // 2
    copies = [
        pltpu.make_async_copy(source, target, out_sem.at[at])
        for at, (source, target) in enumerate(
            (
                (grad_second_ref.at[half:], second_other_ref),
                (grad_second_ref.at[:half], second_own_ref),
                (down_ref.at[half:], down_other_ref),
                (down_ref.at[:half], down_own_ref),
            )
        )
    ]
    for copy in copies:
        copy.start()
    for copy in copies:
        copy.wait()


EARLY = 4


def feed_forward(second, grad_result, shards, early):
    tokens = second.shape[0]
    rows, streamed = shards[0].shape[0], shards[0].shape[1] // LANES
    shard = jnp.stack([part.reshape(rows, streamed, LANES) for part in shards], axis=2)
    shard = jnp.transpose(shard, (1, 0, 2, 3)).reshape(streamed, rows, 3 * LANES)
    tiles = streamed + early.shape[-1] // (3 * LANES)
    down_a = (tiles + 1) // 2
    terms = [
        jax.ShapeDtypeStruct((2, D // 4, count * LANES), bf16)
        for count in (tiles + 1, tiles + 1, down_a, down_a)
        for _ in range(2)
    ]
    part = jax.ShapeDtypeStruct((tokens // 2, D), f32)
    dma = pltpu.SemaphoreType.DMA
    results = pl.pallas_call(
        functools.partial(feed_forward_kernel, tiles),
        out_shape=terms + [part] * 4,
        in_specs=[pl.BlockSpec(memory_space=pltpu.VMEM)] * 3 + [pl.BlockSpec(memory_space=pl.ANY)],
        out_specs=[pl.BlockSpec(memory_space=pl.ANY)] * 12,
        scratch_shapes=[
            pltpu.VMEM((SLOTS + ACROSS, 2, 2, 2, 2, rows, 3 * LANES), bf16),
            pltpu.VMEM((tokens, D), f32),
            pltpu.VMEM((tokens, D), f32),
            pltpu.VMEM((D, tokens), bf16),
            pltpu.VMEM((D, tokens), bf16),
            pltpu.VMEM((tokens, 3 * WIDE), bf16),
            pltpu.VMEM((2, 2, 2, D // 4, 3 * WIDE), bf16),
            dma((4, SLOTS + ACROSS)),
            dma((4, SLOTS + ACROSS)),
            dma((4,)),
            dma((2, 3, 2)),
            dma((2, 3)),
        ],
        compiler_params=pltpu.CompilerParams(
            collective_id=2, has_side_effects=True, vmem_limit_bytes=60 << 20
        ),
        cost_estimate=pl.CostEstimate(flops=0, bytes_accessed=1024, transcendentals=0),
    )(second, grad_result, shard, early)
    return list(zip(results[0:8:2], results[1:8:2])), results[8:]


def norm_scale(values):
    inverse = lax.rsqrt(jnp.mean(values * values, axis=-1, keepdims=True) + norm_epsilon)
    return (values * inverse, inverse)


def norm_backward(grad_normed, scaled, inverse, gain_row):
    grad_scaled = grad_normed * gain_row[None, :]
    grad_input = inverse * (
        grad_scaled - scaled * jnp.mean(grad_scaled * scaled, axis=-1, keepdims=True)
    )
    return (grad_input, jnp.sum(grad_normed * scaled, axis=0))


def adam_update(weight, gradient, first_moment, second_moment, learn_rate, decay_rate):
    first_new = beta_first * first_moment + (1.0 - beta_first) * gradient
    second_new = beta_second * second_moment + (1.0 - beta_second) * gradient * gradient
    first_hat = first_new / (1.0 - beta_first**STEP)
    second_hat = second_new / (1.0 - beta_second**STEP)
    new_weight = (
        weight
        - learn_rate * first_hat / (jnp.sqrt(second_hat) + adam_epsilon)
        - decay_rate * weight
    )
    return (new_weight, second_new)


def local(
    tokens,
    cotangent,
    lengths,
    w_qk,
    w_value,
    w_out,
    w_gu,
    w_down,
    small_params,
    m_qk,
    m_value,
    m_out,
    m_gu,
    m_down,
    m_small,
    v_qk,
    v_value,
    v_out,
    v_gu,
    v_down,
    v_small,
):
    slots, slot_rows, _ = tokens.shape
    owned = w_qk.shape[0]
    rows = slots * slot_rows
    core, z_at = lax.axis_index("core"), lax.axis_index("z")
    other = 1 - core
    first_core = core == 0

    def on_chip(array):
        return jnp.concatenate([array, swapped(array)], axis=0)

    def halves(array):
        return array.reshape(CORES, slots, slot_rows, -1)

    columns_of = [
        w_qk.astype(bf16).reshape(owned, 2, CORES, QC),
        w_value.astype(bf16).reshape(owned, 1, CORES, VC),
        w_out.astype(bf16).reshape(owned, 1, CORES, VC),
        w_gu.astype(bf16).reshape(owned, 2, CORES, FC),
        w_down.astype(bf16).reshape(owned, 1, CORES, FC),
    ]
    small_low = jnp.pad(small_params.astype(bf16), ((0, 0), (0, LANES - (KS + 2))))

    def shard(which, index):
        parts = [part_of(columns_of[i], 2, index).reshape(owned, -1) for i in which]
        return jnp.concatenate(parts, axis=1) if len(parts) > 1 else parts[0]

    def chip_shard(which, extra=None):
        mine, theirs = shard(which, core), shard(which, other)
        arrived = swapped(theirs if extra is None else jnp.concatenate([theirs, extra], axis=1))
        mine = mine if extra is None else jnp.concatenate([mine, extra], axis=1)
        return both_cores(mine, arrived, 0)

    attention_shard = chip_shard((0, 1), small_low)
    rest_shard = chip_shard((2, 3, 4))
    in_kernel = tuple(lax.axis_size(axis) for axis in ("y", "x", "z")) == (2, 2, 4)
    early_width = 2 * QC + VC + LANES
    half = early_width // 2
    cut = FC // 2 // LANES * LANES
    down_at = VC + 2 * FC
    own_tokens = tokens.reshape(rows, D)
    other_tokens = swapped(own_tokens)
    wide_part = 4 * LANES
    if in_kernel:
        full = gathered_rows(jnp.concatenate([attention_shard, rest_shard[:, :VC]], axis=1))
        starts, split = (VC, VC + FC, down_at), EARLY * LANES
        late_shards = [rest_shard[:, start + split : start + FC] for start in starts]
        early_shard = jnp.concatenate([rest_shard[:, start : start + split] for start in starts], axis=1)
        early, out_half = full[:, :early_width], full[:, early_width:]
        early_shard, small_full = tied(early_shard, full[:, early_width - LANES : early_width])
        early_tiles = lax.all_gather(early_shard, ("y", "x", "z"), axis=0)
        early_tiles = early_tiles.reshape(2, 2, 2, 2, rest_shard.shape[0], -1)
    else:
        early_a = Gather(attention_shard[:, :half], True)
        early_b = Gather(attention_shard[:, half:], False)
        early = jnp.concatenate([early_a.rest(), early_b.rest()], axis=1)

        def gathered(start, width):
            return lax.all_gather(rest_shard[:, start : start + width], ("y", "x", "z"), axis=0, tiled=True)

        out_half = gathered(0, VC)
        gate_full = gathered(VC, FC)
        up_full = gathered(VC + FC, FC)
        last_shard, early = tied(rest_shard[:, down_at:], early)
        down_a = Gather(last_shard[:, :cut], True)
        down_b = Gather(last_shard[:, cut:], False)
        down_full = jnp.concatenate([down_a.rest(), down_b.rest()], axis=1)
        small_full = early[:, early_width - LANES :]

    qk_full = early[:, : 2 * QC]
    value_full = early[:, 2 * QC : 2 * QC + VC]
    small_float = small_full[:, : KS + 2].astype(f32)
    out_full = both_cores(out_half, swapped(out_half), 1)
    gain_first, gain_second = small_float[:, KS], small_float[:, KS + 1]
    taps = [part_of(small_float[:, j].reshape(CORES, VC), 0, core) for j in range(KS)]

    inputs = tokens.reshape(rows, D).astype(f32)
    scaled_first, inverse_first = norm_scale(inputs)
    scaled_chip, _ = norm_scale(
        jnp.concatenate([own_tokens, other_tokens], axis=0).astype(f32)
    )
    normed_chip = (scaled_chip * gain_first[None, :]).astype(bf16)
    query_key = halves(dot(normed_chip, qk_full).astype(bf16))
    value_pre = halves(dot(normed_chip, value_full).astype(bf16))
    tail = value_pre[:, :, slot_rows - (KS - 1) :, :]
    from_chip = passed_along(part_of(tail, 0, other), "z", 1)
    from_core = part_of(tail, 0, core)
    earlier = jnp.stack(
        [jnp.where(first_core, from_chip, from_core), jnp.where(first_core, from_core, from_chip)]
    )
    extended = jnp.concatenate([earlier, value_pre], axis=2).astype(f32)

    def tap_rows(j):
        return extended[:, :, KS - 1 - j : KS - 1 - j + slot_rows, :]

    convolved = taps[0] * tap_rows(0)
    for j in range(1, KS):
        convolved = convolved + taps[j] * tap_rows(j)
    values = convolved.astype(bf16)

    index_np, scale_np = feature_tables()
    tables = (core.astype(jnp.int32).reshape(1), jnp.asarray(index_np), jnp.asarray(scale_np))
    q_spec, k_spec, v_spec = (LANES, 0), (LANES, 1), (VC,)
    call = functools.partial(per_slot, slots=slots, rows=slot_rows)
    unit = 2 * CORES * rows * HC * LANES * FEATS
    wide = [pltpu.VMEM((CORES * slot_rows, VC), f32)]
    if in_kernel:
        (before,) = linked(key_term, True, 3)(*tables[1:], query_key, values, slots=slots)
    else:
        (state_own,) = call(
            state_kernel, ins=[k_spec, v_spec], outs=[("state", f32)], scratch=[], flops=4 * unit
        )(*tables, query_key, values)
        before = chain(state_own, True)
    mixer, dens = call(
        forward_kernel,
        ins=[q_spec, k_spec, v_spec, "state"],
        outs=[(v_spec, bf16), ((LANES,), f32)],
        scratch=wide,
        flops=8 * unit,
    )(*tables, query_key, query_key, values, before)

    mixer_flat = mixer.reshape(CORES * rows, VC)
    mixer_theirs = swapped(mixer_flat)

    def beside(mine, theirs):
        whole = jnp.zeros((mine.shape[0], CORES * mine.shape[1]), mine.dtype)
        for index, part in ((core, mine), (other, theirs)):
            whole = lax.dynamic_update_slice_in_dim(whole, part, index * mine.shape[1], 1)
        return whole

    mixer_own = beside(mixer_flat[:rows], mixer_theirs[rows:])
    mixer_other = beside(mixer_flat[rows:], mixer_theirs[:rows])
    after_mixer = inputs + dot(mixer_own, out_full)
    scaled_second, inverse_second = norm_scale(after_mixer)
    second_low = (scaled_second * gain_second[None, :]).astype(bf16)
    second_chip = on_chip(second_low)

    half_at = jnp.where(first_core, jnp.arange(CORES), 1 - jnp.arange(CORES))
    positions = (z_at * CORES + half_at)[:, None] * slot_rows + jnp.arange(slot_rows)[None, :]
    valid_chip = positions[:, None, :] < lengths[None, :, None]
    valid_chip = valid_chip.astype(f32).reshape(CORES * rows, 1)
    valid = valid_chip[:rows]
    query_key, cotangent_late = lax.optimization_barrier((query_key, cotangent))
    cotangent_chip = on_chip(cotangent_late.reshape(rows, D))
    mixer, cotangent_chip = tied(mixer, cotangent_chip)
    grad_result_chip = (valid_chip * cotangent_chip.astype(f32)).astype(bf16)
    grad_result = valid * cotangent.reshape(rows, D).astype(f32)

    if in_kernel:
        ffn_terms, ffn_parts = feed_forward(
            second_chip, grad_result_chip, late_shards, early_tiles
        )
        down_own, down_other, second_own, second_other = ffn_parts
        grad_second = second_own + swapped(second_other)
        down_result = down_own + swapped(down_other)
        (send_gate, keep_gate), (send_up, keep_up), *down_pairs = ffn_terms
        (send_down_a, keep_down_a), (send_down_b, keep_down_b) = down_pairs
        got_gate, got_up = exchanged(send_gate, "y", 0), exchanged(send_up, "x", 0)
    else:
        gate = dot(second_chip, gate_full)
        upward = dot(second_chip, up_full)
        sigmoid_gate = jax.nn.sigmoid(gate)
        silu_gate = gate * sigmoid_gate
        hidden = (silu_gate * upward).astype(bf16)
        grad_hidden = dot(grad_result_chip, down_full)
        grad_upward = (grad_hidden * silu_gate).astype(bf16)
        grad_gate = (
            grad_hidden * upward * sigmoid_gate * (1.0 + gate * (1.0 - sigmoid_gate))
        ).astype(bf16)
        second_part = dot_nt(grad_gate, gate_full) + dot_nt(grad_upward, up_full)
        grad_second = second_part[:rows] + swapped(second_part[rows:])
        down_part = dot_nt(hidden, down_full)
        down_result = down_part[:rows] + swapped(down_part[rows:])
    layer_out = (valid * (after_mixer + down_result)).astype(bf16).reshape(tokens.shape)

    grad_after_norm, grad_gain_second = norm_backward(
        grad_second, scaled_second, inverse_second, gain_second
    )
    grad_after = grad_result + grad_after_norm
    grad_after_low = grad_after.astype(bf16)
    grad_mixer = dot_nt(grad_after_low, out_full).astype(bf16)

    def core_columns(array):
        mine, theirs = (
            lax.dynamic_slice_in_dim(array, index * VC, VC, axis=1) for index in (core, other)
        )
        return jnp.concatenate([mine, swapped(theirs)], axis=0)

    grad_mixer_chip = core_columns(grad_mixer)
    grad_after_chip = core_columns(grad_after_low)
    mixer_chip = lax.optimization_barrier(jnp.concatenate([mixer_own, mixer_other], axis=0))

    wide_spec = (HC * LANES,)
    if in_kernel:
        grad_num, from_later = linked(query_term, False, 4)(
            *tables[1:],
            query_key,
            halves(grad_mixer_chip),
            mixer,
            dens,
            slots=slots,
            extra=(jax.ShapeDtypeStruct((CORES, slots, slot_rows, HC * LANES), bf16),),
        )
    else:
        pulled, grad_num = call(
            pull_kernel,
            ins=[q_spec, v_spec, v_spec, (LANES,)],
            outs=[("state", f32), (wide_spec, bf16)],
            scratch=[],
            flops=4 * unit,
        )(*tables, query_key, halves(grad_mixer_chip), mixer, dens)
        from_later = chain(pulled, False)
    grad_query_key, grad_values = call(
        backward_kernel,
        ins=[q_spec, k_spec, v_spec, wide_spec, "state", "state"],
        outs=[((2 * LANES,), bf16), (v_spec, bf16)],
        scratch=wide,
        flops=24 * unit,
    )(*tables, query_key, query_key, values, grad_num, before, from_later)

    if in_kernel:
        got_gate, got_up, send_down_a, send_down_b, grad_values = tied(
            got_gate, got_up, send_down_a, send_down_b, grad_values
        )

        def summed(keep, got):
            return (keep.astype(f32) + got.astype(f32)).astype(bf16)

        sum_gate, sum_up = summed(keep_gate, got_gate), summed(keep_up, got_up)
        sum_down_a = summed(keep_down_a, exchanged(send_down_a, "y", 0))
        sum_down_b = summed(keep_down_b, exchanged(send_down_b, "x", 0))
    head = grad_values[:, :, : KS - 1, :]
    from_chip = passed_along(part_of(head, 0, core), "z", -1)
    from_core = part_of(head, 0, other)
    later = jnp.stack(
        [jnp.where(first_core, from_core, from_chip), jnp.where(first_core, from_chip, from_core)]
    )
    grad_extended = jnp.concatenate([grad_values, later], axis=2).astype(f32)
    grad_pre = taps[0] * grad_extended[:, :, :slot_rows, :]
    for j in range(1, KS):
        grad_pre = grad_pre + taps[j] * grad_extended[:, :, j : j + slot_rows, :]
    grad_pre = grad_pre.reshape(CORES * rows, VC).astype(bf16)
    grad_query_key = grad_query_key.reshape(CORES * rows, 2 * QC)
    grad_values_float = grad_values.astype(f32)
    tap_grads = [jnp.sum(grad_values_float * tap_rows(j), axis=(0, 1, 2)) for j in range(KS)]

    first_other = dot_nt(grad_query_key[rows:], qk_full) + dot_nt(grad_pre[rows:], value_full)
    first_own = dot_nt(grad_query_key[:rows], qk_full) + dot_nt(grad_pre[:rows], value_full)
    grad_first = first_own + swapped(first_other)
    grad_gain_first = jnp.sum(first_own * scaled_chip[:rows], axis=0) + jnp.sum(
        first_other * scaled_chip[rows:], axis=0
    )

    def whole_feature(part):
        return lax.dynamic_update_slice(jnp.zeros((D,), f32), part, (core * VC,))

    small_terms = jnp.stack(
        [whole_feature(part) for part in tap_grads] + [grad_gain_first, grad_gain_second], axis=1
    )
    small_terms = jnp.pad(small_terms, ((0, 0), (0, LANES - (KS + 2)))).astype(bf16)
    if in_kernel:
        empty = jnp.zeros((CORES * rows, LANES), bf16)
        last_a = jnp.concatenate([grad_pre, grad_query_key, empty], axis=1)
        last_b = jnp.concatenate([grad_after_chip, empty], axis=1)
        grad_qk_own, grad_value_own, grad_out_own, grad_gu_own, grad_down_own, small_both = reduced(
            sum_down_a,
            sum_gate,
            sum_down_b,
            sum_up,
            dot_tn(normed_chip, last_a).astype(bf16),
            dot_tn(mixer_chip, last_b).astype(bf16),
            jnp.pad(small_terms, ((0, 0), (0, LANES))),
            owned,
        )
        grad_small_own = (small_both[:, :LANES] + small_both[:, LANES:])[:, : KS + 2]
    else:
        sum_down = Scatter(dot_tn(grad_result_chip, hidden).astype(bf16), True).rest()
        sum_gate = Scatter(dot_tn(second_chip, grad_gate).astype(bf16), False).rest()
        sum_up = Scatter(dot_tn(second_chip, grad_upward).astype(bf16), True).rest()
        sum_value = Scatter(dot_tn(normed_chip, grad_pre).astype(bf16), False).rest()
        sum_out = Scatter(dot_tn(mixer_chip, grad_after_chip).astype(bf16), True).rest()
        qk_terms = dot_tn(normed_chip, grad_query_key).astype(bf16)
        sum_last = Scatter(jnp.concatenate([qk_terms, small_terms], axis=1), True).rest()
    grad_input_norm, _ = norm_backward(grad_first, scaled_first, inverse_first, gain_first)
    input_grad = (grad_after + grad_input_norm).reshape(tokens.shape)

    def rows_of(array, index):
        return part_of(array.reshape(CORES, owned, -1), 0, index)

    def finish(*parts):
        merged = jnp.concatenate(parts, axis=1) if len(parts) > 1 else parts[0]
        mine, theirs = rows_of(merged, core), swapped(rows_of(merged, other))
        return mine.astype(f32), theirs.astype(f32)

    def columns(*parts):
        mine, theirs = finish(*parts)
        return both_cores(mine, theirs, 1)

    def two_columns(mine, theirs, width):
        shape = (owned, 2, 1, width)
        return both_cores(mine.reshape(shape), theirs.reshape(shape), 2).reshape(owned, -1)

    if not in_kernel:
        grad_down_own = columns(sum_down)
        grad_gu_own = two_columns(*finish(sum_gate, sum_up), FC)
        grad_out_own = columns(sum_out)
        grad_value_own = columns(sum_value)
        last_mine, last_theirs = finish(sum_last)
        grad_qk_own = two_columns(last_mine[:, : 2 * QC], last_theirs[:, : 2 * QC], QC)
        grad_small_own = (last_mine + last_theirs)[:, 2 * QC : 2 * QC + KS + 2]

    grads_all = (
        grad_qk_own,
        grad_value_own,
        grad_out_own,
        grad_gu_own,
        grad_down_own,
        grad_small_own,
    )
    masters = (w_qk, w_value, w_out, w_gu, w_down, small_params)
    firsts = (m_qk, m_value, m_out, m_gu, m_down, m_small)
    seconds = (v_qk, v_value, v_out, v_gu, v_down, v_small)
    learn_rates = (
        0.05 / math.sqrt(D),
        0.05 / math.sqrt(D),
        0.05 / math.sqrt(max(D // 128, 1)),
        0.05 / math.sqrt(D),
        0.05 / math.sqrt(0.0003 * FF * SLOT**0.825),
        0.014,
    )
    decays = (weight_decay, weight_decay, weight_decay, weight_decay, weight_decay, 0.0)
    new_weights = []
    new_seconds = []
    for position in range(6):
        updated, moment = adam_update(
            masters[position],
            grads_all[position],
            firsts[position],
            seconds[position],
            learn_rates[position],
            decays[position],
        )
        new_weights.append(updated)
        new_seconds.append(moment)
    return (layer_out, input_grad) + grads_all + tuple(new_weights) + tuple(new_seconds)


def solution(mesh):
    dp, fsdp = mesh.shape["dp"], mesh.shape["fsdp"]
    y_size = 2 if dp % 2 == 0 else 1
    split = Mesh(
        mesh.devices.reshape(y_size, dp // y_size, fsdp // CORES, CORES), ("y", "x", "z", "core")
    )
    slot_axes, row_axes = ("y", "x"), ("z", "core")
    activation = P(slot_axes, row_axes, None)
    weight = P(slot_axes + row_axes, None)
    return jax.shard_map(
        local,
        mesh=split,
        in_specs=(activation, activation, P(slot_axes)) + (weight,) * 18,
        out_specs=(activation, activation) + (weight,) * 18,
        check_vma=False,
    )
```

```python
import functools
import math

import jax
import jax.numpy as jnp
import numpy as np
from jax import lax
from jax.experimental import pallas as pl
from jax.experimental.pallas import tpu as pltpu
from jax.sharding import Mesh
from jax.sharding import PartitionSpec as P

D = 1792
H = 16
F = 16
FF = 4864
KS = 3
SLOT = 2048
STEP = 10

CORES = 2
HC = H // CORES
HW = D // H
VC = HC * HW
QC = HC * F
FC = FF // CORES
LANES = 128
FEATS = 256
FROWS = 160
SCALE = 1.0 / math.sqrt(F)

norm_epsilon = 1e-06
beta_first = 0.9
beta_second = 0.95
adam_epsilon = 1e-08
weight_decay = 3e-05

bf16 = jnp.bfloat16
f32 = jnp.float32


def feature_tables():
    index = np.full((8, FEATS), -4096, np.int32)
    scale = np.zeros((8, FEATS), np.float32)
    scale[0, 0] = scale[1, 0] = scale[2, 0] = 1.0
    at = 1
    for i in range(F):
        index[0, at] = i
        scale[1, at] = 1.0
        scale[2, at] = SCALE
        at += 1
    for i in range(F):
        for j in range(i, F):
            index[0, at] = i
            index[1, at] = j
            scale[2, at] = (1.0 if i == j else 2.0) * 0.5 * SCALE * SCALE
            at += 1
    return index, scale


def dot(a, b):
    return lax.dot_general(a, b, (((1,), (0,)), ((), ())), preferred_element_type=f32)


def dot_nt(a, b):
    return lax.dot_general(a, b, (((1,), (1,)), ((), ())), preferred_element_type=f32)


def dot_tn(a, b):
    return lax.dot_general(a, b, (((0,), (0,)), ((), ())), preferred_element_type=f32)


def selectors(index_ref, head):
    lane = lax.broadcasted_iota(jnp.int32, (LANES, FEATS), 0) - head * F
    first = jnp.where(lane == index_ref[0:1, :], 1.0, 0.0).astype(bf16)
    second = jnp.where(lane == index_ref[1:2, :], 1.0, 0.0).astype(bf16)
    return first, second


def factors(rows, first, second, scale_ref):
    return (dot(rows, first) + scale_ref[0:1, :], dot(rows, second) + scale_ref[1:2, :])


def window(head):
    start = head * HW
    base = min(start // LANES * LANES, VC - 2 * LANES)
    return base, start - base


def both_halves(core_ref, ref, columns):
    core = core_ref[0]
    return jnp.concatenate([ref[core, :, columns], ref[1 - core, :, columns]], axis=0)


def store_halves(core_ref, ref, rows, columns):
    core, half = core_ref[0], rows.shape[0] // CORES
    ref[core, :, columns] = rows[:half]
    ref[1 - core, :, columns] = rows[half:]


def head_columns(core_ref, ref, head):
    base, offset = window(head)
    wide = both_halves(core_ref, ref, slice(base, base + 2 * LANES)).astype(f32)
    if offset:
        wide = pltpu.roll(wide, 2 * LANES - offset, 1)
    return wide[:, :LANES]


def add_head_columns(ref, head, block):
    base, offset = window(head)
    wide = jnp.concatenate([block, jnp.zeros_like(block)], axis=1)
    if offset:
        wide = pltpu.roll(wide, offset, 1)
    ref[:, base : base + 2 * LANES] += wide


def with_one(block):
    lane = lax.broadcasted_iota(jnp.int32, block.shape, 1)
    return jnp.where(lane < HW, block, jnp.where(lane == HW, 1.0, 0.0))


def only_head(rows, head):
    lane = lax.broadcasted_iota(jnp.int32, rows.shape, 1)
    inside = (lane >= head * F) & (lane < head * F + F)
    return jnp.where(inside, rows.astype(f32), 0.0).astype(bf16)


def state_kernel(core_ref, index_ref, scale_ref, k_ref, v_ref, state_ref):
    keys = both_halves(core_ref, k_ref, slice(None))
    for head in range(HC):
        first, second = selectors(index_ref, head)
        one, two = factors(keys, first, second, scale_ref)
        phi = (one * two * scale_ref[2:3, :]).astype(bf16)
        values = with_one(head_columns(core_ref, v_ref, head)).astype(bf16)
        state_ref[0, head] = dot_tn(phi, values)[:FROWS]


def scores_of(q_head, keys):
    scores = dot_nt(q_head, keys) * SCALE
    row = lax.broadcasted_iota(jnp.int32, scores.shape, 0)
    column = lax.broadcasted_iota(jnp.int32, scores.shape, 1)
    return scores, column <= row


def forward_kernel(core_ref, index_ref, scale_ref, q_ref, k_ref, v_ref, before_ref, mixer_ref, den_ref, wide):
    queries = both_halves(core_ref, q_ref, slice(None))
    keys = both_halves(core_ref, k_ref, slice(None))
    wide[...] = jnp.zeros_like(wide)
    lane = lax.broadcasted_iota(jnp.int32, (queries.shape[0], LANES), 1)
    dens = jnp.zeros((queries.shape[0], LANES), f32)
    for head in range(HC):
        first, second = selectors(index_ref, head)
        one, two = factors(queries, first, second, scale_ref)
        phi = (one * two).astype(bf16)
        values = with_one(head_columns(core_ref, v_ref, head)).astype(bf16)
        scores, allowed = scores_of(only_head(queries, head), keys)
        kernel = jnp.where(allowed, 1.0 + scores + 0.5 * scores * scores, 0.0).astype(bf16)
        total = dot(kernel, values) + dot(phi[:, :FROWS], before_ref[0, head])
        den = total[:, HW : HW + 1]
        add_head_columns(wide, head, jnp.where(lane < HW, total / den, 0.0))
        dens = jnp.where(lane == head, den, dens)
    store_halves(core_ref, mixer_ref, wide[...].astype(bf16), slice(None))
    store_halves(core_ref, den_ref, dens, slice(None))


def pull_kernel(core_ref, index_ref, scale_ref, q_ref, gm_ref, mixer_ref, den_ref, state_ref, gnum_ref):
    queries = both_halves(core_ref, q_ref, slice(None))
    lane = lax.broadcasted_iota(jnp.int32, (queries.shape[0], LANES), 1)
    dens = both_halves(core_ref, den_ref, slice(None))
    for head in range(HC):
        first, second = selectors(index_ref, head)
        one, two = factors(queries, first, second, scale_ref)
        phi = (one * two).astype(bf16)
        den = dens[:, head : head + 1]
        grad = jnp.where(lane < HW, head_columns(core_ref, gm_ref, head), 0.0)
        mixer = head_columns(core_ref, mixer_ref, head)
        pulled = -jnp.sum(grad * mixer, axis=1, keepdims=True)
        grad = (jnp.where(lane == HW, pulled, grad) / den).astype(bf16)
        store_halves(core_ref, gnum_ref, grad, slice(head * LANES, (head + 1) * LANES))
        state_ref[0, head] = dot_tn(phi, grad)[:FROWS]


def backward_kernel(
    core_ref, index_ref, scale_ref, q_ref, k_ref, v_ref, gnum_ref, before_ref, after_ref, gqk_ref, gv_ref, wide
):
    queries = both_halves(core_ref, q_ref, slice(None))
    keys = both_halves(core_ref, k_ref, slice(None))
    wide[...] = jnp.zeros_like(wide)
    lane = lax.broadcasted_iota(jnp.int32, (queries.shape[0], LANES), 1)
    grad_q = jnp.zeros((queries.shape[0], LANES), f32)
    grad_k = jnp.zeros((queries.shape[0], LANES), f32)
    for head in range(HC):
        first, second = selectors(index_ref, head)
        coef = scale_ref[2:3, :]
        q_one, q_two = factors(queries, first, second, scale_ref)
        k_one, k_two = factors(keys, first, second, scale_ref)
        values = with_one(head_columns(core_ref, v_ref, head)).astype(bf16)
        gnum = both_halves(core_ref, gnum_ref, slice(head * LANES, (head + 1) * LANES))
        q_head = only_head(queries, head)
        k_head = only_head(keys, head)
        scores, allowed = scores_of(q_head, keys)
        kernel = jnp.where(allowed, 1.0 + scores + 0.5 * scores * scores, 0.0).astype(bf16)
        grad_kernel = dot_nt(gnum, values)
        grad_scores = (jnp.where(allowed, grad_kernel * (1.0 + scores), 0.0) * SCALE).astype(bf16)
        phi_k = (k_one * k_two * coef).astype(bf16)
        after = after_ref[0, head]
        before = before_ref[0, head]
        grad_v = dot_tn(kernel, gnum) + dot(phi_k[:, :FROWS], after)
        add_head_columns(wide, head, jnp.where(lane < HW, grad_v, 0.0))
        empty = jnp.zeros((FEATS - FROWS, LANES), bf16)
        grad_phi_q = dot_nt(gnum, jnp.concatenate([before, empty], axis=0))
        grad_phi_k = dot_nt(values, jnp.concatenate([after, empty], axis=0)) * coef
        grad_q += dot(grad_scores, k_head)
        grad_q += dot_nt((grad_phi_q * q_two).astype(bf16), first)
        grad_q += dot_nt((grad_phi_q * q_one).astype(bf16), second)
        grad_k += dot_tn(grad_scores, q_head)
        grad_k += dot_nt((grad_phi_k * k_two).astype(bf16), first)
        grad_k += dot_nt((grad_phi_k * k_one).astype(bf16), second)
    store_halves(core_ref, gqk_ref, grad_q.astype(bf16), slice(0, LANES))
    store_halves(core_ref, gqk_ref, grad_k.astype(bf16), slice(LANES, 2 * LANES))
    store_halves(core_ref, gv_ref, wide[...].astype(bf16), slice(None))


def per_slot(kernel, slots, rows, ins, outs, scratch, flops):
    def table():
        return pl.BlockSpec((8, FEATS), lambda s, core: (0, 0))

    def row_spec(width, column=0):
        return pl.BlockSpec((CORES, None, rows, width), lambda s, core: (0, s, 0, column))

    def state_spec():
        return pl.BlockSpec((1, HC, FROWS, LANES), lambda s, core: (s, 0, 0, 0))

    def spec(kind):
        return state_spec() if kind == "state" else row_spec(*kind)

    def shape(kind, dtype):
        if kind == "state":
            return jax.ShapeDtypeStruct((slots, HC, FROWS, LANES), dtype)
        return jax.ShapeDtypeStruct((CORES, slots, rows, kind[0]), dtype)

    return pl.pallas_call(
        kernel,
        grid_spec=pltpu.PrefetchScalarGridSpec(
            num_scalar_prefetch=1,
            grid=(slots,),
            in_specs=[table(), table()] + [spec(kind) for kind in ins],
            out_specs=[spec(kind) for kind, _ in outs],
            scratch_shapes=scratch,
        ),
        out_shape=[shape(kind, dtype) for kind, dtype in outs],
        compiler_params=pltpu.CompilerParams(vmem_limit_bytes=56 << 20),
        cost_estimate=pl.CostEstimate(flops=flops, bytes_accessed=8 << 20, transcendentals=0),
    )


def linked(kernel, up, ids):
    def run(*refs):
        y, x, z, core = places_of()
        last = lax.axis_size("z") - 1
        *refs, sent, send_sem, recv_sem = refs
        total_ref = refs[-1]
        by = 1 if up else last
        receives, sends = (z > 0, z < last) if up else (z < last, z > 0)

        barrier = pltpu.get_barrier_semaphore()
        for step in (1, last):
            pl.semaphore_signal(
                barrier,
                inc=1,
                device_id=(y, x, lax.rem(z + step, last + 1), core),
                device_id_type=pl.DeviceIdType.MESH,
            )
        pl.semaphore_wait(barrier, 2)

        def transfer(slot, head):
            return pltpu.make_async_remote_copy(
                src_ref=sent.at[slot, head],
                dst_ref=total_ref.at[slot, head],
                send_sem=send_sem.at[slot, head],
                recv_sem=recv_sem.at[slot, head],
                device_id=(y, x, lax.rem(z + by, last + 1), core),
                device_id_type=pl.DeviceIdType.MESH,
            )

        @pl.when(jnp.logical_not(receives))
        def _():
            total_ref[...] = jnp.zeros_like(total_ref)

        @pl.loop(0, sent.shape[0])
        def _(slot):
            for head in range(HC):
                term = kernel([core], slot, head, *refs[:-1])

                @pl.when(receives)
                def _(head=head):
                    transfer(slot, head).wait_recv()

                @pl.when(sends)
                def _(head=head, term=term):
                    sent[slot, head] = (total_ref[slot, head].astype(f32) + term).astype(bf16)
                    transfer(slot, head).start()

        @pl.when(sends)
        def _():
            @pl.loop(0, sent.shape[0])
            def _(slot):
                for head in range(HC):
                    transfer(slot, head).wait_send()

    def call(*operands, slots, extra=()):
        state = jax.ShapeDtypeStruct((slots, HC, FROWS, LANES), bf16)
        vmem = pl.BlockSpec(memory_space=pltpu.VMEM)
        return pl.pallas_call(
            run,
            out_shape=list(extra) + [state],
            in_specs=[vmem] * len(operands),
            out_specs=[vmem] * (len(extra) + 1),
            scratch_shapes=[
                pltpu.VMEM((slots, HC, FROWS, LANES), bf16),
                pltpu.SemaphoreType.DMA((slots, HC)),
                pltpu.SemaphoreType.DMA((slots, HC)),
            ],
            compiler_params=pltpu.CompilerParams(
                collective_id=ids, has_side_effects=True, vmem_limit_bytes=40 << 20
            ),
            cost_estimate=pl.CostEstimate(flops=0, bytes_accessed=1024, transcendentals=0),
        )(*operands)

    return call


def key_term(core_ref, slot, head, index_ref, scale_ref, qk_ref, v_ref):
    keys = both_halves(core_ref, qk_ref.at[:, slot], slice(LANES, 2 * LANES))
    first, second = selectors(index_ref, head)
    one, two = factors(keys, first, second, scale_ref)
    phi = (one * two * scale_ref[2:3, :]).astype(bf16)
    values = with_one(head_columns(core_ref, v_ref.at[:, slot], head)).astype(bf16)
    return dot_tn(phi, values)[:FROWS]


def query_term(core_ref, slot, head, index_ref, scale_ref, qk_ref, gm_ref, mixer_ref, den_ref, gnum_ref):
    queries = both_halves(core_ref, qk_ref.at[:, slot], slice(0, LANES))
    first, second = selectors(index_ref, head)
    one, two = factors(queries, first, second, scale_ref)
    phi = (one * two).astype(bf16)
    den = both_halves(core_ref, den_ref.at[:, slot], slice(None))[:, head : head + 1]
    lane = lax.broadcasted_iota(jnp.int32, (queries.shape[0], LANES), 1)
    grad = jnp.where(lane < HW, head_columns(core_ref, gm_ref.at[:, slot], head), 0.0)
    mixer = head_columns(core_ref, mixer_ref.at[:, slot], head)
    pulled = -jnp.sum(grad * mixer, axis=1, keepdims=True)
    grad = (jnp.where(lane == HW, pulled, grad) / den).astype(bf16)
    store_halves(core_ref, gnum_ref.at[:, slot], grad, slice(head * LANES, (head + 1) * LANES))
    return dot_tn(phi, grad)[:FROWS]


def passed_along(array, axis, by):
    count = lax.axis_size(axis)
    pairs = [(i, i + by) for i in range(count) if 0 <= i + by < count]
    return lax.ppermute(array, axis, pairs)


def both_cores(mine, theirs, axis):
    first = lax.axis_index("core") == 0
    return jnp.concatenate(
        [jnp.where(first, mine, theirs), jnp.where(first, theirs, mine)], axis=axis
    )


def swapped(array):
    return lax.ppermute(array, "core", [(0, 1), (1, 0)])


def part_of(array, axis, index):
    return lax.dynamic_index_in_dim(array, index, axis, keepdims=False)


def bits_of(axis):
    return [(axis, bit) for bit in reversed(range(lax.axis_size(axis).bit_length() - 1))]


def bit_at(axis, bit):
    return (lax.axis_index(axis) >> bit) & 1


def exchanged(array, axis, bit):
    count = lax.axis_size(axis)
    return lax.ppermute(array, axis, [(i, i ^ (1 << bit)) for i in range(count)])


def tied(*arrays):
    return lax.optimization_barrier(arrays)


class Gather:
    def __init__(self, piece, x_first):
        self.columns = piece.shape[1]
        self.block = piece
        low_first = lambda axis: bits_of(axis)[::-1]
        self.plan = [(step, at) for at, step in enumerate(bits_of("z"))]
        if x_first:
            self.plan += [(step, 0) for step in low_first("x") + low_first("y")]
        else:
            self.plan += [(step, 0) for step in low_first("y")]
            self.plan += [(step, len(bits_of("y"))) for step in low_first("x")]

    def stage(self):
        (axis, bit), dim = self.plan.pop(0)
        mine = bit_at(axis, bit)
        arrived = exchanged(self.block, axis, bit)
        shape = self.block.shape[:dim] + (2,) + self.block.shape[dim:]
        whole = jnp.zeros(shape, self.block.dtype)
        whole = lax.dynamic_update_index_in_dim(whole, self.block, mine, dim)
        self.block = lax.dynamic_update_index_in_dim(whole, arrived, 1 - mine, dim)
        return self

    def along_z(self):
        while self.plan[0][0][0] == "z":
            self.stage()
        return self

    def rest(self):
        while self.plan:
            self.stage()
        return self.block.reshape(D, self.columns)


class Scatter:
    def __init__(self, terms, x_first):
        self.dims = bits_of("y") + bits_of("x") + bits_of("z")
        order = ("x", "y") if x_first else ("y", "x")
        self.plan = bits_of(order[0]) + bits_of(order[1]) + bits_of("z")[::-1]
        rows = D >> len(self.dims)
        self.terms = [terms.reshape((2,) * len(self.dims) + (rows, terms.shape[1]))]

    def total(self, terms):
        total = terms[0].astype(f32)
        for term in terms[1:]:
            total = total + term.astype(f32)
        return total

    def stage(self):
        step = self.plan.pop(0)
        dim, mine = self.dims.index(step), bit_at(*step)
        self.dims.remove(step)
        sent = self.total([part_of(term, dim, 1 - mine) for term in self.terms]).astype(bf16)
        self.terms = [part_of(term, dim, mine) for term in self.terms]
        self.terms.append(exchanged(sent, *step))
        return self

    def rest(self):
        while self.plan:
            self.stage()
        return self.total(self.terms)


def chain(local, up):
    count = lax.axis_size("z")
    total = jnp.zeros_like(local)
    for hop in range(1, count):
        pair = (hop - 1, hop) if up else (count - hop, count - hop - 1)
        message = (total + local).astype(bf16)
        total = total + lax.ppermute(message, "z", [pair]).astype(f32)
    return total.astype(bf16)


def mesh_exchange(y, x, z, core, axis):
    if axis == "core":
        return (y, x, z, 1 - core)
    if axis == "y":
        return (1 - y, x, z, core)
    if axis == "x":
        return (y, 1 - x, z, core)
    if axis == "z0":
        return (y, x, z + 1 - 2 * (z % 2), core)
    return (y, x, (z + 2) % 4, core)


ORDERS = (("y", "x", "z0", "z1"), ("x", "y", "z0", "z1"))


WIDE = 2 * LANES


def reduce_kernel(
    down_a_ref,
    gate_ref,
    down_b_ref,
    up_ref,
    last_a_ref,
    last_b_ref,
    small_terms_ref,
    qk_ref,
    value_ref,
    out_ref,
    gu_ref,
    down_ref,
    small_ref,
    sums,
    halves,
    quarters,
    finals,
    got_terms,
    got_sums,
    got_halves,
    got_quarters,
    send_sem,
    recv_sem,
):
    y, x, z, core = places_of()
    places = {"y": y, "x": x, "z0": z % 2, "z1": z // 2}

    parts, count = ([], []), 0
    all_refs = (
        (down_a_ref, gate_ref, last_a_ref),
        (down_b_ref, up_ref, last_b_ref, small_terms_ref),
    )
    for stream, refs in enumerate(all_refs):
        at = 0
        for ref in refs:
            chunks = ref.shape[-1] // WIDE
            parts[stream].append((ref, len(ref.shape) == 3, at, at + chunks))
            at += chunks
        count = max(count, at)
    hidden, width = FC // LANES, VC // LANES
    down_a = (hidden + 1) // 2
    down_b = hidden - down_a
    gate_at, last_a = 2 * parts[0][1][2], 2 * parts[0][2][2]
    up_at, last_b, small_at = (2 * parts[1][at][2] for at in (1, 2, 3))
    places_out = (
        (
            (down_ref, core * hidden, 0, down_a),
            (gu_ref, core * hidden, gate_at, gate_at + hidden),
            (value_ref, core * width, last_a, last_a + width),
            (qk_ref, core, last_a + width, last_a + width + 1),
            (qk_ref, CORES + core, last_a + width + 1, last_a + width + 2),
        ),
        (
            (down_ref, core * hidden + down_a, 0, down_b),
            (gu_ref, (CORES + core) * hidden, up_at, up_at + hidden),
            (out_ref, core * width, last_b, last_b + width),
            (small_ref, core, small_at, small_at + 1),
        ),
    )
    greet(y, x, z, core, True)

    def columns(tile):
        return pl.ds(pl.multiple_of(tile * LANES, LANES), LANES)

    def wide_columns(chunk):
        return pl.ds(pl.multiple_of(chunk * WIDE, WIDE), WIDE)

    def transfer(stream, stage, chunk, source, target=None):
        landing = chunk % 4
        if target is None:
            target = (got_terms, got_sums, got_halves, got_quarters)[stage].at[stream, landing]
        axis = (ORDERS[stream] + ("core", "core"))[stage]
        return pltpu.make_async_remote_copy(
            src_ref=source,
            dst_ref=target,
            send_sem=send_sem.at[stream, stage, landing],
            recv_sem=recv_sem.at[stream, stage, landing],
            device_id=mesh_exchange(y, x, z, core, axis),
            device_id_type=pl.DeviceIdType.MESH,
        )

    def first_view(stream, ref, tile, place):
        ref = ref.at[:, :, :, wide_columns(tile)]
        return ref.at[place] if stream == 0 else ref.at[:, place]

    def source_of(stream, stage, chunk):
        there = 1 - places[ORDERS[stream][stage]]
        if stage == 1:
            return sums.at[stream, chunk % 2, there]
        if stage == 2:
            return halves.at[stream, chunk % 2, :, there]
        return quarters.at[stream, chunk % 2, there]

    def add(a, b):
        return a.astype(f32) + b.astype(f32)

    def begin(stream, chunk):
        for ref, _, start, stop in parts[stream][2:]:

            @pl.when((chunk >= start) & (chunk < stop))
            def _(ref=ref, start=start):
                there = 1 - places[ORDERS[stream][0]]
                transfer(stream, 0, chunk, first_view(stream, ref, chunk - start, there)).start()

    def second(stream, chunk):
        for ref, summed, start, stop in parts[stream]:

            @pl.when((chunk >= start) & (chunk < stop))
            def _(ref=ref, summed=summed, start=start):
                tile = chunk - start
                if summed:
                    sums[stream, chunk % 2] = ref[:, :, wide_columns(tile)]
                else:
                    there = 1 - places[ORDERS[stream][0]]
                    transfer(stream, 0, chunk, first_view(stream, ref, tile, there)).wait()
                    own = first_view(stream, ref, tile, places[ORDERS[stream][0]])[...]
                    sums[stream, chunk % 2] = add(own, got_terms[stream, chunk % 4]).astype(bf16)

        transfer(stream, 1, chunk, source_of(stream, 1, chunk)).start()

    def advance(stream, stage, chunk):
        here = places[ORDERS[stream][stage]]
        slot, landing = chunk % 2, chunk % 4
        transfer(stream, stage, chunk, source_of(stream, stage, chunk)).wait()
        if stage == 1:
            total = add(sums[stream, slot, here], got_sums[stream, landing]).astype(bf16)
            halves[stream, slot] = total.reshape(halves.shape[2:])
        elif stage == 2:
            own = halves[stream, slot, :, here]
            quarters[stream, slot] = add(own, got_halves[stream, landing]).astype(bf16)
        else:
            total = add(quarters[stream, slot, here], got_quarters[stream, landing])
            finals[stream, slot] = total.reshape(finals.shape[2:])
        if stage < 3:
            transfer(stream, stage + 1, chunk, source_of(stream, stage + 1, chunk)).start()

    def hand_over(stream, chunk, waiting):
        for at in range(2):
            tile = 2 * chunk + at
            lanes = slice(at * LANES, (at + 1) * LANES)
            for ref, first, start, stop in places_out[stream]:

                @pl.when((tile >= start) & (tile < stop))
                def _(at=at, tile=tile, lanes=lanes, ref=ref, first=first, start=start):
                    target = ref.at[:, columns(first + tile - start)]
                    source = finals.at[stream, chunk % 2, 1 - core, :, lanes]
                    copy = transfer(stream, 4 + at, chunk, source, target)
                    if waiting:
                        copy.wait()
                    else:
                        target[...] = finals[stream, chunk % 2, core, :, lanes]
                        copy.start()

    @pl.loop(0, count + 5)
    def _(step):
        for stream in range(2):
            total = parts[stream][-1][3]

            @pl.when(step < total)
            def _(stream=stream):
                begin(stream, step)

        for stage in range(5):
            for stream in range(2):
                total = parts[stream][-1][3]

                @pl.when((step >= stage + 1) & (step < total + stage + 1))
                def _(stage=stage, stream=stream):
                    chunk = step - stage - 1
                    if stage == 0:
                        second(stream, chunk)
                    elif stage < 4:
                        advance(stream, stage, chunk)
                    else:
                        hand_over(stream, chunk, True)
                    if stage == 3:
                        hand_over(stream, chunk, False)


def reduced(down_a, gate, down_b, up, last_a, last_b, small, owned):
    block, rows = D // 4, D // 16
    dma = pltpu.SemaphoreType.DMA
    last_a, last_b, small = (last.reshape(2, 2, block, -1) for last in (last_a, last_b, small))
    widths = (2 * CORES * QC, CORES * VC, CORES * VC, 2 * CORES * FC, CORES * FC, CORES * LANES)
    return pl.pallas_call(
        reduce_kernel,
        out_shape=[jax.ShapeDtypeStruct((owned, width), f32) for width in widths],
        in_specs=[pl.BlockSpec(memory_space=pltpu.VMEM)] * 7,
        out_specs=[pl.BlockSpec(memory_space=pltpu.VMEM)] * 6,
        scratch_shapes=[
            pltpu.VMEM((2, 2, 2, block, WIDE), bf16),
            pltpu.VMEM((2, 2, 2, 2, rows, WIDE), bf16),
            pltpu.VMEM((2, 2, 2, rows, WIDE), bf16),
            pltpu.VMEM((2, 2, CORES, owned, WIDE), f32),
            pltpu.VMEM((2, 4, 2, block, WIDE), bf16),
            pltpu.VMEM((2, 4, block, WIDE), bf16),
            pltpu.VMEM((2, 4, 2, rows, WIDE), bf16),
            pltpu.VMEM((2, 4, rows, WIDE), bf16),
            dma((2, 6, 4)),
            dma((2, 6, 4)),
        ],
        compiler_params=pltpu.CompilerParams(
            collective_id=0, has_side_effects=True, vmem_limit_bytes=56 << 20
        ),
        cost_estimate=pl.CostEstimate(flops=0, bytes_accessed=1024, transcendentals=0),
    )(down_a, gate, down_b, up, last_a, last_b, small)


def places_of():
    y, x, z, core = (lax.axis_index(axis) for axis in ("y", "x", "z", "core"))
    return y, x, z, core


def greet(y, x, z, core, both_cores=False):
    barrier = pltpu.get_barrier_semaphore()
    partners = ORDERS[0] + (("core",) if both_cores else ())
    for axis in partners:
        pl.semaphore_signal(
            barrier,
            inc=1,
            device_id=mesh_exchange(y, x, z, core, axis),
            device_id_type=pl.DeviceIdType.MESH,
        )
    pl.semaphore_wait(barrier, len(partners))


GATHER_ORDERS = (("z1", "z0", "x", "y"), ("z1", "z0", "y", "x"), ("x", "y", "z1", "z0"))


def gather_view(ref, order, stage, y, x, z):
    if stage == 0:
        return ref.at[y, x, z // 2, z % 2]
    if order == 2:
        if stage == 1:
            return ref.at[y, :, z // 2, z % 2]
        return ref.at[:, :, z // 2, z % 2] if stage == 2 else ref.at[:, :, :, z % 2]
    if stage == 1:
        return ref.at[y, x, :, z % 2]
    if stage == 2:
        return ref.at[y, x]
    return ref.at[y] if order == 0 else ref.at[:, x]


ATTENTION = 2 * QC + 2 * VC + LANES


def gather_kernel(
    qk_ref,
    value_ref,
    out_ref,
    gu_ref,
    down_ref,
    small_ref,
    full_ref,
    late_ref,
    early_ref,
    merged,
    send_sem,
    recv_sem,
    core_send_sem,
    core_recv_sem,
    own_sem,
):
    y, x, z, core = places_of()
    owned = qk_ref.shape[0]
    greet(y, x, z, core, True)

    at, parts = 0, []
    for ref, start, width, apart in (
        (qk_ref, 0, QC, True),
        (qk_ref, CORES * QC, QC, True),
        (value_ref, 0, VC, True),
        (small_ref, 0, LANES, False),
        (out_ref, 0, VC, True),
        (gu_ref, 0, FC, True),
        (gu_ref, FF, FC, True),
        (down_ref, 0, FC, True),
    ):
        parts.append((ref, start, width, apart, at))
        at += width
    my_rows = pl.ds(pl.multiple_of(core * owned, 8), owned)

    def copies(index):
        ref, start, width, apart, at = parts[index]

        def source(which):
            first = pl.multiple_of(start + (which * width if apart else 0), LANES)
            return ref.at[:, pl.ds(first, width)]

        target = merged.at[my_rows, at : at + width]
        remote = pltpu.make_async_remote_copy(
            src_ref=source(1 - core),
            dst_ref=target,
            send_sem=core_send_sem.at[index],
            recv_sem=core_recv_sem.at[index],
            device_id=mesh_exchange(y, x, z, core, "core"),
            device_id_type=pl.DeviceIdType.MESH,
        )
        return remote, pltpu.make_async_copy(source(core), target, own_sem.at[index])

    for index in range(len(parts)):
        for copy in copies(index):
            copy.start()
    for index in range(5):
        for copy in copies(index):
            copy.wait()
    full_ref[y, x, z // 2, z % 2] = merged[:, :ATTENTION].astype(bf16)

    def transfer(stage, tile, order):
        columns = pl.ds(pl.multiple_of(tile * LANES, LANES), LANES)
        view = gather_view(full_ref.at[:, :, :, :, :, columns], order, stage, y, x, z)
        return pltpu.make_async_remote_copy(
            src_ref=view,
            dst_ref=view,
            send_sem=send_sem.at[stage, tile],
            recv_sem=recv_sem.at[stage, tile],
            device_id=mesh_exchange(y, x, z, core, GATHER_ORDERS[order][stage]),
            device_id_type=pl.DeviceIdType.MESH,
        )

    paired = ATTENTION // LANES - ACROSS
    pairs = paired // 2

    def each(step, behind, act):
        for order in range(2):
            tile = 2 * (step - behind) + order

            @pl.when((tile >= 0) & (tile < paired))
            def _(tile=tile, order=order):
                act(tile, order)

    def go_on(tile, order, stage):
        transfer(stage, tile, order).wait()
        if stage < 3:
            transfer(stage + 1, tile, order).start()

    hidden = FC // LANES

    @pl.loop(0, pairs + 4)
    def _(step):
        each(step, 0, lambda tile, order: transfer(0, tile, order).start())
        for stage in range(4):
            each(step, stage + 1, functools.partial(go_on, stage=stage))
        for across in range(ACROSS):

            @pl.when(step == 2 * across)
            def _(across=across):
                transfer(0, paired + across, 2).start()

            for stage in range(4):

                @pl.when(step == 2 * across + stage + 1)
                def _(across=across, stage=stage):
                    go_on(paired + across, 2, stage)

        @pl.when(step == 0)
        def _():
            for index in range(5, len(parts)):
                for copy in copies(index):
                    copy.wait()

        for tile in range(hidden):

            @pl.when(step == tile // 2)
            def _(tile=tile):
                for part in range(3):
                    first = ATTENTION + part * FC + tile * LANES
                    block = merged[:, first : first + LANES].astype(bf16)
                    if tile < EARLY:
                        start = (part * EARLY + tile) * LANES
                        early_ref[:, start : start + LANES] = block
                    else:
                        late_ref[tile - EARLY, :, part * LANES : (part + 1) * LANES] = block


def gathered_weights(w_qk, w_value, w_out, w_gu, w_down, small):
    owned = w_qk.shape[0]
    rows, tiles = CORES * owned, ATTENTION // LANES
    dma = pltpu.SemaphoreType.DMA
    vmem = pl.BlockSpec(memory_space=pltpu.VMEM)
    full, late, early = pl.pallas_call(
        gather_kernel,
        out_shape=[
            jax.ShapeDtypeStruct((2, 2, 2, 2, rows, ATTENTION), bf16),
            jax.ShapeDtypeStruct((FC // LANES - EARLY, rows, 3 * LANES), bf16),
            jax.ShapeDtypeStruct((rows, 3 * EARLY * LANES), bf16),
        ],
        in_specs=[vmem] * 6,
        out_specs=[vmem] * 3,
        scratch_shapes=[
            pltpu.VMEM((rows, ATTENTION + 3 * FC), f32),
            dma((4, tiles)),
            dma((4, tiles)),
            dma((8,)),
            dma((8,)),
            dma((8,)),
        ],
        compiler_params=pltpu.CompilerParams(
            collective_id=1, has_side_effects=True, vmem_limit_bytes=48 << 20
        ),
        cost_estimate=pl.CostEstimate(flops=0, bytes_accessed=1024, transcendentals=0),
    )(w_qk, w_value, w_out, w_gu, w_down, small)
    return full.reshape(D, ATTENTION), late, early


SLOTS = 10
ACROSS = 3


def feed_forward_kernel(
    tiles,
    second_ref,
    grad_ref,
    shard_ref,
    early_ref,
    gate_send_ref,
    gate_keep_ref,
    up_send_ref,
    up_keep_ref,
    down_a_send_ref,
    down_a_keep_ref,
    down_b_send_ref,
    down_b_keep_ref,
    down_own_ref,
    down_other_ref,
    second_own_ref,
    second_other_ref,
    held,
    down_ref,
    grad_second_ref,
    second_t_ref,
    grad_t_ref,
    narrow,
    terms,
    send_sem,
    recv_sem,
    out_sem,
    terms_sem,
    early_sem,
):
    y, x, z, core = places_of()
    streamed = shard_ref.shape[0]
    ready = tiles - streamed
    paired = streamed - ACROSS
    before_across = (ready + paired) // 2 - 2
    count = (tiles + 1) // 2

    def pair_of(turn):
        within = turn - before_across
        between = jnp.where(within % 2 == 0, count - 2 + within // 2, before_across + within // 2)
        return jnp.where(within < 0, turn, between)

    def early_copies(pair):
        copies = []
        for at in range(2):
            for part in range(3):
                start = (part * ready + 2 * pair + at) * LANES
                copies.append(
                    pltpu.make_async_copy(
                        early_ref.at[:, :, :, :, :, start : start + LANES],
                        held.at[SLOTS - 2 + at, :, :, :, :, :, part * LANES : (part + 1) * LANES],
                        early_sem.at[at, part],
                    )
                )
        return copies

    if ready:
        for copy in early_copies(0):
            copy.start()
    down_ref[...] = jnp.zeros_like(down_ref)
    grad_second_ref[...] = jnp.zeros_like(grad_second_ref)
    greet(y, x, z, core)
    tokens = second_ref.shape[0]
    block = 512 if tokens % 512 == 0 else tokens

    def transfer(stage, tile, order):
        slot = SLOTS + tile if order == 2 else tile % SLOTS
        view = gather_view(held.at[slot], order, stage, y, x, z)
        return pltpu.make_async_remote_copy(
            src_ref=view,
            dst_ref=view,
            send_sem=send_sem.at[stage, slot],
            recv_sem=recv_sem.at[stage, slot],
            device_id=mesh_exchange(y, x, z, core, GATHER_ORDERS[order][stage]),
            device_id_type=pl.DeviceIdType.MESH,
        )


    def compute(slots):
        def both(part):
            lanes = slice(part * LANES, (part + 1) * LANES)
            return jnp.concatenate(
                [held[slot, :, :, :, :, :, lanes].reshape(D, LANES) for slot in slots], axis=1
            )

        @pl.loop(0, tokens // block)
        def _(at):
            rows = pl.ds(pl.multiple_of(at * block, block), block)
            gate = dot(second_ref[rows, :], both(0))
            upward = dot(second_ref[rows, :], both(1))
            grad_hidden = dot(grad_ref[rows, :], both(2))
            sigmoid_gate = 1.0 / (1.0 + jnp.exp(-gate))
            silu_gate = gate * sigmoid_gate
            narrow[rows, 2 * WIDE :] = (silu_gate * upward).astype(bf16)
            narrow[rows, WIDE : 2 * WIDE] = (grad_hidden * silu_gate).astype(bf16)
            narrow[rows, :WIDE] = (
                grad_hidden * upward * sigmoid_gate * (1.0 + gate * (1.0 - sigmoid_gate))
            ).astype(bf16)
            down_ref[rows, :] += dot_nt(narrow[rows, 2 * WIDE :], both(2))
            grad_second_ref[rows, :] += dot_nt(narrow[rows, :WIDE], both(0)) + dot_nt(
                narrow[rows, WIDE : 2 * WIDE], both(1)
            )

    quarter = D // 4

    def weight_terms(turn):
        slot = turn % 2

        @pl.loop(0, 4)
        def _(part):
            rows = pl.ds(pl.multiple_of(part * quarter, quarter), quarter)
            grads = dot(second_t_ref[rows, :], narrow[:, : 2 * WIDE])
            terms[slot, part // 2, part % 2, :, : 2 * WIDE] = grads.astype(bf16)
            down = dot(grad_t_ref[rows, :], narrow[:, 2 * WIDE :])
            terms[slot, part // 2, part % 2, :, 2 * WIDE :] = down.astype(bf16)

    def terms_copies(turn):
        slot, pair = turn % 2, pair_of(turn)
        gate, up = (gate_send_ref, gate_keep_ref), (up_send_ref, up_keep_ref)
        first, second = (down_a_send_ref, down_a_keep_ref), (down_b_send_ref, down_b_keep_ref)

        def apart(index, stream, refs, at):
            here = (y, x)[stream]
            columns = pl.ds(pl.multiple_of(at * WIDE, WIDE), WIDE)
            copies = []
            for way, (place, ref) in enumerate(zip((1 - here, here), refs)):
                source = terms.at[slot, :, :, :, index * WIDE : (index + 1) * WIDE]
                source = source.at[place] if stream == 0 else source.at[:, place]
                copies.append(
                    pltpu.make_async_copy(source, ref.at[:, :, columns], terms_sem.at[slot, index, way])
                )
            return copies

        split = (tiles + 1) // 4
        early = pair < split
        return (
            (None, apart(0, 0, gate, pair)),
            (None, apart(1, 1, up, pair)),
            (early, apart(2, 0, first, jnp.where(early, pair, 0))),
            (pair >= split, apart(2, 1, second, jnp.where(early, 0, pair - split))),
        )

    def all_copies(turn, act):
        for condition, copies in terms_copies(turn):
            if condition is None:
                for copy in copies:
                    act(copy)
            else:

                @pl.when(condition)
                def _(copies=copies):
                    for copy in copies:
                        act(copy)

    pairs = paired // 2

    def each(step, behind, act):
        for order in range(2):
            tile = 2 * (step - behind) + order

            @pl.when((tile >= 0) & (tile < paired))
            def _(tile=tile, order=order):
                act(tile, order)

    def send_on(stage):
        def act(tile, order):
            transfer(stage, tile, order).wait()
            transfer(stage + 1, tile, order).start()

        return act

    def work(slots, turn):
        compute(slots)

        @pl.when(turn >= 2)
        def _():
            all_copies(turn - 2, lambda copy: copy.wait())

        weight_terms(turn)
        all_copies(turn, lambda copy: copy.start())

    def begin(tile, order):
        held[tile % SLOTS, y, x, z // 2, z % 2] = shard_ref[tile]
        transfer(0, tile, order).start()

    def finish(pair):
        for order in range(2):
            transfer(3, 2 * pair + order, order).wait()
        slots = tuple((2 * pair + order) % SLOTS for order in range(2))
        turn = ready // 2 + pair
        work(slots, jnp.where(turn >= before_across, 2 * turn - before_across + 1, turn))

    def begin_across(tile):
        held[SLOTS + tile, y, x, z // 2, z % 2] = shard_ref[paired + tile]
        transfer(0, tile, 2).start()

    def advance_across(step):
        for tile in range(ACROSS):

            @pl.when(step == 2 * tile)
            def _(tile=tile):
                begin_across(tile)

            for stage in range(4):

                @pl.when(step == 2 * tile + stage + 1)
                def _(tile=tile, stage=stage):
                    transfer(stage, tile, 2).wait()
                    if stage < 3:
                        transfer(stage + 1, tile, 2).start()

    def on_early(pair):
        for copy in early_copies(pair):
            copy.wait()
        work((SLOTS - 2, SLOTS - 1), jnp.int32(pair))
        if 2 * pair + 2 < ready:
            for copy in early_copies(pair + 1):
                copy.start()

    @pl.loop(0, pairs + 4)
    def _(step):
        each(step, 2, send_on(1))
        each(step, 3, send_on(2))
        advance_across(step)
        for pair in range(ready // 2):

            @pl.when(step == 2 + pair)
            def _(pair=pair):
                on_early(pair)


        @pl.when(step >= 4)
        def _():
            finish(step - 4)

        @pl.when(step == pairs + 1)
        def _():
            work((SLOTS, SLOTS + 1), jnp.int32(before_across))

        @pl.when(step == pairs + 2)
        def _():
            held[2] = jnp.zeros(held.shape[1:], bf16)
            work((SLOTS + 2, 2), jnp.int32(before_across + 2))

        each(step, 1, send_on(0))
        each(step, 0, begin)

        @pl.when(step < 2)
        def _():
            rows = pl.ds(pl.multiple_of(step * (tokens // 2), tokens // 2), tokens // 2)
            second_t_ref[:, rows] = second_ref[rows, :].T
            grad_t_ref[:, rows] = grad_ref[rows, :].T

    @pl.loop(count - 2, count)
    def _(turn):
        all_copies(turn, lambda copy: copy.wait())

    half = tokens // 2
    copies = [
        pltpu.make_async_copy(source, target, out_sem.at[at])
        for at, (source, target) in enumerate(
            (
                (grad_second_ref.at[half:], second_other_ref),
                (grad_second_ref.at[:half], second_own_ref),
                (down_ref.at[half:], down_other_ref),
                (down_ref.at[:half], down_own_ref),
            )
        )
    ]
    for copy in copies:
        copy.start()
    for copy in copies:
        copy.wait()


EARLY = 4


def feed_forward(second, grad_result, shard, early):
    tokens = second.shape[0]
    streamed, rows, _ = shard.shape
    tiles = streamed + early.shape[-1] // (3 * LANES)
    down_a = (tiles + 1) // 2
    terms = [
        jax.ShapeDtypeStruct((2, D // 4, count * LANES), bf16)
        for count in (tiles + 1, tiles + 1, down_a, down_a)
        for _ in range(2)
    ]
    part = jax.ShapeDtypeStruct((tokens // 2, D), f32)
    dma = pltpu.SemaphoreType.DMA
    results = pl.pallas_call(
        functools.partial(feed_forward_kernel, tiles),
        out_shape=terms + [part] * 4,
        in_specs=[pl.BlockSpec(memory_space=pltpu.VMEM)] * 3 + [pl.BlockSpec(memory_space=pl.ANY)],
        out_specs=[pl.BlockSpec(memory_space=pl.ANY)] * 12,
        scratch_shapes=[
            pltpu.VMEM((SLOTS + ACROSS, 2, 2, 2, 2, rows, 3 * LANES), bf16),
            pltpu.VMEM((tokens, D), f32),
            pltpu.VMEM((tokens, D), f32),
            pltpu.VMEM((D, tokens), bf16),
            pltpu.VMEM((D, tokens), bf16),
            pltpu.VMEM((tokens, 3 * WIDE), bf16),
            pltpu.VMEM((2, 2, 2, D // 4, 3 * WIDE), bf16),
            dma((4, SLOTS + ACROSS)),
            dma((4, SLOTS + ACROSS)),
            dma((4,)),
            dma((2, 3, 2)),
            dma((2, 3)),
        ],
        compiler_params=pltpu.CompilerParams(
            collective_id=2, has_side_effects=True, vmem_limit_bytes=60 << 20
        ),
        cost_estimate=pl.CostEstimate(flops=0, bytes_accessed=1024, transcendentals=0),
    )(second, grad_result, shard, early)
    return list(zip(results[0:8:2], results[1:8:2])), results[8:]


def norm_scale(values):
    inverse = lax.rsqrt(jnp.mean(values * values, axis=-1, keepdims=True) + norm_epsilon)
    return (values * inverse, inverse)


def norm_backward(grad_normed, scaled, inverse, gain_row):
    grad_scaled = grad_normed * gain_row[None, :]
    grad_input = inverse * (
        grad_scaled - scaled * jnp.mean(grad_scaled * scaled, axis=-1, keepdims=True)
    )
    return (grad_input, jnp.sum(grad_normed * scaled, axis=0))


def adam_update(weight, gradient, first_moment, second_moment, learn_rate, decay_rate):
    first_new = beta_first * first_moment + (1.0 - beta_first) * gradient
    second_new = beta_second * second_moment + (1.0 - beta_second) * gradient * gradient
    first_hat = first_new / (1.0 - beta_first**STEP)
    second_hat = second_new / (1.0 - beta_second**STEP)
    new_weight = (
        weight
        - learn_rate * first_hat / (jnp.sqrt(second_hat) + adam_epsilon)
        - decay_rate * weight
    )
    return (new_weight, second_new)


def local(
    tokens,
    cotangent,
    lengths,
    w_qk,
    w_value,
    w_out,
    w_gu,
    w_down,
    small_params,
    m_qk,
    m_value,
    m_out,
    m_gu,
    m_down,
    m_small,
    v_qk,
    v_value,
    v_out,
    v_gu,
    v_down,
    v_small,
):
    slots, slot_rows, _ = tokens.shape
    owned = w_qk.shape[0]
    rows = slots * slot_rows
    core, z_at = lax.axis_index("core"), lax.axis_index("z")
    other = 1 - core
    first_core = core == 0

    def on_chip(array):
        return jnp.concatenate([array, swapped(array)], axis=0)

    def halves(array):
        return array.reshape(CORES, slots, slot_rows, -1)

    columns_of = [
        w_qk.astype(bf16).reshape(owned, 2, CORES, QC),
        w_value.astype(bf16).reshape(owned, 1, CORES, VC),
        w_out.astype(bf16).reshape(owned, 1, CORES, VC),
        w_gu.astype(bf16).reshape(owned, 2, CORES, FC),
        w_down.astype(bf16).reshape(owned, 1, CORES, FC),
    ]
    small_low = jnp.pad(small_params.astype(bf16), ((0, 0), (0, LANES - (KS + 2))))

    def shard(which, index):
        parts = [part_of(columns_of[i], 2, index).reshape(owned, -1) for i in which]
        return jnp.concatenate(parts, axis=1) if len(parts) > 1 else parts[0]

    def chip_shard(which, extra=None):
        mine, theirs = shard(which, core), shard(which, other)
        arrived = swapped(theirs if extra is None else jnp.concatenate([theirs, extra], axis=1))
        mine = mine if extra is None else jnp.concatenate([mine, extra], axis=1)
        return both_cores(mine, arrived, 0)

    in_kernel = tuple(lax.axis_size(axis) for axis in ("y", "x", "z")) == (2, 2, 4)
    early_width = 2 * QC + VC + LANES
    half = early_width // 2
    cut = FC // 2 // LANES * LANES
    down_at = VC + 2 * FC
    own_tokens = tokens.reshape(rows, D)
    other_tokens = swapped(own_tokens)
    wide_part = 4 * LANES
    if in_kernel:
        small_wide = jnp.pad(small_params, ((0, 0), (0, LANES - (KS + 2))))
        full, late_shard, early_shard = gathered_weights(
            w_qk, w_value, w_out, w_gu, w_down, small_wide
        )
        early, out_half = full[:, :early_width], full[:, early_width:]
        small_full = early[:, early_width - LANES :]
        early_tiles = lax.all_gather(early_shard, ("y", "x", "z"), axis=0)
        early_tiles = early_tiles.reshape(2, 2, 2, 2, CORES * owned, -1)
    else:
        attention_shard = chip_shard((0, 1), small_low)
        rest_shard = chip_shard((2, 3, 4))
        early_a = Gather(attention_shard[:, :half], True)
        early_b = Gather(attention_shard[:, half:], False)
        early = jnp.concatenate([early_a.rest(), early_b.rest()], axis=1)

        def gathered(start, width):
            return lax.all_gather(rest_shard[:, start : start + width], ("y", "x", "z"), axis=0, tiled=True)

        out_half = gathered(0, VC)
        gate_full = gathered(VC, FC)
        up_full = gathered(VC + FC, FC)
        last_shard, early = tied(rest_shard[:, down_at:], early)
        down_a = Gather(last_shard[:, :cut], True)
        down_b = Gather(last_shard[:, cut:], False)
        down_full = jnp.concatenate([down_a.rest(), down_b.rest()], axis=1)
        small_full = early[:, early_width - LANES :]

    qk_full = early[:, : 2 * QC]
    value_full = early[:, 2 * QC : 2 * QC + VC]
    small_float = small_full[:, : KS + 2].astype(f32)
    out_full = both_cores(out_half, swapped(out_half), 1)
    gain_first, gain_second = small_float[:, KS], small_float[:, KS + 1]
    taps = [part_of(small_float[:, j].reshape(CORES, VC), 0, core) for j in range(KS)]

    inputs = tokens.reshape(rows, D).astype(f32)
    scaled_first, inverse_first = norm_scale(inputs)
    scaled_chip, _ = norm_scale(
        jnp.concatenate([own_tokens, other_tokens], axis=0).astype(f32)
    )
    normed_chip = (scaled_chip * gain_first[None, :]).astype(bf16)
    query_key = halves(dot(normed_chip, qk_full).astype(bf16))
    value_pre = halves(dot(normed_chip, value_full).astype(bf16))
    tail = value_pre[:, :, slot_rows - (KS - 1) :, :]
    from_chip = passed_along(part_of(tail, 0, other), "z", 1)
    from_core = part_of(tail, 0, core)
    earlier = jnp.stack(
        [jnp.where(first_core, from_chip, from_core), jnp.where(first_core, from_core, from_chip)]
    )
    extended = jnp.concatenate([earlier, value_pre], axis=2).astype(f32)

    def tap_rows(j):
        return extended[:, :, KS - 1 - j : KS - 1 - j + slot_rows, :]

    convolved = taps[0] * tap_rows(0)
    for j in range(1, KS):
        convolved = convolved + taps[j] * tap_rows(j)
    values = convolved.astype(bf16)

    index_np, scale_np = feature_tables()
    tables = (core.astype(jnp.int32).reshape(1), jnp.asarray(index_np), jnp.asarray(scale_np))
    q_spec, k_spec, v_spec = (LANES, 0), (LANES, 1), (VC,)
    call = functools.partial(per_slot, slots=slots, rows=slot_rows)
    unit = 2 * CORES * rows * HC * LANES * FEATS
    wide = [pltpu.VMEM((CORES * slot_rows, VC), f32)]
    if in_kernel:
        (before,) = linked(key_term, True, 3)(*tables[1:], query_key, values, slots=slots)
    else:
        (state_own,) = call(
            state_kernel, ins=[k_spec, v_spec], outs=[("state", f32)], scratch=[], flops=4 * unit
        )(*tables, query_key, values)
        before = chain(state_own, True)
    mixer, dens = call(
        forward_kernel,
        ins=[q_spec, k_spec, v_spec, "state"],
        outs=[(v_spec, bf16), ((LANES,), f32)],
        scratch=wide,
        flops=8 * unit,
    )(*tables, query_key, query_key, values, before)

    mixer_flat = mixer.reshape(CORES * rows, VC)
    mixer_theirs = swapped(mixer_flat)

    def beside(mine, theirs):
        whole = jnp.zeros((mine.shape[0], CORES * mine.shape[1]), mine.dtype)
        for index, part in ((core, mine), (other, theirs)):
            whole = lax.dynamic_update_slice_in_dim(whole, part, index * mine.shape[1], 1)
        return whole

    mixer_own = beside(mixer_flat[:rows], mixer_theirs[rows:])
    mixer_other = beside(mixer_flat[rows:], mixer_theirs[:rows])
    after_mixer = inputs + dot(mixer_own, out_full)
    scaled_second, inverse_second = norm_scale(after_mixer)
    second_low = (scaled_second * gain_second[None, :]).astype(bf16)
    second_chip = on_chip(second_low)

    half_at = jnp.where(first_core, jnp.arange(CORES), 1 - jnp.arange(CORES))
    positions = (z_at * CORES + half_at)[:, None] * slot_rows + jnp.arange(slot_rows)[None, :]
    valid_chip = positions[:, None, :] < lengths[None, :, None]
    valid_chip = valid_chip.astype(f32).reshape(CORES * rows, 1)
    valid = valid_chip[:rows]
    query_key, cotangent_late = lax.optimization_barrier((query_key, cotangent))
    cotangent_chip = on_chip(cotangent_late.reshape(rows, D))
    mixer, cotangent_chip = tied(mixer, cotangent_chip)
    grad_result_chip = (valid_chip * cotangent_chip.astype(f32)).astype(bf16)
    grad_result = valid * cotangent.reshape(rows, D).astype(f32)

    if in_kernel:
        ffn_terms, ffn_parts = feed_forward(
            second_chip, grad_result_chip, late_shard, early_tiles
        )
        down_own, down_other, second_own, second_other = ffn_parts
        grad_second = second_own + swapped(second_other)
        down_result = down_own + swapped(down_other)
        (send_gate, keep_gate), (send_up, keep_up), *down_pairs = ffn_terms
        (send_down_a, keep_down_a), (send_down_b, keep_down_b) = down_pairs
        got_gate, got_up = exchanged(send_gate, "y", 0), exchanged(send_up, "x", 0)
    else:
        gate = dot(second_chip, gate_full)
        upward = dot(second_chip, up_full)
        sigmoid_gate = jax.nn.sigmoid(gate)
        silu_gate = gate * sigmoid_gate
        hidden = (silu_gate * upward).astype(bf16)
        grad_hidden = dot(grad_result_chip, down_full)
        grad_upward = (grad_hidden * silu_gate).astype(bf16)
        grad_gate = (
            grad_hidden * upward * sigmoid_gate * (1.0 + gate * (1.0 - sigmoid_gate))
        ).astype(bf16)
        second_part = dot_nt(grad_gate, gate_full) + dot_nt(grad_upward, up_full)
        grad_second = second_part[:rows] + swapped(second_part[rows:])
        down_part = dot_nt(hidden, down_full)
        down_result = down_part[:rows] + swapped(down_part[rows:])
    layer_out = (valid * (after_mixer + down_result)).astype(bf16).reshape(tokens.shape)

    grad_after_norm, grad_gain_second = norm_backward(
        grad_second, scaled_second, inverse_second, gain_second
    )
    grad_after = grad_result + grad_after_norm
    grad_after_low = grad_after.astype(bf16)
    grad_mixer = dot_nt(grad_after_low, out_full).astype(bf16)

    def core_columns(array):
        mine, theirs = (
            lax.dynamic_slice_in_dim(array, index * VC, VC, axis=1) for index in (core, other)
        )
        return jnp.concatenate([mine, swapped(theirs)], axis=0)

    grad_mixer_chip = core_columns(grad_mixer)
    grad_after_chip = core_columns(grad_after_low)
    mixer_chip = lax.optimization_barrier(jnp.concatenate([mixer_own, mixer_other], axis=0))

    wide_spec = (HC * LANES,)
    if in_kernel:
        grad_num, from_later = linked(query_term, False, 4)(
            *tables[1:],
            query_key,
            halves(grad_mixer_chip),
            mixer,
            dens,
            slots=slots,
            extra=(jax.ShapeDtypeStruct((CORES, slots, slot_rows, HC * LANES), bf16),),
        )
    else:
        pulled, grad_num = call(
            pull_kernel,
            ins=[q_spec, v_spec, v_spec, (LANES,)],
            outs=[("state", f32), (wide_spec, bf16)],
            scratch=[],
            flops=4 * unit,
        )(*tables, query_key, halves(grad_mixer_chip), mixer, dens)
        from_later = chain(pulled, False)
    grad_query_key, grad_values = call(
        backward_kernel,
        ins=[q_spec, k_spec, v_spec, wide_spec, "state", "state"],
        outs=[((2 * LANES,), bf16), (v_spec, bf16)],
        scratch=wide,
        flops=24 * unit,
    )(*tables, query_key, query_key, values, grad_num, before, from_later)

    if in_kernel:
        got_gate, got_up, send_down_a, send_down_b, grad_values = tied(
            got_gate, got_up, send_down_a, send_down_b, grad_values
        )

        def summed(keep, got):
            return (keep.astype(f32) + got.astype(f32)).astype(bf16)

        sum_gate, sum_up = summed(keep_gate, got_gate), summed(keep_up, got_up)
        sum_down_a = summed(keep_down_a, exchanged(send_down_a, "y", 0))
        sum_down_b = summed(keep_down_b, exchanged(send_down_b, "x", 0))
    head = grad_values[:, :, : KS - 1, :]
    from_chip = passed_along(part_of(head, 0, core), "z", -1)
    from_core = part_of(head, 0, other)
    later = jnp.stack(
        [jnp.where(first_core, from_core, from_chip), jnp.where(first_core, from_chip, from_core)]
    )
    grad_extended = jnp.concatenate([grad_values, later], axis=2).astype(f32)
    grad_pre = taps[0] * grad_extended[:, :, :slot_rows, :]
    for j in range(1, KS):
        grad_pre = grad_pre + taps[j] * grad_extended[:, :, j : j + slot_rows, :]
    grad_pre = grad_pre.reshape(CORES * rows, VC).astype(bf16)
    grad_query_key = grad_query_key.reshape(CORES * rows, 2 * QC)
    grad_values_float = grad_values.astype(f32)
    tap_grads = [jnp.sum(grad_values_float * tap_rows(j), axis=(0, 1, 2)) for j in range(KS)]

    first_other = dot_nt(grad_query_key[rows:], qk_full) + dot_nt(grad_pre[rows:], value_full)
    first_own = dot_nt(grad_query_key[:rows], qk_full) + dot_nt(grad_pre[:rows], value_full)
    grad_first = first_own + swapped(first_other)
    grad_gain_first = jnp.sum(first_own * scaled_chip[:rows], axis=0) + jnp.sum(
        first_other * scaled_chip[rows:], axis=0
    )

    def whole_feature(part):
        return lax.dynamic_update_slice(jnp.zeros((D,), f32), part, (core * VC,))

    small_terms = jnp.stack(
        [whole_feature(part) for part in tap_grads] + [grad_gain_first, grad_gain_second], axis=1
    )
    small_terms = jnp.pad(small_terms, ((0, 0), (0, LANES - (KS + 2)))).astype(bf16)
    if in_kernel:
        empty = jnp.zeros((CORES * rows, LANES), bf16)
        last_a = jnp.concatenate([grad_pre, grad_query_key, empty], axis=1)
        last_b = jnp.concatenate([grad_after_chip, empty], axis=1)
        grad_qk_own, grad_value_own, grad_out_own, grad_gu_own, grad_down_own, small_both = reduced(
            sum_down_a,
            sum_gate,
            sum_down_b,
            sum_up,
            dot_tn(normed_chip, last_a).astype(bf16),
            dot_tn(mixer_chip, last_b).astype(bf16),
            jnp.pad(small_terms, ((0, 0), (0, LANES))),
            owned,
        )
        grad_small_own = (small_both[:, :LANES] + small_both[:, LANES:])[:, : KS + 2]
    else:
        sum_down = Scatter(dot_tn(grad_result_chip, hidden).astype(bf16), True).rest()
        sum_gate = Scatter(dot_tn(second_chip, grad_gate).astype(bf16), False).rest()
        sum_up = Scatter(dot_tn(second_chip, grad_upward).astype(bf16), True).rest()
        sum_value = Scatter(dot_tn(normed_chip, grad_pre).astype(bf16), False).rest()
        sum_out = Scatter(dot_tn(mixer_chip, grad_after_chip).astype(bf16), True).rest()
        qk_terms = dot_tn(normed_chip, grad_query_key).astype(bf16)
        sum_last = Scatter(jnp.concatenate([qk_terms, small_terms], axis=1), True).rest()
    grad_input_norm, _ = norm_backward(grad_first, scaled_first, inverse_first, gain_first)
    input_grad = (grad_after + grad_input_norm).reshape(tokens.shape)

    def rows_of(array, index):
        return part_of(array.reshape(CORES, owned, -1), 0, index)

    def finish(*parts):
        merged = jnp.concatenate(parts, axis=1) if len(parts) > 1 else parts[0]
        mine, theirs = rows_of(merged, core), swapped(rows_of(merged, other))
        return mine.astype(f32), theirs.astype(f32)

    def columns(*parts):
        mine, theirs = finish(*parts)
        return both_cores(mine, theirs, 1)

    def two_columns(mine, theirs, width):
        shape = (owned, 2, 1, width)
        return both_cores(mine.reshape(shape), theirs.reshape(shape), 2).reshape(owned, -1)

    if not in_kernel:
        grad_down_own = columns(sum_down)
        grad_gu_own = two_columns(*finish(sum_gate, sum_up), FC)
        grad_out_own = columns(sum_out)
        grad_value_own = columns(sum_value)
        last_mine, last_theirs = finish(sum_last)
        grad_qk_own = two_columns(last_mine[:, : 2 * QC], last_theirs[:, : 2 * QC], QC)
        grad_small_own = (last_mine + last_theirs)[:, 2 * QC : 2 * QC + KS + 2]

    grads_all = (
        grad_qk_own,
        grad_value_own,
        grad_out_own,
        grad_gu_own,
        grad_down_own,
        grad_small_own,
    )
    masters = (w_qk, w_value, w_out, w_gu, w_down, small_params)
    firsts = (m_qk, m_value, m_out, m_gu, m_down, m_small)
    seconds = (v_qk, v_value, v_out, v_gu, v_down, v_small)
    learn_rates = (
        0.05 / math.sqrt(D),
        0.05 / math.sqrt(D),
        0.05 / math.sqrt(max(D // 128, 1)),
        0.05 / math.sqrt(D),
        0.05 / math.sqrt(0.0003 * FF * SLOT**0.825),
        0.014,
    )
    decays = (weight_decay, weight_decay, weight_decay, weight_decay, weight_decay, 0.0)
    new_weights = []
    new_seconds = []
    for position in range(6):
        updated, moment = adam_update(
            masters[position],
            grads_all[position],
            firsts[position],
            seconds[position],
            learn_rates[position],
            decays[position],
        )
        new_weights.append(updated)
        new_seconds.append(moment)
    return (layer_out, input_grad) + grads_all + tuple(new_weights) + tuple(new_seconds)


def solution(mesh):
    dp, fsdp = mesh.shape["dp"], mesh.shape["fsdp"]
    y_size = 2 if dp % 2 == 0 else 1
    split = Mesh(
        mesh.devices.reshape(y_size, dp // y_size, fsdp // CORES, CORES), ("y", "x", "z", "core")
    )
    slot_axes, row_axes = ("y", "x"), ("z", "core")
    activation = P(slot_axes, row_axes, None)
    weight = P(slot_axes + row_axes, None)
    return jax.shard_map(
        local,
        mesh=split,
        in_specs=(activation, activation, P(slot_axes)) + (weight,) * 18,
        out_specs=(activation, activation) + (weight,) * 18,
        check_vma=False,
    )
```

```python
import functools
import math

import jax
import jax.numpy as jnp
import numpy as np
from jax import lax
from jax.experimental import pallas as pl
from jax.experimental.pallas import tpu as pltpu
from jax.sharding import Mesh
from jax.sharding import PartitionSpec as P

D = 1792
H = 16
F = 16
FF = 4864
KS = 3
SLOT = 2048
STEP = 10

CORES = 2
HC = H // CORES
HW = D // H
VC = HC * HW
QC = HC * F
FC = FF // CORES
LANES = 128
FEATS = 256
FROWS = 160
SCALE = 1.0 / math.sqrt(F)

norm_epsilon = 1e-06
beta_first = 0.9
beta_second = 0.95
adam_epsilon = 1e-08
weight_decay = 3e-05

bf16 = jnp.bfloat16
f32 = jnp.float32


def feature_tables():
    index = np.full((8, FEATS), -4096, np.int32)
    scale = np.zeros((8, FEATS), np.float32)
    scale[0, 0] = scale[1, 0] = scale[2, 0] = 1.0
    at = 1
    for i in range(F):
        index[0, at] = i
        scale[1, at] = 1.0
        scale[2, at] = SCALE
        at += 1
    for i in range(F):
        for j in range(i, F):
            index[0, at] = i
            index[1, at] = j
            scale[2, at] = (1.0 if i == j else 2.0) * 0.5 * SCALE * SCALE
            at += 1
    return index, scale


def dot(a, b):
    return lax.dot_general(a, b, (((1,), (0,)), ((), ())), preferred_element_type=f32)


def dot_nt(a, b):
    return lax.dot_general(a, b, (((1,), (1,)), ((), ())), preferred_element_type=f32)


def dot_tn(a, b):
    return lax.dot_general(a, b, (((0,), (0,)), ((), ())), preferred_element_type=f32)


def selectors(index_ref, head):
    lane = lax.broadcasted_iota(jnp.int32, (LANES, FEATS), 0) - head * F
    first = jnp.where(lane == index_ref[0:1, :], 1.0, 0.0).astype(bf16)
    second = jnp.where(lane == index_ref[1:2, :], 1.0, 0.0).astype(bf16)
    return first, second


def factors(rows, first, second, scale_ref):
    return (dot(rows, first) + scale_ref[0:1, :], dot(rows, second) + scale_ref[1:2, :])


def window(head):
    start = head * HW
    base = min(start // LANES * LANES, VC - 2 * LANES)
    return base, start - base


def both_halves(core_ref, ref, columns):
    core = core_ref[0]
    return jnp.concatenate([ref[core, :, columns], ref[1 - core, :, columns]], axis=0)


def store_halves(core_ref, ref, rows, columns):
    core, half = core_ref[0], rows.shape[0] // CORES
    ref[core, :, columns] = rows[:half]
    ref[1 - core, :, columns] = rows[half:]


def head_columns(core_ref, ref, head):
    base, offset = window(head)
    wide = both_halves(core_ref, ref, slice(base, base + 2 * LANES)).astype(f32)
    if offset:
        wide = pltpu.roll(wide, 2 * LANES - offset, 1)
    return wide[:, :LANES]


def add_head_columns(ref, head, block):
    base, offset = window(head)
    wide = jnp.concatenate([block, jnp.zeros_like(block)], axis=1)
    if offset:
        wide = pltpu.roll(wide, offset, 1)
    ref[:, base : base + 2 * LANES] += wide


def with_one(block):
    lane = lax.broadcasted_iota(jnp.int32, block.shape, 1)
    return jnp.where(lane < HW, block, jnp.where(lane == HW, 1.0, 0.0))


def only_head(rows, head):
    lane = lax.broadcasted_iota(jnp.int32, rows.shape, 1)
    inside = (lane >= head * F) & (lane < head * F + F)
    return jnp.where(inside, rows.astype(f32), 0.0).astype(bf16)


def state_kernel(core_ref, index_ref, scale_ref, k_ref, v_ref, state_ref):
    keys = both_halves(core_ref, k_ref, slice(None))
    for head in range(HC):
        first, second = selectors(index_ref, head)
        one, two = factors(keys, first, second, scale_ref)
        phi = (one * two * scale_ref[2:3, :]).astype(bf16)
        values = with_one(head_columns(core_ref, v_ref, head)).astype(bf16)
        state_ref[0, head] = dot_tn(phi, values)[:FROWS]


def scores_of(q_head, keys):
    scores = dot_nt(q_head, keys) * SCALE
    row = lax.broadcasted_iota(jnp.int32, scores.shape, 0)
    column = lax.broadcasted_iota(jnp.int32, scores.shape, 1)
    return scores, column <= row


def forward_kernel(core_ref, index_ref, scale_ref, q_ref, k_ref, v_ref, before_ref, mixer_ref, den_ref, wide):
    queries = both_halves(core_ref, q_ref, slice(None))
    keys = both_halves(core_ref, k_ref, slice(None))
    wide[...] = jnp.zeros_like(wide)
    lane = lax.broadcasted_iota(jnp.int32, (queries.shape[0], LANES), 1)
    dens = jnp.zeros((queries.shape[0], LANES), f32)
    for head in range(HC):
        first, second = selectors(index_ref, head)
        one, two = factors(queries, first, second, scale_ref)
        phi = (one * two).astype(bf16)
        values = with_one(head_columns(core_ref, v_ref, head)).astype(bf16)
        scores, allowed = scores_of(only_head(queries, head), keys)
        kernel = jnp.where(allowed, 1.0 + scores + 0.5 * scores * scores, 0.0).astype(bf16)
        total = dot(kernel, values) + dot(phi[:, :FROWS], before_ref[0, head])
        den = total[:, HW : HW + 1]
        add_head_columns(wide, head, jnp.where(lane < HW, total / den, 0.0))
        dens = jnp.where(lane == head, den, dens)
    store_halves(core_ref, mixer_ref, wide[...].astype(bf16), slice(None))
    store_halves(core_ref, den_ref, dens, slice(None))


def pull_kernel(core_ref, index_ref, scale_ref, q_ref, gm_ref, mixer_ref, den_ref, state_ref, gnum_ref):
    queries = both_halves(core_ref, q_ref, slice(None))
    lane = lax.broadcasted_iota(jnp.int32, (queries.shape[0], LANES), 1)
    dens = both_halves(core_ref, den_ref, slice(None))
    for head in range(HC):
        first, second = selectors(index_ref, head)
        one, two = factors(queries, first, second, scale_ref)
        phi = (one * two).astype(bf16)
        den = dens[:, head : head + 1]
        grad = jnp.where(lane < HW, head_columns(core_ref, gm_ref, head), 0.0)
        mixer = head_columns(core_ref, mixer_ref, head)
        pulled = -jnp.sum(grad * mixer, axis=1, keepdims=True)
        grad = (jnp.where(lane == HW, pulled, grad) / den).astype(bf16)
        store_halves(core_ref, gnum_ref, grad, slice(head * LANES, (head + 1) * LANES))
        state_ref[0, head] = dot_tn(phi, grad)[:FROWS]


def backward_kernel(
    core_ref, index_ref, scale_ref, q_ref, k_ref, v_ref, gnum_ref, before_ref, after_ref, gqk_ref, gv_ref, wide
):
    queries = both_halves(core_ref, q_ref, slice(None))
    keys = both_halves(core_ref, k_ref, slice(None))
    wide[...] = jnp.zeros_like(wide)
    lane = lax.broadcasted_iota(jnp.int32, (queries.shape[0], LANES), 1)
    grad_q = jnp.zeros((queries.shape[0], LANES), f32)
    grad_k = jnp.zeros((queries.shape[0], LANES), f32)
    for head in range(HC):
        first, second = selectors(index_ref, head)
        coef = scale_ref[2:3, :]
        q_one, q_two = factors(queries, first, second, scale_ref)
        k_one, k_two = factors(keys, first, second, scale_ref)
        values = with_one(head_columns(core_ref, v_ref, head)).astype(bf16)
        gnum = both_halves(core_ref, gnum_ref, slice(head * LANES, (head + 1) * LANES))
        q_head = only_head(queries, head)
        k_head = only_head(keys, head)
        scores, allowed = scores_of(q_head, keys)
        kernel = jnp.where(allowed, 1.0 + scores + 0.5 * scores * scores, 0.0).astype(bf16)
        grad_kernel = dot_nt(gnum, values)
        grad_scores = (jnp.where(allowed, grad_kernel * (1.0 + scores), 0.0) * SCALE).astype(bf16)
        phi_k = (k_one * k_two * coef).astype(bf16)
        after = after_ref[0, head]
        before = before_ref[0, head]
        grad_v = dot_tn(kernel, gnum) + dot(phi_k[:, :FROWS], after)
        add_head_columns(wide, head, jnp.where(lane < HW, grad_v, 0.0))
        empty = jnp.zeros((FEATS - FROWS, LANES), bf16)
        grad_phi_q = dot_nt(gnum, jnp.concatenate([before, empty], axis=0))
        grad_phi_k = dot_nt(values, jnp.concatenate([after, empty], axis=0)) * coef
        grad_q += dot(grad_scores, k_head)
        grad_q += dot_nt((grad_phi_q * q_two).astype(bf16), first)
        grad_q += dot_nt((grad_phi_q * q_one).astype(bf16), second)
        grad_k += dot_tn(grad_scores, q_head)
        grad_k += dot_nt((grad_phi_k * k_two).astype(bf16), first)
        grad_k += dot_nt((grad_phi_k * k_one).astype(bf16), second)
    store_halves(core_ref, gqk_ref, grad_q.astype(bf16), slice(0, LANES))
    store_halves(core_ref, gqk_ref, grad_k.astype(bf16), slice(LANES, 2 * LANES))
    store_halves(core_ref, gv_ref, wide[...].astype(bf16), slice(None))


def per_slot(kernel, slots, rows, ins, outs, scratch, flops):
    def table():
        return pl.BlockSpec((8, FEATS), lambda s, core: (0, 0))

    def row_spec(width, column=0):
        return pl.BlockSpec((CORES, None, rows, width), lambda s, core: (0, s, 0, column))

    def state_spec():
        return pl.BlockSpec((1, HC, FROWS, LANES), lambda s, core: (s, 0, 0, 0))

    def spec(kind):
        return state_spec() if kind == "state" else row_spec(*kind)

    def shape(kind, dtype):
        if kind == "state":
            return jax.ShapeDtypeStruct((slots, HC, FROWS, LANES), dtype)
        return jax.ShapeDtypeStruct((CORES, slots, rows, kind[0]), dtype)

    return pl.pallas_call(
        kernel,
        grid_spec=pltpu.PrefetchScalarGridSpec(
            num_scalar_prefetch=1,
            grid=(slots,),
            in_specs=[table(), table()] + [spec(kind) for kind in ins],
            out_specs=[spec(kind) for kind, _ in outs],
            scratch_shapes=scratch,
        ),
        out_shape=[shape(kind, dtype) for kind, dtype in outs],
        compiler_params=pltpu.CompilerParams(vmem_limit_bytes=56 << 20),
        cost_estimate=pl.CostEstimate(flops=flops, bytes_accessed=8 << 20, transcendentals=0),
    )


def linked(kernel, up, ids):
    def run(*refs):
        y, x, z, core = places_of()
        last = lax.axis_size("z") - 1
        *refs, sent, send_sem, recv_sem = refs
        total_ref = refs[-1]
        by = 1 if up else last
        receives, sends = (z > 0, z < last) if up else (z < last, z > 0)

        barrier = pltpu.get_barrier_semaphore()
        for step in (1, last):
            pl.semaphore_signal(
                barrier,
                inc=1,
                device_id=(y, x, lax.rem(z + step, last + 1), core),
                device_id_type=pl.DeviceIdType.MESH,
            )
        pl.semaphore_wait(barrier, 2)

        def transfer(slot, head):
            return pltpu.make_async_remote_copy(
                src_ref=sent.at[slot, head],
                dst_ref=total_ref.at[slot, head],
                send_sem=send_sem.at[slot, head],
                recv_sem=recv_sem.at[slot, head],
                device_id=(y, x, lax.rem(z + by, last + 1), core),
                device_id_type=pl.DeviceIdType.MESH,
            )

        @pl.when(jnp.logical_not(receives))
        def _():
            total_ref[...] = jnp.zeros_like(total_ref)

        @pl.loop(0, sent.shape[0])
        def _(slot):
            for head in range(HC):
                term = kernel([core], slot, head, *refs[:-1])

                @pl.when(receives)
                def _(head=head):
                    transfer(slot, head).wait_recv()

                @pl.when(sends)
                def _(head=head, term=term):
                    sent[slot, head] = (total_ref[slot, head].astype(f32) + term).astype(bf16)
                    transfer(slot, head).start()

        @pl.when(sends)
        def _():
            @pl.loop(0, sent.shape[0])
            def _(slot):
                for head in range(HC):
                    transfer(slot, head).wait_send()

    def call(*operands, slots, extra=()):
        state = jax.ShapeDtypeStruct((slots, HC, FROWS, LANES), bf16)
        vmem = pl.BlockSpec(memory_space=pltpu.VMEM)
        return pl.pallas_call(
            run,
            out_shape=list(extra) + [state],
            in_specs=[vmem] * len(operands),
            out_specs=[vmem] * (len(extra) + 1),
            scratch_shapes=[
                pltpu.VMEM((slots, HC, FROWS, LANES), bf16),
                pltpu.SemaphoreType.DMA((slots, HC)),
                pltpu.SemaphoreType.DMA((slots, HC)),
            ],
            compiler_params=pltpu.CompilerParams(
                collective_id=ids, has_side_effects=True, vmem_limit_bytes=40 << 20
            ),
            cost_estimate=pl.CostEstimate(flops=0, bytes_accessed=1024, transcendentals=0),
        )(*operands)

    return call


def key_term(core_ref, slot, head, index_ref, scale_ref, qk_ref, v_ref):
    keys = both_halves(core_ref, qk_ref.at[:, slot], slice(LANES, 2 * LANES))
    first, second = selectors(index_ref, head)
    one, two = factors(keys, first, second, scale_ref)
    phi = (one * two * scale_ref[2:3, :]).astype(bf16)
    values = with_one(head_columns(core_ref, v_ref.at[:, slot], head)).astype(bf16)
    return dot_tn(phi, values)[:FROWS]


def query_term(core_ref, slot, head, index_ref, scale_ref, qk_ref, gm_ref, mixer_ref, den_ref, gnum_ref):
    queries = both_halves(core_ref, qk_ref.at[:, slot], slice(0, LANES))
    first, second = selectors(index_ref, head)
    one, two = factors(queries, first, second, scale_ref)
    phi = (one * two).astype(bf16)
    den = both_halves(core_ref, den_ref.at[:, slot], slice(None))[:, head : head + 1]
    lane = lax.broadcasted_iota(jnp.int32, (queries.shape[0], LANES), 1)
    grad = jnp.where(lane < HW, head_columns(core_ref, gm_ref.at[:, slot], head), 0.0)
    mixer = head_columns(core_ref, mixer_ref.at[:, slot], head)
    pulled = -jnp.sum(grad * mixer, axis=1, keepdims=True)
    grad = (jnp.where(lane == HW, pulled, grad) / den).astype(bf16)
    store_halves(core_ref, gnum_ref.at[:, slot], grad, slice(head * LANES, (head + 1) * LANES))
    return dot_tn(phi, grad)[:FROWS]


def passed_along(array, axis, by):
    count = lax.axis_size(axis)
    pairs = [(i, i + by) for i in range(count) if 0 <= i + by < count]
    return lax.ppermute(array, axis, pairs)


def both_cores(mine, theirs, axis):
    first = lax.axis_index("core") == 0
    return jnp.concatenate(
        [jnp.where(first, mine, theirs), jnp.where(first, theirs, mine)], axis=axis
    )


def swapped(array):
    return lax.ppermute(array, "core", [(0, 1), (1, 0)])


def part_of(array, axis, index):
    return lax.dynamic_index_in_dim(array, index, axis, keepdims=False)


def bits_of(axis):
    return [(axis, bit) for bit in reversed(range(lax.axis_size(axis).bit_length() - 1))]


def bit_at(axis, bit):
    return (lax.axis_index(axis) >> bit) & 1


def exchanged(array, axis, bit):
    count = lax.axis_size(axis)
    return lax.ppermute(array, axis, [(i, i ^ (1 << bit)) for i in range(count)])


def tied(*arrays):
    return lax.optimization_barrier(arrays)


class Gather:
    def __init__(self, piece, x_first):
        self.columns = piece.shape[1]
        self.block = piece
        low_first = lambda axis: bits_of(axis)[::-1]
        self.plan = [(step, at) for at, step in enumerate(bits_of("z"))]
        if x_first:
            self.plan += [(step, 0) for step in low_first("x") + low_first("y")]
        else:
            self.plan += [(step, 0) for step in low_first("y")]
            self.plan += [(step, len(bits_of("y"))) for step in low_first("x")]

    def stage(self):
        (axis, bit), dim = self.plan.pop(0)
        mine = bit_at(axis, bit)
        arrived = exchanged(self.block, axis, bit)
        shape = self.block.shape[:dim] + (2,) + self.block.shape[dim:]
        whole = jnp.zeros(shape, self.block.dtype)
        whole = lax.dynamic_update_index_in_dim(whole, self.block, mine, dim)
        self.block = lax.dynamic_update_index_in_dim(whole, arrived, 1 - mine, dim)
        return self

    def along_z(self):
        while self.plan[0][0][0] == "z":
            self.stage()
        return self

    def rest(self):
        while self.plan:
            self.stage()
        return self.block.reshape(D, self.columns)


class Scatter:
    def __init__(self, terms, x_first):
        self.dims = bits_of("y") + bits_of("x") + bits_of("z")
        order = ("x", "y") if x_first else ("y", "x")
        self.plan = bits_of(order[0]) + bits_of(order[1]) + bits_of("z")[::-1]
        rows = D >> len(self.dims)
        self.terms = [terms.reshape((2,) * len(self.dims) + (rows, terms.shape[1]))]

    def total(self, terms):
        total = terms[0].astype(f32)
        for term in terms[1:]:
            total = total + term.astype(f32)
        return total

    def stage(self):
        step = self.plan.pop(0)
        dim, mine = self.dims.index(step), bit_at(*step)
        self.dims.remove(step)
        sent = self.total([part_of(term, dim, 1 - mine) for term in self.terms]).astype(bf16)
        self.terms = [part_of(term, dim, mine) for term in self.terms]
        self.terms.append(exchanged(sent, *step))
        return self

    def rest(self):
        while self.plan:
            self.stage()
        return self.total(self.terms)


def chain(local, up):
    count = lax.axis_size("z")
    total = jnp.zeros_like(local)
    for hop in range(1, count):
        pair = (hop - 1, hop) if up else (count - hop, count - hop - 1)
        message = (total + local).astype(bf16)
        total = total + lax.ppermute(message, "z", [pair]).astype(f32)
    return total.astype(bf16)


def mesh_exchange(y, x, z, core, axis):
    if axis == "core":
        return (y, x, z, 1 - core)
    if axis == "y":
        return (1 - y, x, z, core)
    if axis == "x":
        return (y, 1 - x, z, core)
    if axis == "z0":
        return (y, x, z + 1 - 2 * (z % 2), core)
    return (y, x, (z + 2) % 4, core)


ORDERS = (("y", "x", "z0", "z1"), ("x", "y", "z0", "z1"))


WIDE = 2 * LANES


def reduce_kernel(
    down_a_ref,
    gate_ref,
    down_b_ref,
    up_ref,
    last_a_ref,
    last_b_ref,
    small_terms_ref,
    qk_ref,
    value_ref,
    out_ref,
    gu_ref,
    down_ref,
    small_ref,
    sums,
    halves,
    quarters,
    finals,
    got_terms,
    got_sums,
    got_halves,
    got_quarters,
    send_sem,
    recv_sem,
    load_sem,
):
    y, x, z, core = places_of()
    places = {"y": y, "x": x, "z0": z % 2, "z1": z // 2}

    parts, count = ([], []), 0
    all_refs = (
        (down_a_ref, gate_ref, last_a_ref),
        (down_b_ref, up_ref, last_b_ref, small_terms_ref),
    )
    for stream, refs in enumerate(all_refs):
        at = 0
        for ref in refs:
            chunks = ref.shape[-1] // WIDE
            parts[stream].append((ref, len(ref.shape) == 3, at, at + chunks))
            at += chunks
        count = max(count, at)
    hidden, width = FC // LANES, VC // LANES
    down_a = (hidden + 1) // 2
    down_b = hidden - down_a
    gate_at, last_a = 2 * parts[0][1][2], 2 * parts[0][2][2]
    up_at, last_b, small_at = (2 * parts[1][at][2] for at in (1, 2, 3))
    places_out = (
        (
            (down_ref, core * hidden, 0, down_a),
            (gu_ref, core * hidden, gate_at, gate_at + hidden),
            (value_ref, core * width, last_a, last_a + width),
            (qk_ref, core, last_a + width, last_a + width + 1),
            (qk_ref, CORES + core, last_a + width + 1, last_a + width + 2),
        ),
        (
            (down_ref, core * hidden + down_a, 0, down_b),
            (gu_ref, (CORES + core) * hidden, up_at, up_at + hidden),
            (out_ref, core * width, last_b, last_b + width),
            (small_ref, core, small_at, small_at + 1),
        ),
    )
    greet(y, x, z, core, True)

    def columns(tile):
        return pl.ds(pl.multiple_of(tile * LANES, LANES), LANES)

    def wide_columns(chunk):
        return pl.ds(pl.multiple_of(chunk * WIDE, WIDE), WIDE)

    def transfer(stream, stage, chunk, source, target=None):
        landing = chunk % 4
        if target is None:
            target = (got_terms, got_sums, got_halves, got_quarters)[stage].at[stream, landing]
        axis = (ORDERS[stream] + ("core", "core"))[stage]
        return pltpu.make_async_remote_copy(
            src_ref=source,
            dst_ref=target,
            send_sem=send_sem.at[stream, stage, landing],
            recv_sem=recv_sem.at[stream, stage, landing],
            device_id=mesh_exchange(y, x, z, core, axis),
            device_id_type=pl.DeviceIdType.MESH,
        )

    def first_view(stream, ref, tile, place):
        ref = ref.at[:, :, :, wide_columns(tile)]
        return ref.at[place] if stream == 0 else ref.at[:, place]

    def source_of(stream, stage, chunk):
        there = 1 - places[ORDERS[stream][stage]]
        if stage == 1:
            return sums.at[stream, chunk % 4, there]
        if stage == 2:
            return halves.at[stream, chunk % 2, :, there]
        return quarters.at[stream, chunk % 2, there]

    def add(a, b):
        return a.astype(f32) + b.astype(f32)

    def load(stream, chunk, ref, start):
        slot = chunk % 4
        return pltpu.make_async_copy(
            ref.at[:, :, wide_columns(chunk - start)], sums.at[stream, slot], load_sem.at[stream, slot]
        )

    def begin(stream, chunk):
        for ref, summed, start, stop in parts[stream]:
            if summed:

                @pl.when((chunk >= start) & (chunk < stop))
                def _(ref=ref, start=start):
                    load(stream, chunk, ref, start).start()

        for ref, _, start, stop in parts[stream][2:]:

            @pl.when((chunk >= start) & (chunk < stop))
            def _(ref=ref, start=start):
                there = 1 - places[ORDERS[stream][0]]
                transfer(stream, 0, chunk, first_view(stream, ref, chunk - start, there)).start()

    def second(stream, chunk):
        for ref, summed, start, stop in parts[stream]:

            @pl.when((chunk >= start) & (chunk < stop))
            def _(ref=ref, summed=summed, start=start):
                tile = chunk - start
                if summed:
                    load(stream, chunk, ref, start).wait()
                else:
                    there = 1 - places[ORDERS[stream][0]]
                    transfer(stream, 0, chunk, first_view(stream, ref, tile, there)).wait()
                    own = first_view(stream, ref, tile, places[ORDERS[stream][0]])[...]
                    sums[stream, chunk % 4] = add(own, got_terms[stream, chunk % 4]).astype(bf16)

        transfer(stream, 1, chunk, source_of(stream, 1, chunk)).start()

    def advance(stream, stage, chunk):
        here = places[ORDERS[stream][stage]]
        slot, landing = chunk % 2, chunk % 4
        transfer(stream, stage, chunk, source_of(stream, stage, chunk)).wait()
        if stage == 1:
            total = add(sums[stream, landing, here], got_sums[stream, landing]).astype(bf16)
            halves[stream, slot] = total.reshape(halves.shape[2:])
        elif stage == 2:
            own = halves[stream, slot, :, here]
            quarters[stream, slot] = add(own, got_halves[stream, landing]).astype(bf16)
        else:
            total = add(quarters[stream, slot, here], got_quarters[stream, landing])
            finals[stream, slot] = total.reshape(finals.shape[2:])
        if stage < 3:
            transfer(stream, stage + 1, chunk, source_of(stream, stage + 1, chunk)).start()

    def hand_over(stream, chunk, waiting):
        for at in range(2):
            tile = 2 * chunk + at
            lanes = slice(at * LANES, (at + 1) * LANES)
            for ref, first, start, stop in places_out[stream]:

                @pl.when((tile >= start) & (tile < stop))
                def _(at=at, tile=tile, lanes=lanes, ref=ref, first=first, start=start):
                    target = ref.at[:, columns(first + tile - start)]
                    source = finals.at[stream, chunk % 2, 1 - core, :, lanes]
                    copy = transfer(stream, 4 + at, chunk, source, target)
                    if waiting:
                        copy.wait()
                    else:
                        target[...] = finals[stream, chunk % 2, core, :, lanes]
                        copy.start()

    @pl.loop(0, count + 5)
    def _(step):
        for stream in range(2):
            total = parts[stream][-1][3]

            @pl.when(step < total)
            def _(stream=stream):
                begin(stream, step)

        for stage in range(5):
            for stream in range(2):
                total = parts[stream][-1][3]

                @pl.when((step >= stage + 1) & (step < total + stage + 1))
                def _(stage=stage, stream=stream):
                    chunk = step - stage - 1
                    if stage == 0:
                        second(stream, chunk)
                    elif stage < 4:
                        advance(stream, stage, chunk)
                    else:
                        hand_over(stream, chunk, True)
                    if stage == 3:
                        hand_over(stream, chunk, False)


def reduced(down_a, gate, down_b, up, last_a, last_b, small, owned):
    block, rows = D // 4, D // 16
    dma = pltpu.SemaphoreType.DMA
    last_a, last_b, small = (last.reshape(2, 2, block, -1) for last in (last_a, last_b, small))
    widths = (2 * CORES * QC, CORES * VC, CORES * VC, 2 * CORES * FC, CORES * FC, CORES * LANES)
    return pl.pallas_call(
        reduce_kernel,
        out_shape=[jax.ShapeDtypeStruct((owned, width), f32) for width in widths],
        in_specs=[pl.BlockSpec(memory_space=pl.ANY)] * 4
        + [pl.BlockSpec(memory_space=pltpu.VMEM)] * 3,
        out_specs=[pl.BlockSpec(memory_space=pltpu.VMEM)] * 6,
        scratch_shapes=[
            pltpu.VMEM((2, 4, 2, block, WIDE), bf16),
            pltpu.VMEM((2, 2, 2, 2, rows, WIDE), bf16),
            pltpu.VMEM((2, 2, 2, rows, WIDE), bf16),
            pltpu.VMEM((2, 2, CORES, owned, WIDE), f32),
            pltpu.VMEM((2, 4, 2, block, WIDE), bf16),
            pltpu.VMEM((2, 4, block, WIDE), bf16),
            pltpu.VMEM((2, 4, 2, rows, WIDE), bf16),
            pltpu.VMEM((2, 4, rows, WIDE), bf16),
            dma((2, 6, 4)),
            dma((2, 6, 4)),
            dma((2, 4)),
        ],
        compiler_params=pltpu.CompilerParams(
            collective_id=0, has_side_effects=True, vmem_limit_bytes=56 << 20
        ),
        cost_estimate=pl.CostEstimate(flops=0, bytes_accessed=1024, transcendentals=0),
    )(down_a, gate, down_b, up, last_a, last_b, small)


def places_of():
    y, x, z, core = (lax.axis_index(axis) for axis in ("y", "x", "z", "core"))
    return y, x, z, core


def greet(y, x, z, core, both_cores=False):
    barrier = pltpu.get_barrier_semaphore()
    partners = ORDERS[0] + (("core",) if both_cores else ())
    for axis in partners:
        pl.semaphore_signal(
            barrier,
            inc=1,
            device_id=mesh_exchange(y, x, z, core, axis),
            device_id_type=pl.DeviceIdType.MESH,
        )
    pl.semaphore_wait(barrier, len(partners))


GATHER_ORDERS = (("z1", "z0", "x", "y"), ("z1", "z0", "y", "x"), ("x", "y", "z1", "z0"))


def gather_view(ref, order, stage, y, x, z):
    if stage == 0:
        return ref.at[y, x, z // 2, z % 2]
    if order == 2:
        if stage == 1:
            return ref.at[y, :, z // 2, z % 2]
        return ref.at[:, :, z // 2, z % 2] if stage == 2 else ref.at[:, :, :, z % 2]
    if stage == 1:
        return ref.at[y, x, :, z % 2]
    if stage == 2:
        return ref.at[y, x]
    return ref.at[y] if order == 0 else ref.at[:, x]


ATTENTION = 2 * QC + 2 * VC + LANES


def gather_kernel(
    qk_ref,
    value_ref,
    out_ref,
    gu_ref,
    down_ref,
    small_ref,
    full_ref,
    late_ref,
    early_ref,
    merged,
    send_sem,
    recv_sem,
    core_send_sem,
    core_recv_sem,
    own_sem,
):
    y, x, z, core = places_of()
    owned = qk_ref.shape[0]
    greet(y, x, z, core, True)

    at, parts = 0, []
    for ref, start, width, apart in (
        (qk_ref, 0, QC, True),
        (qk_ref, CORES * QC, QC, True),
        (value_ref, 0, VC, True),
        (small_ref, 0, LANES, False),
        (out_ref, 0, VC, True),
        (gu_ref, 0, FC, True),
        (gu_ref, FF, FC, True),
        (down_ref, 0, FC, True),
    ):
        parts.append((ref, start, width, apart, at))
        at += width
    my_rows = pl.ds(pl.multiple_of(core * owned, 8), owned)

    def copies(index):
        ref, start, width, apart, at = parts[index]

        def source(which):
            first = pl.multiple_of(start + (which * width if apart else 0), LANES)
            return ref.at[:, pl.ds(first, width)]

        target = merged.at[my_rows, at : at + width]
        remote = pltpu.make_async_remote_copy(
            src_ref=source(1 - core),
            dst_ref=target,
            send_sem=core_send_sem.at[index],
            recv_sem=core_recv_sem.at[index],
            device_id=mesh_exchange(y, x, z, core, "core"),
            device_id_type=pl.DeviceIdType.MESH,
        )
        return remote, pltpu.make_async_copy(source(core), target, own_sem.at[index])

    for index in range(len(parts)):
        for copy in copies(index):
            copy.start()
    for index in range(5):
        for copy in copies(index):
            copy.wait()
    full_ref[y, x, z // 2, z % 2] = merged[:, :ATTENTION].astype(bf16)

    def transfer(stage, tile, order):
        columns = pl.ds(pl.multiple_of(tile * LANES, LANES), LANES)
        view = gather_view(full_ref.at[:, :, :, :, :, columns], order, stage, y, x, z)
        return pltpu.make_async_remote_copy(
            src_ref=view,
            dst_ref=view,
            send_sem=send_sem.at[stage, tile],
            recv_sem=recv_sem.at[stage, tile],
            device_id=mesh_exchange(y, x, z, core, GATHER_ORDERS[order][stage]),
            device_id_type=pl.DeviceIdType.MESH,
        )

    paired = ATTENTION // LANES - ACROSS
    pairs = paired // 2

    def each(step, behind, act):
        for order in range(2):
            tile = 2 * (step - behind) + order

            @pl.when((tile >= 0) & (tile < paired))
            def _(tile=tile, order=order):
                act(tile, order)

    def go_on(tile, order, stage):
        transfer(stage, tile, order).wait()
        if stage < 3:
            transfer(stage + 1, tile, order).start()

    hidden = FC // LANES

    @pl.loop(0, pairs + 4)
    def _(step):
        each(step, 0, lambda tile, order: transfer(0, tile, order).start())
        for stage in range(4):
            each(step, stage + 1, functools.partial(go_on, stage=stage))
        for across in range(ACROSS):

            @pl.when(step == 2 * across)
            def _(across=across):
                transfer(0, paired + across, 2).start()

            for stage in range(4):

                @pl.when(step == 2 * across + stage + 1)
                def _(across=across, stage=stage):
                    go_on(paired + across, 2, stage)

        @pl.when(step == 0)
        def _():
            for index in range(5, len(parts)):
                for copy in copies(index):
                    copy.wait()

        for tile in range(hidden):

            @pl.when(step == tile // 2)
            def _(tile=tile):
                for part in range(3):
                    first = ATTENTION + part * FC + tile * LANES
                    block = merged[:, first : first + LANES].astype(bf16)
                    if tile < EARLY:
                        start = (part * EARLY + tile) * LANES
                        early_ref[:, start : start + LANES] = block
                    else:
                        late_ref[tile - EARLY, :, part * LANES : (part + 1) * LANES] = block


def gathered_weights(w_qk, w_value, w_out, w_gu, w_down, small):
    owned = w_qk.shape[0]
    rows, tiles = CORES * owned, ATTENTION // LANES
    dma = pltpu.SemaphoreType.DMA
    vmem = pl.BlockSpec(memory_space=pltpu.VMEM)
    full, late, early = pl.pallas_call(
        gather_kernel,
        out_shape=[
            jax.ShapeDtypeStruct((2, 2, 2, 2, rows, ATTENTION), bf16),
            jax.ShapeDtypeStruct((FC // LANES - EARLY, rows, 3 * LANES), bf16),
            jax.ShapeDtypeStruct((rows, 3 * EARLY * LANES), bf16),
        ],
        in_specs=[vmem] * 6,
        out_specs=[vmem] * 3,
        scratch_shapes=[
            pltpu.VMEM((rows, ATTENTION + 3 * FC), f32),
            dma((4, tiles)),
            dma((4, tiles)),
            dma((8,)),
            dma((8,)),
            dma((8,)),
        ],
        compiler_params=pltpu.CompilerParams(
            collective_id=1, has_side_effects=True, vmem_limit_bytes=48 << 20
        ),
        cost_estimate=pl.CostEstimate(flops=0, bytes_accessed=1024, transcendentals=0),
    )(w_qk, w_value, w_out, w_gu, w_down, small)
    return full.reshape(D, ATTENTION), late, early


SLOTS = 10
ACROSS = 3


def feed_forward_kernel(
    tiles,
    second_ref,
    grad_ref,
    shard_ref,
    early_ref,
    gate_send_ref,
    gate_keep_ref,
    up_send_ref,
    up_keep_ref,
    down_a_send_ref,
    down_a_keep_ref,
    down_b_send_ref,
    down_b_keep_ref,
    down_own_ref,
    down_other_ref,
    second_own_ref,
    second_other_ref,
    held,
    down_ref,
    grad_second_ref,
    second_t_ref,
    grad_t_ref,
    narrow,
    terms,
    send_sem,
    recv_sem,
    out_sem,
    terms_sem,
    early_sem,
):
    y, x, z, core = places_of()
    streamed = shard_ref.shape[0]
    ready = tiles - streamed
    paired = streamed - ACROSS
    before_across = (ready + paired) // 2 - 2
    count = (tiles + 1) // 2

    def pair_of(turn):
        within = turn - before_across
        between = jnp.where(within % 2 == 0, count - 2 + within // 2, before_across + within // 2)
        return jnp.where(within < 0, turn, between)

    def early_copies(pair):
        copies = []
        for at in range(2):
            for part in range(3):
                start = (part * ready + 2 * pair + at) * LANES
                copies.append(
                    pltpu.make_async_copy(
                        early_ref.at[:, :, :, :, :, start : start + LANES],
                        held.at[SLOTS - 2 + at, :, :, :, :, :, part * LANES : (part + 1) * LANES],
                        early_sem.at[at, part],
                    )
                )
        return copies

    if ready:
        for copy in early_copies(0):
            copy.start()
    down_ref[...] = jnp.zeros_like(down_ref)
    grad_second_ref[...] = jnp.zeros_like(grad_second_ref)
    greet(y, x, z, core)
    tokens = second_ref.shape[0]
    block = 512 if tokens % 512 == 0 else tokens

    def transfer(stage, tile, order):
        slot = SLOTS + tile if order == 2 else tile % SLOTS
        view = gather_view(held.at[slot], order, stage, y, x, z)
        return pltpu.make_async_remote_copy(
            src_ref=view,
            dst_ref=view,
            send_sem=send_sem.at[stage, slot],
            recv_sem=recv_sem.at[stage, slot],
            device_id=mesh_exchange(y, x, z, core, GATHER_ORDERS[order][stage]),
            device_id_type=pl.DeviceIdType.MESH,
        )


    def compute(slots):
        def both(part):
            lanes = slice(part * LANES, (part + 1) * LANES)
            return jnp.concatenate(
                [held[slot, :, :, :, :, :, lanes].reshape(D, LANES) for slot in slots], axis=1
            )

        @pl.loop(0, tokens // block)
        def _(at):
            rows = pl.ds(pl.multiple_of(at * block, block), block)
            gate = dot(second_ref[rows, :], both(0))
            upward = dot(second_ref[rows, :], both(1))
            grad_hidden = dot(grad_ref[rows, :], both(2))
            sigmoid_gate = 1.0 / (1.0 + jnp.exp(-gate))
            silu_gate = gate * sigmoid_gate
            narrow[rows, 2 * WIDE :] = (silu_gate * upward).astype(bf16)
            narrow[rows, WIDE : 2 * WIDE] = (grad_hidden * silu_gate).astype(bf16)
            narrow[rows, :WIDE] = (
                grad_hidden * upward * sigmoid_gate * (1.0 + gate * (1.0 - sigmoid_gate))
            ).astype(bf16)
            down_ref[rows, :] += dot_nt(narrow[rows, 2 * WIDE :], both(2))
            grad_second_ref[rows, :] += dot_nt(narrow[rows, :WIDE], both(0)) + dot_nt(
                narrow[rows, WIDE : 2 * WIDE], both(1)
            )

    quarter = D // 4

    def weight_terms(turn):
        slot = turn % 2

        @pl.loop(0, 4)
        def _(part):
            rows = pl.ds(pl.multiple_of(part * quarter, quarter), quarter)
            grads = dot(second_t_ref[rows, :], narrow[:, : 2 * WIDE])
            terms[slot, part // 2, part % 2, :, : 2 * WIDE] = grads.astype(bf16)
            down = dot(grad_t_ref[rows, :], narrow[:, 2 * WIDE :])
            terms[slot, part // 2, part % 2, :, 2 * WIDE :] = down.astype(bf16)

    def terms_copies(turn):
        slot, pair = turn % 2, pair_of(turn)
        gate, up = (gate_send_ref, gate_keep_ref), (up_send_ref, up_keep_ref)
        first, second = (down_a_send_ref, down_a_keep_ref), (down_b_send_ref, down_b_keep_ref)

        def apart(index, stream, refs, at):
            here = (y, x)[stream]
            columns = pl.ds(pl.multiple_of(at * WIDE, WIDE), WIDE)
            copies = []
            for way, (place, ref) in enumerate(zip((1 - here, here), refs)):
                source = terms.at[slot, :, :, :, index * WIDE : (index + 1) * WIDE]
                source = source.at[place] if stream == 0 else source.at[:, place]
                copies.append(
                    pltpu.make_async_copy(source, ref.at[:, :, columns], terms_sem.at[slot, index, way])
                )
            return copies

        split = (tiles + 1) // 4
        early = pair < split
        return (
            (None, apart(0, 0, gate, pair)),
            (None, apart(1, 1, up, pair)),
            (early, apart(2, 0, first, jnp.where(early, pair, 0))),
            (pair >= split, apart(2, 1, second, jnp.where(early, 0, pair - split))),
        )

    def all_copies(turn, act):
        for condition, copies in terms_copies(turn):
            if condition is None:
                for copy in copies:
                    act(copy)
            else:

                @pl.when(condition)
                def _(copies=copies):
                    for copy in copies:
                        act(copy)

    pairs = paired // 2

    def each(step, behind, act):
        for order in range(2):
            tile = 2 * (step - behind) + order

            @pl.when((tile >= 0) & (tile < paired))
            def _(tile=tile, order=order):
                act(tile, order)

    def send_on(stage):
        def act(tile, order):
            transfer(stage, tile, order).wait()
            transfer(stage + 1, tile, order).start()

        return act

    def work(slots, turn):
        compute(slots)

        @pl.when(turn >= 2)
        def _():
            all_copies(turn - 2, lambda copy: copy.wait())

        weight_terms(turn)
        all_copies(turn, lambda copy: copy.start())

    def begin(tile, order):
        held[tile % SLOTS, y, x, z // 2, z % 2] = shard_ref[tile]
        transfer(0, tile, order).start()

    def work_of(step, across):
        late, first = step - 4, step == pairs + 1
        turn = ready // 2 + late
        turn = jnp.where(turn >= before_across, 2 * turn - before_across + 1, turn)
        turn = jnp.where(step < 4, step - 4 + ready // 2, turn)
        slots = [
            jnp.where(step < 4, SLOTS - 2 + order, (2 * late + order + 2 * SLOTS) % SLOTS)
            for order in range(2)
        ]
        others = (jnp.where(first, SLOTS, SLOTS + 2), jnp.where(first, SLOTS + 1, 2))
        slots = [jnp.where(across == 1, there, here) for here, there in zip(slots, others)]
        return slots, jnp.where(across == 1, before_across + 2 * (step - pairs - 1), turn)

    def begin_across(tile):
        held[SLOTS + tile, y, x, z // 2, z % 2] = shard_ref[paired + tile]
        transfer(0, tile, 2).start()

    def advance_across(step):
        for tile in range(ACROSS):

            @pl.when(step == 2 * tile)
            def _(tile=tile):
                begin_across(tile)

            for stage in range(4):

                @pl.when(step == 2 * tile + stage + 1)
                def _(tile=tile, stage=stage):
                    transfer(stage, tile, 2).wait()
                    if stage < 3:
                        transfer(stage + 1, tile, 2).start()

    @pl.loop(0, pairs + 4)
    def _(step):
        each(step, 2, send_on(1))
        each(step, 3, send_on(2))
        advance_across(step)
        for pair in range(ready // 2):

            @pl.when(step == 4 - ready // 2 + pair)
            def _(pair=pair):
                for copy in early_copies(pair):
                    copy.wait()

        @pl.when(step >= 4)
        def _():
            for order in range(2):
                transfer(3, 2 * (step - 4) + order, order).wait()

        @pl.when(step == pairs + 2)
        def _():
            held[2] = jnp.zeros(held.shape[1:], bf16)

        works = jnp.where((step == pairs + 1) | (step == pairs + 2), 2, 1)

        @pl.loop(0, 2)
        def _(across):
            @pl.when((step >= 4 - ready // 2) & (across < works))
            def _():
                slots, turn = work_of(step, across)
                work(slots, turn)

        for pair in range(ready // 2 - 1):

            @pl.when(step == 4 - ready // 2 + pair)
            def _(pair=pair):
                for copy in early_copies(pair + 1):
                    copy.start()

        each(step, 1, send_on(0))
        each(step, 0, begin)

        @pl.when(step < 2)
        def _():
            rows = pl.ds(pl.multiple_of(step * (tokens // 2), tokens // 2), tokens // 2)
            second_t_ref[:, rows] = second_ref[rows, :].T
            grad_t_ref[:, rows] = grad_ref[rows, :].T

    @pl.loop(count - 2, count)
    def _(turn):
        all_copies(turn, lambda copy: copy.wait())

    half = tokens // 2
    copies = [
        pltpu.make_async_copy(source, target, out_sem.at[at])
        for at, (source, target) in enumerate(
            (
                (grad_second_ref.at[half:], second_other_ref),
                (grad_second_ref.at[:half], second_own_ref),
                (down_ref.at[half:], down_other_ref),
                (down_ref.at[:half], down_own_ref),
            )
        )
    ]
    for copy in copies:
        copy.start()
    for copy in copies:
        copy.wait()


EARLY = 4


def feed_forward(second, grad_result, shard, early):
    tokens = second.shape[0]
    streamed, rows, _ = shard.shape
    tiles = streamed + early.shape[-1] // (3 * LANES)
    down_a = (tiles + 1) // 2
    terms = [
        jax.ShapeDtypeStruct((2, D // 4, count * LANES), bf16)
        for count in (tiles + 1, tiles + 1, down_a, down_a)
        for _ in range(2)
    ]
    part = jax.ShapeDtypeStruct((tokens // 2, D), f32)
    dma = pltpu.SemaphoreType.DMA
    results = pl.pallas_call(
        functools.partial(feed_forward_kernel, tiles),
        out_shape=terms + [part] * 4,
        in_specs=[pl.BlockSpec(memory_space=pltpu.VMEM)] * 3 + [pl.BlockSpec(memory_space=pl.ANY)],
        out_specs=[pl.BlockSpec(memory_space=pl.ANY)] * 12,
        scratch_shapes=[
            pltpu.VMEM((SLOTS + ACROSS, 2, 2, 2, 2, rows, 3 * LANES), bf16),
            pltpu.VMEM((tokens, D), f32),
            pltpu.VMEM((tokens, D), f32),
            pltpu.VMEM((D, tokens), bf16),
            pltpu.VMEM((D, tokens), bf16),
            pltpu.VMEM((tokens, 3 * WIDE), bf16),
            pltpu.VMEM((2, 2, 2, D // 4, 3 * WIDE), bf16),
            dma((4, SLOTS + ACROSS)),
            dma((4, SLOTS + ACROSS)),
            dma((4,)),
            dma((2, 3, 2)),
            dma((2, 3)),
        ],
        compiler_params=pltpu.CompilerParams(
            collective_id=2, has_side_effects=True, vmem_limit_bytes=60 << 20
        ),
        cost_estimate=pl.CostEstimate(flops=0, bytes_accessed=1024, transcendentals=0),
    )(second, grad_result, shard, early)
    return list(zip(results[0:8:2], results[1:8:2])), results[8:]


def norm_scale(values):
    inverse = lax.rsqrt(jnp.mean(values * values, axis=-1, keepdims=True) + norm_epsilon)
    return (values * inverse, inverse)


def norm_backward(grad_normed, scaled, inverse, gain_row):
    grad_scaled = grad_normed * gain_row[None, :]
    grad_input = inverse * (
        grad_scaled - scaled * jnp.mean(grad_scaled * scaled, axis=-1, keepdims=True)
    )
    return (grad_input, jnp.sum(grad_normed * scaled, axis=0))


def adam_update(weight, gradient, first_moment, second_moment, learn_rate, decay_rate):
    first_new = beta_first * first_moment + (1.0 - beta_first) * gradient
    second_new = beta_second * second_moment + (1.0 - beta_second) * gradient * gradient
    first_hat = first_new / (1.0 - beta_first**STEP)
    second_hat = second_new / (1.0 - beta_second**STEP)
    new_weight = (
        weight
        - learn_rate * first_hat / (jnp.sqrt(second_hat) + adam_epsilon)
        - decay_rate * weight
    )
    return (new_weight, second_new)


def local(
    tokens,
    cotangent,
    lengths,
    w_qk,
    w_value,
    w_out,
    w_gu,
    w_down,
    small_params,
    m_qk,
    m_value,
    m_out,
    m_gu,
    m_down,
    m_small,
    v_qk,
    v_value,
    v_out,
    v_gu,
    v_down,
    v_small,
):
    slots, slot_rows, _ = tokens.shape
    owned = w_qk.shape[0]
    rows = slots * slot_rows
    core, z_at = lax.axis_index("core"), lax.axis_index("z")
    other = 1 - core
    first_core = core == 0

    def on_chip(array):
        return jnp.concatenate([array, swapped(array)], axis=0)

    def halves(array):
        return array.reshape(CORES, slots, slot_rows, -1)

    columns_of = [
        w_qk.astype(bf16).reshape(owned, 2, CORES, QC),
        w_value.astype(bf16).reshape(owned, 1, CORES, VC),
        w_out.astype(bf16).reshape(owned, 1, CORES, VC),
        w_gu.astype(bf16).reshape(owned, 2, CORES, FC),
        w_down.astype(bf16).reshape(owned, 1, CORES, FC),
    ]
    small_low = jnp.pad(small_params.astype(bf16), ((0, 0), (0, LANES - (KS + 2))))

    def shard(which, index):
        parts = [part_of(columns_of[i], 2, index).reshape(owned, -1) for i in which]
        return jnp.concatenate(parts, axis=1) if len(parts) > 1 else parts[0]

    def chip_shard(which, extra=None):
        mine, theirs = shard(which, core), shard(which, other)
        arrived = swapped(theirs if extra is None else jnp.concatenate([theirs, extra], axis=1))
        mine = mine if extra is None else jnp.concatenate([mine, extra], axis=1)
        return both_cores(mine, arrived, 0)

    in_kernel = tuple(lax.axis_size(axis) for axis in ("y", "x", "z")) == (2, 2, 4)
    early_width = 2 * QC + VC + LANES
    half = early_width // 2
    cut = FC // 2 // LANES * LANES
    down_at = VC + 2 * FC
    own_tokens = tokens.reshape(rows, D)
    other_tokens = swapped(own_tokens)
    wide_part = 4 * LANES
    if in_kernel:
        small_wide = jnp.pad(small_params, ((0, 0), (0, LANES - (KS + 2))))
        full, late_shard, early_shard = gathered_weights(
            w_qk, w_value, w_out, w_gu, w_down, small_wide
        )
        early, out_half = full[:, :early_width], full[:, early_width:]
        small_full = early[:, early_width - LANES :]
        early_tiles = lax.all_gather(early_shard, ("y", "x", "z"), axis=0)
        early_tiles = early_tiles.reshape(2, 2, 2, 2, CORES * owned, -1)
    else:
        attention_shard = chip_shard((0, 1), small_low)
        rest_shard = chip_shard((2, 3, 4))
        early_a = Gather(attention_shard[:, :half], True)
        early_b = Gather(attention_shard[:, half:], False)
        early = jnp.concatenate([early_a.rest(), early_b.rest()], axis=1)

        def gathered(start, width):
            return lax.all_gather(rest_shard[:, start : start + width], ("y", "x", "z"), axis=0, tiled=True)

        out_half = gathered(0, VC)
        gate_full = gathered(VC, FC)
        up_full = gathered(VC + FC, FC)
        last_shard, early = tied(rest_shard[:, down_at:], early)
        down_a = Gather(last_shard[:, :cut], True)
        down_b = Gather(last_shard[:, cut:], False)
        down_full = jnp.concatenate([down_a.rest(), down_b.rest()], axis=1)
        small_full = early[:, early_width - LANES :]

    qk_full = early[:, : 2 * QC]
    value_full = early[:, 2 * QC : 2 * QC + VC]
    small_float = small_full[:, : KS + 2].astype(f32)
    out_full = both_cores(out_half, swapped(out_half), 1)
    gain_first, gain_second = small_float[:, KS], small_float[:, KS + 1]
    taps = [part_of(small_float[:, j].reshape(CORES, VC), 0, core) for j in range(KS)]

    inputs = tokens.reshape(rows, D).astype(f32)
    scaled_first, inverse_first = norm_scale(inputs)
    scaled_chip, _ = norm_scale(
        jnp.concatenate([own_tokens, other_tokens], axis=0).astype(f32)
    )
    normed_chip = (scaled_chip * gain_first[None, :]).astype(bf16)
    query_key = halves(dot(normed_chip, qk_full).astype(bf16))
    value_pre = halves(dot(normed_chip, value_full).astype(bf16))
    tail = value_pre[:, :, slot_rows - (KS - 1) :, :]
    from_chip = passed_along(part_of(tail, 0, other), "z", 1)
    from_core = part_of(tail, 0, core)
    earlier = jnp.stack(
        [jnp.where(first_core, from_chip, from_core), jnp.where(first_core, from_core, from_chip)]
    )
    extended = jnp.concatenate([earlier, value_pre], axis=2).astype(f32)

    def tap_rows(j):
        return extended[:, :, KS - 1 - j : KS - 1 - j + slot_rows, :]

    convolved = taps[0] * tap_rows(0)
    for j in range(1, KS):
        convolved = convolved + taps[j] * tap_rows(j)
    values = convolved.astype(bf16)

    index_np, scale_np = feature_tables()
    tables = (core.astype(jnp.int32).reshape(1), jnp.asarray(index_np), jnp.asarray(scale_np))
    q_spec, k_spec, v_spec = (LANES, 0), (LANES, 1), (VC,)
    call = functools.partial(per_slot, slots=slots, rows=slot_rows)
    unit = 2 * CORES * rows * HC * LANES * FEATS
    wide = [pltpu.VMEM((CORES * slot_rows, VC), f32)]
    if in_kernel:
        (before,) = linked(key_term, True, 3)(*tables[1:], query_key, values, slots=slots)
    else:
        (state_own,) = call(
            state_kernel, ins=[k_spec, v_spec], outs=[("state", f32)], scratch=[], flops=4 * unit
        )(*tables, query_key, values)
        before = chain(state_own, True)
    mixer, dens = call(
        forward_kernel,
        ins=[q_spec, k_spec, v_spec, "state"],
        outs=[(v_spec, bf16), ((LANES,), f32)],
        scratch=wide,
        flops=8 * unit,
    )(*tables, query_key, query_key, values, before)

    mixer_flat = mixer.reshape(CORES * rows, VC)
    mixer_theirs = swapped(mixer_flat)

    def beside(mine, theirs):
        whole = jnp.zeros((mine.shape[0], CORES * mine.shape[1]), mine.dtype)
        for index, part in ((core, mine), (other, theirs)):
            whole = lax.dynamic_update_slice_in_dim(whole, part, index * mine.shape[1], 1)
        return whole

    mixer_own = beside(mixer_flat[:rows], mixer_theirs[rows:])
    mixer_other = beside(mixer_flat[rows:], mixer_theirs[:rows])
    after_mixer = inputs + dot(mixer_own, out_full)
    scaled_second, inverse_second = norm_scale(after_mixer)
    second_low = (scaled_second * gain_second[None, :]).astype(bf16)
    second_chip = on_chip(second_low)

    half_at = jnp.where(first_core, jnp.arange(CORES), 1 - jnp.arange(CORES))
    positions = (z_at * CORES + half_at)[:, None] * slot_rows + jnp.arange(slot_rows)[None, :]
    valid_chip = positions[:, None, :] < lengths[None, :, None]
    valid_chip = valid_chip.astype(f32).reshape(CORES * rows, 1)
    valid = valid_chip[:rows]
    query_key, cotangent_late = lax.optimization_barrier((query_key, cotangent))
    cotangent_chip = on_chip(cotangent_late.reshape(rows, D))
    mixer, cotangent_chip = tied(mixer, cotangent_chip)
    grad_result_chip = (valid_chip * cotangent_chip.astype(f32)).astype(bf16)
    grad_result = valid * cotangent.reshape(rows, D).astype(f32)

    if in_kernel:
        ffn_terms, ffn_parts = feed_forward(
            second_chip, grad_result_chip, late_shard, early_tiles
        )
        down_own, down_other, second_own, second_other = ffn_parts
        grad_second = second_own + swapped(second_other)
        down_result = down_own + swapped(down_other)
        (send_gate, keep_gate), (send_up, keep_up), *down_pairs = ffn_terms
        (send_down_a, keep_down_a), (send_down_b, keep_down_b) = down_pairs
        got_gate, got_up = exchanged(send_gate, "y", 0), exchanged(send_up, "x", 0)
    else:
        gate = dot(second_chip, gate_full)
        upward = dot(second_chip, up_full)
        sigmoid_gate = jax.nn.sigmoid(gate)
        silu_gate = gate * sigmoid_gate
        hidden = (silu_gate * upward).astype(bf16)
        grad_hidden = dot(grad_result_chip, down_full)
        grad_upward = (grad_hidden * silu_gate).astype(bf16)
        grad_gate = (
            grad_hidden * upward * sigmoid_gate * (1.0 + gate * (1.0 - sigmoid_gate))
        ).astype(bf16)
        second_part = dot_nt(grad_gate, gate_full) + dot_nt(grad_upward, up_full)
        grad_second = second_part[:rows] + swapped(second_part[rows:])
        down_part = dot_nt(hidden, down_full)
        down_result = down_part[:rows] + swapped(down_part[rows:])
    layer_out = (valid * (after_mixer + down_result)).astype(bf16).reshape(tokens.shape)

    grad_after_norm, grad_gain_second = norm_backward(
        grad_second, scaled_second, inverse_second, gain_second
    )
    grad_after = grad_result + grad_after_norm
    grad_after_low = grad_after.astype(bf16)
    grad_mixer = dot_nt(grad_after_low, out_full).astype(bf16)

    def core_columns(array):
        mine, theirs = (
            lax.dynamic_slice_in_dim(array, index * VC, VC, axis=1) for index in (core, other)
        )
        return jnp.concatenate([mine, swapped(theirs)], axis=0)

    grad_mixer_chip = core_columns(grad_mixer)
    grad_after_chip = core_columns(grad_after_low)
    mixer_chip = lax.optimization_barrier(jnp.concatenate([mixer_own, mixer_other], axis=0))

    wide_spec = (HC * LANES,)
    if in_kernel:
        grad_num, from_later = linked(query_term, False, 4)(
            *tables[1:],
            query_key,
            halves(grad_mixer_chip),
            mixer,
            dens,
            slots=slots,
            extra=(jax.ShapeDtypeStruct((CORES, slots, slot_rows, HC * LANES), bf16),),
        )
    else:
        pulled, grad_num = call(
            pull_kernel,
            ins=[q_spec, v_spec, v_spec, (LANES,)],
            outs=[("state", f32), (wide_spec, bf16)],
            scratch=[],
            flops=4 * unit,
        )(*tables, query_key, halves(grad_mixer_chip), mixer, dens)
        from_later = chain(pulled, False)
    grad_query_key, grad_values = call(
        backward_kernel,
        ins=[q_spec, k_spec, v_spec, wide_spec, "state", "state"],
        outs=[((2 * LANES,), bf16), (v_spec, bf16)],
        scratch=wide,
        flops=24 * unit,
    )(*tables, query_key, query_key, values, grad_num, before, from_later)

    if in_kernel:
        got_gate, got_up, send_down_a, send_down_b, grad_values = tied(
            got_gate, got_up, send_down_a, send_down_b, grad_values
        )

        def summed(keep, got):
            return (keep.astype(f32) + got.astype(f32)).astype(bf16)

        sum_gate, sum_up = summed(keep_gate, got_gate), summed(keep_up, got_up)
        sum_down_a = summed(keep_down_a, exchanged(send_down_a, "y", 0))
        sum_down_b = summed(keep_down_b, exchanged(send_down_b, "x", 0))
    head = grad_values[:, :, : KS - 1, :]
    from_chip = passed_along(part_of(head, 0, core), "z", -1)
    from_core = part_of(head, 0, other)
    later = jnp.stack(
        [jnp.where(first_core, from_core, from_chip), jnp.where(first_core, from_chip, from_core)]
    )
    grad_extended = jnp.concatenate([grad_values, later], axis=2).astype(f32)
    grad_pre = taps[0] * grad_extended[:, :, :slot_rows, :]
    for j in range(1, KS):
        grad_pre = grad_pre + taps[j] * grad_extended[:, :, j : j + slot_rows, :]
    grad_pre = grad_pre.reshape(CORES * rows, VC).astype(bf16)
    grad_query_key = grad_query_key.reshape(CORES * rows, 2 * QC)
    grad_values_float = grad_values.astype(f32)
    tap_grads = [jnp.sum(grad_values_float * tap_rows(j), axis=(0, 1, 2)) for j in range(KS)]

    first_other = dot_nt(grad_query_key[rows:], qk_full) + dot_nt(grad_pre[rows:], value_full)
    first_own = dot_nt(grad_query_key[:rows], qk_full) + dot_nt(grad_pre[:rows], value_full)
    grad_first = first_own + swapped(first_other)
    grad_gain_first = jnp.sum(first_own * scaled_chip[:rows], axis=0) + jnp.sum(
        first_other * scaled_chip[rows:], axis=0
    )

    def whole_feature(part):
        return lax.dynamic_update_slice(jnp.zeros((D,), f32), part, (core * VC,))

    small_terms = jnp.stack(
        [whole_feature(part) for part in tap_grads] + [grad_gain_first, grad_gain_second], axis=1
    )
    small_terms = jnp.pad(small_terms, ((0, 0), (0, LANES - (KS + 2)))).astype(bf16)
    if in_kernel:
        empty = jnp.zeros((CORES * rows, LANES), bf16)
        last_a = jnp.concatenate([grad_pre, grad_query_key, empty], axis=1)
        last_b = jnp.concatenate([grad_after_chip, empty], axis=1)
        grad_qk_own, grad_value_own, grad_out_own, grad_gu_own, grad_down_own, small_both = reduced(
            sum_down_a,
            sum_gate,
            sum_down_b,
            sum_up,
            dot_tn(normed_chip, last_a).astype(bf16),
            dot_tn(mixer_chip, last_b).astype(bf16),
            jnp.pad(small_terms, ((0, 0), (0, LANES))),
            owned,
        )
        grad_small_own = (small_both[:, :LANES] + small_both[:, LANES:])[:, : KS + 2]
    else:
        sum_down = Scatter(dot_tn(grad_result_chip, hidden).astype(bf16), True).rest()
        sum_gate = Scatter(dot_tn(second_chip, grad_gate).astype(bf16), False).rest()
        sum_up = Scatter(dot_tn(second_chip, grad_upward).astype(bf16), True).rest()
        sum_value = Scatter(dot_tn(normed_chip, grad_pre).astype(bf16), False).rest()
        sum_out = Scatter(dot_tn(mixer_chip, grad_after_chip).astype(bf16), True).rest()
        qk_terms = dot_tn(normed_chip, grad_query_key).astype(bf16)
        sum_last = Scatter(jnp.concatenate([qk_terms, small_terms], axis=1), True).rest()
    grad_input_norm, _ = norm_backward(grad_first, scaled_first, inverse_first, gain_first)
    input_grad = (grad_after + grad_input_norm).reshape(tokens.shape)

    def rows_of(array, index):
        return part_of(array.reshape(CORES, owned, -1), 0, index)

    def finish(*parts):
        merged = jnp.concatenate(parts, axis=1) if len(parts) > 1 else parts[0]
        mine, theirs = rows_of(merged, core), swapped(rows_of(merged, other))
        return mine.astype(f32), theirs.astype(f32)

    def columns(*parts):
        mine, theirs = finish(*parts)
        return both_cores(mine, theirs, 1)

    def two_columns(mine, theirs, width):
        shape = (owned, 2, 1, width)
        return both_cores(mine.reshape(shape), theirs.reshape(shape), 2).reshape(owned, -1)

    if not in_kernel:
        grad_down_own = columns(sum_down)
        grad_gu_own = two_columns(*finish(sum_gate, sum_up), FC)
        grad_out_own = columns(sum_out)
        grad_value_own = columns(sum_value)
        last_mine, last_theirs = finish(sum_last)
        grad_qk_own = two_columns(last_mine[:, : 2 * QC], last_theirs[:, : 2 * QC], QC)
        grad_small_own = (last_mine + last_theirs)[:, 2 * QC : 2 * QC + KS + 2]

    grads_all = (
        grad_qk_own,
        grad_value_own,
        grad_out_own,
        grad_gu_own,
        grad_down_own,
        grad_small_own,
    )
    masters = (w_qk, w_value, w_out, w_gu, w_down, small_params)
    firsts = (m_qk, m_value, m_out, m_gu, m_down, m_small)
    seconds = (v_qk, v_value, v_out, v_gu, v_down, v_small)
    learn_rates = (
        0.05 / math.sqrt(D),
        0.05 / math.sqrt(D),
        0.05 / math.sqrt(max(D // 128, 1)),
        0.05 / math.sqrt(D),
        0.05 / math.sqrt(0.0003 * FF * SLOT**0.825),
        0.014,
    )
    decays = (weight_decay, weight_decay, weight_decay, weight_decay, weight_decay, 0.0)
    new_weights = []
    new_seconds = []
    for position in range(6):
        updated, moment = adam_update(
            masters[position],
            grads_all[position],
            firsts[position],
            seconds[position],
            learn_rates[position],
            decays[position],
        )
        new_weights.append(updated)
        new_seconds.append(moment)
    return (layer_out, input_grad) + grads_all + tuple(new_weights) + tuple(new_seconds)


def solution(mesh):
    dp, fsdp = mesh.shape["dp"], mesh.shape["fsdp"]
    y_size = 2 if dp % 2 == 0 else 1
    split = Mesh(
        mesh.devices.reshape(y_size, dp // y_size, fsdp // CORES, CORES), ("y", "x", "z", "core")
    )
    slot_axes, row_axes = ("y", "x"), ("z", "core")
    activation = P(slot_axes, row_axes, None)
    weight = P(slot_axes + row_axes, None)
    return jax.shard_map(
        local,
        mesh=split,
        in_specs=(activation, activation, P(slot_axes)) + (weight,) * 18,
        out_specs=(activation, activation) + (weight,) * 18,
        check_vma=False,
    )
```

```python
import functools
import math

import jax
import jax.numpy as jnp
import numpy as np
from jax import lax
from jax.experimental import pallas as pl
from jax.experimental.pallas import tpu as pltpu
from jax.sharding import Mesh
from jax.sharding import PartitionSpec as P

D = 1792
H = 16
F = 16
FF = 4864
KS = 3
SLOT = 2048
STEP = 10

CORES = 2
HC = H // CORES
HW = D // H
VC = HC * HW
QC = HC * F
FC = FF // CORES
LANES = 128
FEATS = 256
FROWS = 160
SCALE = 1.0 / math.sqrt(F)

norm_epsilon = 1e-06
beta_first = 0.9
beta_second = 0.95
adam_epsilon = 1e-08
weight_decay = 3e-05

bf16 = jnp.bfloat16
f32 = jnp.float32


def feature_tables():
    index = np.full((8, FEATS), -4096, np.int32)
    scale = np.zeros((8, FEATS), np.float32)
    scale[0, 0] = scale[1, 0] = scale[2, 0] = 1.0
    at = 1
    for i in range(F):
        index[0, at] = i
        scale[1, at] = 1.0
        scale[2, at] = SCALE
        at += 1
    for i in range(F):
        for j in range(i, F):
            index[0, at] = i
            index[1, at] = j
            scale[2, at] = (1.0 if i == j else 2.0) * 0.5 * SCALE * SCALE
            at += 1
    return index, scale


def dot(a, b):
    return lax.dot_general(a, b, (((1,), (0,)), ((), ())), preferred_element_type=f32)


def dot_nt(a, b):
    return lax.dot_general(a, b, (((1,), (1,)), ((), ())), preferred_element_type=f32)


def dot_tn(a, b):
    return lax.dot_general(a, b, (((0,), (0,)), ((), ())), preferred_element_type=f32)


def selectors(index_ref, head):
    lane = lax.broadcasted_iota(jnp.int32, (LANES, FEATS), 0) - head * F
    first = jnp.where(lane == index_ref[0:1, :], 1.0, 0.0).astype(bf16)
    second = jnp.where(lane == index_ref[1:2, :], 1.0, 0.0).astype(bf16)
    return first, second


def factors(rows, first, second, scale_ref):
    return (dot(rows, first) + scale_ref[0:1, :], dot(rows, second) + scale_ref[1:2, :])


def window(head):
    start = head * HW
    base = min(start // LANES * LANES, VC - 2 * LANES)
    return base, start - base


def both_halves(core_ref, ref, columns):
    core = core_ref[0]
    return jnp.concatenate([ref[core, :, columns], ref[1 - core, :, columns]], axis=0)


def store_halves(core_ref, ref, rows, columns):
    core, half = core_ref[0], rows.shape[0] // CORES
    ref[core, :, columns] = rows[:half]
    ref[1 - core, :, columns] = rows[half:]


def head_columns(core_ref, ref, head):
    base, offset = window(head)
    wide = both_halves(core_ref, ref, slice(base, base + 2 * LANES)).astype(f32)
    if offset:
        wide = pltpu.roll(wide, 2 * LANES - offset, 1)
    return wide[:, :LANES]


def add_head_columns(ref, head, block):
    base, offset = window(head)
    wide = jnp.concatenate([block, jnp.zeros_like(block)], axis=1)
    if offset:
        wide = pltpu.roll(wide, offset, 1)
    ref[:, base : base + 2 * LANES] += wide


def with_one(block):
    lane = lax.broadcasted_iota(jnp.int32, block.shape, 1)
    return jnp.where(lane < HW, block, jnp.where(lane == HW, 1.0, 0.0))


def only_head(rows, head):
    lane = lax.broadcasted_iota(jnp.int32, rows.shape, 1)
    inside = (lane >= head * F) & (lane < head * F + F)
    return jnp.where(inside, rows.astype(f32), 0.0).astype(bf16)


def state_kernel(core_ref, index_ref, scale_ref, k_ref, v_ref, state_ref):
    keys = both_halves(core_ref, k_ref, slice(None))
    for head in range(HC):
        first, second = selectors(index_ref, head)
        one, two = factors(keys, first, second, scale_ref)
        phi = (one * two * scale_ref[2:3, :]).astype(bf16)
        values = with_one(head_columns(core_ref, v_ref, head)).astype(bf16)
        state_ref[0, head] = dot_tn(phi, values)[:FROWS]


def scores_of(q_head, keys):
    scores = dot_nt(q_head, keys) * SCALE
    row = lax.broadcasted_iota(jnp.int32, scores.shape, 0)
    column = lax.broadcasted_iota(jnp.int32, scores.shape, 1)
    return scores, column <= row


def forward_kernel(core_ref, index_ref, scale_ref, q_ref, k_ref, v_ref, before_ref, mixer_ref, den_ref, wide):
    queries = both_halves(core_ref, q_ref, slice(None))
    keys = both_halves(core_ref, k_ref, slice(None))
    wide[...] = jnp.zeros_like(wide)
    lane = lax.broadcasted_iota(jnp.int32, (queries.shape[0], LANES), 1)
    dens = jnp.zeros((queries.shape[0], LANES), f32)
    for head in range(HC):
        first, second = selectors(index_ref, head)
        one, two = factors(queries, first, second, scale_ref)
        phi = (one * two).astype(bf16)
        values = with_one(head_columns(core_ref, v_ref, head)).astype(bf16)
        scores, allowed = scores_of(only_head(queries, head), keys)
        kernel = jnp.where(allowed, 1.0 + scores + 0.5 * scores * scores, 0.0).astype(bf16)
        total = dot(kernel, values) + dot(phi[:, :FROWS], before_ref[0, head])
        den = total[:, HW : HW + 1]
        add_head_columns(wide, head, jnp.where(lane < HW, total / den, 0.0))
        dens = jnp.where(lane == head, den, dens)
    store_halves(core_ref, mixer_ref, wide[...].astype(bf16), slice(None))
    store_halves(core_ref, den_ref, dens, slice(None))


def pull_kernel(core_ref, index_ref, scale_ref, q_ref, gm_ref, mixer_ref, den_ref, state_ref, gnum_ref):
    queries = both_halves(core_ref, q_ref, slice(None))
    lane = lax.broadcasted_iota(jnp.int32, (queries.shape[0], LANES), 1)
    dens = both_halves(core_ref, den_ref, slice(None))
    for head in range(HC):
        first, second = selectors(index_ref, head)
        one, two = factors(queries, first, second, scale_ref)
        phi = (one * two).astype(bf16)
        den = dens[:, head : head + 1]
        grad = jnp.where(lane < HW, head_columns(core_ref, gm_ref, head), 0.0)
        mixer = head_columns(core_ref, mixer_ref, head)
        pulled = -jnp.sum(grad * mixer, axis=1, keepdims=True)
        grad = (jnp.where(lane == HW, pulled, grad) / den).astype(bf16)
        store_halves(core_ref, gnum_ref, grad, slice(head * LANES, (head + 1) * LANES))
        state_ref[0, head] = dot_tn(phi, grad)[:FROWS]


def backward_kernel(
    core_ref, index_ref, scale_ref, q_ref, k_ref, v_ref, gnum_ref, before_ref, after_ref, gqk_ref, gv_ref, wide
):
    queries = both_halves(core_ref, q_ref, slice(None))
    keys = both_halves(core_ref, k_ref, slice(None))
    wide[...] = jnp.zeros_like(wide)
    lane = lax.broadcasted_iota(jnp.int32, (queries.shape[0], LANES), 1)
    grad_q = jnp.zeros((queries.shape[0], LANES), f32)
    grad_k = jnp.zeros((queries.shape[0], LANES), f32)
    for head in range(HC):
        first, second = selectors(index_ref, head)
        coef = scale_ref[2:3, :]
        q_one, q_two = factors(queries, first, second, scale_ref)
        k_one, k_two = factors(keys, first, second, scale_ref)
        values = with_one(head_columns(core_ref, v_ref, head)).astype(bf16)
        gnum = both_halves(core_ref, gnum_ref, slice(head * LANES, (head + 1) * LANES))
        q_head = only_head(queries, head)
        k_head = only_head(keys, head)
        scores, allowed = scores_of(q_head, keys)
        kernel = jnp.where(allowed, 1.0 + scores + 0.5 * scores * scores, 0.0).astype(bf16)
        grad_kernel = dot_nt(gnum, values)
        grad_scores = (jnp.where(allowed, grad_kernel * (1.0 + scores), 0.0) * SCALE).astype(bf16)
        phi_k = (k_one * k_two * coef).astype(bf16)
        after = after_ref[0, head]
        before = before_ref[0, head]
        grad_v = dot_tn(kernel, gnum) + dot(phi_k[:, :FROWS], after)
        add_head_columns(wide, head, jnp.where(lane < HW, grad_v, 0.0))
        empty = jnp.zeros((FEATS - FROWS, LANES), bf16)
        grad_phi_q = dot_nt(gnum, jnp.concatenate([before, empty], axis=0))
        grad_phi_k = dot_nt(values, jnp.concatenate([after, empty], axis=0)) * coef
        grad_q += dot(grad_scores, k_head)
        grad_q += dot_nt((grad_phi_q * q_two).astype(bf16), first)
        grad_q += dot_nt((grad_phi_q * q_one).astype(bf16), second)
        grad_k += dot_tn(grad_scores, q_head)
        grad_k += dot_nt((grad_phi_k * k_two).astype(bf16), first)
        grad_k += dot_nt((grad_phi_k * k_one).astype(bf16), second)
    store_halves(core_ref, gqk_ref, grad_q.astype(bf16), slice(0, LANES))
    store_halves(core_ref, gqk_ref, grad_k.astype(bf16), slice(LANES, 2 * LANES))
    store_halves(core_ref, gv_ref, wide[...].astype(bf16), slice(None))


def per_slot(kernel, slots, rows, ins, outs, scratch, flops):
    def table():
        return pl.BlockSpec((8, FEATS), lambda s, core: (0, 0))

    def row_spec(width, column=0):
        return pl.BlockSpec((CORES, None, rows, width), lambda s, core: (0, s, 0, column))

    def state_spec():
        return pl.BlockSpec((1, HC, FROWS, LANES), lambda s, core: (s, 0, 0, 0))

    def spec(kind):
        return state_spec() if kind == "state" else row_spec(*kind)

    def shape(kind, dtype):
        if kind == "state":
            return jax.ShapeDtypeStruct((slots, HC, FROWS, LANES), dtype)
        return jax.ShapeDtypeStruct((CORES, slots, rows, kind[0]), dtype)

    return pl.pallas_call(
        kernel,
        grid_spec=pltpu.PrefetchScalarGridSpec(
            num_scalar_prefetch=1,
            grid=(slots,),
            in_specs=[table(), table()] + [spec(kind) for kind in ins],
            out_specs=[spec(kind) for kind, _ in outs],
            scratch_shapes=scratch,
        ),
        out_shape=[shape(kind, dtype) for kind, dtype in outs],
        compiler_params=pltpu.CompilerParams(vmem_limit_bytes=56 << 20),
        cost_estimate=pl.CostEstimate(flops=flops, bytes_accessed=8 << 20, transcendentals=0),
    )


def linked(kernel, up, ids):
    def run(*refs):
        y, x, z, core = places_of()
        last = lax.axis_size("z") - 1
        *refs, sent, send_sem, recv_sem = refs
        total_ref = refs[-1]
        by = 1 if up else last
        receives, sends = (z > 0, z < last) if up else (z < last, z > 0)

        barrier = pltpu.get_barrier_semaphore()
        for step in (1, last):
            pl.semaphore_signal(
                barrier,
                inc=1,
                device_id=(y, x, lax.rem(z + step, last + 1), core),
                device_id_type=pl.DeviceIdType.MESH,
            )
        pl.semaphore_wait(barrier, 2)

        def transfer(slot, head):
            return pltpu.make_async_remote_copy(
                src_ref=sent.at[slot, head],
                dst_ref=total_ref.at[slot, head],
                send_sem=send_sem.at[slot, head],
                recv_sem=recv_sem.at[slot, head],
                device_id=(y, x, lax.rem(z + by, last + 1), core),
                device_id_type=pl.DeviceIdType.MESH,
            )

        @pl.when(jnp.logical_not(receives))
        def _():
            total_ref[...] = jnp.zeros_like(total_ref)

        @pl.loop(0, sent.shape[0])
        def _(slot):
            for head in range(HC):
                term = kernel([core], slot, head, *refs[:-1])

                @pl.when(receives)
                def _(head=head):
                    transfer(slot, head).wait_recv()

                @pl.when(sends)
                def _(head=head, term=term):
                    sent[slot, head] = (total_ref[slot, head].astype(f32) + term).astype(bf16)
                    transfer(slot, head).start()

        @pl.when(sends)
        def _():
            @pl.loop(0, sent.shape[0])
            def _(slot):
                for head in range(HC):
                    transfer(slot, head).wait_send()

    def call(*operands, slots, extra=()):
        state = jax.ShapeDtypeStruct((slots, HC, FROWS, LANES), bf16)
        vmem = pl.BlockSpec(memory_space=pltpu.VMEM)
        return pl.pallas_call(
            run,
            out_shape=list(extra) + [state],
            in_specs=[vmem] * len(operands),
            out_specs=[vmem] * (len(extra) + 1),
            scratch_shapes=[
                pltpu.VMEM((slots, HC, FROWS, LANES), bf16),
                pltpu.SemaphoreType.DMA((slots, HC)),
                pltpu.SemaphoreType.DMA((slots, HC)),
            ],
            compiler_params=pltpu.CompilerParams(
                collective_id=ids, has_side_effects=True, vmem_limit_bytes=40 << 20
            ),
            cost_estimate=pl.CostEstimate(flops=0, bytes_accessed=1024, transcendentals=0),
        )(*operands)

    return call


def key_term(core_ref, slot, head, index_ref, scale_ref, qk_ref, v_ref):
    keys = both_halves(core_ref, qk_ref.at[:, slot], slice(LANES, 2 * LANES))
    first, second = selectors(index_ref, head)
    one, two = factors(keys, first, second, scale_ref)
    phi = (one * two * scale_ref[2:3, :]).astype(bf16)
    values = with_one(head_columns(core_ref, v_ref.at[:, slot], head)).astype(bf16)
    return dot_tn(phi, values)[:FROWS]


def query_term(core_ref, slot, head, index_ref, scale_ref, qk_ref, gm_ref, mixer_ref, den_ref, gnum_ref):
    queries = both_halves(core_ref, qk_ref.at[:, slot], slice(0, LANES))
    first, second = selectors(index_ref, head)
    one, two = factors(queries, first, second, scale_ref)
    phi = (one * two).astype(bf16)
    den = both_halves(core_ref, den_ref.at[:, slot], slice(None))[:, head : head + 1]
    lane = lax.broadcasted_iota(jnp.int32, (queries.shape[0], LANES), 1)
    grad = jnp.where(lane < HW, head_columns(core_ref, gm_ref.at[:, slot], head), 0.0)
    mixer = head_columns(core_ref, mixer_ref.at[:, slot], head)
    pulled = -jnp.sum(grad * mixer, axis=1, keepdims=True)
    grad = (jnp.where(lane == HW, pulled, grad) / den).astype(bf16)
    store_halves(core_ref, gnum_ref.at[:, slot], grad, slice(head * LANES, (head + 1) * LANES))
    return dot_tn(phi, grad)[:FROWS]


def passed_along(array, axis, by):
    count = lax.axis_size(axis)
    pairs = [(i, i + by) for i in range(count) if 0 <= i + by < count]
    return lax.ppermute(array, axis, pairs)


def both_cores(mine, theirs, axis):
    first = lax.axis_index("core") == 0
    return jnp.concatenate(
        [jnp.where(first, mine, theirs), jnp.where(first, theirs, mine)], axis=axis
    )


def swapped(array):
    return lax.ppermute(array, "core", [(0, 1), (1, 0)])


def part_of(array, axis, index):
    return lax.dynamic_index_in_dim(array, index, axis, keepdims=False)


def bits_of(axis):
    return [(axis, bit) for bit in reversed(range(lax.axis_size(axis).bit_length() - 1))]


def bit_at(axis, bit):
    return (lax.axis_index(axis) >> bit) & 1


def exchanged(array, axis, bit):
    count = lax.axis_size(axis)
    return lax.ppermute(array, axis, [(i, i ^ (1 << bit)) for i in range(count)])


def tied(*arrays):
    return lax.optimization_barrier(arrays)


class Gather:
    def __init__(self, piece, x_first):
        self.columns = piece.shape[1]
        self.block = piece
        low_first = lambda axis: bits_of(axis)[::-1]
        self.plan = [(step, at) for at, step in enumerate(bits_of("z"))]
        if x_first:
            self.plan += [(step, 0) for step in low_first("x") + low_first("y")]
        else:
            self.plan += [(step, 0) for step in low_first("y")]
            self.plan += [(step, len(bits_of("y"))) for step in low_first("x")]

    def stage(self):
        (axis, bit), dim = self.plan.pop(0)
        mine = bit_at(axis, bit)
        arrived = exchanged(self.block, axis, bit)
        shape = self.block.shape[:dim] + (2,) + self.block.shape[dim:]
        whole = jnp.zeros(shape, self.block.dtype)
        whole = lax.dynamic_update_index_in_dim(whole, self.block, mine, dim)
        self.block = lax.dynamic_update_index_in_dim(whole, arrived, 1 - mine, dim)
        return self

    def along_z(self):
        while self.plan[0][0][0] == "z":
            self.stage()
        return self

    def rest(self):
        while self.plan:
            self.stage()
        return self.block.reshape(D, self.columns)


class Scatter:
    def __init__(self, terms, x_first):
        self.dims = bits_of("y") + bits_of("x") + bits_of("z")
        order = ("x", "y") if x_first else ("y", "x")
        self.plan = bits_of(order[0]) + bits_of(order[1]) + bits_of("z")[::-1]
        rows = D >> len(self.dims)
        self.terms = [terms.reshape((2,) * len(self.dims) + (rows, terms.shape[1]))]

    def total(self, terms):
        total = terms[0].astype(f32)
        for term in terms[1:]:
            total = total + term.astype(f32)
        return total

    def stage(self):
        step = self.plan.pop(0)
        dim, mine = self.dims.index(step), bit_at(*step)
        self.dims.remove(step)
        sent = self.total([part_of(term, dim, 1 - mine) for term in self.terms]).astype(bf16)
        self.terms = [part_of(term, dim, mine) for term in self.terms]
        self.terms.append(exchanged(sent, *step))
        return self

    def rest(self):
        while self.plan:
            self.stage()
        return self.total(self.terms)


def chain(local, up):
    count = lax.axis_size("z")
    total = jnp.zeros_like(local)
    for hop in range(1, count):
        pair = (hop - 1, hop) if up else (count - hop, count - hop - 1)
        message = (total + local).astype(bf16)
        total = total + lax.ppermute(message, "z", [pair]).astype(f32)
    return total.astype(bf16)


def mesh_exchange(y, x, z, core, axis):
    if axis == "core":
        return (y, x, z, 1 - core)
    if axis == "y":
        return (1 - y, x, z, core)
    if axis == "x":
        return (y, 1 - x, z, core)
    if axis == "z0":
        return (y, x, z + 1 - 2 * (z % 2), core)
    return (y, x, (z + 2) % 4, core)


ORDERS = (("y", "x", "z0", "z1"), ("x", "y", "z0", "z1"))


WIDE = 2 * LANES


def reduce_kernel(
    down_a_ref,
    gate_ref,
    down_b_ref,
    up_ref,
    last_a_ref,
    last_b_ref,
    small_terms_ref,
    qk_ref,
    value_ref,
    out_ref,
    gu_ref,
    down_ref,
    small_ref,
    sums,
    halves,
    quarters,
    finals,
    got_terms,
    got_sums,
    got_halves,
    got_quarters,
    send_sem,
    recv_sem,
    load_sem,
):
    y, x, z, core = places_of()
    places = {"y": y, "x": x, "z0": z % 2, "z1": z // 2}

    parts, count = ([], []), 0
    all_refs = (
        (down_a_ref, gate_ref, last_a_ref),
        (down_b_ref, up_ref, last_b_ref, small_terms_ref),
    )
    for stream, refs in enumerate(all_refs):
        at = 0
        for ref in refs:
            chunks = ref.shape[-1] // WIDE
            parts[stream].append((ref, len(ref.shape) == 3, at, at + chunks))
            at += chunks
        count = max(count, at)
    hidden, width = FC // LANES, VC // LANES
    down_a = (hidden + 1) // 2
    down_b = hidden - down_a
    gate_at, last_a = 2 * parts[0][1][2], 2 * parts[0][2][2]
    up_at, last_b, small_at = (2 * parts[1][at][2] for at in (1, 2, 3))
    places_out = (
        (
            (down_ref, core * hidden, 0, down_a),
            (gu_ref, core * hidden, gate_at, gate_at + hidden),
            (value_ref, core * width, last_a, last_a + width),
            (qk_ref, core, last_a + width, last_a + width + 1),
            (qk_ref, CORES + core, last_a + width + 1, last_a + width + 2),
        ),
        (
            (down_ref, core * hidden + down_a, 0, down_b),
            (gu_ref, (CORES + core) * hidden, up_at, up_at + hidden),
            (out_ref, core * width, last_b, last_b + width),
            (small_ref, core, small_at, small_at + 1),
        ),
    )
    greet(y, x, z, core, True)

    def columns(tile):
        return pl.ds(pl.multiple_of(tile * LANES, LANES), LANES)

    def wide_columns(chunk):
        return pl.ds(pl.multiple_of(chunk * WIDE, WIDE), WIDE)

    def transfer(stream, stage, chunk, source, target=None):
        landing = chunk % 4
        if target is None:
            target = (got_terms, got_sums, got_halves, got_quarters)[stage].at[stream, landing]
        axis = (ORDERS[stream] + ("core", "core"))[stage]
        return pltpu.make_async_remote_copy(
            src_ref=source,
            dst_ref=target,
            send_sem=send_sem.at[stream, stage, landing],
            recv_sem=recv_sem.at[stream, stage, landing],
            device_id=mesh_exchange(y, x, z, core, axis),
            device_id_type=pl.DeviceIdType.MESH,
        )

    def first_view(stream, ref, tile, place):
        ref = ref.at[:, :, :, wide_columns(tile)]
        return ref.at[place] if stream == 0 else ref.at[:, place]

    def source_of(stream, stage, chunk):
        there = 1 - places[ORDERS[stream][stage]]
        if stage == 1:
            return sums.at[stream, chunk % 4, there]
        if stage == 2:
            return halves.at[stream, chunk % 2, :, there]
        return quarters.at[stream, chunk % 2, there]

    def add(a, b):
        return a.astype(f32) + b.astype(f32)

    def load(stream, chunk, ref, start):
        slot = chunk % 4
        return pltpu.make_async_copy(
            ref.at[:, :, wide_columns(chunk - start)], sums.at[stream, slot], load_sem.at[stream, slot]
        )

    def begin(stream, chunk):
        for ref, summed, start, stop in parts[stream]:
            if summed:

                @pl.when((chunk >= start) & (chunk < stop))
                def _(ref=ref, start=start):
                    load(stream, chunk, ref, start).start()

        for ref, _, start, stop in parts[stream][2:]:

            @pl.when((chunk >= start) & (chunk < stop))
            def _(ref=ref, start=start):
                there = 1 - places[ORDERS[stream][0]]
                transfer(stream, 0, chunk, first_view(stream, ref, chunk - start, there)).start()

    def second(stream, chunk):
        for ref, summed, start, stop in parts[stream]:

            @pl.when((chunk >= start) & (chunk < stop))
            def _(ref=ref, summed=summed, start=start):
                tile = chunk - start
                if summed:
                    load(stream, chunk, ref, start).wait()
                else:
                    there = 1 - places[ORDERS[stream][0]]
                    transfer(stream, 0, chunk, first_view(stream, ref, tile, there)).wait()
                    own = first_view(stream, ref, tile, places[ORDERS[stream][0]])[...]
                    sums[stream, chunk % 4] = add(own, got_terms[stream, chunk % 4]).astype(bf16)

        transfer(stream, 1, chunk, source_of(stream, 1, chunk)).start()

    def advance(stream, stage, chunk):
        here = places[ORDERS[stream][stage]]
        slot, landing = chunk % 2, chunk % 4
        transfer(stream, stage, chunk, source_of(stream, stage, chunk)).wait()
        if stage == 1:
            total = add(sums[stream, landing, here], got_sums[stream, landing]).astype(bf16)
            halves[stream, slot] = total.reshape(halves.shape[2:])
        elif stage == 2:
            own = halves[stream, slot, :, here]
            quarters[stream, slot] = add(own, got_halves[stream, landing]).astype(bf16)
        else:
            total = add(quarters[stream, slot, here], got_quarters[stream, landing])
            finals[stream, slot] = total.reshape(finals.shape[2:])
        if stage < 3:
            transfer(stream, stage + 1, chunk, source_of(stream, stage + 1, chunk)).start()

    def hand_over(stream, chunk, waiting):
        for at in range(2):
            tile = 2 * chunk + at
            lanes = slice(at * LANES, (at + 1) * LANES)
            for ref, first, start, stop in places_out[stream]:

                @pl.when((tile >= start) & (tile < stop))
                def _(at=at, tile=tile, lanes=lanes, ref=ref, first=first, start=start):
                    target = ref.at[:, columns(first + tile - start)]
                    source = finals.at[stream, chunk % 2, 1 - core, :, lanes]
                    copy = transfer(stream, 4 + at, chunk, source, target)
                    if waiting:
                        copy.wait()
                    else:
                        target[...] = finals[stream, chunk % 2, core, :, lanes]
                        copy.start()

    @pl.loop(0, count + 5)
    def _(step):
        for stream in range(2):
            total = parts[stream][-1][3]

            @pl.when(step < total)
            def _(stream=stream):
                begin(stream, step)

        for stage in range(5):
            for stream in range(2):
                total = parts[stream][-1][3]

                @pl.when((step >= stage + 1) & (step < total + stage + 1))
                def _(stage=stage, stream=stream):
                    chunk = step - stage - 1
                    if stage == 0:
                        second(stream, chunk)
                    elif stage < 4:
                        advance(stream, stage, chunk)
                    else:
                        hand_over(stream, chunk, True)
                    if stage == 3:
                        hand_over(stream, chunk, False)


def reduced(down_a, gate, down_b, up, last_a, last_b, small, owned):
    block, rows = D // 4, D // 16
    dma = pltpu.SemaphoreType.DMA
    last_a, last_b, small = (last.reshape(2, 2, block, -1) for last in (last_a, last_b, small))
    widths = (2 * CORES * QC, CORES * VC, CORES * VC, 2 * CORES * FC, CORES * FC, CORES * LANES)
    return pl.pallas_call(
        reduce_kernel,
        out_shape=[jax.ShapeDtypeStruct((owned, width), f32) for width in widths],
        in_specs=[pl.BlockSpec(memory_space=pl.ANY)] * 4
        + [pl.BlockSpec(memory_space=pltpu.VMEM)] * 3,
        out_specs=[pl.BlockSpec(memory_space=pltpu.VMEM)] * 6,
        scratch_shapes=[
            pltpu.VMEM((2, 4, 2, block, WIDE), bf16),
            pltpu.VMEM((2, 2, 2, 2, rows, WIDE), bf16),
            pltpu.VMEM((2, 2, 2, rows, WIDE), bf16),
            pltpu.VMEM((2, 2, CORES, owned, WIDE), f32),
            pltpu.VMEM((2, 4, 2, block, WIDE), bf16),
            pltpu.VMEM((2, 4, block, WIDE), bf16),
            pltpu.VMEM((2, 4, 2, rows, WIDE), bf16),
            pltpu.VMEM((2, 4, rows, WIDE), bf16),
            dma((2, 6, 4)),
            dma((2, 6, 4)),
            dma((2, 4)),
        ],
        compiler_params=pltpu.CompilerParams(
            collective_id=0, has_side_effects=True, vmem_limit_bytes=56 << 20
        ),
        cost_estimate=pl.CostEstimate(flops=0, bytes_accessed=1024, transcendentals=0),
    )(down_a, gate, down_b, up, last_a, last_b, small)


def places_of():
    y, x, z, core = (lax.axis_index(axis) for axis in ("y", "x", "z", "core"))
    return y, x, z, core


def greet(y, x, z, core, both_cores=False):
    barrier = pltpu.get_barrier_semaphore()
    partners = ORDERS[0] + (("core",) if both_cores else ())
    for axis in partners:
        pl.semaphore_signal(
            barrier,
            inc=1,
            device_id=mesh_exchange(y, x, z, core, axis),
            device_id_type=pl.DeviceIdType.MESH,
        )
    pl.semaphore_wait(barrier, len(partners))


GATHER_ORDERS = (("z1", "z0", "x", "y"), ("z1", "z0", "y", "x"), ("x", "y", "z1", "z0"))


def gather_view(ref, order, stage, y, x, z):
    if stage == 0:
        return ref.at[y, x, z // 2, z % 2]
    if order == 2:
        if stage == 1:
            return ref.at[y, :, z // 2, z % 2]
        return ref.at[:, :, z // 2, z % 2] if stage == 2 else ref.at[:, :, :, z % 2]
    if stage == 1:
        return ref.at[y, x, :, z % 2]
    if stage == 2:
        return ref.at[y, x]
    return ref.at[y] if order == 0 else ref.at[:, x]


ATTENTION = 2 * QC + 2 * VC + LANES


def gather_kernel(
    qk_ref,
    value_ref,
    out_ref,
    gu_ref,
    down_ref,
    small_ref,
    full_ref,
    late_ref,
    early_ref,
    merged,
    send_sem,
    recv_sem,
    core_send_sem,
    core_recv_sem,
    own_sem,
):
    y, x, z, core = places_of()
    owned = qk_ref.shape[0]
    greet(y, x, z, core, True)

    at, parts = 0, []
    for ref, start, width, apart in (
        (qk_ref, 0, QC, True),
        (qk_ref, CORES * QC, QC, True),
        (value_ref, 0, VC, True),
        (small_ref, 0, LANES, False),
        (out_ref, 0, VC, True),
        (gu_ref, 0, FC, True),
        (gu_ref, FF, FC, True),
        (down_ref, 0, FC, True),
    ):
        parts.append((ref, start, width, apart, at))
        at += width
    my_rows = pl.ds(pl.multiple_of(core * owned, 8), owned)

    def copies(index):
        ref, start, width, apart, at = parts[index]

        def source(which):
            first = pl.multiple_of(start + (which * width if apart else 0), LANES)
            return ref.at[:, pl.ds(first, width)]

        target = merged.at[my_rows, at : at + width]
        remote = pltpu.make_async_remote_copy(
            src_ref=source(1 - core),
            dst_ref=target,
            send_sem=core_send_sem.at[index],
            recv_sem=core_recv_sem.at[index],
            device_id=mesh_exchange(y, x, z, core, "core"),
            device_id_type=pl.DeviceIdType.MESH,
        )
        return remote, pltpu.make_async_copy(source(core), target, own_sem.at[index])

    for index in range(len(parts)):
        for copy in copies(index):
            copy.start()
    for index in range(5):
        for copy in copies(index):
            copy.wait()
    full_ref[y, x, z // 2, z % 2] = merged[:, :ATTENTION].astype(bf16)

    def transfer(stage, tile, order):
        columns = pl.ds(pl.multiple_of(tile * LANES, LANES), LANES)
        view = gather_view(full_ref.at[:, :, :, :, :, columns], order, stage, y, x, z)
        return pltpu.make_async_remote_copy(
            src_ref=view,
            dst_ref=view,
            send_sem=send_sem.at[stage, tile],
            recv_sem=recv_sem.at[stage, tile],
            device_id=mesh_exchange(y, x, z, core, GATHER_ORDERS[order][stage]),
            device_id_type=pl.DeviceIdType.MESH,
        )

    paired = ATTENTION // LANES - ACROSS
    pairs = paired // 2

    def each(step, behind, act):
        for order in range(2):
            tile = 2 * (step - behind) + order

            @pl.when((tile >= 0) & (tile < paired))
            def _(tile=tile, order=order):
                act(tile, order)

    def go_on(tile, order, stage):
        transfer(stage, tile, order).wait()
        if stage < 3:
            transfer(stage + 1, tile, order).start()

    hidden = FC // LANES

    @pl.loop(0, pairs + 4)
    def _(step):
        each(step, 0, lambda tile, order: transfer(0, tile, order).start())
        for stage in range(4):
            each(step, stage + 1, functools.partial(go_on, stage=stage))
        for across in range(ACROSS):

            @pl.when(step == 2 * across)
            def _(across=across):
                transfer(0, paired + across, 2).start()

            for stage in range(4):

                @pl.when(step == 2 * across + stage + 1)
                def _(across=across, stage=stage):
                    go_on(paired + across, 2, stage)

        @pl.when(step == 0)
        def _():
            for index in range(5, len(parts)):
                for copy in copies(index):
                    copy.wait()

        for tile in range(hidden):

            @pl.when(step == tile // 2)
            def _(tile=tile):
                for part in range(3):
                    first = ATTENTION + part * FC + tile * LANES
                    block = merged[:, first : first + LANES].astype(bf16)
                    if tile < EARLY:
                        start = (part * EARLY + tile) * LANES
                        early_ref[:, start : start + LANES] = block
                    else:
                        late_ref[tile - EARLY, :, part * LANES : (part + 1) * LANES] = block


def gathered_weights(w_qk, w_value, w_out, w_gu, w_down, small):
    owned = w_qk.shape[0]
    rows, tiles = CORES * owned, ATTENTION // LANES
    dma = pltpu.SemaphoreType.DMA
    vmem = pl.BlockSpec(memory_space=pltpu.VMEM)
    full, late, early = pl.pallas_call(
        gather_kernel,
        out_shape=[
            jax.ShapeDtypeStruct((2, 2, 2, 2, rows, ATTENTION), bf16),
            jax.ShapeDtypeStruct((FC // LANES - EARLY, rows, 3 * LANES), bf16),
            jax.ShapeDtypeStruct((rows, 3 * EARLY * LANES), bf16),
        ],
        in_specs=[vmem] * 6,
        out_specs=[vmem] * 3,
        scratch_shapes=[
            pltpu.VMEM((rows, ATTENTION + 3 * FC), f32),
            dma((4, tiles)),
            dma((4, tiles)),
            dma((8,)),
            dma((8,)),
            dma((8,)),
        ],
        compiler_params=pltpu.CompilerParams(
            collective_id=1, has_side_effects=True, vmem_limit_bytes=48 << 20
        ),
        cost_estimate=pl.CostEstimate(flops=0, bytes_accessed=1024, transcendentals=0),
    )(w_qk, w_value, w_out, w_gu, w_down, small)
    return full.reshape(D, ATTENTION), late, early


SLOTS = 10
ACROSS = 3


def feed_forward_kernel(
    tiles,
    second_ref,
    grad_ref,
    shard_ref,
    early_ref,
    gate_send_ref,
    gate_keep_ref,
    up_send_ref,
    up_keep_ref,
    down_a_send_ref,
    down_a_keep_ref,
    down_b_send_ref,
    down_b_keep_ref,
    down_own_ref,
    down_other_ref,
    second_own_ref,
    second_other_ref,
    held,
    down_ref,
    grad_second_ref,
    second_t_ref,
    grad_t_ref,
    narrow,
    terms,
    send_sem,
    recv_sem,
    out_sem,
    terms_sem,
    early_sem,
):
    y, x, z, core = places_of()
    streamed = shard_ref.shape[0]
    ready = tiles - streamed
    paired = streamed - ACROSS
    before_across = (ready + paired) // 2 - 2
    count = (tiles + 1) // 2

    def pair_of(turn):
        within = turn - before_across
        between = jnp.where(within % 2 == 0, count - 2 + within // 2, before_across + within // 2)
        return jnp.where(within < 0, turn, between)

    def early_copies(pair):
        copies = []
        for at in range(2):
            for part in range(3):
                start = (part * ready + 2 * pair + at) * LANES
                copies.append(
                    pltpu.make_async_copy(
                        early_ref.at[:, :, :, :, :, start : start + LANES],
                        held.at[SLOTS - 2 + at, :, :, :, :, :, part * LANES : (part + 1) * LANES],
                        early_sem.at[at, part],
                    )
                )
        return copies

    if ready:
        for copy in early_copies(0):
            copy.start()
    down_ref[...] = jnp.zeros_like(down_ref)
    grad_second_ref[...] = jnp.zeros_like(grad_second_ref)
    greet(y, x, z, core)
    tokens = second_ref.shape[0]
    block = 512 if tokens % 512 == 0 else tokens

    def transfer(stage, tile, order):
        slot = SLOTS + tile if order == 2 else tile % SLOTS
        view = gather_view(held.at[slot], order, stage, y, x, z)
        return pltpu.make_async_remote_copy(
            src_ref=view,
            dst_ref=view,
            send_sem=send_sem.at[stage, slot],
            recv_sem=recv_sem.at[stage, slot],
            device_id=mesh_exchange(y, x, z, core, GATHER_ORDERS[order][stage]),
            device_id_type=pl.DeviceIdType.MESH,
        )


    def compute(slots):
        def both(part):
            lanes = slice(part * LANES, (part + 1) * LANES)
            return jnp.concatenate(
                [held[slot, :, :, :, :, :, lanes].reshape(D, LANES) for slot in slots], axis=1
            )

        @pl.loop(0, tokens // block)
        def _(at):
            rows = pl.ds(pl.multiple_of(at * block, block), block)
            gate = dot(second_ref[rows, :], both(0))
            upward = dot(second_ref[rows, :], both(1))
            grad_hidden = dot(grad_ref[rows, :], both(2))
            sigmoid_gate = 1.0 / (1.0 + jnp.exp(-gate))
            silu_gate = gate * sigmoid_gate
            narrow[rows, 2 * WIDE :] = (silu_gate * upward).astype(bf16)
            narrow[rows, WIDE : 2 * WIDE] = (grad_hidden * silu_gate).astype(bf16)
            narrow[rows, :WIDE] = (
                grad_hidden * upward * sigmoid_gate * (1.0 + gate * (1.0 - sigmoid_gate))
            ).astype(bf16)
            down_ref[rows, :] += dot_nt(narrow[rows, 2 * WIDE :], both(2))
            grad_second_ref[rows, :] += dot_nt(narrow[rows, :WIDE], both(0)) + dot_nt(
                narrow[rows, WIDE : 2 * WIDE], both(1)
            )

    quarter = D // 4

    def weight_terms(turn):
        slot = turn % 2

        @pl.loop(0, 2)
        def _(part):
            rows = pl.ds(pl.multiple_of(part * 2 * quarter, 2 * quarter), 2 * quarter)
            grads = dot(second_t_ref[rows, :], narrow[:, : 2 * WIDE]).astype(bf16)
            terms[slot, part, :, :, : 2 * WIDE] = grads.reshape(2, quarter, 2 * WIDE)
            down = dot(grad_t_ref[rows, :], narrow[:, 2 * WIDE :]).astype(bf16)
            terms[slot, part, :, :, 2 * WIDE :] = down.reshape(2, quarter, WIDE)

    def terms_copies(turn):
        slot, pair = turn % 2, pair_of(turn)
        gate, up = (gate_send_ref, gate_keep_ref), (up_send_ref, up_keep_ref)
        first, second = (down_a_send_ref, down_a_keep_ref), (down_b_send_ref, down_b_keep_ref)

        def apart(index, stream, refs, at):
            here = (y, x)[stream]
            columns = pl.ds(pl.multiple_of(at * WIDE, WIDE), WIDE)
            copies = []
            for way, (place, ref) in enumerate(zip((1 - here, here), refs)):
                source = terms.at[slot, :, :, :, index * WIDE : (index + 1) * WIDE]
                source = source.at[place] if stream == 0 else source.at[:, place]
                copies.append(
                    pltpu.make_async_copy(source, ref.at[:, :, columns], terms_sem.at[slot, index, way])
                )
            return copies

        split = (tiles + 1) // 4
        early = pair < split
        return (
            (None, apart(0, 0, gate, pair)),
            (None, apart(1, 1, up, pair)),
            (early, apart(2, 0, first, jnp.where(early, pair, 0))),
            (pair >= split, apart(2, 1, second, jnp.where(early, 0, pair - split))),
        )

    def all_copies(turn, act):
        for condition, copies in terms_copies(turn):
            if condition is None:
                for copy in copies:
                    act(copy)
            else:

                @pl.when(condition)
                def _(copies=copies):
                    for copy in copies:
                        act(copy)

    pairs = paired // 2

    def each(step, behind, act):
        for order in range(2):
            tile = 2 * (step - behind) + order

            @pl.when((tile >= 0) & (tile < paired))
            def _(tile=tile, order=order):
                act(tile, order)

    def send_on(stage):
        def act(tile, order):
            transfer(stage, tile, order).wait()
            transfer(stage + 1, tile, order).start()

        return act

    def work(slots, turn):
        compute(slots)

        @pl.when(turn >= 2)
        def _():
            all_copies(turn - 2, lambda copy: copy.wait())

        weight_terms(turn)
        all_copies(turn, lambda copy: copy.start())

    def begin(tile, order):
        held[tile % SLOTS, y, x, z // 2, z % 2] = shard_ref[tile]
        transfer(0, tile, order).start()

    def work_of(step, across):
        late, first = step - 4, step == pairs + 1
        turn = ready // 2 + late
        turn = jnp.where(turn >= before_across, 2 * turn - before_across + 1, turn)
        turn = jnp.where(step < 4, step - 4 + ready // 2, turn)
        slots = [
            jnp.where(step < 4, SLOTS - 2 + order, (2 * late + order + 2 * SLOTS) % SLOTS)
            for order in range(2)
        ]
        others = (jnp.where(first, SLOTS, SLOTS + 2), jnp.where(first, SLOTS + 1, 2))
        slots = [jnp.where(across == 1, there, here) for here, there in zip(slots, others)]
        return slots, jnp.where(across == 1, before_across + 2 * (step - pairs - 1), turn)

    def begin_across(tile):
        held[SLOTS + tile, y, x, z // 2, z % 2] = shard_ref[paired + tile]
        transfer(0, tile, 2).start()

    def advance_across(step):
        for tile in range(ACROSS):

            @pl.when(step == 2 * tile)
            def _(tile=tile):
                begin_across(tile)

            for stage in range(4):

                @pl.when(step == 2 * tile + stage + 1)
                def _(tile=tile, stage=stage):
                    transfer(stage, tile, 2).wait()
                    if stage < 3:
                        transfer(stage + 1, tile, 2).start()

    @pl.loop(0, pairs + 4)
    def _(step):
        each(step, 2, send_on(1))
        each(step, 3, send_on(2))
        advance_across(step)
        for pair in range(ready // 2):

            @pl.when(step == 4 - ready // 2 + pair)
            def _(pair=pair):
                for copy in early_copies(pair):
                    copy.wait()

        @pl.when(step >= 4)
        def _():
            for order in range(2):
                transfer(3, 2 * (step - 4) + order, order).wait()

        @pl.when(step == pairs + 2)
        def _():
            held[2] = jnp.zeros(held.shape[1:], bf16)

        works = jnp.where((step == pairs + 1) | (step == pairs + 2), 2, 1)

        @pl.loop(0, 2)
        def _(across):
            @pl.when((step >= 4 - ready // 2) & (across < works))
            def _():
                slots, turn = work_of(step, across)
                work(slots, turn)

        for pair in range(ready // 2 - 1):

            @pl.when(step == 4 - ready // 2 + pair)
            def _(pair=pair):
                for copy in early_copies(pair + 1):
                    copy.start()

        each(step, 1, send_on(0))
        each(step, 0, begin)

        @pl.when(step < 2)
        def _():
            rows = pl.ds(pl.multiple_of(step * (tokens // 2), tokens // 2), tokens // 2)
            second_t_ref[:, rows] = second_ref[rows, :].T
            grad_t_ref[:, rows] = grad_ref[rows, :].T

    @pl.loop(count - 2, count)
    def _(turn):
        all_copies(turn, lambda copy: copy.wait())

    half = tokens // 2
    copies = [
        pltpu.make_async_copy(source, target, out_sem.at[at])
        for at, (source, target) in enumerate(
            (
                (grad_second_ref.at[half:], second_other_ref),
                (grad_second_ref.at[:half], second_own_ref),
                (down_ref.at[half:], down_other_ref),
                (down_ref.at[:half], down_own_ref),
            )
        )
    ]
    for copy in copies:
        copy.start()
    for copy in copies:
        copy.wait()


EARLY = 4


def feed_forward(second, grad_result, shard, early):
    tokens = second.shape[0]
    streamed, rows, _ = shard.shape
    tiles = streamed + early.shape[-1] // (3 * LANES)
    down_a = (tiles + 1) // 2
    terms = [
        jax.ShapeDtypeStruct((2, D // 4, count * LANES), bf16)
        for count in (tiles + 1, tiles + 1, down_a, down_a)
        for _ in range(2)
    ]
    part = jax.ShapeDtypeStruct((tokens // 2, D), f32)
    dma = pltpu.SemaphoreType.DMA
    results = pl.pallas_call(
        functools.partial(feed_forward_kernel, tiles),
        out_shape=terms + [part] * 4,
        in_specs=[pl.BlockSpec(memory_space=pltpu.VMEM)] * 3 + [pl.BlockSpec(memory_space=pl.ANY)],
        out_specs=[pl.BlockSpec(memory_space=pl.ANY)] * 12,
        scratch_shapes=[
            pltpu.VMEM((SLOTS + ACROSS, 2, 2, 2, 2, rows, 3 * LANES), bf16),
            pltpu.VMEM((tokens, D), f32),
            pltpu.VMEM((tokens, D), f32),
            pltpu.VMEM((D, tokens), bf16),
            pltpu.VMEM((D, tokens), bf16),
            pltpu.VMEM((tokens, 3 * WIDE), bf16),
            pltpu.VMEM((2, 2, 2, D // 4, 3 * WIDE), bf16),
            dma((4, SLOTS + ACROSS)),
            dma((4, SLOTS + ACROSS)),
            dma((4,)),
            dma((2, 3, 2)),
            dma((2, 3)),
        ],
        compiler_params=pltpu.CompilerParams(
            collective_id=2, has_side_effects=True, vmem_limit_bytes=60 << 20
        ),
        cost_estimate=pl.CostEstimate(flops=0, bytes_accessed=1024, transcendentals=0),
    )(second, grad_result, shard, early)
    return list(zip(results[0:8:2], results[1:8:2])), results[8:]


def norm_scale(values):
    inverse = lax.rsqrt(jnp.mean(values * values, axis=-1, keepdims=True) + norm_epsilon)
    return (values * inverse, inverse)


def norm_backward(grad_normed, scaled, inverse, gain_row):
    grad_scaled = grad_normed * gain_row[None, :]
    grad_input = inverse * (
        grad_scaled - scaled * jnp.mean(grad_scaled * scaled, axis=-1, keepdims=True)
    )
    return (grad_input, jnp.sum(grad_normed * scaled, axis=0))


def adam_update(weight, gradient, first_moment, second_moment, learn_rate, decay_rate):
    first_new = beta_first * first_moment + (1.0 - beta_first) * gradient
    second_new = beta_second * second_moment + (1.0 - beta_second) * gradient * gradient
    first_hat = first_new / (1.0 - beta_first**STEP)
    second_hat = second_new / (1.0 - beta_second**STEP)
    new_weight = (
        weight
        - learn_rate * first_hat / (jnp.sqrt(second_hat) + adam_epsilon)
        - decay_rate * weight
    )
    return (new_weight, second_new)


def local(
    tokens,
    cotangent,
    lengths,
    w_qk,
    w_value,
    w_out,
    w_gu,
    w_down,
    small_params,
    m_qk,
    m_value,
    m_out,
    m_gu,
    m_down,
    m_small,
    v_qk,
    v_value,
    v_out,
    v_gu,
    v_down,
    v_small,
):
    slots, slot_rows, _ = tokens.shape
    owned = w_qk.shape[0]
    rows = slots * slot_rows
    core, z_at = lax.axis_index("core"), lax.axis_index("z")
    other = 1 - core
    first_core = core == 0

    def on_chip(array):
        return jnp.concatenate([array, swapped(array)], axis=0)

    def halves(array):
        return array.reshape(CORES, slots, slot_rows, -1)

    columns_of = [
        w_qk.astype(bf16).reshape(owned, 2, CORES, QC),
        w_value.astype(bf16).reshape(owned, 1, CORES, VC),
        w_out.astype(bf16).reshape(owned, 1, CORES, VC),
        w_gu.astype(bf16).reshape(owned, 2, CORES, FC),
        w_down.astype(bf16).reshape(owned, 1, CORES, FC),
    ]
    small_low = jnp.pad(small_params.astype(bf16), ((0, 0), (0, LANES - (KS + 2))))

    def shard(which, index):
        parts = [part_of(columns_of[i], 2, index).reshape(owned, -1) for i in which]
        return jnp.concatenate(parts, axis=1) if len(parts) > 1 else parts[0]

    def chip_shard(which, extra=None):
        mine, theirs = shard(which, core), shard(which, other)
        arrived = swapped(theirs if extra is None else jnp.concatenate([theirs, extra], axis=1))
        mine = mine if extra is None else jnp.concatenate([mine, extra], axis=1)
        return both_cores(mine, arrived, 0)

    in_kernel = tuple(lax.axis_size(axis) for axis in ("y", "x", "z")) == (2, 2, 4)
    early_width = 2 * QC + VC + LANES
    half = early_width // 2
    cut = FC // 2 // LANES * LANES
    down_at = VC + 2 * FC
    own_tokens = tokens.reshape(rows, D)
    other_tokens = swapped(own_tokens)
    wide_part = 4 * LANES
    if in_kernel:
        small_wide = jnp.pad(small_params, ((0, 0), (0, LANES - (KS + 2))))
        full, late_shard, early_shard = gathered_weights(
            w_qk, w_value, w_out, w_gu, w_down, small_wide
        )
        early, out_half = full[:, :early_width], full[:, early_width:]
        small_full = early[:, early_width - LANES :]
        early_tiles = lax.all_gather(early_shard, ("y", "x", "z"), axis=0)
        early_tiles = early_tiles.reshape(2, 2, 2, 2, CORES * owned, -1)
    else:
        attention_shard = chip_shard((0, 1), small_low)
        rest_shard = chip_shard((2, 3, 4))
        early_a = Gather(attention_shard[:, :half], True)
        early_b = Gather(attention_shard[:, half:], False)
        early = jnp.concatenate([early_a.rest(), early_b.rest()], axis=1)

        def gathered(start, width):
            return lax.all_gather(rest_shard[:, start : start + width], ("y", "x", "z"), axis=0, tiled=True)

        out_half = gathered(0, VC)
        gate_full = gathered(VC, FC)
        up_full = gathered(VC + FC, FC)
        last_shard, early = tied(rest_shard[:, down_at:], early)
        down_a = Gather(last_shard[:, :cut], True)
        down_b = Gather(last_shard[:, cut:], False)
        down_full = jnp.concatenate([down_a.rest(), down_b.rest()], axis=1)
        small_full = early[:, early_width - LANES :]

    qk_full = early[:, : 2 * QC]
    value_full = early[:, 2 * QC : 2 * QC + VC]
    small_float = small_full[:, : KS + 2].astype(f32)
    out_full = both_cores(out_half, swapped(out_half), 1)
    gain_first, gain_second = small_float[:, KS], small_float[:, KS + 1]
    taps = [part_of(small_float[:, j].reshape(CORES, VC), 0, core) for j in range(KS)]

    inputs = tokens.reshape(rows, D).astype(f32)
    scaled_first, inverse_first = norm_scale(inputs)
    scaled_chip, _ = norm_scale(
        jnp.concatenate([own_tokens, other_tokens], axis=0).astype(f32)
    )
    normed_chip = (scaled_chip * gain_first[None, :]).astype(bf16)
    query_key = halves(dot(normed_chip, qk_full).astype(bf16))
    value_pre = halves(dot(normed_chip, value_full).astype(bf16))
    tail = value_pre[:, :, slot_rows - (KS - 1) :, :]
    from_chip = passed_along(part_of(tail, 0, other), "z", 1)
    from_core = part_of(tail, 0, core)
    earlier = jnp.stack(
        [jnp.where(first_core, from_chip, from_core), jnp.where(first_core, from_core, from_chip)]
    )
    extended = jnp.concatenate([earlier, value_pre], axis=2).astype(f32)

    def tap_rows(j):
        return extended[:, :, KS - 1 - j : KS - 1 - j + slot_rows, :]

    convolved = taps[0] * tap_rows(0)
    for j in range(1, KS):
        convolved = convolved + taps[j] * tap_rows(j)
    values = convolved.astype(bf16)

    index_np, scale_np = feature_tables()
    tables = (core.astype(jnp.int32).reshape(1), jnp.asarray(index_np), jnp.asarray(scale_np))
    q_spec, k_spec, v_spec = (LANES, 0), (LANES, 1), (VC,)
    call = functools.partial(per_slot, slots=slots, rows=slot_rows)
    unit = 2 * CORES * rows * HC * LANES * FEATS
    wide = [pltpu.VMEM((CORES * slot_rows, VC), f32)]
    if in_kernel:
        (before,) = linked(key_term, True, 3)(*tables[1:], query_key, values, slots=slots)
    else:
        (state_own,) = call(
            state_kernel, ins=[k_spec, v_spec], outs=[("state", f32)], scratch=[], flops=4 * unit
        )(*tables, query_key, values)
        before = chain(state_own, True)
    mixer, dens = call(
        forward_kernel,
        ins=[q_spec, k_spec, v_spec, "state"],
        outs=[(v_spec, bf16), ((LANES,), f32)],
        scratch=wide,
        flops=8 * unit,
    )(*tables, query_key, query_key, values, before)

    mixer_flat = mixer.reshape(CORES * rows, VC)
    mixer_theirs = swapped(mixer_flat)

    def beside(mine, theirs):
        whole = jnp.zeros((mine.shape[0], CORES * mine.shape[1]), mine.dtype)
        for index, part in ((core, mine), (other, theirs)):
            whole = lax.dynamic_update_slice_in_dim(whole, part, index * mine.shape[1], 1)
        return whole

    mixer_own = beside(mixer_flat[:rows], mixer_theirs[rows:])
    mixer_other = beside(mixer_flat[rows:], mixer_theirs[:rows])
    after_mixer = inputs + dot(mixer_own, out_full)
    scaled_second, inverse_second = norm_scale(after_mixer)
    second_low = (scaled_second * gain_second[None, :]).astype(bf16)
    second_chip = on_chip(second_low)

    half_at = jnp.where(first_core, jnp.arange(CORES), 1 - jnp.arange(CORES))
    positions = (z_at * CORES + half_at)[:, None] * slot_rows + jnp.arange(slot_rows)[None, :]
    valid_chip = positions[:, None, :] < lengths[None, :, None]
    valid_chip = valid_chip.astype(f32).reshape(CORES * rows, 1)
    valid = valid_chip[:rows]
    query_key, cotangent_late = lax.optimization_barrier((query_key, cotangent))
    cotangent_chip = on_chip(cotangent_late.reshape(rows, D))
    mixer, cotangent_chip = tied(mixer, cotangent_chip)
    grad_result_chip = (valid_chip * cotangent_chip.astype(f32)).astype(bf16)
    grad_result = valid * cotangent.reshape(rows, D).astype(f32)

    if in_kernel:
        ffn_terms, ffn_parts = feed_forward(
            second_chip, grad_result_chip, late_shard, early_tiles
        )
        down_own, down_other, second_own, second_other = ffn_parts
        grad_second = second_own + swapped(second_other)
        down_result = down_own + swapped(down_other)
        (send_gate, keep_gate), (send_up, keep_up), *down_pairs = ffn_terms
        (send_down_a, keep_down_a), (send_down_b, keep_down_b) = down_pairs
        got_gate, got_up = exchanged(send_gate, "y", 0), exchanged(send_up, "x", 0)
    else:
        gate = dot(second_chip, gate_full)
        upward = dot(second_chip, up_full)
        sigmoid_gate = jax.nn.sigmoid(gate)
        silu_gate = gate * sigmoid_gate
        hidden = (silu_gate * upward).astype(bf16)
        grad_hidden = dot(grad_result_chip, down_full)
        grad_upward = (grad_hidden * silu_gate).astype(bf16)
        grad_gate = (
            grad_hidden * upward * sigmoid_gate * (1.0 + gate * (1.0 - sigmoid_gate))
        ).astype(bf16)
        second_part = dot_nt(grad_gate, gate_full) + dot_nt(grad_upward, up_full)
        grad_second = second_part[:rows] + swapped(second_part[rows:])
        down_part = dot_nt(hidden, down_full)
        down_result = down_part[:rows] + swapped(down_part[rows:])
    layer_out = (valid * (after_mixer + down_result)).astype(bf16).reshape(tokens.shape)

    grad_after_norm, grad_gain_second = norm_backward(
        grad_second, scaled_second, inverse_second, gain_second
    )
    grad_after = grad_result + grad_after_norm
    grad_after_low = grad_after.astype(bf16)
    grad_mixer = dot_nt(grad_after_low, out_full).astype(bf16)

    def core_columns(array):
        mine, theirs = (
            lax.dynamic_slice_in_dim(array, index * VC, VC, axis=1) for index in (core, other)
        )
        return jnp.concatenate([mine, swapped(theirs)], axis=0)

    grad_mixer_chip = core_columns(grad_mixer)
    grad_after_chip = core_columns(grad_after_low)
    mixer_chip = lax.optimization_barrier(jnp.concatenate([mixer_own, mixer_other], axis=0))

    wide_spec = (HC * LANES,)
    if in_kernel:
        grad_num, from_later = linked(query_term, False, 4)(
            *tables[1:],
            query_key,
            halves(grad_mixer_chip),
            mixer,
            dens,
            slots=slots,
            extra=(jax.ShapeDtypeStruct((CORES, slots, slot_rows, HC * LANES), bf16),),
        )
    else:
        pulled, grad_num = call(
            pull_kernel,
            ins=[q_spec, v_spec, v_spec, (LANES,)],
            outs=[("state", f32), (wide_spec, bf16)],
            scratch=[],
            flops=4 * unit,
        )(*tables, query_key, halves(grad_mixer_chip), mixer, dens)
        from_later = chain(pulled, False)
    grad_query_key, grad_values = call(
        backward_kernel,
        ins=[q_spec, k_spec, v_spec, wide_spec, "state", "state"],
        outs=[((2 * LANES,), bf16), (v_spec, bf16)],
        scratch=wide,
        flops=24 * unit,
    )(*tables, query_key, query_key, values, grad_num, before, from_later)

    if in_kernel:
        got_gate, got_up, send_down_a, send_down_b, grad_values = tied(
            got_gate, got_up, send_down_a, send_down_b, grad_values
        )

        def summed(keep, got):
            return (keep.astype(f32) + got.astype(f32)).astype(bf16)

        sum_gate, sum_up = summed(keep_gate, got_gate), summed(keep_up, got_up)
        sum_down_a = summed(keep_down_a, exchanged(send_down_a, "y", 0))
        sum_down_b = summed(keep_down_b, exchanged(send_down_b, "x", 0))
    head = grad_values[:, :, : KS - 1, :]
    from_chip = passed_along(part_of(head, 0, core), "z", -1)
    from_core = part_of(head, 0, other)
    later = jnp.stack(
        [jnp.where(first_core, from_core, from_chip), jnp.where(first_core, from_chip, from_core)]
    )
    grad_extended = jnp.concatenate([grad_values, later], axis=2).astype(f32)
    grad_pre = taps[0] * grad_extended[:, :, :slot_rows, :]
    for j in range(1, KS):
        grad_pre = grad_pre + taps[j] * grad_extended[:, :, j : j + slot_rows, :]
    grad_pre = grad_pre.reshape(CORES * rows, VC).astype(bf16)
    grad_query_key = grad_query_key.reshape(CORES * rows, 2 * QC)
    grad_values_float = grad_values.astype(f32)
    tap_grads = [jnp.sum(grad_values_float * tap_rows(j), axis=(0, 1, 2)) for j in range(KS)]

    first_other = dot_nt(grad_query_key[rows:], qk_full) + dot_nt(grad_pre[rows:], value_full)
    first_own = dot_nt(grad_query_key[:rows], qk_full) + dot_nt(grad_pre[:rows], value_full)
    grad_first = first_own + swapped(first_other)
    grad_gain_first = jnp.sum(first_own * scaled_chip[:rows], axis=0) + jnp.sum(
        first_other * scaled_chip[rows:], axis=0
    )

    def whole_feature(part):
        return lax.dynamic_update_slice(jnp.zeros((D,), f32), part, (core * VC,))

    small_terms = jnp.stack(
        [whole_feature(part) for part in tap_grads] + [grad_gain_first, grad_gain_second], axis=1
    )
    small_terms = jnp.pad(small_terms, ((0, 0), (0, LANES - (KS + 2)))).astype(bf16)
    if in_kernel:
        empty = jnp.zeros((CORES * rows, LANES), bf16)
        last_a = jnp.concatenate([grad_pre, grad_query_key, empty], axis=1)
        last_b = jnp.concatenate([grad_after_chip, empty], axis=1)
        grad_qk_own, grad_value_own, grad_out_own, grad_gu_own, grad_down_own, small_both = reduced(
            sum_down_a,
            sum_gate,
            sum_down_b,
            sum_up,
            dot_tn(normed_chip, last_a).astype(bf16),
            dot_tn(mixer_chip, last_b).astype(bf16),
            jnp.pad(small_terms, ((0, 0), (0, LANES))),
            owned,
        )
        grad_small_own = (small_both[:, :LANES] + small_both[:, LANES:])[:, : KS + 2]
    else:
        sum_down = Scatter(dot_tn(grad_result_chip, hidden).astype(bf16), True).rest()
        sum_gate = Scatter(dot_tn(second_chip, grad_gate).astype(bf16), False).rest()
        sum_up = Scatter(dot_tn(second_chip, grad_upward).astype(bf16), True).rest()
        sum_value = Scatter(dot_tn(normed_chip, grad_pre).astype(bf16), False).rest()
        sum_out = Scatter(dot_tn(mixer_chip, grad_after_chip).astype(bf16), True).rest()
        qk_terms = dot_tn(normed_chip, grad_query_key).astype(bf16)
        sum_last = Scatter(jnp.concatenate([qk_terms, small_terms], axis=1), True).rest()
    grad_input_norm, _ = norm_backward(grad_first, scaled_first, inverse_first, gain_first)
    input_grad = (grad_after + grad_input_norm).reshape(tokens.shape)

    def rows_of(array, index):
        return part_of(array.reshape(CORES, owned, -1), 0, index)

    def finish(*parts):
        merged = jnp.concatenate(parts, axis=1) if len(parts) > 1 else parts[0]
        mine, theirs = rows_of(merged, core), swapped(rows_of(merged, other))
        return mine.astype(f32), theirs.astype(f32)

    def columns(*parts):
        mine, theirs = finish(*parts)
        return both_cores(mine, theirs, 1)

    def two_columns(mine, theirs, width):
        shape = (owned, 2, 1, width)
        return both_cores(mine.reshape(shape), theirs.reshape(shape), 2).reshape(owned, -1)

    if not in_kernel:
        grad_down_own = columns(sum_down)
        grad_gu_own = two_columns(*finish(sum_gate, sum_up), FC)
        grad_out_own = columns(sum_out)
        grad_value_own = columns(sum_value)
        last_mine, last_theirs = finish(sum_last)
        grad_qk_own = two_columns(last_mine[:, : 2 * QC], last_theirs[:, : 2 * QC], QC)
        grad_small_own = (last_mine + last_theirs)[:, 2 * QC : 2 * QC + KS + 2]

    grads_all = (
        grad_qk_own,
        grad_value_own,
        grad_out_own,
        grad_gu_own,
        grad_down_own,
        grad_small_own,
    )
    masters = (w_qk, w_value, w_out, w_gu, w_down, small_params)
    firsts = (m_qk, m_value, m_out, m_gu, m_down, m_small)
    seconds = (v_qk, v_value, v_out, v_gu, v_down, v_small)
    learn_rates = (
        0.05 / math.sqrt(D),
        0.05 / math.sqrt(D),
        0.05 / math.sqrt(max(D // 128, 1)),
        0.05 / math.sqrt(D),
        0.05 / math.sqrt(0.0003 * FF * SLOT**0.825),
        0.014,
    )
    decays = (weight_decay, weight_decay, weight_decay, weight_decay, weight_decay, 0.0)
    new_weights = []
    new_seconds = []
    for position in range(6):
        updated, moment = adam_update(
            masters[position],
            grads_all[position],
            firsts[position],
            seconds[position],
            learn_rates[position],
            decays[position],
        )
        new_weights.append(updated)
        new_seconds.append(moment)
    return (layer_out, input_grad) + grads_all + tuple(new_weights) + tuple(new_seconds)


def solution(mesh):
    dp, fsdp = mesh.shape["dp"], mesh.shape["fsdp"]
    y_size = 2 if dp % 2 == 0 else 1
    split = Mesh(
        mesh.devices.reshape(y_size, dp // y_size, fsdp // CORES, CORES), ("y", "x", "z", "core")
    )
    slot_axes, row_axes = ("y", "x"), ("z", "core")
    activation = P(slot_axes, row_axes, None)
    weight = P(slot_axes + row_axes, None)
    return jax.shard_map(
        local,
        mesh=split,
        in_specs=(activation, activation, P(slot_axes)) + (weight,) * 18,
        out_specs=(activation, activation) + (weight,) * 18,
        check_vma=False,
    )
```
